32 devices in a mesh: gx: 8 (over z, core), gy: 4 (over y, x).
Axes of the slice: x: 2, y: 2, z: 4, core: 2. Of those that a mesh axis runs over, the one named last changes fastest.
Arguments:
- source: float32 [128, 64, 512], P('gx', 'gy'), may hold values from -20 to 20
- reaction: float32 [128, 64, 512], P('gx', 'gy'), may hold values from 0.005 to 0.5
- boundary_kind: int32 [128, 64, 512], P('gx', 'gy'), may hold values from 0 to 2
- disk_id: int32 [128, 64, 512], P('gx', 'gy'), may hold values from 0 to 119
- disk_mask: int32 [128, 64, 512], P('gx', 'gy'), may hold values 0 or 1
- thrust: float32 [120], replicated, may hold values from -16 to 16
Outputs:
- pressure: float32 [128, 64, 512], P('gx', 'gy')
- coarse_correction: float32 [32, 16, 128], P('gx')
The draws below stay inside these ranges and needn't reach their ends.
All inputs are finite; a program needn't handle non-finite values. No bound on the sum of `disk_mask` on one device may be relied on, other than what follows from the above.
Results may differ from the reference program's by a relative error of at most 0.00002.
Values sent between devices are 32-bit elements; how exact they have to be, the bound alone decides.
No kernel may reach another device: no remote copies, remote signals or barrier semaphores. Data moves between devices by JAX's collectives and lax.ppermute only.
A program may use at most 64 MiB of HBM per device.

```python
import math
import jax
import jax.numpy as jnp

SWEEPS = 4
DISKS = 120
NX = 128
NY = 64
NZ = 512


def draw_source(key, part):
    return jnp.clip(4.0 * jax.random.normal(key, (NX, NY, NZ), jnp.float32), -20.0, 20.0)


def plant(result, stream_key, least, largest):
    longest = result.shape.index(max(result.shape))
    spots = []
    for shift in (0, 1):
        where = [jax.random.randint(jax.random.fold_in(stream_key, axis), (), 0, length) for axis, length in enumerate(result.shape)]
        where[longest] = (where[longest] + shift) % result.shape[longest]
        spots.append(tuple(where))
    return result.at[spots[0]].set(least).at[spots[1]].set(largest)


def block_scale(own_key, dims, pieces, smallest, top_value):
    level, own = 1.0, jax.random.fold_in(own_key, 6)
    for axis_at, parts in pieces:
        steps = jnp.exp(jax.random.uniform(jax.random.fold_in(own, axis_at), (parts,), jnp.float32, smallest / len(pieces), top_value / len(pieces)))
        level = level * jnp.repeat(steps, dims[axis_at] // parts).reshape([-1 if axis == axis_at else 1 for axis in range(len(dims))])
    return level


def noise(own_key, extent, deviation, reach, kind=jnp.bfloat16):
    return jnp.clip(deviation * jax.random.normal(own_key, extent, jnp.float32), -reach, reach).astype(kind)


def setup_inputs(seed: int = 0) -> dict:
    keys = jax.random.split(jax.random.key(seed), 7)
    return {
        "source": draw_source(jax.random.fold_in(keys[6], 71), 0),
        "reaction": jnp.clip(jnp.exp(math.log(0.5) - 4.6051702 * jax.random.uniform(keys[1], (NX, NY, NZ), jnp.float32) ** block_scale(keys[1], (NX, NY, NZ), ((0, 8), (1, 4)), -0.2, 0.2)), 0.005, 0.5),
        "boundary_kind": plant(jax.random.randint(keys[2], (NX, NY, NZ), 0, 3), jax.random.fold_in(keys[2], 1), 0, 2).astype(jnp.int32),
        "disk_id": plant(jax.random.randint(keys[3], (NX, NY, NZ), 0, DISKS), jax.random.fold_in(keys[3], 1), 0, DISKS - 1).astype(jnp.int32),
        "disk_mask": plant((jax.random.randint(keys[4], (NX, NY, NZ), 0, 6) < 1).astype(jnp.int32), jax.random.fold_in(keys[4], 1), 0, 1),
        "thrust": noise(keys[5], (DISKS,), 4.0, 16.0, jnp.float32),
    }


OMEGA = 0.8
WALL_PENALTY = 0.4
INFLOW_PENALTY = 0.2
CHEB_LOW = 0.1
CHEB_HIGH = 2.0


def neighbours(values):
    padded = jnp.pad(values, 1)
    summed = padded[2:, 1:-1, 1:-1] + padded[:-2, 1:-1, 1:-1]
    summed = summed + padded[1:-1, 2:, 1:-1] + padded[1:-1, :-2, 1:-1]
    return summed + padded[1:-1, 1:-1, 2:] + padded[1:-1, 1:-1, :-2]


def relax_once(values, right_side, diagonal):
    applied = diagonal * values - neighbours(values)
    return values + OMEGA * (right_side - applied) / diagonal


def restrict(values):
    return values.reshape(NX // 4, 4, NY // 4, 4, NZ // 4, 4).sum(axis=(1, 3, 5))


def chebyshev(residual, coarse_diagonal):
    centre = (CHEB_HIGH + CHEB_LOW) / 2.0
    half_range = (CHEB_HIGH - CHEB_LOW) / 2.0
    aspect = centre / half_range
    factor = 1.0 / aspect
    inverse = 1.0 / (16.0 * coarse_diagonal)
    direction = inverse * residual / centre
    solution = jnp.zeros_like(residual)
    for number in range(SWEEPS):
        solution = solution + direction
        if number + 1 < SWEEPS:
            applied = 16.0 * (coarse_diagonal * direction - neighbours(direction))
            residual = residual - applied
            factor_next = 1.0 / (2.0 * aspect - factor)
            direction = factor_next * factor * direction + (2.0 * factor_next / half_range) * inverse * residual
            factor = factor_next
    return solution


def reference(source, reaction, boundary_kind, disk_id, disk_mask, thrust):
    penalty = jnp.where(boundary_kind == 1, WALL_PENALTY, jnp.where(boundary_kind == 2, INFLOW_PENALTY, 0.0))
    absorb = reaction + penalty
    diagonal = 6.0 + absorb
    right_side = source + thrust[disk_id] * disk_mask.astype(jnp.float32)
    first = OMEGA * right_side / diagonal
    second = relax_once(first, right_side, diagonal)
    fine_residual = right_side - (diagonal * second - neighbours(second))
    coarse_residual = restrict(fine_residual)
    coarse_absorb = restrict(absorb) / 16.0
    correction = chebyshev(coarse_residual, 6.0 + coarse_absorb)
    spread_out = jnp.repeat(jnp.repeat(jnp.repeat(correction, 4, axis=0), 4, axis=1), 4, axis=2)
    third = second + spread_out
    fourth = relax_once(third, right_side, diagonal)
    pressure = relax_once(fourth, right_side, diagonal)
    return pressure, correction
```

```python
import jax
import jax.numpy as jnp
from jax import lax
from jax.experimental import pallas as pl
from jax.experimental.pallas import tpu as pltpu
from jax.sharding import PartitionSpec as P

SWEEPS = 4
OMEGA = 0.8
WALL_PENALTY = 0.4
INFLOW_PENALTY = 0.2
CHEB_LOW = 0.1
CHEB_HIGH = 2.0
F32 = jnp.float32
VMEM = pl.BlockSpec(memory_space=pltpu.VMEM)


def call(kernel, outs, *args, scratch=(), name=None):
    return pl.pallas_call(
        kernel,
        out_shape=[jax.ShapeDtypeStruct(s, F32) for s in outs],
        in_specs=[VMEM] * len(args),
        out_specs=[VMEM] * len(outs),
        scratch_shapes=[pltpu.VMEM(s, F32) for s in scratch],
        compiler_params=pltpu.CompilerParams(vmem_limit_bytes=16 << 20),
        name=name,
    )(*args)


def pairs_core(nx, ny):
    return [(x * ny + y, (x ^ 1) * ny + y) for x in range(nx) for y in range(ny)]


def pairs_chip(nx, ny):
    found = []
    for x in range(nx):
        for y in range(ny):
            if x in (0, nx - 1):
                found.append((x * ny + y, x * ny + (y ^ 1)))
            else:
                found.append((x * ny + y, (x + 1 if x % 2 else x - 1) * ny + y))
    return found


def pairs_row(nx, ny, step):
    return [(x * ny + y, x * ny + (y ^ step)) for x in range(nx) for y in range(ny)]


def pairs_odd(nx, ny):
    return [
        (x * ny + y, x * ny + (y + 1 if y % 2 else y - 1) % ny) for x in range(nx) for y in range(ny)
    ]


def put(ref, row, slab):
    rows = slab.shape[0]
    for j in range(slab.shape[1] // 128):
        ref[row + rows * j : row + rows * (j + 1), :] = slab[:, 128 * j : 128 * (j + 1)]


def get(ref, row, rows, width):
    return jnp.concatenate(
        [ref[row + rows * j : row + rows * (j + 1), :] for j in range(width // 128)], axis=1
    )


def iota(shape, dim):
    return lax.broadcasted_iota(jnp.int32, shape, dim)


def beside_z(slab):
    depth = slab.shape[1]
    lane = iota(slab.shape, 1)
    above = jnp.where(lane == depth - 1, 0.0, pltpu.roll(slab, depth - 1, 1))
    below = jnp.where(lane == 0, 0.0, pltpu.roll(slab, 1, 1))
    return above + below


def beside_rows(slab, low, high):
    rows = slab.shape[0]
    row = iota(slab.shape, 0)
    above = jnp.where(row == rows - 1, jnp.broadcast_to(high, slab.shape), pltpu.roll(slab, rows - 1, 0))
    below = jnp.where(row == 0, jnp.broadcast_to(low, slab.shape), pltpu.roll(slab, 1, 0))
    return above + below


def dot(left, right):
    return lax.dot_general(
        left,
        right,
        (((1,), (0,)), ((), ())),
        precision=lax.Precision.HIGHEST,
        preferred_element_type=F32,
    )


def group_lanes(depth):
    return (iota((depth, depth // 4), 0) // 4 == iota((depth, depth // 4), 1)).astype(F32)


def spread_lanes(rows):
    count, lanes = rows.shape
    pad = -count % 8
    if pad:
        rows = jnp.concatenate([rows, jnp.zeros((pad, lanes), F32)], axis=0)
    parts = []
    for j in range(4):
        index = iota(rows.shape, 1) // 4 + (lanes // 4) * j
        parts.append(jnp.take_along_axis(rows, index, axis=1, mode="promise_in_bounds"))
    return jnp.concatenate(parts, axis=1)[:count]


def spread_rows(ref, plane, start):
    row = iota((16, 128), 0) // 4
    value = jnp.zeros((16, 128), F32)
    for q in range(4):
        value = jnp.where(row == q, jnp.broadcast_to(ref[plane, start + q : start + q + 1, :], (16, 128)), value)
    return value


def spread_planes(ref, plane, column):
    row = iota((16, 128), 0) // 4
    value = jnp.zeros((16, 128), F32)
    for q in range(4):
        value = jnp.where(row == q, jnp.broadcast_to(ref[plane + q, column : column + 1, :], (16, 128)), value)
    return value


def solution(mesh):
    nx, ny = mesh.shape["gx"], mesh.shape["gy"]
    assert nx % 2 == 0 and ny % 2 == 0 and ny & (ny - 1) == 0
    axes = ("gx", "gy")

    def where_am_i():
        x, y = lax.axis_index("gx"), lax.axis_index("gy")
        return x, y, x % 2 == 0, y % 2 == 0

    def set_up(source, reaction, kind, disk_id, disk_mask, thrust, f, g, d, absorb, core, chip, row, odd, table, y_low, y_high):
        _, _, x_even, y_even = where_am_i()
        table[...] = jnp.zeros(table.shape, F32)
        table[0:1, 0 : thrust.shape[1]] = thrust[...]
        lookup = jnp.broadcast_to(table[0:1, :], (16, 128))

        def group(k, carry):
            total = jnp.zeros((16, 512), F32)
            for q in range(4):
                x = 4 * k + q
                kinds = kind[x]
                a = reaction[x] + jnp.where(kinds == 1, WALL_PENALTY, jnp.where(kinds == 2, INFLOW_PENALTY, 0.0))
                total = total + a
                diagonal = 6.0 + a
                scale = OMEGA / diagonal
                ids = disk_id[x]
                picked = jnp.concatenate(
                    [
                        jnp.take_along_axis(lookup, ids[:, 128 * j : 128 * (j + 1)], axis=1, mode="promise_in_bounds")
                        for j in range(4)
                    ],
                    axis=1,
                )
                first = (source[x] + disk_mask[x].astype(F32) * picked) * scale
                f[x] = first
                g[x] = scale
                d[x] = diagonal
                y_low[pl.ds(x, 1), :] = first[0:1, :]
                y_high[pl.ds(x, 1), :] = first[15:16, :]
            absorb[pl.ds(pl.multiple_of(16 * k, 16), 16), :] = total
            return carry

        lax.fori_loop(0, 4, group, 0)
        near, far = jnp.where(x_even, 15, 0), jnp.where(x_even, 0, 15)
        put(core, 0, f[near])
        put(core, 64, g[near])
        put(chip, 0, f[far])
        put(chip, 64, g[far])
        low, high = y_low[...], y_high[...]
        put(row, 0, jnp.where(y_even, high, low))
        put(odd, 0, jnp.where(y_even, low, high))

    def halo_x(core, chip, row, x, x_even):
        a, b = get(core, row, 16, 512), get(chip, row, 16, 512)
        left = jnp.where(x > 0, jnp.where(x_even, b, a), 0.0)
        right = jnp.where(x < nx - 1, jnp.where(x_even, a, b), 0.0)
        return left, right

    def halo_y(row, odd, at, y, y_even):
        a, b = get(row, at, 16, 512), get(odd, at, 16, 512)
        low = jnp.where(y > 0, jnp.where(y_even, b, a), 0.0)
        high = jnp.where(y < ny - 1, jnp.where(y_even, a, b), 0.0)
        return low, high

    def smooth(f, g, d, absorb, core, chip, row, odd, s, to_core, to_row, to_odd, block, F, lo, hi, S, V, y0, y1, y14, y15, g0, g15):
        x_at, y_at, x_even, y_even = where_am_i()
        left, right = halo_x(core, chip, 0, x_at, x_even)
        F[0], F[17] = left, right
        lo[...], hi[...] = halo_y(row, odd, 0, y_at, y_even)
        zero = jnp.zeros((16, 512), F32)
        S[0], S[17] = zero, zero

        def fill(x, carry):
            F[x + 1] = f[x]
            return carry

        lax.fori_loop(0, 16, fill, 0)

        def sweep(x, carry):
            here = F[x + 1]
            scale = g[x]
            total = F[x] + F[x + 2] + beside_rows(here, lo[pl.ds(x, 1), :], hi[pl.ds(x, 1), :]) + beside_z(here)
            value = 1.2 * here + scale * total
            S[x + 1] = value
            s[x] = value
            y0[pl.ds(x, 1), :] = value[0:1, :]
            y1[pl.ds(x, 1), :] = value[1:2, :]
            y14[pl.ds(x, 1), :] = value[14:15, :]
            y15[pl.ds(x, 1), :] = value[15:16, :]
            g0[pl.ds(x, 1), :] = scale[0:1, :]
            g15[pl.ds(x, 1), :] = scale[15:16, :]
            return carry

        lax.fori_loop(0, 16, sweep, 0)
        nothing = jnp.zeros((1, 512), F32)

        def residual(k, carry):
            total = jnp.zeros((16, 512), F32)
            for q in range(4):
                x = 4 * k + q
                here = S[x + 1]
                total = total + d[x] * (1.25 * F[x + 1] - here) + S[x] + S[x + 2]
                total = total + beside_rows(here, nothing, nothing) + beside_z(here)
            V[pl.ds(pl.multiple_of(16 * k, 16), 16), :] = total
            return carry

        lax.fori_loop(0, 4, residual, 0)
        V[64:128, :] = absorb[...]
        V[128:144, :] = S[1]
        V[144:160, :] = S[16]
        V[160:176, :] = y0[...]
        V[176:192, :] = y15[...]
        out, src = iota((48, 192), 0), iota((48, 192), 1)
        cx, cy = out % 4, out // 8
        in_bulk = (out < 32) & (src < 128) & (src // 64 == (out // 4) % 2)
        bulk = in_bulk & ((src % 64) // 16 == cx) & ((src % 16) // 4 == cy)
        faces = (out >= 32) & (src >= 128) & ((out - 32) // 4 == (src - 128) // 16) & ((src % 16) // 4 == cx)
        picked = dot((bulk | faces).astype(F32), V[...])
        block[...] = dot(picked, group_lanes(512))
        near = jnp.where(x_even, 16, 1)
        inner = jnp.where(x_even, 15, 2)
        put(to_core, 0, S[near])
        put(to_core, 64, S[inner])
        to_core[128:132, :] = jnp.where(x_even, block[36:40, :], block[32:36, :])
        to_core[132:136, :] = jnp.zeros((4, 128), F32)
        for at, (low, high) in enumerate(((y0, y15), (y1, y14), (g0, g15))):
            a, b = low[...], high[...]
            put(to_row, 64 * at, jnp.where(y_even, b, a))
            put(to_odd, 64 * at, jnp.where(y_even, a, b))

    def to_chip_kernel(block, core, s, mine, to_chip):
        _, _, x_even, _ = where_am_i()
        mine[...] = jnp.concatenate([block[0:32, :], block[40:48, :]], axis=0)
        face = core[128:136, :]
        for cy in range(4):
            line = face[cy : cy + 1, :]
            mine[8 * cy : 8 * cy + 1, :] = block[8 * cy : 8 * cy + 1, :] + jnp.where(x_even, 0.0, line)
            mine[8 * cy + 3 : 8 * cy + 4, :] = block[8 * cy + 3 : 8 * cy + 4, :] + jnp.where(x_even, line, 0.0)
        put(to_chip, 0, s[jnp.where(x_even, 0, 15)])
        put(to_chip, 64, s[jnp.where(x_even, 1, 14)])
        to_chip[128:168, :] = mine[...]
        to_chip[168:172, :] = jnp.where(x_even, block[32:36, :], block[36:40, :])
        to_chip[172:176, :] = jnp.zeros((4, 128), F32)

    def from_chip_kernel(mine, block, chip, full, beyond):
        x_at, _, x_even, _ = where_am_i()
        has = jnp.where(x_even, x_at > 0, x_at < nx - 1)
        full[...] = mine[...]
        beyond[...] = chip[128:168, :]
        mine_face = jnp.where(x_even, block[32:36, :], block[36:40, :])
        face = chip[168:176, :]
        for cy in range(4):
            line = jnp.where(has, face[cy : cy + 1, :], 0.0)
            own = mine_face[cy : cy + 1, :]
            a, b = 8 * cy, 8 * cy + 3
            full[a : a + 1, :] = mine[a : a + 1, :] + jnp.where(x_even, line, 0.0)
            full[b : b + 1, :] = mine[b : b + 1, :] + jnp.where(x_even, 0.0, line)
            beyond[a : a + 1, :] = chip[128 + a : 129 + a, :] + jnp.where(x_even, 0.0, own)
            beyond[b : b + 1, :] = chip[128 + b : 129 + b, :] + jnp.where(x_even, own, 0.0)

    def window_kernel(full, beyond, core, chip, s_core, s, window):
        x_at, _, x_even, _ = where_am_i()
        mid = full[...]
        a, b = core[...], beyond[...]
        left, right = jnp.where(x_even, b, a), jnp.where(x_even, a, b)
        for at, block in enumerate((left, mid, right)):
            for cy in range(4):
                window[24 * cy + 4 * at : 24 * cy + 4 * at + 4, :] = block[8 * cy : 8 * cy + 4, :]
                window[24 * cy + 12 + 4 * at : 24 * cy + 16 + 4 * at, :] = block[8 * cy + 4 : 8 * cy + 8, :]
            window[96 + 4 * at : 100 + 4 * at, :] = block[32:36, :]
            window[108 + 4 * at : 112 + 4 * at, :] = block[36:40, :]
        low, high = halo_x(s_core, chip, 0, x_at, x_even)
        for at, line in enumerate((low[0:1, :], low[15:16, :], high[0:1, :], high[15:16, :])):
            put(window, 120 + 4 * at, line)

    planes = 4 * ny

    def finish(*refs):
        f, g, s, a_core, a_chip, a_row, a_odd, s_core, s_chip, s_row, s_odd = refs[:11]
        windows = refs[11 : 11 + ny]
        pressure, coarse = refs[11 + ny : 13 + ny]
        every, res, diag, inv, one, two, sol, Pc, T, U, yl, yh, tl, th, ul, uh = refs[13 + ny :]
        x_at, y_at, x_even, y_even = where_am_i()
        for step, window in enumerate(windows):
            every[jnp.bitwise_xor(y_at, step)] = window[...]

        row = iota((16, 128), 0)
        valid = ((row >= 4) | (x_at > 0)) & ((row < 8) | (x_at < nx - 1)) & (row < 12)
        blank = jnp.zeros((4, 128), F32)

        def twelve(value):
            return jnp.concatenate([value, blank], axis=0)

        centre = (CHEB_HIGH + CHEB_LOW) / 2.0
        half_range = (CHEB_HIGH - CHEB_LOW) / 2.0
        aspect = centre / half_range
        factor = 1.0 / aspect
        empty = jnp.zeros((16, 128), F32)
        for ref in (one, two, sol):
            ref[0] = empty
            ref[planes + 1] = empty
        for at in range(ny):
            for cy in range(4):
                plane = 4 * at + cy
                value = every[at, 24 * cy : 24 * cy + 12, :]
                if cy == 0 and at > 0:
                    value = value + every[at - 1, 108:120, :]
                if cy == 3 and at < ny - 1:
                    value = value + every[at + 1, 96:108, :]
                value = jnp.where(valid, twelve(value), 0.0)
                centre_value = 6.0 + twelve(every[at, 24 * cy + 12 : 24 * cy + 24, :]) / 16.0
                inverse = jnp.where(valid, 1.0 / (16.0 * centre_value), 0.0)
                res[plane] = value
                diag[plane] = centre_value
                inv[plane] = inverse
                direction = inverse * value / centre
                one[plane + 1] = direction
                sol[plane + 1] = direction
        now, later = one, two
        for number in range(1, SWEEPS):
            factor_next = 1.0 / (2.0 * aspect - factor)
            keep, gain = factor_next * factor, 2.0 * factor_next / half_range

            def step(plane, carry, now=now, later=later, keep=keep, gain=gain):
                here = now[plane + 1]
                lane = iota((16, 128), 1)
                total = now[plane] + now[plane + 2]
                total = total + pltpu.roll(here, 15, 0) + pltpu.roll(here, 1, 0)
                total = total + jnp.where(lane == 127, 0.0, pltpu.roll(here, 127, 1))
                total = total + jnp.where(lane == 0, 0.0, pltpu.roll(here, 1, 1))
                residual = res[plane] - 16.0 * (diag[plane] * here - total)
                res[plane] = residual
                direction = keep * here + gain * inv[plane] * residual
                later[plane + 1] = direction
                sol[plane + 1] = sol[plane + 1] + direction
                return carry

            lax.fori_loop(0, planes, step, 0)
            now, later = later, now
            factor = factor_next
        for plane in range(planes):
            for cx in range(4):
                coarse[cx, plane : plane + 1, :] = sol[plane + 1, 4 + cx : 5 + cx, :]

        first_plane = 4 * y_at + 1
        for at in range(6):
            Pc[at] = spread_lanes(spread_planes(sol, first_plane, 3 + at))
        s_left, s_right = halo_x(s_core, s_chip, 0, x_at, x_even)
        s_left2, s_right2 = halo_x(s_core, s_chip, 64, x_at, x_even)
        T[0], T[1] = s_left2 + Pc[0], s_left + Pc[0]
        T[18], T[19] = s_right + Pc[5], s_right2 + Pc[5]

        def third(x, carry):
            T[x + 2] = s[x] + Pc[x // 4 + 1]
            return carry

        lax.fori_loop(0, 16, third, 0)
        below, above = first_plane - 1, first_plane + 4
        y1_low, y1_high = halo_y(s_row, s_odd, 0, y_at, y_even)
        y2_low, y2_high = halo_y(s_row, s_odd, 64, y_at, y_even)
        g_low, g_high = halo_y(s_row, s_odd, 128, y_at, y_even)
        f_low, f_high = halo_y(a_row, a_odd, 0, y_at, y_even)
        before, after = jnp.maximum(y_at - 1, 0), jnp.minimum(y_at + 1, ny - 1)
        outer = {}
        for name, ref, plane, s1, s2, who, inside, line in (
            ("low", tl, below, y1_low, y2_low, before, y_at > 0, 1),
            ("high", th, above, y1_high, y2_high, after, y_at < ny - 1, 0),
        ):
            spread = spread_lanes(spread_rows(sol, plane, 4))
            ref[8:24, :] = s1 + spread
            outer[name] = s2 + spread
            for at, cx, base, there in ((7, 3, 0, x_at > 0), (24, 8, 2, x_at < nx - 1)):
                corner = jnp.concatenate(
                    [every[who, pl.ds(120 + 4 * (base + line) + j, 1), :] for j in range(4)], axis=1
                )
                corner = jnp.where(inside & there, corner, 0.0)
                ref[at : at + 1, :] = corner + spread_lanes(sol[plane, cx : cx + 1, :])

        f_left, f_right = halo_x(a_core, a_chip, 0, x_at, x_even)
        g_left, g_right = halo_x(a_core, a_chip, 64, x_at, x_even)

        def fourth_at(at, forcing, scale):
            here = T[at + 1]
            total = T[at] + T[at + 2] + beside_z(here)
            total = total + beside_rows(here, tl[pl.ds(at + 7, 1), :], th[pl.ds(at + 7, 1), :])
            return 0.2 * here + forcing + scale * total

        U[0] = fourth_at(0, f_left, g_left)
        U[17] = fourth_at(17, f_right, g_right)

        def fourth(x, carry):
            U[x + 1] = fourth_at(x + 1, f[x], g[x])
            here = T[x + 2]
            yl[pl.ds(x, 1), :] = here[0:1, :]
            yh[pl.ds(x, 1), :] = here[15:16, :]
            return carry

        lax.fori_loop(0, 16, fourth, 0)
        for ref, out, edge, far, forcing, scale in (
            (tl, ul, yl, outer["low"], f_low, g_low),
            (th, uh, yh, outer["high"], f_high, g_high),
        ):
            here = ref[8:24, :]
            total = far + edge[...] + ref[7:23, :] + ref[9:25, :] + beside_z(here)
            out[...] = 0.2 * here + forcing + scale * total

        def fifth(x, carry):
            here = U[x + 1]
            total = U[x] + U[x + 2] + beside_z(here)
            total = total + beside_rows(here, ul[pl.ds(x, 1), :], uh[pl.ds(x, 1), :])
            pressure[x] = 0.2 * here + f[x] + g[x] * total
            return carry

        lax.fori_loop(0, 16, fifth, 0)

    slab, field, long = (16, 512), (16, 16, 512), (18, 16, 512)
    core_pairs, chip_pairs = pairs_core(nx, ny), pairs_chip(nx, ny)
    row_pairs = [pairs_row(nx, ny, step) for step in range(1, ny)]
    odd_pairs = pairs_odd(nx, ny)

    def swap(array, pairs):
        return lax.ppermute(array, axes, pairs)

    def local(source, reaction, boundary_kind, disk_id, disk_mask, thrust):
        f, g, d, absorb, core, chip, row, odd = call(
            set_up,
            [field, field, field, (64, 512), (128, 128), (128, 128), (64, 128), (64, 128)],
            source, reaction, boundary_kind, disk_id, disk_mask, thrust.reshape(1, -1),
            scratch=[(8, 128), slab, slab],
            name="set_up",
        )
        a_row, a_odd = swap(row, row_pairs[0]), swap(odd, odd_pairs)
        a_chip, a_core = swap(chip, chip_pairs), swap(core, core_pairs)
        s, to_core, to_row, to_odd, block = call(
            smooth,
            [field, (136, 128), (192, 128), (192, 128), (48, 128)],
            f, g, d, absorb, a_core, a_chip, a_row, a_odd,
            scratch=[long, slab, slab, long, (192, 512), slab, slab, slab, slab, slab, slab],
            name="smooth",
        )
        s_core = swap(to_core, core_pairs)
        s_row, s_odd = swap(to_row, row_pairs[0]), swap(to_odd, odd_pairs)
        mine, to_chip = call(to_chip_kernel, [(40, 128), (176, 128)], block, s_core, s, name="to_chip")
        s_chip = swap(to_chip, chip_pairs)
        full, beyond = call(from_chip_kernel, [(40, 128), (40, 128)], mine, block, s_chip, name="from_chip")
        c_core = swap(full, core_pairs)
        (window,) = call(window_kernel, [(136, 128)], full, beyond, c_core, s_chip, s_core, s, name="window")
        windows = [window] + [swap(window, pairs) for pairs in row_pairs]
        pressure, coarse = call(
            finish,
            [field, (4, planes, 128)],
            f, g, s, a_core, a_chip, a_row, a_odd, s_core, s_chip, s_row, s_odd, *windows,
            scratch=[(ny, 136, 128)]
            + [(planes, 16, 128)] * 3
            + [(planes + 2, 16, 128)] * 3
            + [(6, 16, 512), (20, 16, 512), long, slab, slab, (32, 512), (32, 512), slab, slab],
            name="finish",
        )
        return pressure, coarse

    spec = P("gx", "gy", None)
    return jax.shard_map(
        local,
        mesh=mesh,
        in_specs=(spec, spec, spec, spec, spec, P()),
        out_specs=(spec, P("gx", None, None)),
        check_vma=False,
    )
```

```python
import jax
import jax.numpy as jnp
from jax import lax
from jax.experimental import pallas as pl
from jax.experimental.pallas import tpu as pltpu
from jax.sharding import PartitionSpec as P

SWEEPS = 4
OMEGA = 0.8
WALL_PENALTY = 0.4
INFLOW_PENALTY = 0.2
CHEB_LOW = 0.1
CHEB_HIGH = 2.0
F32 = jnp.float32
VMEM = pl.BlockSpec(memory_space=pltpu.VMEM)


HBM = pl.BlockSpec(memory_space=pltpu.HBM)


def call(kernel, outs, *args, scratch=(), name=None, in_specs=None, out_specs=None):
    return pl.pallas_call(
        kernel,
        out_shape=[jax.ShapeDtypeStruct(s, F32) for s in outs],
        in_specs=in_specs or [VMEM] * len(args),
        out_specs=out_specs or [VMEM] * len(outs),
        scratch_shapes=[pltpu.VMEM(s, F32) if isinstance(s, tuple) else s for s in scratch],
        compiler_params=pltpu.CompilerParams(vmem_limit_bytes=16 << 20),
        name=name,
    )(*args)


def pairs_core(nx, ny):
    return [(x * ny + y, (x ^ 1) * ny + y) for x in range(nx) for y in range(ny)]


def pairs_chip(nx, ny):
    found = []
    for x in range(nx):
        for y in range(ny):
            if x in (0, nx - 1):
                found.append((x * ny + y, x * ny + (y ^ 1)))
            else:
                found.append((x * ny + y, (x + 1 if x % 2 else x - 1) * ny + y))
    return found


def pairs_row(nx, ny, step):
    return [(x * ny + y, x * ny + (y ^ step)) for x in range(nx) for y in range(ny)]


def pairs_odd(nx, ny):
    return [
        (x * ny + y, x * ny + (y + 1 if y % 2 else y - 1) % ny) for x in range(nx) for y in range(ny)
    ]


def put(ref, row, slab):
    rows = slab.shape[0]
    for j in range(slab.shape[1] // 128):
        ref[row + rows * j : row + rows * (j + 1), :] = slab[:, 128 * j : 128 * (j + 1)]


def get(ref, row, rows, width):
    return jnp.concatenate(
        [ref[row + rows * j : row + rows * (j + 1), :] for j in range(width // 128)], axis=1
    )


def iota(shape, dim):
    return lax.broadcasted_iota(jnp.int32, shape, dim)


def beside_z(slab):
    depth = slab.shape[1]
    lane = iota(slab.shape, 1)
    above = jnp.where(lane == depth - 1, 0.0, pltpu.roll(slab, depth - 1, 1))
    below = jnp.where(lane == 0, 0.0, pltpu.roll(slab, 1, 1))
    return above + below


def beside_rows(slab, low, high):
    rows = slab.shape[0]
    row = iota(slab.shape, 0)
    above = jnp.where(row == rows - 1, jnp.broadcast_to(high, slab.shape), pltpu.roll(slab, rows - 1, 0))
    below = jnp.where(row == 0, jnp.broadcast_to(low, slab.shape), pltpu.roll(slab, 1, 0))
    return above + below


def dot(left, right):
    return lax.dot_general(
        left,
        right,
        (((1,), (0,)), ((), ())),
        precision=lax.Precision.HIGHEST,
        preferred_element_type=F32,
    )


def group_lanes(depth):
    return (iota((depth, depth // 4), 0) // 4 == iota((depth, depth // 4), 1)).astype(F32)


def spread_lanes(rows):
    count, lanes = rows.shape
    pad = -count % 8
    if pad:
        rows = jnp.concatenate([rows, jnp.zeros((pad, lanes), F32)], axis=0)
    parts = []
    for j in range(4):
        index = iota(rows.shape, 1) // 4 + (lanes // 4) * j
        parts.append(jnp.take_along_axis(rows, index, axis=1, mode="promise_in_bounds"))
    return jnp.concatenate(parts, axis=1)[:count]


def spread_rows(ref, plane, start):
    row = iota((16, 128), 0) // 4
    value = jnp.zeros((16, 128), F32)
    for q in range(4):
        value = jnp.where(row == q, jnp.broadcast_to(ref[plane, start + q : start + q + 1, :], (16, 128)), value)
    return value


def spread_planes(ref, plane, column):
    row = iota((16, 128), 0) // 4
    value = jnp.zeros((16, 128), F32)
    for q in range(4):
        value = jnp.where(row == q, jnp.broadcast_to(ref[plane + q, column : column + 1, :], (16, 128)), value)
    return value


def solution(mesh):
    nx, ny = mesh.shape["gx"], mesh.shape["gy"]
    assert nx % 2 == 0 and ny % 2 == 0 and ny & (ny - 1) == 0
    axes = ("gx", "gy")

    def where_am_i():
        x, y = lax.axis_index("gx"), lax.axis_index("gy")
        return x, y, x % 2 == 0, y % 2 == 0

    def set_up(
        source_hbm, reaction_hbm, kind_hbm, id_hbm, mask_hbm, thrust_hbm,
        f, g, d, absorb, core, chip, row, odd,
        source, reaction, kind, disk_id, disk_mask, table, y_low, y_high, sems, table_sem,
    ):
        _, _, x_even, y_even = where_am_i()
        moves = []
        arrays = (
            (source_hbm, source), (reaction_hbm, reaction), (kind_hbm, kind), (id_hbm, disk_id), (mask_hbm, disk_mask)
        )
        table_move = pltpu.make_async_copy(thrust_hbm, table, table_sem)
        table_move.start()
        for k in range(4):
            part = pl.ds(4 * k, 4)
            moves.append(
                [pltpu.make_async_copy(a.at[part], b.at[part], sems.at[k, i]) for i, (a, b) in enumerate(arrays)]
            )
            for move in moves[k]:
                move.start()
        table_move.wait()
        spare = jnp.zeros((1, 128 - table.shape[1]), F32)
        lookup = jnp.broadcast_to(jnp.concatenate([table[...], spare], axis=1), (16, 128))

        for k in range(4):
            for move in moves[k]:
                move.wait()
            total = jnp.zeros((16, 512), F32)
            for x in range(4 * k, 4 * k + 4):
                kinds = kind[x]
                a = reaction[x] + jnp.where(kinds == 1, WALL_PENALTY, jnp.where(kinds == 2, INFLOW_PENALTY, 0.0))
                total = total + a
                diagonal = 6.0 + a
                scale = OMEGA / diagonal
                ids = disk_id[x]
                picked = jnp.concatenate(
                    [
                        jnp.take_along_axis(lookup, ids[:, 128 * j : 128 * (j + 1)], axis=1, mode="promise_in_bounds")
                        for j in range(4)
                    ],
                    axis=1,
                )
                first = (source[x] + disk_mask[x].astype(F32) * picked) * scale
                f[x] = first
                g[x] = scale
                d[x] = diagonal
                y_low[x : x + 1, :] = first[0:1, :]
                y_high[x : x + 1, :] = first[15:16, :]
            absorb[16 * k : 16 * k + 16, :] = total
        near, far = jnp.where(x_even, 15, 0), jnp.where(x_even, 0, 15)
        put(core, 0, f[near])
        put(core, 64, g[near])
        put(chip, 0, f[far])
        put(chip, 64, g[far])
        low, high = y_low[...], y_high[...]
        put(row, 0, jnp.where(y_even, high, low))
        put(odd, 0, jnp.where(y_even, low, high))

    def halo_x(core, chip, row, x, x_even):
        a, b = get(core, row, 16, 512), get(chip, row, 16, 512)
        left = jnp.where(x > 0, jnp.where(x_even, b, a), 0.0)
        right = jnp.where(x < nx - 1, jnp.where(x_even, a, b), 0.0)
        return left, right

    def halo_y(row, odd, at, y, y_even):
        a, b = get(row, at, 16, 512), get(odd, at, 16, 512)
        low = jnp.where(y > 0, jnp.where(y_even, b, a), 0.0)
        high = jnp.where(y < ny - 1, jnp.where(y_even, a, b), 0.0)
        return low, high

    def smooth(f, g, d, absorb, core, chip, row, odd, s, to_core, to_row, to_odd, block, lo, hi, V, y0, y1, y14, y15, g0, g15):
        x_at, y_at, x_even, y_even = where_am_i()
        left, right = halo_x(core, chip, 0, x_at, x_even)
        lo[...], hi[...] = halo_y(row, odd, 0, y_at, y_even)
        for x in range(16):
            here = f[x]
            scale = g[x]
            total = (f[x - 1] if x > 0 else left) + (f[x + 1] if x < 15 else right)
            total = total + beside_rows(here, lo[x : x + 1, :], hi[x : x + 1, :]) + beside_z(here)
            value = 1.2 * here + scale * total
            s[x] = value
            y0[x : x + 1, :] = value[0:1, :]
            y1[x : x + 1, :] = value[1:2, :]
            y14[x : x + 1, :] = value[14:15, :]
            y15[x : x + 1, :] = value[15:16, :]
            g0[x : x + 1, :] = scale[0:1, :]
            g15[x : x + 1, :] = scale[15:16, :]
        nothing = jnp.zeros((1, 512), F32)
        for k in range(4):
            total = jnp.zeros((16, 512), F32)
            for x in range(4 * k, 4 * k + 4):
                here = s[x]
                total = total + d[x] * (1.25 * f[x] - here)
                total = total + beside_rows(here, nothing, nothing) + beside_z(here)
                if x > 0:
                    total = total + s[x - 1]
                if x < 15:
                    total = total + s[x + 1]
            V[16 * k : 16 * k + 16, :] = total
        V[64:128, :] = absorb[...]
        V[128:144, :] = s[0]
        V[144:160, :] = s[15]
        V[160:176, :] = y0[...]
        V[176:192, :] = y15[...]
        out, src = iota((48, 192), 0), iota((48, 192), 1)
        cx, cy = out % 4, out // 8
        in_bulk = (out < 32) & (src < 128) & (src // 64 == (out // 4) % 2)
        bulk = in_bulk & ((src % 64) // 16 == cx) & ((src % 16) // 4 == cy)
        faces = (out >= 32) & (src >= 128) & ((out - 32) // 4 == (src - 128) // 16) & ((src % 16) // 4 == cx)
        picked = dot((bulk | faces).astype(F32), V[...])
        block[...] = dot(picked, group_lanes(512))
        put(to_core, 0, s[jnp.where(x_even, 15, 0)])
        put(to_core, 64, s[jnp.where(x_even, 14, 1)])
        to_core[128:132, :] = jnp.where(x_even, block[36:40, :], block[32:36, :])
        to_core[132:136, :] = jnp.zeros((4, 128), F32)
        for at, (low, high) in enumerate(((y0, y15), (y1, y14), (g0, g15))):
            a, b = low[...], high[...]
            put(to_row, 64 * at, jnp.where(y_even, b, a))
            put(to_odd, 64 * at, jnp.where(y_even, a, b))

    def to_chip_kernel(block, core, s, mine, to_chip):
        _, _, x_even, _ = where_am_i()
        mine[...] = jnp.concatenate([block[0:32, :], block[40:48, :]], axis=0)
        face = core[128:136, :]
        for cy in range(4):
            line = face[cy : cy + 1, :]
            mine[8 * cy : 8 * cy + 1, :] = block[8 * cy : 8 * cy + 1, :] + jnp.where(x_even, 0.0, line)
            mine[8 * cy + 3 : 8 * cy + 4, :] = block[8 * cy + 3 : 8 * cy + 4, :] + jnp.where(x_even, line, 0.0)
        put(to_chip, 0, s[jnp.where(x_even, 0, 15)])
        put(to_chip, 64, s[jnp.where(x_even, 1, 14)])
        to_chip[128:168, :] = mine[...]
        to_chip[168:172, :] = jnp.where(x_even, block[32:36, :], block[36:40, :])
        to_chip[172:176, :] = jnp.zeros((4, 128), F32)

    def from_chip_kernel(mine, block, chip, full, beyond):
        x_at, _, x_even, _ = where_am_i()
        has = jnp.where(x_even, x_at > 0, x_at < nx - 1)
        full[...] = mine[...]
        beyond[...] = chip[128:168, :]
        mine_face = jnp.where(x_even, block[32:36, :], block[36:40, :])
        face = chip[168:176, :]
        for cy in range(4):
            line = jnp.where(has, face[cy : cy + 1, :], 0.0)
            own = mine_face[cy : cy + 1, :]
            a, b = 8 * cy, 8 * cy + 3
            full[a : a + 1, :] = mine[a : a + 1, :] + jnp.where(x_even, line, 0.0)
            full[b : b + 1, :] = mine[b : b + 1, :] + jnp.where(x_even, 0.0, line)
            beyond[a : a + 1, :] = chip[128 + a : 129 + a, :] + jnp.where(x_even, 0.0, own)
            beyond[b : b + 1, :] = chip[128 + b : 129 + b, :] + jnp.where(x_even, own, 0.0)

    def window_kernel(full, beyond, core, chip, s_core, s, window):
        x_at, _, x_even, _ = where_am_i()
        mid = full[...]
        a, b = core[...], beyond[...]
        left, right = jnp.where(x_even, b, a), jnp.where(x_even, a, b)
        for at, block in enumerate((left, mid, right)):
            for cy in range(4):
                window[24 * cy + 4 * at : 24 * cy + 4 * at + 4, :] = block[8 * cy : 8 * cy + 4, :]
                window[24 * cy + 12 + 4 * at : 24 * cy + 16 + 4 * at, :] = block[8 * cy + 4 : 8 * cy + 8, :]
            window[96 + 4 * at : 100 + 4 * at, :] = block[32:36, :]
            window[108 + 4 * at : 112 + 4 * at, :] = block[36:40, :]
        low, high = halo_x(s_core, chip, 0, x_at, x_even)
        for at, line in enumerate((low[0:1, :], low[15:16, :], high[0:1, :], high[15:16, :])):
            put(window, 120 + 4 * at, line)

    planes = 4 * ny

    def finish(*refs):
        f, g, s, a_core, a_chip, a_row, a_odd, s_core, s_chip, s_row, s_odd = refs[:11]
        windows = refs[11 : 11 + ny]
        pressure, coarse = refs[11 + ny : 13 + ny]
        every, res, diag, inv, one, two, sol, Pc, T, U, yl, yh, tl, th, ul, uh, result, sems = refs[13 + ny :]
        x_at, y_at, x_even, y_even = where_am_i()
        for step, window in enumerate(windows):
            every[jnp.bitwise_xor(y_at, step)] = window[...]

        row = iota((16, 128), 0)
        valid = ((row >= 4) | (x_at > 0)) & ((row < 8) | (x_at < nx - 1)) & (row < 12)
        blank = jnp.zeros((4, 128), F32)

        def twelve(value):
            return jnp.concatenate([value, blank], axis=0)

        centre = (CHEB_HIGH + CHEB_LOW) / 2.0
        half_range = (CHEB_HIGH - CHEB_LOW) / 2.0
        aspect = centre / half_range
        factor = 1.0 / aspect
        empty = jnp.zeros((16, 128), F32)
        for ref in (one, two, sol):
            ref[0] = empty
            ref[planes + 1] = empty
        for at in range(ny):
            for cy in range(4):
                plane = 4 * at + cy
                value = every[at, 24 * cy : 24 * cy + 12, :]
                if cy == 0 and at > 0:
                    value = value + every[at - 1, 108:120, :]
                if cy == 3 and at < ny - 1:
                    value = value + every[at + 1, 96:108, :]
                value = jnp.where(valid, twelve(value), 0.0)
                centre_value = 6.0 + twelve(every[at, 24 * cy + 12 : 24 * cy + 24, :]) / 16.0
                inverse = jnp.where(valid, 1.0 / (16.0 * centre_value), 0.0)
                res[plane] = value
                diag[plane] = centre_value
                inv[plane] = inverse
                direction = inverse * value / centre
                one[plane + 1] = direction
                sol[plane + 1] = direction
        now, later = one, two
        for number in range(1, SWEEPS):
            factor_next = 1.0 / (2.0 * aspect - factor)
            keep, gain = factor_next * factor, 2.0 * factor_next / half_range

            lane = iota((16, 128), 1)
            for plane in range(planes):
                here = now[plane + 1]
                total = now[plane] + now[plane + 2]
                total = total + pltpu.roll(here, 15, 0) + pltpu.roll(here, 1, 0)
                total = total + jnp.where(lane == 127, 0.0, pltpu.roll(here, 127, 1))
                total = total + jnp.where(lane == 0, 0.0, pltpu.roll(here, 1, 1))
                residual = res[plane] - 16.0 * (diag[plane] * here - total)
                res[plane] = residual
                direction = keep * here + gain * inv[plane] * residual
                later[plane + 1] = direction
                sol[plane + 1] = sol[plane + 1] + direction
            now, later = later, now
            factor = factor_next
        for plane in range(planes):
            for cx in range(4):
                coarse[cx, plane : plane + 1, :] = sol[plane + 1, 4 + cx : 5 + cx, :]

        first_plane = 4 * y_at + 1
        for at in range(6):
            Pc[at] = spread_lanes(spread_planes(sol, first_plane, 3 + at))
        s_left, s_right = halo_x(s_core, s_chip, 0, x_at, x_even)
        s_left2, s_right2 = halo_x(s_core, s_chip, 64, x_at, x_even)
        T[0], T[1] = s_left2 + Pc[0], s_left + Pc[0]
        T[18], T[19] = s_right + Pc[5], s_right2 + Pc[5]

        for x in range(16):
            T[x + 2] = s[x] + Pc[x // 4 + 1]
        below, above = first_plane - 1, first_plane + 4
        y1_low, y1_high = halo_y(s_row, s_odd, 0, y_at, y_even)
        y2_low, y2_high = halo_y(s_row, s_odd, 64, y_at, y_even)
        g_low, g_high = halo_y(s_row, s_odd, 128, y_at, y_even)
        f_low, f_high = halo_y(a_row, a_odd, 0, y_at, y_even)
        before, after = jnp.maximum(y_at - 1, 0), jnp.minimum(y_at + 1, ny - 1)
        outer = {}
        for name, ref, plane, s1, s2, who, inside, line in (
            ("low", tl, below, y1_low, y2_low, before, y_at > 0, 1),
            ("high", th, above, y1_high, y2_high, after, y_at < ny - 1, 0),
        ):
            spread = spread_lanes(spread_rows(sol, plane, 4))
            ref[8:24, :] = s1 + spread
            outer[name] = s2 + spread
            for at, cx, base, there in ((7, 3, 0, x_at > 0), (24, 8, 2, x_at < nx - 1)):
                corner = jnp.concatenate(
                    [every[who, pl.ds(120 + 4 * (base + line) + j, 1), :] for j in range(4)], axis=1
                )
                corner = jnp.where(inside & there, corner, 0.0)
                ref[at : at + 1, :] = corner + spread_lanes(sol[plane, cx : cx + 1, :])

        f_left, f_right = halo_x(a_core, a_chip, 0, x_at, x_even)
        g_left, g_right = halo_x(a_core, a_chip, 64, x_at, x_even)

        def fourth_at(at, forcing, scale):
            here = T[at + 1]
            total = T[at] + T[at + 2] + beside_z(here)
            total = total + beside_rows(here, tl[at + 7 : at + 8, :], th[at + 7 : at + 8, :])
            return 0.2 * here + forcing + scale * total

        U[0] = fourth_at(0, f_left, g_left)
        U[17] = fourth_at(17, f_right, g_right)

        for x in range(16):
            U[x + 1] = fourth_at(x + 1, f[x], g[x])
            here = T[x + 2]
            yl[x : x + 1, :] = here[0:1, :]
            yh[x : x + 1, :] = here[15:16, :]
        for ref, out, edge, far, forcing, scale in (
            (tl, ul, yl, outer["low"], f_low, g_low),
            (th, uh, yh, outer["high"], f_high, g_high),
        ):
            here = ref[8:24, :]
            total = far + edge[...] + ref[7:23, :] + ref[9:25, :] + beside_z(here)
            out[...] = 0.2 * here + forcing + scale * total

        moves = []
        for x in range(16):
            here = U[x + 1]
            total = U[x] + U[x + 2] + beside_z(here)
            total = total + beside_rows(here, ul[x : x + 1, :], uh[x : x + 1, :])
            result[x] = 0.2 * here + f[x] + g[x] * total
            if x % 4 == 3:
                part = pl.ds(x - 3, 4)
                moves.append(pltpu.make_async_copy(result.at[part], pressure.at[part], sems.at[x // 4]))
                moves[-1].start()
        for move in moves:
            move.wait()

    slab, field, long = (16, 512), (16, 16, 512), (18, 16, 512)
    core_pairs, chip_pairs = pairs_core(nx, ny), pairs_chip(nx, ny)
    row_pairs = [pairs_row(nx, ny, step) for step in range(1, ny)]
    odd_pairs = pairs_odd(nx, ny)

    def swap(array, pairs):
        return lax.ppermute(array, axes, pairs)

    def local(source, reaction, boundary_kind, disk_id, disk_mask, thrust):
        f, g, d, absorb, core, chip, row, odd = call(
            set_up,
            [field, field, field, (64, 512), (128, 128), (128, 128), (64, 128), (64, 128)],
            source, reaction, boundary_kind, disk_id, disk_mask, thrust.reshape(1, -1),
            in_specs=[HBM] * 6,
            scratch=[field, field]
            + [pltpu.VMEM(field, jnp.int32)] * 3
            + [(1, thrust.shape[0]), slab, slab, pltpu.SemaphoreType.DMA((4, 5)), pltpu.SemaphoreType.DMA(())],
            name="set_up",
        )
        a_row, a_odd = swap(row, row_pairs[0]), swap(odd, odd_pairs)
        a_chip, a_core = swap(chip, chip_pairs), swap(core, core_pairs)
        s, to_core, to_row, to_odd, block = call(
            smooth,
            [field, (136, 128), (192, 128), (192, 128), (48, 128)],
            f, g, d, absorb, a_core, a_chip, a_row, a_odd,
            scratch=[slab, slab, (192, 512), slab, slab, slab, slab, slab, slab],
            name="smooth",
        )
        s_core = swap(to_core, core_pairs)
        s_row, s_odd = swap(to_row, row_pairs[0]), swap(to_odd, odd_pairs)
        mine, to_chip = call(to_chip_kernel, [(40, 128), (176, 128)], block, s_core, s, name="to_chip")
        s_chip = swap(to_chip, chip_pairs)
        full, beyond = call(from_chip_kernel, [(40, 128), (40, 128)], mine, block, s_chip, name="from_chip")
        c_core = swap(full, core_pairs)
        (window,) = call(window_kernel, [(136, 128)], full, beyond, c_core, s_chip, s_core, s, name="window")
        windows = [window] + [swap(window, pairs) for pairs in row_pairs]
        pressure, coarse = call(
            finish,
            [field, (4, planes, 128)],
            f, g, s, a_core, a_chip, a_row, a_odd, s_core, s_chip, s_row, s_odd, *windows,
            scratch=[(ny, 136, 128)]
            + [(planes, 16, 128)] * 3
            + [(planes + 2, 16, 128)] * 3
            + [(6, 16, 512), (20, 16, 512), long, slab, slab, (32, 512), (32, 512), slab, slab, field]
            + [pltpu.SemaphoreType.DMA((4,))],
            out_specs=[HBM, VMEM],
            name="finish",
        )
        return pressure, coarse

    spec = P("gx", "gy", None)
    return jax.shard_map(
        local,
        mesh=mesh,
        in_specs=(spec, spec, spec, spec, spec, P()),
        out_specs=(spec, P("gx", None, None)),
        check_vma=False,
    )
```

```python
import jax
import jax.numpy as jnp
from jax import lax
from jax.experimental import pallas as pl
from jax.experimental.pallas import tpu as pltpu
from jax.sharding import PartitionSpec as P

SWEEPS = 4
OMEGA = 0.8
WALL_PENALTY = 0.4
INFLOW_PENALTY = 0.2
CHEB_LOW = 0.1
CHEB_HIGH = 2.0
F32 = jnp.float32
VMEM = pl.BlockSpec(memory_space=pltpu.VMEM)


HBM = pl.BlockSpec(memory_space=pltpu.HBM)


def call(kernel, outs, *args, scratch=(), name=None, in_specs=None, out_specs=None):
    return pl.pallas_call(
        kernel,
        out_shape=[jax.ShapeDtypeStruct(s, F32) for s in outs],
        in_specs=in_specs or [VMEM] * len(args),
        out_specs=out_specs or [VMEM] * len(outs),
        scratch_shapes=[pltpu.VMEM(s, F32) if isinstance(s, tuple) else s for s in scratch],
        compiler_params=pltpu.CompilerParams(vmem_limit_bytes=16 << 20),
        name=name,
    )(*args)


def pairs_core(nx, ny):
    return [(x * ny + y, (x ^ 1) * ny + y) for x in range(nx) for y in range(ny)]


def pairs_chip(nx, ny):
    found = []
    for x in range(nx):
        for y in range(ny):
            if x in (0, nx - 1):
                found.append((x * ny + y, x * ny + (y ^ 1)))
            else:
                found.append((x * ny + y, (x + 1 if x % 2 else x - 1) * ny + y))
    return found


def pairs_row(nx, ny, step):
    return [(x * ny + y, x * ny + (y ^ step)) for x in range(nx) for y in range(ny)]


def pairs_odd(nx, ny):
    return [
        (x * ny + y, x * ny + (y + 1 if y % 2 else y - 1) % ny) for x in range(nx) for y in range(ny)
    ]


def put(ref, row, slab):
    rows = slab.shape[0]
    for j in range(slab.shape[1] // 128):
        ref[row + rows * j : row + rows * (j + 1), :] = slab[:, 128 * j : 128 * (j + 1)]


def get(ref, row, rows, width):
    return jnp.concatenate(
        [ref[row + rows * j : row + rows * (j + 1), :] for j in range(width // 128)], axis=1
    )


def iota(shape, dim):
    return lax.broadcasted_iota(jnp.int32, shape, dim)


def beside_z(slab):
    depth = slab.shape[1]
    lane = iota(slab.shape, 1)
    above = jnp.where(lane == depth - 1, 0.0, pltpu.roll(slab, depth - 1, 1))
    below = jnp.where(lane == 0, 0.0, pltpu.roll(slab, 1, 1))
    return above + below


def beside_rows(slab, low, high):
    rows = slab.shape[0]
    row = iota(slab.shape, 0)
    above = jnp.where(row == rows - 1, jnp.broadcast_to(high, slab.shape), pltpu.roll(slab, rows - 1, 0))
    below = jnp.where(row == 0, jnp.broadcast_to(low, slab.shape), pltpu.roll(slab, 1, 0))
    return above + below


def dot(left, right):
    return lax.dot_general(
        left,
        right,
        (((1,), (0,)), ((), ())),
        precision=lax.Precision.HIGHEST,
        preferred_element_type=F32,
    )


def group_lanes(depth):
    return (iota((depth, depth // 4), 0) // 4 == iota((depth, depth // 4), 1)).astype(F32)


def spread_lanes(rows):
    count, lanes = rows.shape
    pad = -count % 8
    if pad:
        rows = jnp.concatenate([rows, jnp.zeros((pad, lanes), F32)], axis=0)
    parts = []
    for j in range(4):
        index = iota(rows.shape, 1) // 4 + (lanes // 4) * j
        parts.append(jnp.take_along_axis(rows, index, axis=1, mode="promise_in_bounds"))
    return jnp.concatenate(parts, axis=1)[:count]


def spread_rows(ref, plane, start):
    row = iota((16, 128), 0) // 4
    value = jnp.zeros((16, 128), F32)
    for q in range(4):
        value = jnp.where(row == q, jnp.broadcast_to(ref[plane, start + q : start + q + 1, :], (16, 128)), value)
    return value


def spread_planes(ref, plane, column):
    row = iota((16, 128), 0) // 4
    value = jnp.zeros((16, 128), F32)
    for q in range(4):
        value = jnp.where(row == q, jnp.broadcast_to(ref[plane + q, column : column + 1, :], (16, 128)), value)
    return value


def solution(mesh):
    nx, ny = mesh.shape["gx"], mesh.shape["gy"]
    assert nx % 2 == 0 and ny % 2 == 0 and ny & (ny - 1) == 0
    axes = ("gx", "gy")

    def where_am_i():
        x, y = lax.axis_index("gx"), lax.axis_index("gy")
        return x, y, x % 2 == 0, y % 2 == 0

    def set_up(
        source_hbm, reaction_hbm, kind_hbm, id_hbm, mask_hbm, thrust_hbm,
        f, g, d, absorb, core, chip, row, odd,
        source, reaction, kind, disk_id, disk_mask, table, y_low, y_high, sems, table_sem,
    ):
        _, _, x_even, y_even = where_am_i()
        moves = []
        arrays = (
            (source_hbm, source), (reaction_hbm, reaction), (kind_hbm, kind), (id_hbm, disk_id), (mask_hbm, disk_mask)
        )
        table_move = pltpu.make_async_copy(thrust_hbm, table, table_sem)
        table_move.start()
        for k in range(4):
            part = pl.ds(4 * k, 4)
            moves.append(
                [pltpu.make_async_copy(a.at[part], b.at[part], sems.at[k, i]) for i, (a, b) in enumerate(arrays)]
            )
            for move in moves[k]:
                move.start()
        table_move.wait()
        spare = jnp.zeros((1, 128 - table.shape[1]), F32)
        lookup = jnp.broadcast_to(jnp.concatenate([table[...], spare], axis=1), (16, 128))

        for k in range(4):
            for move in moves[k]:
                move.wait()
            total = jnp.zeros((16, 512), F32)
            for x in range(4 * k, 4 * k + 4):
                kinds = kind[x]
                a = reaction[x] + jnp.where(kinds == 1, WALL_PENALTY, jnp.where(kinds == 2, INFLOW_PENALTY, 0.0))
                total = total + a
                diagonal = 6.0 + a
                scale = OMEGA / diagonal
                ids = disk_id[x]
                picked = jnp.concatenate(
                    [
                        jnp.take_along_axis(lookup, ids[:, 128 * j : 128 * (j + 1)], axis=1, mode="promise_in_bounds")
                        for j in range(4)
                    ],
                    axis=1,
                )
                first = (source[x] + disk_mask[x].astype(F32) * picked) * scale
                f[x] = first
                g[x] = scale
                d[x] = diagonal
                y_low[x : x + 1, :] = first[0:1, :]
                y_high[x : x + 1, :] = first[15:16, :]
            absorb[16 * k : 16 * k + 16, :] = total
        near, far = jnp.where(x_even, 15, 0), jnp.where(x_even, 0, 15)
        put(core, 0, f[near])
        put(core, 64, g[near])
        put(chip, 0, f[far])
        put(chip, 64, g[far])
        low, high = y_low[...], y_high[...]
        put(row, 0, jnp.where(y_even, high, low))
        put(odd, 0, jnp.where(y_even, low, high))

    def halo_x(core, chip, row, x, x_even):
        a, b = get(core, row, 16, 512), get(chip, row, 16, 512)
        left = jnp.where(x > 0, jnp.where(x_even, b, a), 0.0)
        right = jnp.where(x < nx - 1, jnp.where(x_even, a, b), 0.0)
        return left, right

    def halo_y(row, odd, at, y, y_even):
        a, b = get(row, at, 16, 512), get(odd, at, 16, 512)
        low = jnp.where(y > 0, jnp.where(y_even, b, a), 0.0)
        high = jnp.where(y < ny - 1, jnp.where(y_even, a, b), 0.0)
        return low, high

    def smooth(f, g, d, absorb, core, chip, row, odd, s, to_core, to_row, to_odd, block, lo, hi, V, y0, y1, y14, y15, g0, g15):
        x_at, y_at, x_even, y_even = where_am_i()
        left, right = halo_x(core, chip, 0, x_at, x_even)
        lo[...], hi[...] = halo_y(row, odd, 0, y_at, y_even)
        for x in range(16):
            here = f[x]
            scale = g[x]
            total = (f[x - 1] if x > 0 else left) + (f[x + 1] if x < 15 else right)
            total = total + beside_rows(here, lo[x : x + 1, :], hi[x : x + 1, :]) + beside_z(here)
            value = 1.2 * here + scale * total
            s[x] = value
            y0[x : x + 1, :] = value[0:1, :]
            y1[x : x + 1, :] = value[1:2, :]
            y14[x : x + 1, :] = value[14:15, :]
            y15[x : x + 1, :] = value[15:16, :]
            g0[x : x + 1, :] = scale[0:1, :]
            g15[x : x + 1, :] = scale[15:16, :]
        nothing = jnp.zeros((1, 512), F32)
        for k in range(4):
            total = jnp.zeros((16, 512), F32)
            for x in range(4 * k, 4 * k + 4):
                here = s[x]
                total = total + d[x] * (1.25 * f[x] - here)
                total = total + beside_rows(here, nothing, nothing) + beside_z(here)
                if x > 0:
                    total = total + s[x - 1]
                if x < 15:
                    total = total + s[x + 1]
            V[16 * k : 16 * k + 16, :] = total
        V[64:128, :] = absorb[...]
        V[128:144, :] = s[0]
        V[144:160, :] = s[15]
        V[160:176, :] = y0[...]
        V[176:192, :] = y15[...]
        out, src = iota((48, 192), 0), iota((48, 192), 1)
        cx, cy = out % 4, out // 8
        in_bulk = (out < 32) & (src < 128) & (src // 64 == (out // 4) % 2)
        bulk = in_bulk & ((src % 64) // 16 == cx) & ((src % 16) // 4 == cy)
        faces = (out >= 32) & (src >= 128) & ((out - 32) // 4 == (src - 128) // 16) & ((src % 16) // 4 == cx)
        picked = dot((bulk | faces).astype(F32), V[...])
        block[...] = dot(picked, group_lanes(512))
        put(to_core, 0, s[jnp.where(x_even, 15, 0)])
        put(to_core, 64, s[jnp.where(x_even, 14, 1)])
        to_core[128:132, :] = jnp.where(x_even, block[36:40, :], block[32:36, :])
        to_core[132:136, :] = jnp.zeros((4, 128), F32)
        for at, (low, high) in enumerate(((y0, y15), (y1, y14), (g0, g15))):
            a, b = low[...], high[...]
            put(to_row, 64 * at, jnp.where(y_even, b, a))
            put(to_odd, 64 * at, jnp.where(y_even, a, b))

    def to_chip_kernel(block, core, s, mine, to_chip):
        _, _, x_even, _ = where_am_i()
        mine[...] = jnp.concatenate([block[0:32, :], block[40:48, :]], axis=0)
        face = core[128:136, :]
        for cy in range(4):
            line = face[cy : cy + 1, :]
            mine[8 * cy : 8 * cy + 1, :] = block[8 * cy : 8 * cy + 1, :] + jnp.where(x_even, 0.0, line)
            mine[8 * cy + 3 : 8 * cy + 4, :] = block[8 * cy + 3 : 8 * cy + 4, :] + jnp.where(x_even, line, 0.0)
        put(to_chip, 0, s[jnp.where(x_even, 0, 15)])
        put(to_chip, 64, s[jnp.where(x_even, 1, 14)])
        to_chip[128:168, :] = mine[...]
        to_chip[168:172, :] = jnp.where(x_even, block[32:36, :], block[36:40, :])
        to_chip[172:176, :] = jnp.zeros((4, 128), F32)

    def from_chip_kernel(mine, block, chip, full, beyond):
        x_at, _, x_even, _ = where_am_i()
        has = jnp.where(x_even, x_at > 0, x_at < nx - 1)
        full[...] = mine[...]
        beyond[...] = chip[128:168, :]
        mine_face = jnp.where(x_even, block[32:36, :], block[36:40, :])
        face = chip[168:176, :]
        for cy in range(4):
            line = jnp.where(has, face[cy : cy + 1, :], 0.0)
            own = mine_face[cy : cy + 1, :]
            a, b = 8 * cy, 8 * cy + 3
            full[a : a + 1, :] = mine[a : a + 1, :] + jnp.where(x_even, line, 0.0)
            full[b : b + 1, :] = mine[b : b + 1, :] + jnp.where(x_even, 0.0, line)
            beyond[a : a + 1, :] = chip[128 + a : 129 + a, :] + jnp.where(x_even, 0.0, own)
            beyond[b : b + 1, :] = chip[128 + b : 129 + b, :] + jnp.where(x_even, own, 0.0)

    def window_kernel(full, beyond, core, chip, s_core, s, window):
        x_at, _, x_even, _ = where_am_i()
        mid = full[...]
        a, b = core[...], beyond[...]
        left, right = jnp.where(x_even, b, a), jnp.where(x_even, a, b)
        for at, block in enumerate((left, mid, right)):
            for cy in range(4):
                window[24 * cy + 4 * at : 24 * cy + 4 * at + 4, :] = block[8 * cy : 8 * cy + 4, :]
                window[24 * cy + 12 + 4 * at : 24 * cy + 16 + 4 * at, :] = block[8 * cy + 4 : 8 * cy + 8, :]
            window[96 + 4 * at : 100 + 4 * at, :] = block[32:36, :]
            window[108 + 4 * at : 112 + 4 * at, :] = block[36:40, :]
        low, high = halo_x(s_core, chip, 0, x_at, x_even)
        for at, line in enumerate((low[0:1, :], low[15:16, :], high[0:1, :], high[15:16, :])):
            put(window, 120 + 4 * at, line)

    planes = 4 * ny

    def finish(*refs):
        f, g, s, a_core, a_chip, a_row, a_odd, s_core, s_chip, s_row, s_odd = refs[:11]
        windows = refs[11 : 11 + ny]
        pressure, coarse = refs[11 + ny : 13 + ny]
        every, res, diag, inv, one, two, sol, Pc, T, U, yl, yh, tl, th, ul, uh, result, sems = refs[13 + ny :]
        x_at, y_at, x_even, y_even = where_am_i()
        for step, window in enumerate(windows):
            every[jnp.bitwise_xor(y_at, step)] = window[...]

        row = iota((16, 128), 0)
        valid = ((row >= 4) | (x_at > 0)) & ((row < 8) | (x_at < nx - 1)) & (row < 12)
        blank = jnp.zeros((4, 128), F32)

        def twelve(value):
            return jnp.concatenate([value, blank], axis=0)

        centre = (CHEB_HIGH + CHEB_LOW) / 2.0
        half_range = (CHEB_HIGH - CHEB_LOW) / 2.0
        aspect = centre / half_range
        factor = 1.0 / aspect
        empty = jnp.zeros((16, 128), F32)
        for ref in (one, two, sol):
            ref[0] = empty
            ref[planes + 1] = empty
        for at in range(ny):
            for cy in range(4):
                plane = 4 * at + cy
                value = every[at, 24 * cy : 24 * cy + 12, :]
                if cy == 0 and at > 0:
                    value = value + every[at - 1, 108:120, :]
                if cy == 3 and at < ny - 1:
                    value = value + every[at + 1, 96:108, :]
                value = jnp.where(valid, twelve(value), 0.0)
                centre_value = 6.0 + twelve(every[at, 24 * cy + 12 : 24 * cy + 24, :]) / 16.0
                inverse = jnp.where(valid, 1.0 / (16.0 * centre_value), 0.0)
                res[plane] = value
                diag[plane] = centre_value
                inv[plane] = inverse
                direction = inverse * value / centre
                one[plane + 1] = direction
                sol[plane + 1] = direction
        now, later = one, two
        for number in range(1, SWEEPS):
            factor_next = 1.0 / (2.0 * aspect - factor)
            keep, gain = factor_next * factor, 2.0 * factor_next / half_range

            lane = iota((16, 128), 1)
            for plane in range(planes):
                here = now[plane + 1]
                total = now[plane] + now[plane + 2]
                total = total + pltpu.roll(here, 15, 0) + pltpu.roll(here, 1, 0)
                total = total + jnp.where(lane == 127, 0.0, pltpu.roll(here, 127, 1))
                total = total + jnp.where(lane == 0, 0.0, pltpu.roll(here, 1, 1))
                residual = res[plane] - 16.0 * (diag[plane] * here - total)
                res[plane] = residual
                direction = keep * here + gain * inv[plane] * residual
                later[plane + 1] = direction
                sol[plane + 1] = sol[plane + 1] + direction
            now, later = later, now
            factor = factor_next
        for plane in range(planes):
            for cx in range(4):
                coarse[cx, plane : plane + 1, :] = sol[plane + 1, 4 + cx : 5 + cx, :]

        first_plane = 4 * y_at + 1
        for at in range(6):
            Pc[at] = spread_lanes(spread_planes(sol, first_plane, 3 + at))
        s_left, s_right = halo_x(s_core, s_chip, 0, x_at, x_even)
        s_left2, s_right2 = halo_x(s_core, s_chip, 64, x_at, x_even)
        T[0], T[1] = s_left2 + Pc[0], s_left + Pc[0]
        T[18], T[19] = s_right + Pc[5], s_right2 + Pc[5]

        for x in range(16):
            T[x + 2] = s[x] + Pc[x // 4 + 1]
        below, above = first_plane - 1, first_plane + 4
        y1_low, y1_high = halo_y(s_row, s_odd, 0, y_at, y_even)
        y2_low, y2_high = halo_y(s_row, s_odd, 64, y_at, y_even)
        g_low, g_high = halo_y(s_row, s_odd, 128, y_at, y_even)
        f_low, f_high = halo_y(a_row, a_odd, 0, y_at, y_even)
        before, after = jnp.maximum(y_at - 1, 0), jnp.minimum(y_at + 1, ny - 1)
        outer = {}
        for name, ref, plane, s1, s2, who, inside, line in (
            ("low", tl, below, y1_low, y2_low, before, y_at > 0, 1),
            ("high", th, above, y1_high, y2_high, after, y_at < ny - 1, 0),
        ):
            spread = spread_lanes(spread_rows(sol, plane, 4))
            ref[8:24, :] = s1 + spread
            outer[name] = s2 + spread
            for at, cx, base, there in ((7, 3, 0, x_at > 0), (24, 8, 2, x_at < nx - 1)):
                corner = jnp.concatenate(
                    [every[who, pl.ds(120 + 4 * (base + line) + j, 1), :] for j in range(4)], axis=1
                )
                corner = jnp.where(inside & there, corner, 0.0)
                ref[at : at + 1, :] = corner + spread_lanes(sol[plane, cx : cx + 1, :])

        f_left, f_right = halo_x(a_core, a_chip, 0, x_at, x_even)
        g_left, g_right = halo_x(a_core, a_chip, 64, x_at, x_even)

        def fourth_at(at, forcing, scale):
            here = T[at + 1]
            total = T[at] + T[at + 2] + beside_z(here)
            total = total + beside_rows(here, tl[at + 7 : at + 8, :], th[at + 7 : at + 8, :])
            return 0.2 * here + forcing + scale * total

        U[0] = fourth_at(0, f_left, g_left)
        U[17] = fourth_at(17, f_right, g_right)

        for x in range(16):
            U[x + 1] = fourth_at(x + 1, f[x], g[x])
            here = T[x + 2]
            yl[x : x + 1, :] = here[0:1, :]
            yh[x : x + 1, :] = here[15:16, :]
        for ref, out, edge, far, forcing, scale in (
            (tl, ul, yl, outer["low"], f_low, g_low),
            (th, uh, yh, outer["high"], f_high, g_high),
        ):
            here = ref[8:24, :]
            total = far + edge[...] + ref[7:23, :] + ref[9:25, :] + beside_z(here)
            out[...] = 0.2 * here + forcing + scale * total

        moves = []
        for x in range(16):
            here = U[x + 1]
            total = U[x] + U[x + 2] + beside_z(here)
            total = total + beside_rows(here, ul[x : x + 1, :], uh[x : x + 1, :])
            result[x] = 0.2 * here + f[x] + g[x] * total
            if x % 4 == 3:
                part = pl.ds(x - 3, 4)
                moves.append(pltpu.make_async_copy(result.at[part], pressure.at[part], sems.at[x // 4]))
                moves[-1].start()
        for move in moves:
            move.wait()

    slab, field, long = (16, 512), (16, 16, 512), (18, 16, 512)
    core_pairs, chip_pairs = pairs_core(nx, ny), pairs_chip(nx, ny)
    row_pairs = [pairs_row(nx, ny, step) for step in range(1, ny)]
    odd_pairs = pairs_odd(nx, ny)

    def swap(array, pairs):
        return lax.ppermute(array, axes, pairs)

    def local(source, reaction, boundary_kind, disk_id, disk_mask, thrust):
        f, g, d, absorb, core, chip, row, odd = call(
            set_up,
            [field, field, field, (64, 512), (128, 128), (128, 128), (64, 128), (64, 128)],
            *(
                pltpu.with_memory_space_constraint(array, pltpu.HBM)
                for array in (source, reaction, boundary_kind, disk_id, disk_mask, thrust.reshape(1, -1))
            ),
            in_specs=[HBM] * 6,
            scratch=[field, field]
            + [pltpu.VMEM(field, jnp.int32)] * 3
            + [(1, thrust.shape[0]), slab, slab, pltpu.SemaphoreType.DMA((4, 5)), pltpu.SemaphoreType.DMA(())],
            name="set_up",
        )
        a_row, a_odd = swap(row, row_pairs[0]), swap(odd, odd_pairs)
        a_chip, a_core = swap(chip, chip_pairs), swap(core, core_pairs)
        s, to_core, to_row, to_odd, block = call(
            smooth,
            [field, (136, 128), (192, 128), (192, 128), (48, 128)],
            f, g, d, absorb, a_core, a_chip, a_row, a_odd,
            scratch=[slab, slab, (192, 512), slab, slab, slab, slab, slab, slab],
            name="smooth",
        )
        s_core = swap(to_core, core_pairs)
        s_row, s_odd = swap(to_row, row_pairs[0]), swap(to_odd, odd_pairs)
        mine, to_chip = call(to_chip_kernel, [(40, 128), (176, 128)], block, s_core, s, name="to_chip")
        s_chip = swap(to_chip, chip_pairs)
        full, beyond = call(from_chip_kernel, [(40, 128), (40, 128)], mine, block, s_chip, name="from_chip")
        c_core = swap(full, core_pairs)
        (window,) = call(window_kernel, [(136, 128)], full, beyond, c_core, s_chip, s_core, s, name="window")
        windows = [window] + [swap(window, pairs) for pairs in row_pairs]
        pressure, coarse = call(
            finish,
            [field, (4, planes, 128)],
            f, g, s, a_core, a_chip, a_row, a_odd, s_core, s_chip, s_row, s_odd, *windows,
            scratch=[(ny, 136, 128)]
            + [(planes, 16, 128)] * 3
            + [(planes + 2, 16, 128)] * 3
            + [(6, 16, 512), (20, 16, 512), long, slab, slab, (32, 512), (32, 512), slab, slab, field]
            + [pltpu.SemaphoreType.DMA((4,))],
            out_specs=[HBM, VMEM],
            name="finish",
        )
        return pressure, coarse

    spec = P("gx", "gy", None)
    return jax.shard_map(
        local,
        mesh=mesh,
        in_specs=(spec, spec, spec, spec, spec, P()),
        out_specs=(spec, P("gx", None, None)),
        check_vma=False,
    )
```

```python
import jax
import jax.numpy as jnp
from jax import lax
from jax.experimental import pallas as pl
from jax.experimental.pallas import tpu as pltpu
from jax.sharding import PartitionSpec as P

SWEEPS = 4
OMEGA = 0.8
WALL_PENALTY = 0.4
INFLOW_PENALTY = 0.2
CHEB_LOW = 0.1
CHEB_HIGH = 2.0
F32 = jnp.float32
VMEM = pl.BlockSpec(memory_space=pltpu.VMEM)


HBM = pl.BlockSpec(memory_space=pltpu.HBM)


def call(kernel, outs, *args, scratch=(), name=None, in_specs=None, out_specs=None):
    return pl.pallas_call(
        kernel,
        out_shape=[jax.ShapeDtypeStruct(s, F32) for s in outs],
        in_specs=in_specs or [VMEM] * len(args),
        out_specs=out_specs or [VMEM] * len(outs),
        scratch_shapes=[pltpu.VMEM(s, F32) if isinstance(s, tuple) else s for s in scratch],
        compiler_params=pltpu.CompilerParams(vmem_limit_bytes=16 << 20),
        name=name,
    )(*args)


def pairs_core(nx, ny):
    return [(x * ny + y, (x ^ 1) * ny + y) for x in range(nx) for y in range(ny)]


def pairs_chip(nx, ny):
    found = []
    for x in range(nx):
        for y in range(ny):
            if x in (0, nx - 1):
                found.append((x * ny + y, x * ny + (y ^ 1)))
            else:
                found.append((x * ny + y, (x + 1 if x % 2 else x - 1) * ny + y))
    return found


def pairs_row(nx, ny, step):
    return [(x * ny + y, x * ny + (y ^ step)) for x in range(nx) for y in range(ny)]


def pairs_odd(nx, ny):
    return [
        (x * ny + y, x * ny + (y + 1 if y % 2 else y - 1) % ny) for x in range(nx) for y in range(ny)
    ]


def put(ref, row, slab):
    rows = slab.shape[0]
    for j in range(slab.shape[1] // 128):
        ref[row + rows * j : row + rows * (j + 1), :] = slab[:, 128 * j : 128 * (j + 1)]


def get(ref, row, rows, width):
    return jnp.concatenate(
        [ref[row + rows * j : row + rows * (j + 1), :] for j in range(width // 128)], axis=1
    )


def iota(shape, dim):
    return lax.broadcasted_iota(jnp.int32, shape, dim)


def beside_z(slab):
    depth = slab.shape[1]
    lane = iota(slab.shape, 1)
    above = jnp.where(lane == depth - 1, 0.0, pltpu.roll(slab, depth - 1, 1))
    below = jnp.where(lane == 0, 0.0, pltpu.roll(slab, 1, 1))
    return above + below


def beside_rows(slab, low, high):
    rows = slab.shape[0]
    row = iota(slab.shape, 0)
    above = jnp.where(row == rows - 1, jnp.broadcast_to(high, slab.shape), pltpu.roll(slab, rows - 1, 0))
    below = jnp.where(row == 0, jnp.broadcast_to(low, slab.shape), pltpu.roll(slab, 1, 0))
    return above + below


def dot(left, right):
    return lax.dot_general(
        left,
        right,
        (((1,), (0,)), ((), ())),
        precision=lax.Precision.HIGHEST,
        preferred_element_type=F32,
    )


def group_lanes(depth):
    return (iota((depth, depth // 4), 0) // 4 == iota((depth, depth // 4), 1)).astype(F32)


def spread_lanes(rows):
    count, lanes = rows.shape
    pad = -count % 8
    if pad:
        rows = jnp.concatenate([rows, jnp.zeros((pad, lanes), F32)], axis=0)
    parts = []
    for j in range(4):
        index = iota(rows.shape, 1) // 4 + (lanes // 4) * j
        parts.append(jnp.take_along_axis(rows, index, axis=1, mode="promise_in_bounds"))
    return jnp.concatenate(parts, axis=1)[:count]


def spread_rows(ref, plane, start):
    row = iota((16, 128), 0) // 4
    value = jnp.zeros((16, 128), F32)
    for q in range(4):
        value = jnp.where(row == q, jnp.broadcast_to(ref[plane, start + q : start + q + 1, :], (16, 128)), value)
    return value


def spread_planes(ref, plane, column):
    row = iota((16, 128), 0) // 4
    value = jnp.zeros((16, 128), F32)
    for q in range(4):
        value = jnp.where(row == q, jnp.broadcast_to(ref[plane + q, column : column + 1, :], (16, 128)), value)
    return value


def solution(mesh):
    nx, ny = mesh.shape["gx"], mesh.shape["gy"]
    assert nx % 2 == 0 and ny % 2 == 0 and ny & (ny - 1) == 0
    axes = ("gx", "gy")

    def where_am_i():
        x, y = lax.axis_index("gx"), lax.axis_index("gy")
        return x, y, x % 2 == 0, y % 2 == 0

    def look_up(table, ids):
        spare = jnp.zeros((1, 128 - table.shape[1]), F32)
        row = jnp.broadcast_to(jnp.concatenate([table, spare], axis=1), (16, 128))
        parts = [
            jnp.take_along_axis(row, ids[:, 128 * j : 128 * (j + 1)], axis=1, mode="promise_in_bounds") for j in range(4)
        ]
        return jnp.concatenate(parts, axis=1)

    def first_of(source, reaction, kinds, ids, mask, table):
        a = reaction + jnp.where(kinds == 1, WALL_PENALTY, jnp.where(kinds == 2, INFLOW_PENALTY, 0.0))
        diagonal = 6.0 + a
        scale = OMEGA / diagonal
        return (source + mask.astype(F32) * look_up(table, ids)) * scale, scale, diagonal, a

    def faces(*refs):
        inputs, thrust, messages, buffers, table, sems, table_sem = (
            refs[:5], refs[5], refs[6:10], refs[10:15], refs[15], refs[16], refs[17]
        )
        core, chip, row, odd = messages
        _, _, x_even, y_even = where_am_i()
        near, far = jnp.where(x_even, 15, 0), jnp.where(x_even, 0, 15)
        moves = [pltpu.make_async_copy(thrust, table, table_sem)]
        for i, (hbm, buffer) in enumerate(zip(inputs, buffers)):
            for j, part in enumerate((hbm.at[:, 0, :], hbm.at[:, 15, :], hbm.at[far], hbm.at[near])):
                moves.append(pltpu.make_async_copy(part, buffer.at[j], sems.at[i, j]))
        for move in moves:
            move.start()
        for move in moves:
            move.wait()
        found = [first_of(*(buffer[j] for buffer in buffers), table[...])[:2] for j in range(4)]
        (low, _), (high, _), (f_far, g_far), (f_near, g_near) = found
        put(row, 0, jnp.where(y_even, high, low))
        put(odd, 0, jnp.where(y_even, low, high))
        put(chip, 0, f_far)
        put(chip, 64, g_far)
        put(core, 0, f_near)
        put(core, 64, g_near)

    def set_up(*refs):
        inputs, thrust, (f, g, d, absorb) = refs[:5], refs[5], refs[6:10]
        buffers, table, sems, table_sem = refs[10:15], refs[15], refs[16], refs[17]
        moves = []
        table_move = pltpu.make_async_copy(thrust, table, table_sem)
        table_move.start()
        for k in range(4):
            part = pl.ds(4 * k, 4)
            moves.append(
                [
                    pltpu.make_async_copy(a.at[part], b.at[part], sems.at[k, i])
                    for i, (a, b) in enumerate(zip(inputs, buffers))
                ]
            )
            for move in moves[k]:
                move.start()
        table_move.wait()
        for k in range(4):
            for move in moves[k]:
                move.wait()
            total = jnp.zeros((16, 512), F32)
            for x in range(4 * k, 4 * k + 4):
                f[x], g[x], d[x], a = first_of(*(buffer[x] for buffer in buffers), table[...])
                total = total + a
            absorb[16 * k : 16 * k + 16, :] = total

    def halo_x(core, chip, row, x, x_even):
        a, b = get(core, row, 16, 512), get(chip, row, 16, 512)
        left = jnp.where(x > 0, jnp.where(x_even, b, a), 0.0)
        right = jnp.where(x < nx - 1, jnp.where(x_even, a, b), 0.0)
        return left, right

    def halo_y(row, odd, at, y, y_even):
        a, b = get(row, at, 16, 512), get(odd, at, 16, 512)
        low = jnp.where(y > 0, jnp.where(y_even, b, a), 0.0)
        high = jnp.where(y < ny - 1, jnp.where(y_even, a, b), 0.0)
        return low, high

    def smooth(f, g, d, absorb, core, chip, row, odd, s, to_core, to_row, to_odd, block, lo, hi, V, y0, y1, y14, y15, g0, g15):
        x_at, y_at, x_even, y_even = where_am_i()
        left, right = halo_x(core, chip, 0, x_at, x_even)
        lo[...], hi[...] = halo_y(row, odd, 0, y_at, y_even)
        for x in range(16):
            here = f[x]
            scale = g[x]
            total = (f[x - 1] if x > 0 else left) + (f[x + 1] if x < 15 else right)
            total = total + beside_rows(here, lo[x : x + 1, :], hi[x : x + 1, :]) + beside_z(here)
            value = 1.2 * here + scale * total
            s[x] = value
            y0[x : x + 1, :] = value[0:1, :]
            y1[x : x + 1, :] = value[1:2, :]
            y14[x : x + 1, :] = value[14:15, :]
            y15[x : x + 1, :] = value[15:16, :]
            g0[x : x + 1, :] = scale[0:1, :]
            g15[x : x + 1, :] = scale[15:16, :]
        nothing = jnp.zeros((1, 512), F32)
        for k in range(4):
            total = jnp.zeros((16, 512), F32)
            for x in range(4 * k, 4 * k + 4):
                here = s[x]
                total = total + d[x] * (1.25 * f[x] - here)
                total = total + beside_rows(here, nothing, nothing) + beside_z(here)
                if x > 0:
                    total = total + s[x - 1]
                if x < 15:
                    total = total + s[x + 1]
            V[16 * k : 16 * k + 16, :] = total
        V[64:128, :] = absorb[...]
        V[128:144, :] = s[0]
        V[144:160, :] = s[15]
        V[160:176, :] = y0[...]
        V[176:192, :] = y15[...]
        out, src = iota((48, 192), 0), iota((48, 192), 1)
        cx, cy = out % 4, out // 8
        in_bulk = (out < 32) & (src < 128) & (src // 64 == (out // 4) % 2)
        bulk = in_bulk & ((src % 64) // 16 == cx) & ((src % 16) // 4 == cy)
        faces = (out >= 32) & (src >= 128) & ((out - 32) // 4 == (src - 128) // 16) & ((src % 16) // 4 == cx)
        picked = dot((bulk | faces).astype(F32), V[...])
        block[...] = dot(picked, group_lanes(512))
        put(to_core, 0, s[jnp.where(x_even, 15, 0)])
        put(to_core, 64, s[jnp.where(x_even, 14, 1)])
        to_core[128:132, :] = jnp.where(x_even, block[36:40, :], block[32:36, :])
        to_core[132:136, :] = jnp.zeros((4, 128), F32)
        for at, (low, high) in enumerate(((y0, y15), (y1, y14), (g0, g15))):
            a, b = low[...], high[...]
            put(to_row, 64 * at, jnp.where(y_even, b, a))
            put(to_odd, 64 * at, jnp.where(y_even, a, b))

    def to_chip_kernel(block, core, s, mine, to_chip):
        _, _, x_even, _ = where_am_i()
        mine[...] = jnp.concatenate([block[0:32, :], block[40:48, :]], axis=0)
        face = core[128:136, :]
        for cy in range(4):
            line = face[cy : cy + 1, :]
            mine[8 * cy : 8 * cy + 1, :] = block[8 * cy : 8 * cy + 1, :] + jnp.where(x_even, 0.0, line)
            mine[8 * cy + 3 : 8 * cy + 4, :] = block[8 * cy + 3 : 8 * cy + 4, :] + jnp.where(x_even, line, 0.0)
        put(to_chip, 0, s[jnp.where(x_even, 0, 15)])
        put(to_chip, 64, s[jnp.where(x_even, 1, 14)])
        to_chip[128:168, :] = mine[...]
        to_chip[168:172, :] = jnp.where(x_even, block[32:36, :], block[36:40, :])
        to_chip[172:176, :] = jnp.zeros((4, 128), F32)

    def from_chip_kernel(mine, block, chip, full, beyond):
        x_at, _, x_even, _ = where_am_i()
        has = jnp.where(x_even, x_at > 0, x_at < nx - 1)
        full[...] = mine[...]
        beyond[...] = chip[128:168, :]
        mine_face = jnp.where(x_even, block[32:36, :], block[36:40, :])
        face = chip[168:176, :]
        for cy in range(4):
            line = jnp.where(has, face[cy : cy + 1, :], 0.0)
            own = mine_face[cy : cy + 1, :]
            a, b = 8 * cy, 8 * cy + 3
            full[a : a + 1, :] = mine[a : a + 1, :] + jnp.where(x_even, line, 0.0)
            full[b : b + 1, :] = mine[b : b + 1, :] + jnp.where(x_even, 0.0, line)
            beyond[a : a + 1, :] = chip[128 + a : 129 + a, :] + jnp.where(x_even, 0.0, own)
            beyond[b : b + 1, :] = chip[128 + b : 129 + b, :] + jnp.where(x_even, own, 0.0)

    def window_kernel(full, beyond, core, chip, s_core, s, window):
        x_at, _, x_even, _ = where_am_i()
        mid = full[...]
        a, b = core[...], beyond[...]
        left, right = jnp.where(x_even, b, a), jnp.where(x_even, a, b)
        for at, block in enumerate((left, mid, right)):
            for cy in range(4):
                window[24 * cy + 4 * at : 24 * cy + 4 * at + 4, :] = block[8 * cy : 8 * cy + 4, :]
                window[24 * cy + 12 + 4 * at : 24 * cy + 16 + 4 * at, :] = block[8 * cy + 4 : 8 * cy + 8, :]
            window[96 + 4 * at : 100 + 4 * at, :] = block[32:36, :]
            window[108 + 4 * at : 112 + 4 * at, :] = block[36:40, :]
        low, high = halo_x(s_core, chip, 0, x_at, x_even)
        for at, line in enumerate((low[0:1, :], low[15:16, :], high[0:1, :], high[15:16, :])):
            put(window, 120 + 4 * at, line)

    planes = 4 * ny

    def finish(*refs):
        f, g, s, a_core, a_chip, a_row, a_odd, s_core, s_chip, s_row, s_odd = refs[:11]
        windows = refs[11 : 11 + ny]
        pressure, coarse = refs[11 + ny : 13 + ny]
        every, res, diag, inv, one, two, sol, Pc, T, U, yl, yh, tl, th, ul, uh, result, sems = refs[13 + ny :]
        x_at, y_at, x_even, y_even = where_am_i()
        for step, window in enumerate(windows):
            every[jnp.bitwise_xor(y_at, step)] = window[...]

        row = iota((16, 128), 0)
        valid = ((row >= 4) | (x_at > 0)) & ((row < 8) | (x_at < nx - 1)) & (row < 12)
        blank = jnp.zeros((4, 128), F32)

        def twelve(value):
            return jnp.concatenate([value, blank], axis=0)

        centre = (CHEB_HIGH + CHEB_LOW) / 2.0
        half_range = (CHEB_HIGH - CHEB_LOW) / 2.0
        aspect = centre / half_range
        factor = 1.0 / aspect
        empty = jnp.zeros((16, 128), F32)
        for ref in (one, two, sol):
            ref[0] = empty
            ref[planes + 1] = empty
        for at in range(ny):
            for cy in range(4):
                plane = 4 * at + cy
                value = every[at, 24 * cy : 24 * cy + 12, :]
                if cy == 0 and at > 0:
                    value = value + every[at - 1, 108:120, :]
                if cy == 3 and at < ny - 1:
                    value = value + every[at + 1, 96:108, :]
                value = jnp.where(valid, twelve(value), 0.0)
                centre_value = 6.0 + twelve(every[at, 24 * cy + 12 : 24 * cy + 24, :]) / 16.0
                inverse = jnp.where(valid, 1.0 / (16.0 * centre_value), 0.0)
                res[plane] = value
                diag[plane] = centre_value
                inv[plane] = inverse
                direction = inverse * value / centre
                one[plane + 1] = direction
                sol[plane + 1] = direction
        now, later = one, two
        for number in range(1, SWEEPS):
            factor_next = 1.0 / (2.0 * aspect - factor)
            keep, gain = factor_next * factor, 2.0 * factor_next / half_range

            lane = iota((16, 128), 1)
            for plane in range(planes):
                here = now[plane + 1]
                total = now[plane] + now[plane + 2]
                total = total + pltpu.roll(here, 15, 0) + pltpu.roll(here, 1, 0)
                total = total + jnp.where(lane == 127, 0.0, pltpu.roll(here, 127, 1))
                total = total + jnp.where(lane == 0, 0.0, pltpu.roll(here, 1, 1))
                residual = res[plane] - 16.0 * (diag[plane] * here - total)
                res[plane] = residual
                direction = keep * here + gain * inv[plane] * residual
                later[plane + 1] = direction
                sol[plane + 1] = sol[plane + 1] + direction
            now, later = later, now
            factor = factor_next
        for plane in range(planes):
            for cx in range(4):
                coarse[cx, plane : plane + 1, :] = sol[plane + 1, 4 + cx : 5 + cx, :]

        first_plane = 4 * y_at + 1
        for at in range(6):
            Pc[at] = spread_lanes(spread_planes(sol, first_plane, 3 + at))
        s_left, s_right = halo_x(s_core, s_chip, 0, x_at, x_even)
        s_left2, s_right2 = halo_x(s_core, s_chip, 64, x_at, x_even)
        T[0], T[1] = s_left2 + Pc[0], s_left + Pc[0]
        T[18], T[19] = s_right + Pc[5], s_right2 + Pc[5]

        for x in range(16):
            T[x + 2] = s[x] + Pc[x // 4 + 1]
        below, above = first_plane - 1, first_plane + 4
        y1_low, y1_high = halo_y(s_row, s_odd, 0, y_at, y_even)
        y2_low, y2_high = halo_y(s_row, s_odd, 64, y_at, y_even)
        g_low, g_high = halo_y(s_row, s_odd, 128, y_at, y_even)
        f_low, f_high = halo_y(a_row, a_odd, 0, y_at, y_even)
        before, after = jnp.maximum(y_at - 1, 0), jnp.minimum(y_at + 1, ny - 1)
        outer = {}
        for name, ref, plane, s1, s2, who, inside, line in (
            ("low", tl, below, y1_low, y2_low, before, y_at > 0, 1),
            ("high", th, above, y1_high, y2_high, after, y_at < ny - 1, 0),
        ):
            spread = spread_lanes(spread_rows(sol, plane, 4))
            ref[8:24, :] = s1 + spread
            outer[name] = s2 + spread
            for at, cx, base, there in ((7, 3, 0, x_at > 0), (24, 8, 2, x_at < nx - 1)):
                corner = jnp.concatenate(
                    [every[who, pl.ds(120 + 4 * (base + line) + j, 1), :] for j in range(4)], axis=1
                )
                corner = jnp.where(inside & there, corner, 0.0)
                ref[at : at + 1, :] = corner + spread_lanes(sol[plane, cx : cx + 1, :])

        f_left, f_right = halo_x(a_core, a_chip, 0, x_at, x_even)
        g_left, g_right = halo_x(a_core, a_chip, 64, x_at, x_even)

        def fourth_at(at, forcing, scale):
            here = T[at + 1]
            total = T[at] + T[at + 2] + beside_z(here)
            total = total + beside_rows(here, tl[at + 7 : at + 8, :], th[at + 7 : at + 8, :])
            return 0.2 * here + forcing + scale * total

        U[0] = fourth_at(0, f_left, g_left)
        U[17] = fourth_at(17, f_right, g_right)

        for x in range(16):
            U[x + 1] = fourth_at(x + 1, f[x], g[x])
            here = T[x + 2]
            yl[x : x + 1, :] = here[0:1, :]
            yh[x : x + 1, :] = here[15:16, :]
        for ref, out, edge, far, forcing, scale in (
            (tl, ul, yl, outer["low"], f_low, g_low),
            (th, uh, yh, outer["high"], f_high, g_high),
        ):
            here = ref[8:24, :]
            total = far + edge[...] + ref[7:23, :] + ref[9:25, :] + beside_z(here)
            out[...] = 0.2 * here + forcing + scale * total

        moves = []
        for x in range(16):
            here = U[x + 1]
            total = U[x] + U[x + 2] + beside_z(here)
            total = total + beside_rows(here, ul[x : x + 1, :], uh[x : x + 1, :])
            result[x] = 0.2 * here + f[x] + g[x] * total
            if x % 4 == 3:
                part = pl.ds(x - 3, 4)
                moves.append(pltpu.make_async_copy(result.at[part], pressure.at[part], sems.at[x // 4]))
                moves[-1].start()
        for move in moves:
            move.wait()

    slab, field, long = (16, 512), (16, 16, 512), (18, 16, 512)
    core_pairs, chip_pairs = pairs_core(nx, ny), pairs_chip(nx, ny)
    row_pairs = [pairs_row(nx, ny, step) for step in range(1, ny)]
    odd_pairs = pairs_odd(nx, ny)

    def swap(array, pairs):
        return lax.ppermute(array, axes, pairs)

    def local(source, reaction, boundary_kind, disk_id, disk_mask, thrust):
        inputs = [
            pltpu.with_memory_space_constraint(array, pltpu.HBM)
            for array in (source, reaction, boundary_kind, disk_id, disk_mask, thrust.reshape(1, -1))
        ]

        def staged(shape):
            return (
                [shape, shape]
                + [pltpu.VMEM(shape, jnp.int32)] * 3
                + [(1, thrust.shape[0]), pltpu.SemaphoreType.DMA((5, 5)), pltpu.SemaphoreType.DMA(())]
            )

        core, chip, row, odd = call(
            faces,
            [(128, 128), (128, 128), (64, 128), (64, 128)],
            *inputs,
            in_specs=[HBM] * 6,
            scratch=staged((4, 16, 512)),
            name="faces",
        )
        a_core, a_chip = swap(core, core_pairs), swap(chip, chip_pairs)
        a_odd, a_row = swap(odd, odd_pairs), swap(row, row_pairs[0])
        f, g, d, absorb = call(
            set_up, [field, field, field, (64, 512)], *inputs, in_specs=[HBM] * 6, scratch=staged(field), name="set_up"
        )
        a_core, a_chip, a_odd, a_row, f, g, d, absorb = lax.optimization_barrier(
            (a_core, a_chip, a_odd, a_row, f, g, d, absorb)
        )
        s, to_core, to_row, to_odd, block = call(
            smooth,
            [field, (136, 128), (192, 128), (192, 128), (48, 128)],
            f, g, d, absorb, a_core, a_chip, a_row, a_odd,
            scratch=[slab, slab, (192, 512), slab, slab, slab, slab, slab, slab],
            name="smooth",
        )
        s_core = swap(to_core, core_pairs)
        s_row, s_odd = swap(to_row, row_pairs[0]), swap(to_odd, odd_pairs)
        mine, to_chip = call(to_chip_kernel, [(40, 128), (176, 128)], block, s_core, s, name="to_chip")
        s_chip = swap(to_chip, chip_pairs)
        full, beyond = call(from_chip_kernel, [(40, 128), (40, 128)], mine, block, s_chip, name="from_chip")
        c_core = swap(full, core_pairs)
        (window,) = call(window_kernel, [(136, 128)], full, beyond, c_core, s_chip, s_core, s, name="window")
        windows = [window] + [swap(window, pairs) for pairs in row_pairs]
        pressure, coarse = call(
            finish,
            [field, (4, planes, 128)],
            f, g, s, a_core, a_chip, a_row, a_odd, s_core, s_chip, s_row, s_odd, *windows,
            scratch=[(ny, 136, 128)]
            + [(planes, 16, 128)] * 3
            + [(planes + 2, 16, 128)] * 3
            + [(6, 16, 512), (20, 16, 512), long, slab, slab, (32, 512), (32, 512), slab, slab, field]
            + [pltpu.SemaphoreType.DMA((4,))],
            out_specs=[HBM, VMEM],
            name="finish",
        )
        return pressure, coarse

    spec = P("gx", "gy", None)
    return jax.shard_map(
        local,
        mesh=mesh,
        in_specs=(spec, spec, spec, spec, spec, P()),
        out_specs=(spec, P("gx", None, None)),
        check_vma=False,
    )
```

```python
import jax
import jax.numpy as jnp
from jax import lax
from jax.experimental import pallas as pl
from jax.experimental.pallas import tpu as pltpu
from jax.sharding import PartitionSpec as P

SWEEPS = 4
OMEGA = 0.8
WALL_PENALTY = 0.4
INFLOW_PENALTY = 0.2
CHEB_LOW = 0.1
CHEB_HIGH = 2.0
F32 = jnp.float32
VMEM = pl.BlockSpec(memory_space=pltpu.VMEM)


HBM = pl.BlockSpec(memory_space=pltpu.HBM)


def call(kernel, outs, *args, scratch=(), name=None, in_specs=None, out_specs=None):
    return pl.pallas_call(
        kernel,
        out_shape=[jax.ShapeDtypeStruct(s, F32) for s in outs],
        in_specs=in_specs or [VMEM] * len(args),
        out_specs=out_specs or [VMEM] * len(outs),
        scratch_shapes=[pltpu.VMEM(s, F32) if isinstance(s, tuple) else s for s in scratch],
        compiler_params=pltpu.CompilerParams(vmem_limit_bytes=16 << 20),
        name=name,
    )(*args)


def pairs_core(nx, ny):
    return [(x * ny + y, (x ^ 1) * ny + y) for x in range(nx) for y in range(ny)]


def pairs_chip(nx, ny):
    found = []
    for x in range(nx):
        for y in range(ny):
            if x in (0, nx - 1):
                found.append((x * ny + y, x * ny + (y ^ 1)))
            else:
                found.append((x * ny + y, (x + 1 if x % 2 else x - 1) * ny + y))
    return found


def pairs_row(nx, ny, step):
    return [(x * ny + y, x * ny + (y ^ step)) for x in range(nx) for y in range(ny)]


def pairs_odd(nx, ny):
    return [
        (x * ny + y, x * ny + (y + 1 if y % 2 else y - 1) % ny) for x in range(nx) for y in range(ny)
    ]


def put(ref, row, slab):
    rows = slab.shape[0]
    for j in range(slab.shape[1] // 128):
        ref[row + rows * j : row + rows * (j + 1), :] = slab[:, 128 * j : 128 * (j + 1)]


def get(ref, row, rows, width):
    return jnp.concatenate(
        [ref[row + rows * j : row + rows * (j + 1), :] for j in range(width // 128)], axis=1
    )


def iota(shape, dim):
    return lax.broadcasted_iota(jnp.int32, shape, dim)


def beside_z(slab):
    depth = slab.shape[1]
    lane = iota(slab.shape, 1)
    above = jnp.where(lane == depth - 1, 0.0, pltpu.roll(slab, depth - 1, 1))
    below = jnp.where(lane == 0, 0.0, pltpu.roll(slab, 1, 1))
    return above + below


def beside(slab, low=None, high=None):
    rows, depth = slab.shape
    tiles, columns = rows // 8, depth // 128
    lane, row = iota((8, 128), 1), iota((8, 128), 0)
    piece = [[slab[8 * t : 8 * t + 8, 128 * j : 128 * j + 128] for j in range(columns)] for t in range(tiles)]
    left = [[pltpu.roll(p, 127, 1) for p in line] for line in piece]
    right = [[pltpu.roll(p, 1, 1) for p in line] for line in piece]
    up = [[pltpu.roll(p, 7, 0) for p in line] for line in piece]
    down = [[pltpu.roll(p, 1, 0) for p in line] for line in piece]

    def outer(line, j):
        return 0.0 if line is None else jnp.broadcast_to(line[:, 128 * j : 128 * j + 128], (8, 128))

    lines = []
    for t in range(tiles):
        parts = []
        for j in range(columns):
            above = jnp.where(lane == 127, left[t][j + 1] if j + 1 < columns else 0.0, left[t][j])
            below = jnp.where(lane == 0, right[t][j - 1] if j > 0 else 0.0, right[t][j])
            after = jnp.where(row == 7, up[t + 1][j] if t + 1 < tiles else outer(high, j), up[t][j])
            before = jnp.where(row == 0, down[t - 1][j] if t > 0 else outer(low, j), down[t][j])
            parts.append((above + below) + (after + before))
        lines.append(jnp.concatenate(parts, axis=1))
    return jnp.concatenate(lines, axis=0)


def dot(left, right):
    return lax.dot_general(
        left,
        right,
        (((1,), (0,)), ((), ())),
        precision=lax.Precision.HIGHEST,
        preferred_element_type=F32,
    )


def group_lanes(depth):
    return (iota((depth, depth // 4), 0) // 4 == iota((depth, depth // 4), 1)).astype(F32)


def spread_lanes(rows):
    count, lanes = rows.shape
    pad = -count % 8
    if pad:
        rows = jnp.concatenate([rows, jnp.zeros((pad, lanes), F32)], axis=0)
    parts = []
    for j in range(4):
        index = iota(rows.shape, 1) // 4 + (lanes // 4) * j
        parts.append(jnp.take_along_axis(rows, index, axis=1, mode="promise_in_bounds"))
    return jnp.concatenate(parts, axis=1)[:count]


def spread_rows(ref, plane, start):
    row = iota((16, 128), 0) // 4
    value = jnp.zeros((16, 128), F32)
    for q in range(4):
        value = jnp.where(row == q, jnp.broadcast_to(ref[plane, start + q : start + q + 1, :], (16, 128)), value)
    return value


def spread_planes(ref, plane, column):
    row = iota((16, 128), 0) // 4
    value = jnp.zeros((16, 128), F32)
    for q in range(4):
        value = jnp.where(row == q, jnp.broadcast_to(ref[plane + q, column : column + 1, :], (16, 128)), value)
    return value


def solution(mesh):
    nx, ny = mesh.shape["gx"], mesh.shape["gy"]
    assert nx % 2 == 0 and ny % 2 == 0 and ny & (ny - 1) == 0
    axes = ("gx", "gy")

    def where_am_i():
        x, y = lax.axis_index("gx"), lax.axis_index("gy")
        return x, y, x % 2 == 0, y % 2 == 0

    def look_up(table, ids):
        spare = jnp.zeros((1, 128 - table.shape[1]), F32)
        row = jnp.broadcast_to(jnp.concatenate([table, spare], axis=1), (16, 128))
        parts = [
            jnp.take_along_axis(row, ids[:, 128 * j : 128 * (j + 1)], axis=1, mode="promise_in_bounds") for j in range(4)
        ]
        return jnp.concatenate(parts, axis=1)

    def first_of(source, reaction, kinds, ids, mask, table):
        a = reaction + jnp.where(kinds == 1, WALL_PENALTY, jnp.where(kinds == 2, INFLOW_PENALTY, 0.0))
        diagonal = 6.0 + a
        scale = OMEGA / diagonal
        return (source + mask.astype(F32) * look_up(table, ids)) * scale, scale, diagonal, a

    def faces(*refs):
        inputs, thrust, messages, buffers, table, sems, table_sem = (
            refs[:5], refs[5], refs[6:10], refs[10:15], refs[15], refs[16], refs[17]
        )
        core, chip, row, odd = messages
        _, _, x_even, y_even = where_am_i()
        near, far = jnp.where(x_even, 15, 0), jnp.where(x_even, 0, 15)
        moves = [pltpu.make_async_copy(thrust, table, table_sem)]
        for i, (hbm, buffer) in enumerate(zip(inputs, buffers)):
            for j, part in enumerate((hbm.at[:, 0, :], hbm.at[:, 15, :], hbm.at[far], hbm.at[near])):
                moves.append(pltpu.make_async_copy(part, buffer.at[j], sems.at[i, j]))
        for move in moves:
            move.start()
        for move in moves:
            move.wait()
        found = [first_of(*(buffer[j] for buffer in buffers), table[...])[:2] for j in range(4)]
        (low, _), (high, _), (f_far, g_far), (f_near, g_near) = found
        put(row, 0, jnp.where(y_even, high, low))
        put(odd, 0, jnp.where(y_even, low, high))
        put(chip, 0, f_far)
        put(chip, 64, g_far)
        put(core, 0, f_near)
        put(core, 64, g_near)

    def set_up(source, reaction, kind, disk_id, disk_mask, table, f, g, d, absorb):
        for k in range(4):
            total = jnp.zeros((16, 512), F32)
            for x in range(4 * k, 4 * k + 4):
                f[x], g[x], d[x], a = first_of(source[x], reaction[x], kind[x], disk_id[x], disk_mask[x], table[...])
                total = total + a
            absorb[16 * k : 16 * k + 16, :] = total

    def halo_x(core, chip, row, x, x_even):
        a, b = get(core, row, 16, 512), get(chip, row, 16, 512)
        left = jnp.where(x > 0, jnp.where(x_even, b, a), 0.0)
        right = jnp.where(x < nx - 1, jnp.where(x_even, a, b), 0.0)
        return left, right

    def halo_y(row, odd, at, y, y_even):
        a, b = get(row, at, 16, 512), get(odd, at, 16, 512)
        low = jnp.where(y > 0, jnp.where(y_even, b, a), 0.0)
        high = jnp.where(y < ny - 1, jnp.where(y_even, a, b), 0.0)
        return low, high

    def smooth(f, g, d, absorb, core, chip, row, odd, s, to_core, to_row, to_odd, block, lo, hi, V, y0, y1, y14, y15, g0, g15):
        x_at, y_at, x_even, y_even = where_am_i()
        left, right = halo_x(core, chip, 0, x_at, x_even)
        lo[...], hi[...] = halo_y(row, odd, 0, y_at, y_even)
        for x in range(16):
            here = f[x]
            scale = g[x]
            total = (f[x - 1] if x > 0 else left) + (f[x + 1] if x < 15 else right)
            total = total + beside(here, lo[x : x + 1, :], hi[x : x + 1, :])
            value = 1.2 * here + scale * total
            s[x] = value
            y0[x : x + 1, :] = value[0:1, :]
            y1[x : x + 1, :] = value[1:2, :]
            y14[x : x + 1, :] = value[14:15, :]
            y15[x : x + 1, :] = value[15:16, :]
            g0[x : x + 1, :] = scale[0:1, :]
            g15[x : x + 1, :] = scale[15:16, :]
        for k in range(4):
            total = jnp.zeros((16, 512), F32)
            for x in range(4 * k, 4 * k + 4):
                here = s[x]
                total = total + d[x] * (1.25 * f[x] - here)
                total = total + beside(here)
                if x > 0:
                    total = total + s[x - 1]
                if x < 15:
                    total = total + s[x + 1]
            V[16 * k : 16 * k + 16, :] = total
        V[64:128, :] = absorb[...]
        V[128:144, :] = s[0]
        V[144:160, :] = s[15]
        V[160:176, :] = y0[...]
        V[176:192, :] = y15[...]
        out, src = iota((48, 192), 0), iota((48, 192), 1)
        cx, cy = out % 4, out // 8
        in_bulk = (out < 32) & (src < 128) & (src // 64 == (out // 4) % 2)
        bulk = in_bulk & ((src % 64) // 16 == cx) & ((src % 16) // 4 == cy)
        faces = (out >= 32) & (src >= 128) & ((out - 32) // 4 == (src - 128) // 16) & ((src % 16) // 4 == cx)
        picked = dot((bulk | faces).astype(F32), V[...])
        block[...] = dot(picked, group_lanes(512))
        put(to_core, 0, s[jnp.where(x_even, 15, 0)])
        put(to_core, 64, s[jnp.where(x_even, 14, 1)])
        to_core[128:132, :] = jnp.where(x_even, block[36:40, :], block[32:36, :])
        to_core[132:136, :] = jnp.zeros((4, 128), F32)
        for at, (low, high) in enumerate(((y0, y15), (y1, y14), (g0, g15))):
            a, b = low[...], high[...]
            put(to_row, 64 * at, jnp.where(y_even, b, a))
            put(to_odd, 64 * at, jnp.where(y_even, a, b))

    def to_chip_kernel(block, core, s, mine, to_chip):
        _, _, x_even, _ = where_am_i()
        mine[...] = jnp.concatenate([block[0:32, :], block[40:48, :]], axis=0)
        face = core[128:136, :]
        for cy in range(4):
            line = face[cy : cy + 1, :]
            mine[8 * cy : 8 * cy + 1, :] = block[8 * cy : 8 * cy + 1, :] + jnp.where(x_even, 0.0, line)
            mine[8 * cy + 3 : 8 * cy + 4, :] = block[8 * cy + 3 : 8 * cy + 4, :] + jnp.where(x_even, line, 0.0)
        put(to_chip, 0, s[jnp.where(x_even, 0, 15)])
        put(to_chip, 64, s[jnp.where(x_even, 1, 14)])
        to_chip[128:168, :] = mine[...]
        to_chip[168:172, :] = jnp.where(x_even, block[32:36, :], block[36:40, :])
        to_chip[172:176, :] = jnp.zeros((4, 128), F32)

    def from_chip_kernel(mine, block, chip, full, beyond):
        x_at, _, x_even, _ = where_am_i()
        has = jnp.where(x_even, x_at > 0, x_at < nx - 1)
        full[...] = mine[...]
        beyond[...] = chip[128:168, :]
        mine_face = jnp.where(x_even, block[32:36, :], block[36:40, :])
        face = chip[168:176, :]
        for cy in range(4):
            line = jnp.where(has, face[cy : cy + 1, :], 0.0)
            own = mine_face[cy : cy + 1, :]
            a, b = 8 * cy, 8 * cy + 3
            full[a : a + 1, :] = mine[a : a + 1, :] + jnp.where(x_even, line, 0.0)
            full[b : b + 1, :] = mine[b : b + 1, :] + jnp.where(x_even, 0.0, line)
            beyond[a : a + 1, :] = chip[128 + a : 129 + a, :] + jnp.where(x_even, 0.0, own)
            beyond[b : b + 1, :] = chip[128 + b : 129 + b, :] + jnp.where(x_even, own, 0.0)

    def window_kernel(full, beyond, core, chip, s_core, s, window):
        x_at, _, x_even, _ = where_am_i()
        mid = full[...]
        a, b = core[...], beyond[...]
        left, right = jnp.where(x_even, b, a), jnp.where(x_even, a, b)
        for at, block in enumerate((left, mid, right)):
            for cy in range(4):
                window[24 * cy + 4 * at : 24 * cy + 4 * at + 4, :] = block[8 * cy : 8 * cy + 4, :]
                window[24 * cy + 12 + 4 * at : 24 * cy + 16 + 4 * at, :] = block[8 * cy + 4 : 8 * cy + 8, :]
            window[96 + 4 * at : 100 + 4 * at, :] = block[32:36, :]
            window[108 + 4 * at : 112 + 4 * at, :] = block[36:40, :]
        low, high = halo_x(s_core, chip, 0, x_at, x_even)
        for at, line in enumerate((low[0:1, :], low[15:16, :], high[0:1, :], high[15:16, :])):
            put(window, 120 + 4 * at, line)

    planes = 4 * ny

    def finish(*refs):
        f, g, s, a_core, a_chip, a_row, a_odd, s_core, s_chip, s_row, s_odd = refs[:11]
        windows = refs[11 : 11 + ny]
        pressure, coarse = refs[11 + ny : 13 + ny]
        every, res, diag, inv, one, two, sol, Pc, T, U, yl, yh, tl, th, ul, uh, result, slab_out, sems = refs[13 + ny :]
        x_at, y_at, x_even, y_even = where_am_i()
        for step, window in enumerate(windows):
            every[jnp.bitwise_xor(y_at, step)] = window[...]

        row = iota((16, 128), 0)
        valid = ((row >= 4) | (x_at > 0)) & ((row < 8) | (x_at < nx - 1)) & (row < 12)
        blank = jnp.zeros((4, 128), F32)

        def twelve(value):
            return jnp.concatenate([value, blank], axis=0)

        centre = (CHEB_HIGH + CHEB_LOW) / 2.0
        half_range = (CHEB_HIGH - CHEB_LOW) / 2.0
        aspect = centre / half_range
        factor = 1.0 / aspect
        empty = jnp.zeros((16, 128), F32)
        for ref in (one, two, sol):
            ref[0] = empty
            ref[planes + 1] = empty
        for at in range(ny):
            for cy in range(4):
                plane = 4 * at + cy
                value = every[at, 24 * cy : 24 * cy + 12, :]
                if cy == 0 and at > 0:
                    value = value + every[at - 1, 108:120, :]
                if cy == 3 and at < ny - 1:
                    value = value + every[at + 1, 96:108, :]
                value = jnp.where(valid, twelve(value), 0.0)
                centre_value = 6.0 + twelve(every[at, 24 * cy + 12 : 24 * cy + 24, :]) / 16.0
                inverse = jnp.where(valid, 1.0 / (16.0 * centre_value), 0.0)
                res[plane] = value
                diag[plane] = centre_value
                inv[plane] = inverse
                direction = inverse * value / centre
                one[plane + 1] = direction
                sol[plane + 1] = direction
        now, later = one, two
        for number in range(1, SWEEPS):
            factor_next = 1.0 / (2.0 * aspect - factor)
            keep, gain = factor_next * factor, 2.0 * factor_next / half_range

            lane = iota((16, 128), 1)
            for plane in range(planes):
                here = now[plane + 1]
                total = now[plane] + now[plane + 2]
                total = total + pltpu.roll(here, 15, 0) + pltpu.roll(here, 1, 0)
                total = total + jnp.where(lane == 127, 0.0, pltpu.roll(here, 127, 1))
                total = total + jnp.where(lane == 0, 0.0, pltpu.roll(here, 1, 1))
                residual = res[plane] - 16.0 * (diag[plane] * here - total)
                res[plane] = residual
                direction = keep * here + gain * inv[plane] * residual
                later[plane + 1] = direction
                sol[plane + 1] = sol[plane + 1] + direction
            now, later = later, now
            factor = factor_next
        for plane in range(planes):
            for cx in range(4):
                slab_out[cx, plane : plane + 1, :] = sol[plane + 1, 4 + cx : 5 + cx, :]
        moves = [pltpu.make_async_copy(slab_out, coarse, sems.at[8])]
        moves[0].start()

        first_plane = 4 * y_at + 1
        for at in range(6):
            Pc[at] = spread_lanes(spread_planes(sol, first_plane, 3 + at))
        s_left, s_right = halo_x(s_core, s_chip, 0, x_at, x_even)
        s_left2, s_right2 = halo_x(s_core, s_chip, 64, x_at, x_even)
        T[0], T[1] = s_left2 + Pc[0], s_left + Pc[0]
        T[18], T[19] = s_right + Pc[5], s_right2 + Pc[5]

        for x in range(16):
            T[x + 2] = s[x] + Pc[x // 4 + 1]
        below, above = first_plane - 1, first_plane + 4
        y1_low, y1_high = halo_y(s_row, s_odd, 0, y_at, y_even)
        y2_low, y2_high = halo_y(s_row, s_odd, 64, y_at, y_even)
        g_low, g_high = halo_y(s_row, s_odd, 128, y_at, y_even)
        f_low, f_high = halo_y(a_row, a_odd, 0, y_at, y_even)
        before, after = jnp.maximum(y_at - 1, 0), jnp.minimum(y_at + 1, ny - 1)
        outer = {}
        for name, ref, plane, s1, s2, who, inside, line in (
            ("low", tl, below, y1_low, y2_low, before, y_at > 0, 1),
            ("high", th, above, y1_high, y2_high, after, y_at < ny - 1, 0),
        ):
            spread = spread_lanes(spread_rows(sol, plane, 4))
            ref[8:24, :] = s1 + spread
            outer[name] = s2 + spread
            for at, cx, base, there in ((7, 3, 0, x_at > 0), (24, 8, 2, x_at < nx - 1)):
                corner = jnp.concatenate(
                    [every[who, pl.ds(120 + 4 * (base + line) + j, 1), :] for j in range(4)], axis=1
                )
                corner = jnp.where(inside & there, corner, 0.0)
                ref[at : at + 1, :] = corner + spread_lanes(sol[plane, cx : cx + 1, :])

        f_left, f_right = halo_x(a_core, a_chip, 0, x_at, x_even)
        g_left, g_right = halo_x(a_core, a_chip, 64, x_at, x_even)

        def fourth_at(at, forcing, scale):
            here = T[at + 1]
            total = T[at] + T[at + 2] + beside(here, tl[at + 7 : at + 8, :], th[at + 7 : at + 8, :])
            return 0.2 * here + forcing + scale * total

        U[0] = fourth_at(0, f_left, g_left)
        U[17] = fourth_at(17, f_right, g_right)

        for x in range(16):
            U[x + 1] = fourth_at(x + 1, f[x], g[x])
            here = T[x + 2]
            yl[x : x + 1, :] = here[0:1, :]
            yh[x : x + 1, :] = here[15:16, :]
        for ref, out, edge, far, forcing, scale in (
            (tl, ul, yl, outer["low"], f_low, g_low),
            (th, uh, yh, outer["high"], f_high, g_high),
        ):
            here = ref[8:24, :]
            total = far + edge[...] + ref[7:23, :] + ref[9:25, :] + beside_z(here)
            out[...] = 0.2 * here + forcing + scale * total

        for x in range(16):
            here = U[x + 1]
            total = U[x] + U[x + 2] + beside(here, ul[x : x + 1, :], uh[x : x + 1, :])
            result[x] = 0.2 * here + f[x] + g[x] * total
            if x % 2 == 1:
                part = pl.ds(x - 1, 2)
                moves.append(pltpu.make_async_copy(result.at[part], pressure.at[part], sems.at[x // 2]))
                moves[-1].start()
        for move in moves:
            move.wait()

    slab, field, long = (16, 512), (16, 16, 512), (18, 16, 512)
    core_pairs, chip_pairs = pairs_core(nx, ny), pairs_chip(nx, ny)
    row_pairs = [pairs_row(nx, ny, step) for step in range(1, ny)]
    odd_pairs = pairs_odd(nx, ny)

    def swap(array, pairs):
        return lax.ppermute(array, axes, pairs)

    def local(source, reaction, boundary_kind, disk_id, disk_mask, thrust):
        inputs = (source, reaction, boundary_kind, disk_id, disk_mask, thrust.reshape(1, -1))
        some = (4, 16, 512)
        core, chip, row, odd = call(
            faces,
            [(128, 128), (128, 128), (64, 128), (64, 128)],
            *(pltpu.with_memory_space_constraint(array, pltpu.HBM) for array in inputs),
            in_specs=[HBM] * 6,
            scratch=[some, some]
            + [pltpu.VMEM(some, jnp.int32)] * 3
            + [(1, thrust.shape[0]), pltpu.SemaphoreType.DMA((5, 4)), pltpu.SemaphoreType.DMA(())],
            name="faces",
        )
        a_core, a_chip = swap(core, core_pairs), swap(chip, chip_pairs)
        a_odd, a_row = swap(odd, odd_pairs), swap(row, row_pairs[0])
        f, g, d, absorb = call(set_up, [field, field, field, (64, 512)], *inputs, name="set_up")
        a_core, a_chip, a_odd, a_row, f, g, d, absorb = lax.optimization_barrier(
            (a_core, a_chip, a_odd, a_row, f, g, d, absorb)
        )
        s, to_core, to_row, to_odd, block = call(
            smooth,
            [field, (136, 128), (192, 128), (192, 128), (48, 128)],
            f, g, d, absorb, a_core, a_chip, a_row, a_odd,
            scratch=[slab, slab, (192, 512), slab, slab, slab, slab, slab, slab],
            name="smooth",
        )
        s_core = swap(to_core, core_pairs)
        s_row, s_odd = swap(to_row, row_pairs[0]), swap(to_odd, odd_pairs)
        mine, to_chip = call(to_chip_kernel, [(40, 128), (176, 128)], block, s_core, s, name="to_chip")
        s_chip = swap(to_chip, chip_pairs)
        full, beyond = call(from_chip_kernel, [(40, 128), (40, 128)], mine, block, s_chip, name="from_chip")
        c_core = swap(full, core_pairs)
        (window,) = call(window_kernel, [(136, 128)], full, beyond, c_core, s_chip, s_core, s, name="window")
        windows = [window] + [swap(window, pairs) for pairs in row_pairs]
        pressure, coarse = call(
            finish,
            [field, (4, planes, 128)],
            f, g, s, a_core, a_chip, a_row, a_odd, s_core, s_chip, s_row, s_odd, *windows,
            scratch=[(ny, 136, 128)]
            + [(planes, 16, 128)] * 3
            + [(planes + 2, 16, 128)] * 3
            + [(6, 16, 512), (20, 16, 512), long, slab, slab, (32, 512), (32, 512), slab, slab, field]
            + [(4, planes, 128), pltpu.SemaphoreType.DMA((9,))],
            out_specs=[HBM, HBM],
            name="finish",
        )
        return pressure, coarse

    spec = P("gx", "gy", None)
    return jax.shard_map(
        local,
        mesh=mesh,
        in_specs=(spec, spec, spec, spec, spec, P()),
        out_specs=(spec, P("gx", None, None)),
        check_vma=False,
    )
```

```python
import jax
import jax.numpy as jnp
from jax import lax
from jax.experimental import pallas as pl
from jax.experimental.pallas import tpu as pltpu
from jax.sharding import PartitionSpec as P

SWEEPS = 4
OMEGA = 0.8
WALL_PENALTY = 0.4
INFLOW_PENALTY = 0.2
CHEB_LOW = 0.1
CHEB_HIGH = 2.0
F32 = jnp.float32
VMEM = pl.BlockSpec(memory_space=pltpu.VMEM)


HBM = pl.BlockSpec(memory_space=pltpu.HBM)


def call(kernel, outs, *args, scratch=(), name=None, in_specs=None, out_specs=None):
    return pl.pallas_call(
        kernel,
        out_shape=[jax.ShapeDtypeStruct(s, F32) for s in outs],
        in_specs=in_specs or [VMEM] * len(args),
        out_specs=out_specs or [VMEM] * len(outs),
        scratch_shapes=[pltpu.VMEM(s, F32) if isinstance(s, tuple) else s for s in scratch],
        compiler_params=pltpu.CompilerParams(vmem_limit_bytes=16 << 20),
        name=name,
    )(*args)


def pairs_core(nx, ny):
    return [(x * ny + y, (x ^ 1) * ny + y) for x in range(nx) for y in range(ny)]


def pairs_chip(nx, ny):
    found = []
    for x in range(nx):
        for y in range(ny):
            if x in (0, nx - 1):
                found.append((x * ny + y, x * ny + (y ^ 1)))
            else:
                found.append((x * ny + y, (x + 1 if x % 2 else x - 1) * ny + y))
    return found


def pairs_row(nx, ny, step):
    return [(x * ny + y, x * ny + (y ^ step)) for x in range(nx) for y in range(ny)]


def pairs_odd(nx, ny):
    return [
        (x * ny + y, x * ny + (y + 1 if y % 2 else y - 1) % ny) for x in range(nx) for y in range(ny)
    ]


def put(ref, row, slab):
    rows = slab.shape[0]
    for j in range(slab.shape[1] // 128):
        ref[row + rows * j : row + rows * (j + 1), :] = slab[:, 128 * j : 128 * (j + 1)]


def get(ref, row, rows, width):
    return jnp.concatenate(
        [ref[row + rows * j : row + rows * (j + 1), :] for j in range(width // 128)], axis=1
    )


def iota(shape, dim):
    return lax.broadcasted_iota(jnp.int32, shape, dim)


def beside_z(slab):
    depth = slab.shape[1]
    lane = iota(slab.shape, 1)
    above = jnp.where(lane == depth - 1, 0.0, pltpu.roll(slab, depth - 1, 1))
    below = jnp.where(lane == 0, 0.0, pltpu.roll(slab, 1, 1))
    return above + below


def beside(slab, low=None, high=None):
    rows, depth = slab.shape
    tiles, columns = rows // 8, depth // 128
    lane, row = iota((8, 128), 1), iota((8, 128), 0)
    piece = [[slab[8 * t : 8 * t + 8, 128 * j : 128 * j + 128] for j in range(columns)] for t in range(tiles)]
    left = [[pltpu.roll(p, 127, 1) for p in line] for line in piece]
    right = [[pltpu.roll(p, 1, 1) for p in line] for line in piece]
    up = [[pltpu.roll(p, 7, 0) for p in line] for line in piece]
    down = [[pltpu.roll(p, 1, 0) for p in line] for line in piece]

    def outer(line, j):
        return 0.0 if line is None else jnp.broadcast_to(line[:, 128 * j : 128 * j + 128], (8, 128))

    lines = []
    for t in range(tiles):
        parts = []
        for j in range(columns):
            above = jnp.where(lane == 127, left[t][j + 1] if j + 1 < columns else 0.0, left[t][j])
            below = jnp.where(lane == 0, right[t][j - 1] if j > 0 else 0.0, right[t][j])
            after = jnp.where(row == 7, up[t + 1][j] if t + 1 < tiles else outer(high, j), up[t][j])
            before = jnp.where(row == 0, down[t - 1][j] if t > 0 else outer(low, j), down[t][j])
            parts.append((above + below) + (after + before))
        lines.append(jnp.concatenate(parts, axis=1))
    return jnp.concatenate(lines, axis=0)


def dot(left, right):
    return lax.dot_general(
        left,
        right,
        (((1,), (0,)), ((), ())),
        precision=lax.Precision.HIGHEST,
        preferred_element_type=F32,
    )


def group_lanes(depth):
    return (iota((depth, depth // 4), 0) // 4 == iota((depth, depth // 4), 1)).astype(F32)


def spread_lanes(rows):
    count, lanes = rows.shape
    pad = -count % 8
    if pad:
        rows = jnp.concatenate([rows, jnp.zeros((pad, lanes), F32)], axis=0)
    parts = []
    for j in range(4):
        index = iota(rows.shape, 1) // 4 + (lanes // 4) * j
        parts.append(jnp.take_along_axis(rows, index, axis=1, mode="promise_in_bounds"))
    return jnp.concatenate(parts, axis=1)[:count]


def spread_rows(ref, plane, start):
    row = iota((16, 128), 0) // 4
    value = jnp.zeros((16, 128), F32)
    for q in range(4):
        value = jnp.where(row == q, jnp.broadcast_to(ref[plane, start + q : start + q + 1, :], (16, 128)), value)
    return value


def spread_planes(ref, plane, column):
    row = iota((16, 128), 0) // 4
    value = jnp.zeros((16, 128), F32)
    for q in range(4):
        value = jnp.where(row == q, jnp.broadcast_to(ref[plane + q, column : column + 1, :], (16, 128)), value)
    return value


def solution(mesh):
    nx, ny = mesh.shape["gx"], mesh.shape["gy"]
    assert nx % 2 == 0 and ny % 2 == 0 and ny & (ny - 1) == 0
    axes = ("gx", "gy")

    def where_am_i():
        x, y = lax.axis_index("gx"), lax.axis_index("gy")
        return x, y, x % 2 == 0, y % 2 == 0

    def look_up(table, ids):
        spare = jnp.zeros((1, 128 - table.shape[1]), F32)
        row = jnp.broadcast_to(jnp.concatenate([table, spare], axis=1), (16, 128))
        parts = [
            jnp.take_along_axis(row, ids[:, 128 * j : 128 * (j + 1)], axis=1, mode="promise_in_bounds") for j in range(4)
        ]
        return jnp.concatenate(parts, axis=1)

    def first_of(source, reaction, kinds, ids, mask, table):
        a = reaction + jnp.where(kinds == 1, WALL_PENALTY, jnp.where(kinds == 2, INFLOW_PENALTY, 0.0))
        diagonal = 6.0 + a
        scale = OMEGA / diagonal
        return (source + mask.astype(F32) * look_up(table, ids)) * scale, scale, diagonal, a

    def faces(*refs):
        inputs, thrust, messages, buffers, table, sems, table_sem = (
            refs[:5], refs[5], refs[6:10], refs[10:15], refs[15], refs[16], refs[17]
        )
        core, chip, row, odd = messages
        _, _, x_even, y_even = where_am_i()
        near, far = jnp.where(x_even, 15, 0), jnp.where(x_even, 0, 15)
        moves = [pltpu.make_async_copy(thrust, table, table_sem)]
        for i, (hbm, buffer) in enumerate(zip(inputs, buffers)):
            for j, part in enumerate((hbm.at[:, 0, :], hbm.at[:, 15, :], hbm.at[far], hbm.at[near])):
                moves.append(pltpu.make_async_copy(part, buffer.at[j], sems.at[i, j]))
        for move in moves:
            move.start()
        for move in moves:
            move.wait()
        low, high, f_far, f_near = (first_of(*(buffer[j] for buffer in buffers), table[...])[0] for j in range(4))
        put(row, 0, jnp.where(y_even, high, low))
        put(odd, 0, jnp.where(y_even, low, high))
        put(chip, 0, f_far)
        put(core, 0, f_near)

    def set_up(source, reaction, kind, disk_id, disk_mask, table, f, g, d, absorb):
        for k in range(4):
            total = jnp.zeros((16, 512), F32)
            for x in range(4 * k, 4 * k + 4):
                f[x], g[x], d[x], a = first_of(source[x], reaction[x], kind[x], disk_id[x], disk_mask[x], table[...])
                total = total + a
            absorb[16 * k : 16 * k + 16, :] = total

    def halo_x(core, chip, row, x, x_even):
        a, b = get(core, row, 16, 512), get(chip, row, 16, 512)
        left = jnp.where(x > 0, jnp.where(x_even, b, a), 0.0)
        right = jnp.where(x < nx - 1, jnp.where(x_even, a, b), 0.0)
        return left, right

    def halo_y(row, odd, at, y, y_even):
        a, b = get(row, at, 16, 512), get(odd, at, 16, 512)
        low = jnp.where(y > 0, jnp.where(y_even, b, a), 0.0)
        high = jnp.where(y < ny - 1, jnp.where(y_even, a, b), 0.0)
        return low, high

    def smooth(f, g, d, absorb, core, chip, row, odd, s, to_core, to_row, to_odd, block, lo, hi, V, y0, y1, y14, y15, g0, g15):
        x_at, y_at, x_even, y_even = where_am_i()
        left, right = halo_x(core, chip, 0, x_at, x_even)
        lo[...], hi[...] = halo_y(row, odd, 0, y_at, y_even)
        for x in range(16):
            here = f[x]
            scale = g[x]
            total = (f[x - 1] if x > 0 else left) + (f[x + 1] if x < 15 else right)
            total = total + beside(here, lo[x : x + 1, :], hi[x : x + 1, :])
            value = 1.2 * here + scale * total
            s[x] = value
            y0[x : x + 1, :] = value[0:1, :]
            y1[x : x + 1, :] = value[1:2, :]
            y14[x : x + 1, :] = value[14:15, :]
            y15[x : x + 1, :] = value[15:16, :]
            g0[x : x + 1, :] = scale[0:1, :]
            g15[x : x + 1, :] = scale[15:16, :]
        for k in range(4):
            total = jnp.zeros((16, 512), F32)
            for x in range(4 * k, 4 * k + 4):
                here = s[x]
                total = total + d[x] * (1.25 * f[x] - here)
                total = total + beside(here)
                if x > 0:
                    total = total + s[x - 1]
                if x < 15:
                    total = total + s[x + 1]
            V[16 * k : 16 * k + 16, :] = total
        V[64:128, :] = absorb[...]
        V[128:144, :] = s[0]
        V[144:160, :] = s[15]
        V[160:176, :] = y0[...]
        V[176:192, :] = y15[...]
        out, src = iota((48, 192), 0), iota((48, 192), 1)
        cx, cy = out % 4, out // 8
        in_bulk = (out < 32) & (src < 128) & (src // 64 == (out // 4) % 2)
        bulk = in_bulk & ((src % 64) // 16 == cx) & ((src % 16) // 4 == cy)
        faces = (out >= 32) & (src >= 128) & ((out - 32) // 4 == (src - 128) // 16) & ((src % 16) // 4 == cx)
        picked = dot((bulk | faces).astype(F32), V[...])
        block[...] = dot(picked, group_lanes(512))
        put(to_core, 0, s[jnp.where(x_even, 15, 0)])
        put(to_core, 64, s[jnp.where(x_even, 14, 1)])
        put(to_core, 128, g[jnp.where(x_even, 15, 0)])
        to_core[192:196, :] = jnp.where(x_even, block[36:40, :], block[32:36, :])
        to_core[196:200, :] = jnp.zeros((4, 128), F32)
        for at, (low, high) in enumerate(((y0, y15), (y1, y14), (g0, g15))):
            a, b = low[...], high[...]
            put(to_row, 64 * at, jnp.where(y_even, b, a))
            put(to_odd, 64 * at, jnp.where(y_even, a, b))

    def to_chip_kernel(block, core, s, g, mine, to_chip):
        _, _, x_even, _ = where_am_i()
        mine[...] = jnp.concatenate([block[0:32, :], block[40:48, :]], axis=0)
        face = core[192:200, :]
        for cy in range(4):
            line = face[cy : cy + 1, :]
            mine[8 * cy : 8 * cy + 1, :] = block[8 * cy : 8 * cy + 1, :] + jnp.where(x_even, 0.0, line)
            mine[8 * cy + 3 : 8 * cy + 4, :] = block[8 * cy + 3 : 8 * cy + 4, :] + jnp.where(x_even, line, 0.0)
        put(to_chip, 0, s[jnp.where(x_even, 0, 15)])
        put(to_chip, 64, s[jnp.where(x_even, 1, 14)])
        put(to_chip, 128, g[jnp.where(x_even, 0, 15)])
        to_chip[192:232, :] = mine[...]
        to_chip[232:236, :] = jnp.where(x_even, block[32:36, :], block[36:40, :])
        to_chip[236:240, :] = jnp.zeros((4, 128), F32)

    def from_chip_kernel(mine, block, chip, full, beyond):
        x_at, _, x_even, _ = where_am_i()
        has = jnp.where(x_even, x_at > 0, x_at < nx - 1)
        full[...] = mine[...]
        beyond[...] = chip[192:232, :]
        mine_face = jnp.where(x_even, block[32:36, :], block[36:40, :])
        face = chip[232:240, :]
        for cy in range(4):
            line = jnp.where(has, face[cy : cy + 1, :], 0.0)
            own = mine_face[cy : cy + 1, :]
            a, b = 8 * cy, 8 * cy + 3
            full[a : a + 1, :] = mine[a : a + 1, :] + jnp.where(x_even, line, 0.0)
            full[b : b + 1, :] = mine[b : b + 1, :] + jnp.where(x_even, 0.0, line)
            beyond[a : a + 1, :] = chip[192 + a : 193 + a, :] + jnp.where(x_even, 0.0, own)
            beyond[b : b + 1, :] = chip[192 + b : 193 + b, :] + jnp.where(x_even, own, 0.0)

    def window_kernel(full, beyond, core, chip, s_core, s, window):
        x_at, _, x_even, _ = where_am_i()
        mid = full[...]
        a, b = core[...], beyond[...]
        left, right = jnp.where(x_even, b, a), jnp.where(x_even, a, b)
        for at, block in enumerate((left, mid, right)):
            for cy in range(4):
                window[24 * cy + 4 * at : 24 * cy + 4 * at + 4, :] = block[8 * cy : 8 * cy + 4, :]
                window[24 * cy + 12 + 4 * at : 24 * cy + 16 + 4 * at, :] = block[8 * cy + 4 : 8 * cy + 8, :]
            window[96 + 4 * at : 100 + 4 * at, :] = block[32:36, :]
            window[108 + 4 * at : 112 + 4 * at, :] = block[36:40, :]
        low, high = halo_x(s_core, chip, 0, x_at, x_even)
        for at, line in enumerate((low[0:1, :], low[15:16, :], high[0:1, :], high[15:16, :])):
            put(window, 120 + 4 * at, line)

    planes = 4 * ny

    def finish(*refs):
        f, g, s, a_core, a_chip, a_row, a_odd, s_core, s_chip, s_row, s_odd = refs[:11]
        windows = refs[11 : 11 + ny]
        pressure, coarse = refs[11 + ny : 13 + ny]
        every, res, diag, inv, one, two, sol, Pc, T, U, yl, yh, tl, th, ul, uh, result, slab_out, sems = refs[13 + ny :]
        x_at, y_at, x_even, y_even = where_am_i()
        for step, window in enumerate(windows):
            every[jnp.bitwise_xor(y_at, step)] = window[...]

        row = iota((16, 128), 0)
        valid = ((row >= 4) | (x_at > 0)) & ((row < 8) | (x_at < nx - 1)) & (row < 12)
        blank = jnp.zeros((4, 128), F32)

        def twelve(value):
            return jnp.concatenate([value, blank], axis=0)

        centre = (CHEB_HIGH + CHEB_LOW) / 2.0
        half_range = (CHEB_HIGH - CHEB_LOW) / 2.0
        aspect = centre / half_range
        factor = 1.0 / aspect
        empty = jnp.zeros((16, 128), F32)
        for ref in (one, two, sol):
            ref[0] = empty
            ref[planes + 1] = empty
        for at in range(ny):
            for cy in range(4):
                plane = 4 * at + cy
                value = every[at, 24 * cy : 24 * cy + 12, :]
                if cy == 0 and at > 0:
                    value = value + every[at - 1, 108:120, :]
                if cy == 3 and at < ny - 1:
                    value = value + every[at + 1, 96:108, :]
                value = jnp.where(valid, twelve(value), 0.0)
                centre_value = 6.0 + twelve(every[at, 24 * cy + 12 : 24 * cy + 24, :]) / 16.0
                inverse = jnp.where(valid, 1.0 / (16.0 * centre_value), 0.0)
                res[plane] = value
                diag[plane] = centre_value
                inv[plane] = inverse
                direction = inverse * value / centre
                one[plane + 1] = direction
                sol[plane + 1] = direction
        now, later = one, two
        for number in range(1, SWEEPS):
            factor_next = 1.0 / (2.0 * aspect - factor)
            keep, gain = factor_next * factor, 2.0 * factor_next / half_range

            lane = iota((16, 128), 1)
            for plane in range(planes):
                here = now[plane + 1]
                total = now[plane] + now[plane + 2]
                total = total + pltpu.roll(here, 15, 0) + pltpu.roll(here, 1, 0)
                total = total + jnp.where(lane == 127, 0.0, pltpu.roll(here, 127, 1))
                total = total + jnp.where(lane == 0, 0.0, pltpu.roll(here, 1, 1))
                residual = res[plane] - 16.0 * (diag[plane] * here - total)
                res[plane] = residual
                direction = keep * here + gain * inv[plane] * residual
                later[plane + 1] = direction
                sol[plane + 1] = sol[plane + 1] + direction
            now, later = later, now
            factor = factor_next
        for plane in range(planes):
            for cx in range(4):
                slab_out[cx, plane : plane + 1, :] = sol[plane + 1, 4 + cx : 5 + cx, :]
        moves = [pltpu.make_async_copy(slab_out, coarse, sems.at[8])]
        moves[0].start()

        first_plane = 4 * y_at + 1
        for at in range(6):
            Pc[at] = spread_lanes(spread_planes(sol, first_plane, 3 + at))
        s_left, s_right = halo_x(s_core, s_chip, 0, x_at, x_even)
        s_left2, s_right2 = halo_x(s_core, s_chip, 64, x_at, x_even)
        T[0], T[1] = s_left2 + Pc[0], s_left + Pc[0]
        T[18], T[19] = s_right + Pc[5], s_right2 + Pc[5]

        for x in range(16):
            T[x + 2] = s[x] + Pc[x // 4 + 1]
        below, above = first_plane - 1, first_plane + 4
        y1_low, y1_high = halo_y(s_row, s_odd, 0, y_at, y_even)
        y2_low, y2_high = halo_y(s_row, s_odd, 64, y_at, y_even)
        g_low, g_high = halo_y(s_row, s_odd, 128, y_at, y_even)
        f_low, f_high = halo_y(a_row, a_odd, 0, y_at, y_even)
        before, after = jnp.maximum(y_at - 1, 0), jnp.minimum(y_at + 1, ny - 1)
        outer = {}
        for name, ref, plane, s1, s2, who, inside, line in (
            ("low", tl, below, y1_low, y2_low, before, y_at > 0, 1),
            ("high", th, above, y1_high, y2_high, after, y_at < ny - 1, 0),
        ):
            spread = spread_lanes(spread_rows(sol, plane, 4))
            ref[8:24, :] = s1 + spread
            outer[name] = s2 + spread
            for at, cx, base, there in ((7, 3, 0, x_at > 0), (24, 8, 2, x_at < nx - 1)):
                corner = jnp.concatenate(
                    [every[who, pl.ds(120 + 4 * (base + line) + j, 1), :] for j in range(4)], axis=1
                )
                corner = jnp.where(inside & there, corner, 0.0)
                ref[at : at + 1, :] = corner + spread_lanes(sol[plane, cx : cx + 1, :])

        f_left, f_right = halo_x(a_core, a_chip, 0, x_at, x_even)
        g_left, g_right = halo_x(s_core, s_chip, 128, x_at, x_even)

        def fourth_at(at, forcing, scale):
            here = T[at + 1]
            total = T[at] + T[at + 2] + beside(here, tl[at + 7 : at + 8, :], th[at + 7 : at + 8, :])
            return 0.2 * here + forcing + scale * total

        U[0] = fourth_at(0, f_left, g_left)
        U[17] = fourth_at(17, f_right, g_right)

        for x in range(16):
            U[x + 1] = fourth_at(x + 1, f[x], g[x])
            here = T[x + 2]
            yl[x : x + 1, :] = here[0:1, :]
            yh[x : x + 1, :] = here[15:16, :]
        for ref, out, edge, far, forcing, scale in (
            (tl, ul, yl, outer["low"], f_low, g_low),
            (th, uh, yh, outer["high"], f_high, g_high),
        ):
            here = ref[8:24, :]
            total = far + edge[...] + ref[7:23, :] + ref[9:25, :] + beside_z(here)
            out[...] = 0.2 * here + forcing + scale * total

        for x in range(16):
            here = U[x + 1]
            total = U[x] + U[x + 2] + beside(here, ul[x : x + 1, :], uh[x : x + 1, :])
            result[x] = 0.2 * here + f[x] + g[x] * total
            if x % 2 == 1:
                part = pl.ds(x - 1, 2)
                moves.append(pltpu.make_async_copy(result.at[part], pressure.at[part], sems.at[x // 2]))
                moves[-1].start()
        for move in moves:
            move.wait()

    slab, field, long = (16, 512), (16, 16, 512), (18, 16, 512)
    core_pairs, chip_pairs = pairs_core(nx, ny), pairs_chip(nx, ny)
    row_pairs = [pairs_row(nx, ny, step) for step in range(1, ny)]
    odd_pairs = pairs_odd(nx, ny)

    def swap(array, pairs):
        return lax.ppermute(array, axes, pairs)

    def local(source, reaction, boundary_kind, disk_id, disk_mask, thrust):
        inputs = (source, reaction, boundary_kind, disk_id, disk_mask, thrust.reshape(1, -1))
        some = (4, 16, 512)
        core, chip, row, odd = call(
            faces,
            [(64, 128)] * 4,
            *(pltpu.with_memory_space_constraint(array, pltpu.HBM) for array in inputs),
            in_specs=[HBM] * 6,
            scratch=[some, some]
            + [pltpu.VMEM(some, jnp.int32)] * 3
            + [(1, thrust.shape[0]), pltpu.SemaphoreType.DMA((5, 4)), pltpu.SemaphoreType.DMA(())],
            name="faces",
        )
        a_core, a_chip = swap(core, core_pairs), swap(chip, chip_pairs)
        a_odd, a_row = swap(odd, odd_pairs), swap(row, row_pairs[0])
        f, g, d, absorb = call(set_up, [field, field, field, (64, 512)], *inputs, name="set_up")
        a_odd, a_row, a_chip, a_core, f, g, d, absorb = lax.optimization_barrier(
            (a_odd, a_row, a_chip, a_core, f, g, d, absorb)
        )
        s, to_core, to_row, to_odd, block = call(
            smooth,
            [field, (200, 128), (192, 128), (192, 128), (48, 128)],
            f, g, d, absorb, a_core, a_chip, a_row, a_odd,
            scratch=[slab, slab, (192, 512), slab, slab, slab, slab, slab, slab],
            name="smooth",
        )
        s_core = swap(to_core, core_pairs)
        s_row, s_odd = swap(to_row, row_pairs[0]), swap(to_odd, odd_pairs)
        mine, to_chip = call(to_chip_kernel, [(40, 128), (240, 128)], block, s_core, s, g, name="to_chip")
        s_chip = swap(to_chip, chip_pairs)
        full, beyond = call(from_chip_kernel, [(40, 128), (40, 128)], mine, block, s_chip, name="from_chip")
        c_core = swap(full, core_pairs)
        (window,) = call(window_kernel, [(136, 128)], full, beyond, c_core, s_chip, s_core, s, name="window")
        windows = [window] + [swap(window, pairs) for pairs in row_pairs]
        pressure, coarse = call(
            finish,
            [field, (4, planes, 128)],
            f, g, s, a_core, a_chip, a_row, a_odd, s_core, s_chip, s_row, s_odd, *windows,
            scratch=[(ny, 136, 128)]
            + [(planes, 16, 128)] * 3
            + [(planes + 2, 16, 128)] * 3
            + [(6, 16, 512), (20, 16, 512), long, slab, slab, (32, 512), (32, 512), slab, slab, field]
            + [(4, planes, 128), pltpu.SemaphoreType.DMA((9,))],
            out_specs=[HBM, HBM],
            name="finish",
        )
        return pressure, coarse

    spec = P("gx", "gy", None)
    return jax.shard_map(
        local,
        mesh=mesh,
        in_specs=(spec, spec, spec, spec, spec, P()),
        out_specs=(spec, P("gx", None, None)),
        check_vma=False,
    )
```

```python
import jax
import jax.numpy as jnp
from jax import lax
from jax.experimental import pallas as pl
from jax.experimental.pallas import tpu as pltpu
from jax.sharding import PartitionSpec as P

SWEEPS = 4
OMEGA = 0.8
WALL_PENALTY = 0.4
INFLOW_PENALTY = 0.2
CHEB_LOW = 0.1
CHEB_HIGH = 2.0
F32 = jnp.float32
VMEM = pl.BlockSpec(memory_space=pltpu.VMEM)


HBM = pl.BlockSpec(memory_space=pltpu.HBM)


def call(kernel, outs, *args, scratch=(), name=None, in_specs=None, out_specs=None):
    return pl.pallas_call(
        kernel,
        out_shape=[jax.ShapeDtypeStruct(s, F32) for s in outs],
        in_specs=in_specs or [VMEM] * len(args),
        out_specs=out_specs or [VMEM] * len(outs),
        scratch_shapes=[pltpu.VMEM(s, F32) if isinstance(s, tuple) else s for s in scratch],
        compiler_params=pltpu.CompilerParams(vmem_limit_bytes=16 << 20),
        name=name,
    )(*args)


def pairs_core(nx, ny):
    return [(x * ny + y, (x ^ 1) * ny + y) for x in range(nx) for y in range(ny)]


def pairs_chip(nx, ny):
    found = []
    for x in range(nx):
        for y in range(ny):
            if x in (0, nx - 1):
                found.append((x * ny + y, x * ny + (y ^ (ny // 2))))
            else:
                found.append((x * ny + y, (x + 1 if x % 2 else x - 1) * ny + y))
    return found


def pairs_row(nx, ny, step):
    return [(x * ny + y, x * ny + (y ^ step)) for x in range(nx) for y in range(ny)]


def pairs_odd(nx, ny):
    return [
        (x * ny + y, x * ny + (y + 1 if y % 2 else y - 1) % ny) for x in range(nx) for y in range(ny)
    ]


def put(ref, row, slab):
    rows = slab.shape[0]
    for j in range(slab.shape[1] // 128):
        ref[row + rows * j : row + rows * (j + 1), :] = slab[:, 128 * j : 128 * (j + 1)]


def get(ref, row, rows, width):
    return jnp.concatenate(
        [ref[row + rows * j : row + rows * (j + 1), :] for j in range(width // 128)], axis=1
    )


def iota(shape, dim):
    return lax.broadcasted_iota(jnp.int32, shape, dim)


def beside_z(slab):
    depth = slab.shape[1]
    lane = iota(slab.shape, 1)
    above = jnp.where(lane == depth - 1, 0.0, pltpu.roll(slab, depth - 1, 1))
    below = jnp.where(lane == 0, 0.0, pltpu.roll(slab, 1, 1))
    return above + below


def beside(slab, low=None, high=None):
    rows, depth = slab.shape
    tiles, columns = rows // 8, depth // 128
    lane, row = iota((8, 128), 1), iota((8, 128), 0)
    piece = [[slab[8 * t : 8 * t + 8, 128 * j : 128 * j + 128] for j in range(columns)] for t in range(tiles)]
    left = [[pltpu.roll(p, 127, 1) for p in line] for line in piece]
    right = [[pltpu.roll(p, 1, 1) for p in line] for line in piece]
    up = [[pltpu.roll(p, 7, 0) for p in line] for line in piece]
    down = [[pltpu.roll(p, 1, 0) for p in line] for line in piece]

    def outer(line, j):
        return 0.0 if line is None else jnp.broadcast_to(line[:, 128 * j : 128 * j + 128], (8, 128))

    lines = []
    for t in range(tiles):
        parts = []
        for j in range(columns):
            above = jnp.where(lane == 127, left[t][j + 1] if j + 1 < columns else 0.0, left[t][j])
            below = jnp.where(lane == 0, right[t][j - 1] if j > 0 else 0.0, right[t][j])
            after = jnp.where(row == 7, up[t + 1][j] if t + 1 < tiles else outer(high, j), up[t][j])
            before = jnp.where(row == 0, down[t - 1][j] if t > 0 else outer(low, j), down[t][j])
            parts.append((above + below) + (after + before))
        lines.append(jnp.concatenate(parts, axis=1))
    return jnp.concatenate(lines, axis=0)


def dot(left, right):
    return lax.dot_general(
        left,
        right,
        (((1,), (0,)), ((), ())),
        precision=lax.Precision.HIGHEST,
        preferred_element_type=F32,
    )


def group_lanes(depth):
    return (iota((depth, depth // 4), 0) // 4 == iota((depth, depth // 4), 1)).astype(F32)


def spread_lanes(rows):
    count, lanes = rows.shape
    pad = -count % 8
    if pad:
        rows = jnp.concatenate([rows, jnp.zeros((pad, lanes), F32)], axis=0)
    parts = []
    for j in range(4):
        index = iota(rows.shape, 1) // 4 + (lanes // 4) * j
        parts.append(jnp.take_along_axis(rows, index, axis=1, mode="promise_in_bounds"))
    return jnp.concatenate(parts, axis=1)[:count]


def spread_rows(ref, plane, start):
    row = iota((16, 128), 0) // 4
    value = jnp.zeros((16, 128), F32)
    for q in range(4):
        value = jnp.where(row == q, jnp.broadcast_to(ref[plane, start + q : start + q + 1, :], (16, 128)), value)
    return value


def spread_planes(ref, plane, column):
    row = iota((16, 128), 0) // 4
    value = jnp.zeros((16, 128), F32)
    for q in range(4):
        value = jnp.where(row == q, jnp.broadcast_to(ref[plane + q, column : column + 1, :], (16, 128)), value)
    return value


def solution(mesh):
    nx, ny = mesh.shape["gx"], mesh.shape["gy"]
    assert nx % 2 == 0 and ny % 2 == 0 and ny & (ny - 1) == 0
    axes = ("gx", "gy")

    def where_am_i():
        x, y = lax.axis_index("gx"), lax.axis_index("gy")
        return x, y, x % 2 == 0, y % 2 == 0

    def look_up(table, ids):
        spare = jnp.zeros((1, 128 - table.shape[1]), F32)
        row = jnp.broadcast_to(jnp.concatenate([table, spare], axis=1), (16, 128))
        parts = [
            jnp.take_along_axis(row, ids[:, 128 * j : 128 * (j + 1)], axis=1, mode="promise_in_bounds") for j in range(4)
        ]
        return jnp.concatenate(parts, axis=1)

    def first_of(source, reaction, kinds, ids, mask, table):
        a = reaction + jnp.where(kinds == 1, WALL_PENALTY, jnp.where(kinds == 2, INFLOW_PENALTY, 0.0))
        diagonal = 6.0 + a
        scale = OMEGA / diagonal
        return (source + mask.astype(F32) * look_up(table, ids)) * scale, scale, diagonal, a

    def faces(*refs):
        inputs, thrust, messages, buffers, table, sems, table_sem = (
            refs[:5], refs[5], refs[6:10], refs[10:15], refs[15], refs[16], refs[17]
        )
        core, chip, row, odd = messages
        _, _, x_even, y_even = where_am_i()
        near, far = jnp.where(x_even, 15, 0), jnp.where(x_even, 0, 15)
        moves = [pltpu.make_async_copy(thrust, table, table_sem)]
        for i, (hbm, buffer) in enumerate(zip(inputs, buffers)):
            for j, part in enumerate((hbm.at[:, 0, :], hbm.at[:, 15, :], hbm.at[far], hbm.at[near])):
                moves.append(pltpu.make_async_copy(part, buffer.at[j], sems.at[i, j]))
        for move in moves:
            move.start()
        for move in moves:
            move.wait()
        low, high, f_far, f_near = (first_of(*(buffer[j] for buffer in buffers), table[...])[0] for j in range(4))
        put(row, 0, jnp.where(y_even, high, low))
        put(odd, 0, jnp.where(y_even, low, high))
        put(chip, 0, f_far)
        put(core, 0, f_near)

    def set_up(source, reaction, kind, disk_id, disk_mask, table, f, g, d, absorb):
        for k in range(4):
            total = jnp.zeros((16, 512), F32)
            for x in range(4 * k, 4 * k + 4):
                f[x], g[x], d[x], a = first_of(source[x], reaction[x], kind[x], disk_id[x], disk_mask[x], table[...])
                total = total + a
            absorb[16 * k : 16 * k + 16, :] = total

    def halo_x(core, chip, row, x, x_even):
        a, b = get(core, row, 16, 512), get(chip, row, 16, 512)
        left = jnp.where(x > 0, jnp.where(x_even, b, a), 0.0)
        right = jnp.where(x < nx - 1, jnp.where(x_even, a, b), 0.0)
        return left, right

    def halo_y(row, odd, at, y, y_even):
        a, b = get(row, at, 16, 512), get(odd, at, 16, 512)
        low = jnp.where(y > 0, jnp.where(y_even, b, a), 0.0)
        high = jnp.where(y < ny - 1, jnp.where(y_even, a, b), 0.0)
        return low, high

    def smooth(f, g, d, absorb, core, chip, row, odd, s, to_core, to_row, to_odd, block, lo, hi, V, y0, y1, y14, y15, g0, g15):
        x_at, y_at, x_even, y_even = where_am_i()
        left, right = halo_x(core, chip, 0, x_at, x_even)
        lo[...], hi[...] = halo_y(row, odd, 0, y_at, y_even)
        for x in range(16):
            here = f[x]
            scale = g[x]
            total = (f[x - 1] if x > 0 else left) + (f[x + 1] if x < 15 else right)
            total = total + beside(here, lo[x : x + 1, :], hi[x : x + 1, :])
            value = 1.2 * here + scale * total
            s[x] = value
            y0[x : x + 1, :] = value[0:1, :]
            y1[x : x + 1, :] = value[1:2, :]
            y14[x : x + 1, :] = value[14:15, :]
            y15[x : x + 1, :] = value[15:16, :]
            g0[x : x + 1, :] = scale[0:1, :]
            g15[x : x + 1, :] = scale[15:16, :]
        for k in range(4):
            total = jnp.zeros((16, 512), F32)
            for x in range(4 * k, 4 * k + 4):
                here = s[x]
                total = total + d[x] * (1.25 * f[x] - here)
                total = total + beside(here)
                if x > 0:
                    total = total + s[x - 1]
                if x < 15:
                    total = total + s[x + 1]
            V[16 * k : 16 * k + 16, :] = total
        V[64:128, :] = absorb[...]
        V[128:144, :] = s[0]
        V[144:160, :] = s[15]
        V[160:176, :] = y0[...]
        V[176:192, :] = y15[...]
        out, src = iota((48, 192), 0), iota((48, 192), 1)
        cx, cy = out % 4, out // 8
        in_bulk = (out < 32) & (src < 128) & (src // 64 == (out // 4) % 2)
        bulk = in_bulk & ((src % 64) // 16 == cx) & ((src % 16) // 4 == cy)
        faces = (out >= 32) & (src >= 128) & ((out - 32) // 4 == (src - 128) // 16) & ((src % 16) // 4 == cx)
        picked = dot((bulk | faces).astype(F32), V[...])
        block[...] = dot(picked, group_lanes(512))
        put(to_core, 0, s[jnp.where(x_even, 15, 0)])
        put(to_core, 64, s[jnp.where(x_even, 14, 1)])
        put(to_core, 128, g[jnp.where(x_even, 15, 0)])
        to_core[192:196, :] = jnp.where(x_even, block[36:40, :], block[32:36, :])
        to_core[196:200, :] = jnp.zeros((4, 128), F32)
        for at, (low, high) in enumerate(((y0, y15), (y1, y14), (g0, g15))):
            a, b = low[...], high[...]
            put(to_row, 64 * at, jnp.where(y_even, b, a))
            put(to_odd, 64 * at, jnp.where(y_even, a, b))

    def to_chip_kernel(block, core, s, g, mine, to_chip):
        _, _, x_even, _ = where_am_i()
        mine[...] = jnp.concatenate([block[0:32, :], block[40:48, :]], axis=0)
        face = core[192:200, :]
        for cy in range(4):
            line = face[cy : cy + 1, :]
            mine[8 * cy : 8 * cy + 1, :] = block[8 * cy : 8 * cy + 1, :] + jnp.where(x_even, 0.0, line)
            mine[8 * cy + 3 : 8 * cy + 4, :] = block[8 * cy + 3 : 8 * cy + 4, :] + jnp.where(x_even, line, 0.0)
        put(to_chip, 0, s[jnp.where(x_even, 0, 15)])
        put(to_chip, 64, s[jnp.where(x_even, 1, 14)])
        put(to_chip, 128, g[jnp.where(x_even, 0, 15)])
        to_chip[192:232, :] = mine[...]
        to_chip[232:236, :] = jnp.where(x_even, block[32:36, :], block[36:40, :])
        to_chip[236:240, :] = jnp.zeros((4, 128), F32)

    def from_chip_kernel(mine, block, chip, full, beyond):
        x_at, _, x_even, _ = where_am_i()
        has = jnp.where(x_even, x_at > 0, x_at < nx - 1)
        full[...] = mine[...]
        beyond[...] = chip[192:232, :]
        mine_face = jnp.where(x_even, block[32:36, :], block[36:40, :])
        face = chip[232:240, :]
        for cy in range(4):
            line = jnp.where(has, face[cy : cy + 1, :], 0.0)
            own = mine_face[cy : cy + 1, :]
            a, b = 8 * cy, 8 * cy + 3
            full[a : a + 1, :] = mine[a : a + 1, :] + jnp.where(x_even, line, 0.0)
            full[b : b + 1, :] = mine[b : b + 1, :] + jnp.where(x_even, 0.0, line)
            beyond[a : a + 1, :] = chip[192 + a : 193 + a, :] + jnp.where(x_even, 0.0, own)
            beyond[b : b + 1, :] = chip[192 + b : 193 + b, :] + jnp.where(x_even, own, 0.0)

    def window_kernel(full, beyond, core, chip, s_core, s, window):
        x_at, _, x_even, _ = where_am_i()
        mid = full[...]
        a, b = core[...], beyond[...]
        left, right = jnp.where(x_even, b, a), jnp.where(x_even, a, b)
        for at, block in enumerate((left, mid, right)):
            for cy in range(4):
                window[24 * cy + 4 * at : 24 * cy + 4 * at + 4, :] = block[8 * cy : 8 * cy + 4, :]
                window[24 * cy + 12 + 4 * at : 24 * cy + 16 + 4 * at, :] = block[8 * cy + 4 : 8 * cy + 8, :]
            window[96 + 4 * at : 100 + 4 * at, :] = block[32:36, :]
            window[108 + 4 * at : 112 + 4 * at, :] = block[36:40, :]
        low, high = halo_x(s_core, chip, 0, x_at, x_even)
        for at, line in enumerate((low[0:1, :], low[15:16, :], high[0:1, :], high[15:16, :])):
            put(window, 120 + 4 * at, line)

    planes = 4 * ny

    def finish(*refs):
        f, g, s, a_core, a_chip, a_row, a_odd, s_core, s_chip, s_row, s_odd = refs[:11]
        windows = refs[11 : 11 + ny]
        pressure, coarse = refs[11 + ny : 13 + ny]
        every, res, diag, inv, one, two, sol, Pc, T, U, yl, yh, tl, th, ul, uh, result, slab_out, sems = refs[13 + ny :]
        x_at, y_at, x_even, y_even = where_am_i()
        for step, window in enumerate(windows):
            every[jnp.bitwise_xor(y_at, step)] = window[...]

        row = iota((16, 128), 0)
        valid = ((row >= 4) | (x_at > 0)) & ((row < 8) | (x_at < nx - 1)) & (row < 12)
        blank = jnp.zeros((4, 128), F32)

        def twelve(value):
            return jnp.concatenate([value, blank], axis=0)

        centre = (CHEB_HIGH + CHEB_LOW) / 2.0
        half_range = (CHEB_HIGH - CHEB_LOW) / 2.0
        aspect = centre / half_range
        factor = 1.0 / aspect
        empty = jnp.zeros((16, 128), F32)
        for ref in (one, two, sol):
            ref[0] = empty
            ref[planes + 1] = empty
        for at in range(ny):
            for cy in range(4):
                plane = 4 * at + cy
                value = every[at, 24 * cy : 24 * cy + 12, :]
                if cy == 0 and at > 0:
                    value = value + every[at - 1, 108:120, :]
                if cy == 3 and at < ny - 1:
                    value = value + every[at + 1, 96:108, :]
                value = jnp.where(valid, twelve(value), 0.0)
                centre_value = 6.0 + twelve(every[at, 24 * cy + 12 : 24 * cy + 24, :]) / 16.0
                inverse = jnp.where(valid, 1.0 / (16.0 * centre_value), 0.0)
                res[plane] = value
                diag[plane] = centre_value
                inv[plane] = inverse
                direction = inverse * value / centre
                one[plane + 1] = direction
                sol[plane + 1] = direction
        now, later = one, two
        for number in range(1, SWEEPS):
            factor_next = 1.0 / (2.0 * aspect - factor)
            keep, gain = factor_next * factor, 2.0 * factor_next / half_range

            lane = iota((16, 128), 1)
            for plane in range(planes):
                here = now[plane + 1]
                total = now[plane] + now[plane + 2]
                total = total + pltpu.roll(here, 15, 0) + pltpu.roll(here, 1, 0)
                total = total + jnp.where(lane == 127, 0.0, pltpu.roll(here, 127, 1))
                total = total + jnp.where(lane == 0, 0.0, pltpu.roll(here, 1, 1))
                residual = res[plane] - 16.0 * (diag[plane] * here - total)
                res[plane] = residual
                direction = keep * here + gain * inv[plane] * residual
                later[plane + 1] = direction
                sol[plane + 1] = sol[plane + 1] + direction
            now, later = later, now
            factor = factor_next
        for plane in range(planes):
            for cx in range(4):
                slab_out[cx, plane : plane + 1, :] = sol[plane + 1, 4 + cx : 5 + cx, :]
        moves = [pltpu.make_async_copy(slab_out, coarse, sems.at[8])]
        moves[0].start()

        first_plane = 4 * y_at + 1
        for at in range(6):
            Pc[at] = spread_lanes(spread_planes(sol, first_plane, 3 + at))
        s_left, s_right = halo_x(s_core, s_chip, 0, x_at, x_even)
        s_left2, s_right2 = halo_x(s_core, s_chip, 64, x_at, x_even)
        T[0], T[1] = s_left2 + Pc[0], s_left + Pc[0]
        T[18], T[19] = s_right + Pc[5], s_right2 + Pc[5]

        for x in range(16):
            T[x + 2] = s[x] + Pc[x // 4 + 1]
        below, above = first_plane - 1, first_plane + 4
        y1_low, y1_high = halo_y(s_row, s_odd, 0, y_at, y_even)
        y2_low, y2_high = halo_y(s_row, s_odd, 64, y_at, y_even)
        g_low, g_high = halo_y(s_row, s_odd, 128, y_at, y_even)
        f_low, f_high = halo_y(a_row, a_odd, 0, y_at, y_even)
        before, after = jnp.maximum(y_at - 1, 0), jnp.minimum(y_at + 1, ny - 1)
        outer = {}
        for name, ref, plane, s1, s2, who, inside, line in (
            ("low", tl, below, y1_low, y2_low, before, y_at > 0, 1),
            ("high", th, above, y1_high, y2_high, after, y_at < ny - 1, 0),
        ):
            spread = spread_lanes(spread_rows(sol, plane, 4))
            ref[8:24, :] = s1 + spread
            outer[name] = s2 + spread
            for at, cx, base, there in ((7, 3, 0, x_at > 0), (24, 8, 2, x_at < nx - 1)):
                corner = jnp.concatenate(
                    [every[who, pl.ds(120 + 4 * (base + line) + j, 1), :] for j in range(4)], axis=1
                )
                corner = jnp.where(inside & there, corner, 0.0)
                ref[at : at + 1, :] = corner + spread_lanes(sol[plane, cx : cx + 1, :])

        f_left, f_right = halo_x(a_core, a_chip, 0, x_at, x_even)
        g_left, g_right = halo_x(s_core, s_chip, 128, x_at, x_even)

        def fourth_at(at, forcing, scale):
            here = T[at + 1]
            total = T[at] + T[at + 2] + beside(here, tl[at + 7 : at + 8, :], th[at + 7 : at + 8, :])
            return 0.2 * here + forcing + scale * total

        U[0] = fourth_at(0, f_left, g_left)
        U[17] = fourth_at(17, f_right, g_right)

        for x in range(16):
            U[x + 1] = fourth_at(x + 1, f[x], g[x])
            here = T[x + 2]
            yl[x : x + 1, :] = here[0:1, :]
            yh[x : x + 1, :] = here[15:16, :]
        for ref, out, edge, far, forcing, scale in (
            (tl, ul, yl, outer["low"], f_low, g_low),
            (th, uh, yh, outer["high"], f_high, g_high),
        ):
            here = ref[8:24, :]
            total = far + edge[...] + ref[7:23, :] + ref[9:25, :] + beside_z(here)
            out[...] = 0.2 * here + forcing + scale * total

        for x in range(16):
            here = U[x + 1]
            total = U[x] + U[x + 2] + beside(here, ul[x : x + 1, :], uh[x : x + 1, :])
            result[x] = 0.2 * here + f[x] + g[x] * total
            if x % 2 == 1:
                part = pl.ds(x - 1, 2)
                moves.append(pltpu.make_async_copy(result.at[part], pressure.at[part], sems.at[x // 2]))
                moves[-1].start()
        for move in moves:
            move.wait()

    slab, field, long = (16, 512), (16, 16, 512), (18, 16, 512)
    core_pairs, chip_pairs = pairs_core(nx, ny), pairs_chip(nx, ny)
    row_pairs = [pairs_row(nx, ny, step) for step in range(1, ny)]
    odd_pairs = pairs_odd(nx, ny)

    def swap(array, pairs):
        return lax.ppermute(array, axes, pairs)

    def local(source, reaction, boundary_kind, disk_id, disk_mask, thrust):
        inputs = (source, reaction, boundary_kind, disk_id, disk_mask, thrust.reshape(1, -1))
        some = (4, 16, 512)
        core, chip, row, odd = call(
            faces,
            [(64, 128)] * 4,
            *(pltpu.with_memory_space_constraint(array, pltpu.HBM) for array in inputs),
            in_specs=[HBM] * 6,
            scratch=[some, some]
            + [pltpu.VMEM(some, jnp.int32)] * 3
            + [(1, thrust.shape[0]), pltpu.SemaphoreType.DMA((5, 4)), pltpu.SemaphoreType.DMA(())],
            name="faces",
        )
        a_core, a_chip = swap(core, core_pairs), swap(chip, chip_pairs)
        a_odd, a_row = swap(odd, odd_pairs), swap(row, row_pairs[0])
        f, g, d, absorb = call(set_up, [field, field, field, (64, 512)], *inputs, name="set_up")
        a_odd, a_row, a_chip, a_core, f, g, d, absorb = lax.optimization_barrier(
            (a_odd, a_row, a_chip, a_core, f, g, d, absorb)
        )
        s, to_core, to_row, to_odd, block = call(
            smooth,
            [field, (200, 128), (192, 128), (192, 128), (48, 128)],
            f, g, d, absorb, a_core, a_chip, a_row, a_odd,
            scratch=[slab, slab, (192, 512), slab, slab, slab, slab, slab, slab],
            name="smooth",
        )
        s_core = swap(to_core, core_pairs)
        s_row, s_odd = swap(to_row, row_pairs[0]), swap(to_odd, odd_pairs)
        mine, to_chip = call(to_chip_kernel, [(40, 128), (240, 128)], block, s_core, s, g, name="to_chip")
        s_chip = swap(to_chip, chip_pairs)
        full, beyond = call(from_chip_kernel, [(40, 128), (40, 128)], mine, block, s_chip, name="from_chip")
        c_core = swap(full, core_pairs)
        (window,) = call(window_kernel, [(136, 128)], full, beyond, c_core, s_chip, s_core, s, name="window")
        windows = [window] + [swap(window, pairs) for pairs in row_pairs]
        pressure, coarse = call(
            finish,
            [field, (4, planes, 128)],
            f, g, s, a_core, a_chip, a_row, a_odd, s_core, s_chip, s_row, s_odd, *windows,
            scratch=[(ny, 136, 128)]
            + [(planes, 16, 128)] * 3
            + [(planes + 2, 16, 128)] * 3
            + [(6, 16, 512), (20, 16, 512), long, slab, slab, (32, 512), (32, 512), slab, slab, field]
            + [(4, planes, 128), pltpu.SemaphoreType.DMA((9,))],
            out_specs=[HBM, HBM],
            name="finish",
        )
        return pressure, coarse

    spec = P("gx", "gy", None)
    return jax.shard_map(
        local,
        mesh=mesh,
        in_specs=(spec, spec, spec, spec, spec, P()),
        out_specs=(spec, P("gx", None, None)),
        check_vma=False,
    )
```

```python
import jax
import jax.numpy as jnp
from jax import lax
from jax.experimental import pallas as pl
from jax.experimental.pallas import tpu as pltpu
from jax.sharding import PartitionSpec as P

SWEEPS = 4
OMEGA = 0.8
WALL_PENALTY = 0.4
INFLOW_PENALTY = 0.2
CHEB_LOW = 0.1
CHEB_HIGH = 2.0
F32 = jnp.float32
VMEM = pl.BlockSpec(memory_space=pltpu.VMEM)


HBM = pl.BlockSpec(memory_space=pltpu.HBM)


def call(kernel, outs, *args, scratch=(), name=None, in_specs=None, out_specs=None):
    return pl.pallas_call(
        kernel,
        out_shape=[jax.ShapeDtypeStruct(s, F32) for s in outs],
        in_specs=in_specs or [VMEM] * len(args),
        out_specs=out_specs or [VMEM] * len(outs),
        scratch_shapes=[pltpu.VMEM(s, F32) if isinstance(s, tuple) else s for s in scratch],
        compiler_params=pltpu.CompilerParams(vmem_limit_bytes=16 << 20),
        name=name,
    )(*args)


def pairs_core(nx, ny):
    return [(x * ny + y, (x ^ 1) * ny + y) for x in range(nx) for y in range(ny)]


def pairs_chip(nx, ny):
    found = []
    for x in range(nx):
        for y in range(ny):
            if x in (0, nx - 1):
                found.append((x * ny + y, x * ny + (y ^ (ny // 2))))
            else:
                found.append((x * ny + y, (x + 1 if x % 2 else x - 1) * ny + y))
    return found


def pairs_row(nx, ny, step):
    return [(x * ny + y, x * ny + (y ^ step)) for x in range(nx) for y in range(ny)]


def pairs_odd(nx, ny):
    return [
        (x * ny + y, x * ny + (y + 1 if y % 2 else y - 1) % ny) for x in range(nx) for y in range(ny)
    ]


def put(ref, row, slab):
    rows = slab.shape[0]
    for j in range(slab.shape[1] // 128):
        ref[row + rows * j : row + rows * (j + 1), :] = slab[:, 128 * j : 128 * (j + 1)]


def get(ref, row, rows, width):
    return jnp.concatenate(
        [ref[row + rows * j : row + rows * (j + 1), :] for j in range(width // 128)], axis=1
    )


def iota(shape, dim):
    return lax.broadcasted_iota(jnp.int32, shape, dim)


def beside_z(slab):
    depth = slab.shape[1]
    lane = iota(slab.shape, 1)
    above = jnp.where(lane == depth - 1, 0.0, pltpu.roll(slab, depth - 1, 1))
    below = jnp.where(lane == 0, 0.0, pltpu.roll(slab, 1, 1))
    return above + below


def beside(slab, low=None, high=None):
    rows, depth = slab.shape
    tiles, columns = rows // 8, depth // 128
    lane, row = iota((8, 128), 1), iota((8, 128), 0)
    piece = [[slab[8 * t : 8 * t + 8, 128 * j : 128 * j + 128] for j in range(columns)] for t in range(tiles)]
    left = [[pltpu.roll(p, 127, 1) for p in line] for line in piece]
    right = [[pltpu.roll(p, 1, 1) for p in line] for line in piece]
    up = [[pltpu.roll(p, 7, 0) for p in line] for line in piece]
    down = [[pltpu.roll(p, 1, 0) for p in line] for line in piece]

    def outer(line, j):
        return 0.0 if line is None else jnp.broadcast_to(line[:, 128 * j : 128 * j + 128], (8, 128))

    lines = []
    for t in range(tiles):
        parts = []
        for j in range(columns):
            above = jnp.where(lane == 127, left[t][j + 1] if j + 1 < columns else 0.0, left[t][j])
            below = jnp.where(lane == 0, right[t][j - 1] if j > 0 else 0.0, right[t][j])
            after = jnp.where(row == 7, up[t + 1][j] if t + 1 < tiles else outer(high, j), up[t][j])
            before = jnp.where(row == 0, down[t - 1][j] if t > 0 else outer(low, j), down[t][j])
            parts.append((above + below) + (after + before))
        lines.append(jnp.concatenate(parts, axis=1))
    return jnp.concatenate(lines, axis=0)


def dot(left, right):
    return lax.dot_general(
        left,
        right,
        (((1,), (0,)), ((), ())),
        precision=lax.Precision.HIGHEST,
        preferred_element_type=F32,
    )


def group_lanes(depth):
    return (iota((depth, depth // 4), 0) // 4 == iota((depth, depth // 4), 1)).astype(F32)


def spread_lanes(rows):
    count, lanes = rows.shape
    pad = -count % 8
    if pad:
        rows = jnp.concatenate([rows, jnp.zeros((pad, lanes), F32)], axis=0)
    parts = []
    for j in range(4):
        index = iota(rows.shape, 1) // 4 + (lanes // 4) * j
        parts.append(jnp.take_along_axis(rows, index, axis=1, mode="promise_in_bounds"))
    return jnp.concatenate(parts, axis=1)[:count]


def spread_rows(ref, plane, start):
    row = iota((16, 128), 0) // 4
    value = jnp.zeros((16, 128), F32)
    for q in range(4):
        value = jnp.where(row == q, jnp.broadcast_to(ref[plane, start + q : start + q + 1, :], (16, 128)), value)
    return value


def spread_planes(ref, plane, column):
    row = iota((16, 128), 0) // 4
    value = jnp.zeros((16, 128), F32)
    for q in range(4):
        value = jnp.where(row == q, jnp.broadcast_to(ref[plane + q, column : column + 1, :], (16, 128)), value)
    return value


def solution(mesh):
    nx, ny = mesh.shape["gx"], mesh.shape["gy"]
    assert nx % 2 == 0 and ny % 2 == 0 and ny & (ny - 1) == 0
    axes = ("gx", "gy")

    def where_am_i():
        x, y = lax.axis_index("gx"), lax.axis_index("gy")
        return x, y, x % 2 == 0, y % 2 == 0

    def look_up(table, ids):
        spare = jnp.zeros((1, 128 - table.shape[1]), F32)
        row = jnp.broadcast_to(jnp.concatenate([table, spare], axis=1), (16, 128))
        parts = [
            jnp.take_along_axis(row, ids[:, 128 * j : 128 * (j + 1)], axis=1, mode="promise_in_bounds") for j in range(4)
        ]
        return jnp.concatenate(parts, axis=1)

    def first_of(source, reaction, kinds, ids, mask, table):
        a = reaction + jnp.where(kinds == 1, WALL_PENALTY, jnp.where(kinds == 2, INFLOW_PENALTY, 0.0))
        diagonal = 6.0 + a
        scale = OMEGA / diagonal
        return (source + mask.astype(F32) * look_up(table, ids)) * scale, scale, diagonal, a

    def faces(*refs):
        inputs, thrust, messages, buffers, table, sems, table_sem = (
            refs[:5], refs[5], refs[6:10], refs[10:15], refs[15], refs[16], refs[17]
        )
        core, chip, row, odd = messages
        _, _, x_even, y_even = where_am_i()
        near, far = jnp.where(x_even, 15, 0), jnp.where(x_even, 0, 15)
        moves = [pltpu.make_async_copy(thrust, table, table_sem)]
        for i, (hbm, buffer) in enumerate(zip(inputs, buffers)):
            for j, part in enumerate((hbm.at[:, 0, :], hbm.at[:, 15, :], hbm.at[far], hbm.at[near])):
                moves.append(pltpu.make_async_copy(part, buffer.at[j], sems.at[i, j]))
        for move in moves:
            move.start()
        for move in moves:
            move.wait()
        low, high, f_far, f_near = (first_of(*(buffer[j] for buffer in buffers), table[...])[0] for j in range(4))
        put(row, 0, jnp.where(y_even, high, low))
        put(odd, 0, jnp.where(y_even, low, high))
        put(chip, 0, f_far)
        put(core, 0, f_near)

    def set_up(source, reaction, kind, disk_id, disk_mask, table, f, g, d, absorb):
        for k in range(4):
            total = jnp.zeros((16, 512), F32)
            for x in range(4 * k, 4 * k + 4):
                f[x], g[x], d[x], a = first_of(source[x], reaction[x], kind[x], disk_id[x], disk_mask[x], table[...])
                total = total + a
            absorb[16 * k : 16 * k + 16, :] = total

    def halo_x(core, chip, row, x, x_even):
        a, b = get(core, row, 16, 512), get(chip, row, 16, 512)
        left = jnp.where(x > 0, jnp.where(x_even, b, a), 0.0)
        right = jnp.where(x < nx - 1, jnp.where(x_even, a, b), 0.0)
        return left, right

    def halo_y(row, odd, at, y, y_even):
        a, b = get(row, at, 16, 512), get(odd, at, 16, 512)
        low = jnp.where(y > 0, jnp.where(y_even, b, a), 0.0)
        high = jnp.where(y < ny - 1, jnp.where(y_even, a, b), 0.0)
        return low, high

    def smooth(f, g, core, chip, row, odd, s, to_core, y_faces, x_faces, y_more, lo, hi, y0, y1, y14, y15, g0, g15):
        x_at, y_at, x_even, y_even = where_am_i()
        left, right = halo_x(core, chip, 0, x_at, x_even)
        lo[...], hi[...] = halo_y(row, odd, 0, y_at, y_even)
        for x in range(16):
            here = f[x]
            scale = g[x]
            total = (f[x - 1] if x > 0 else left) + (f[x + 1] if x < 15 else right)
            total = total + beside(here, lo[x : x + 1, :], hi[x : x + 1, :])
            value = 1.2 * here + scale * total
            s[x] = value
            y0[x : x + 1, :] = value[0:1, :]
            y1[x : x + 1, :] = value[1:2, :]
            y14[x : x + 1, :] = value[14:15, :]
            y15[x : x + 1, :] = value[15:16, :]
            g0[x : x + 1, :] = scale[0:1, :]
            g15[x : x + 1, :] = scale[15:16, :]
        y_faces[0:16, :] = y0[...]
        y_faces[16:32, :] = y15[...]
        out, src = iota((8, 32), 0), iota((8, 32), 1)
        pick = ((out // 4 == src // 16) & (out % 4 == (src % 16) // 4)).astype(F32)
        sides = jnp.concatenate([s[0], s[15]], axis=0)
        x_faces[...] = dot(dot(pick, sides), group_lanes(512))
        put(to_core, 0, s[jnp.where(x_even, 15, 0)])
        put(to_core, 64, s[jnp.where(x_even, 14, 1)])
        put(to_core, 128, g[jnp.where(x_even, 15, 0)])
        to_core[192:196, :] = jnp.where(x_even, x_faces[4:8, :], x_faces[0:4, :])
        to_core[196:200, :] = jnp.zeros((4, 128), F32)
        for at, ref in enumerate((y1, y14, g0, g15)):
            y_more[16 * at : 16 * at + 16, :] = ref[...]

    def restrict(f, d, absorb, s, y_faces, block, V):
        for k in range(4):
            total = jnp.zeros((16, 512), F32)
            for x in range(4 * k, 4 * k + 4):
                here = s[x]
                total = total + d[x] * (1.25 * f[x] - here)
                total = total + beside(here)
                if x > 0:
                    total = total + s[x - 1]
                if x < 15:
                    total = total + s[x + 1]
            V[16 * k : 16 * k + 16, :] = total
        V[64:128, :] = absorb[...]
        V[128:160, :] = y_faces[...]
        out, src = iota((40, 160), 0), iota((40, 160), 1)
        cx, cy = out % 4, out // 8
        in_bulk = (out < 32) & (src < 128) & (src // 64 == (out // 4) % 2)
        bulk = in_bulk & ((src % 64) // 16 == cx) & ((src % 16) // 4 == cy)
        faces_too = (out >= 32) & (src >= 128) & ((out - 32) // 4 == (src - 128) // 16) & ((src % 16) // 4 == cx)
        picked = dot((bulk | faces_too).astype(F32), V[...])
        block[...] = dot(picked, group_lanes(512))

    def to_chip_kernel(block, x_faces, core, s, g, y_faces, y_more, mine, to_chip, to_row, to_odd):
        _, _, x_even, y_even = where_am_i()
        mine[...] = block[...]
        face = core[192:200, :]
        for cy in range(4):
            line = face[cy : cy + 1, :]
            a, b = 8 * cy, 8 * cy + 3
            mine[a : a + 1, :] = block[a : a + 1, :] + jnp.where(x_even, 0.0, line)
            mine[b : b + 1, :] = block[b : b + 1, :] + jnp.where(x_even, line, 0.0)
        put(to_chip, 0, s[jnp.where(x_even, 0, 15)])
        put(to_chip, 64, s[jnp.where(x_even, 1, 14)])
        put(to_chip, 128, g[jnp.where(x_even, 0, 15)])
        to_chip[192:232, :] = mine[...]
        to_chip[232:236, :] = jnp.where(x_even, x_faces[0:4, :], x_faces[4:8, :])
        to_chip[236:240, :] = jnp.zeros((4, 128), F32)
        for at, (ref, base) in enumerate(((y_faces, 0), (y_more, 0), (y_more, 32))):
            a, b = ref[base : base + 16, :], ref[base + 16 : base + 32, :]
            put(to_row, 64 * at, jnp.where(y_even, b, a))
            put(to_odd, 64 * at, jnp.where(y_even, a, b))

    def from_chip_kernel(mine, x_faces, chip, full, beyond):
        x_at, _, x_even, _ = where_am_i()
        has = jnp.where(x_even, x_at > 0, x_at < nx - 1)
        full[...] = mine[...]
        beyond[...] = chip[192:232, :]
        mine_face = jnp.where(x_even, x_faces[0:4, :], x_faces[4:8, :])
        face = chip[232:240, :]
        for cy in range(4):
            line = jnp.where(has, face[cy : cy + 1, :], 0.0)
            own = mine_face[cy : cy + 1, :]
            a, b = 8 * cy, 8 * cy + 3
            full[a : a + 1, :] = mine[a : a + 1, :] + jnp.where(x_even, line, 0.0)
            full[b : b + 1, :] = mine[b : b + 1, :] + jnp.where(x_even, 0.0, line)
            beyond[a : a + 1, :] = chip[192 + a : 193 + a, :] + jnp.where(x_even, 0.0, own)
            beyond[b : b + 1, :] = chip[192 + b : 193 + b, :] + jnp.where(x_even, own, 0.0)

    def window_kernel(full, beyond, core, chip, s_core, window):
        x_at, _, x_even, _ = where_am_i()
        mid = full[...]
        a, b = core[...], beyond[...]
        left, right = jnp.where(x_even, b, a), jnp.where(x_even, a, b)
        for at, block in enumerate((left, mid, right)):
            for cy in range(4):
                window[24 * cy + 4 * at : 24 * cy + 4 * at + 4, :] = block[8 * cy : 8 * cy + 4, :]
                window[24 * cy + 12 + 4 * at : 24 * cy + 16 + 4 * at, :] = block[8 * cy + 4 : 8 * cy + 8, :]
            window[96 + 4 * at : 100 + 4 * at, :] = block[32:36, :]
            window[108 + 4 * at : 112 + 4 * at, :] = block[36:40, :]
        for at, line in enumerate((0, 15)):
            near = jnp.concatenate([s_core[16 * j + line : 16 * j + line + 1, :] for j in range(4)], axis=0)
            far = jnp.concatenate([chip[16 * j + line : 16 * j + line + 1, :] for j in range(4)], axis=0)
            window[120 + 4 * at : 124 + 4 * at, :] = jnp.where(x_at > 0, jnp.where(x_even, far, near), 0.0)
            window[128 + 4 * at : 132 + 4 * at, :] = jnp.where(x_at < nx - 1, jnp.where(x_even, near, far), 0.0)

    planes = 4 * ny

    def finish(*refs):
        f, g, s, a_core, a_chip, a_row, a_odd, s_core, s_chip, s_row, s_odd = refs[:11]
        windows = refs[11 : 11 + ny]
        pressure, coarse = refs[11 + ny : 13 + ny]
        every, res, diag, inv, one, two, sol, Pc, T, U, yl, yh, tl, th, ul, uh, result, slab_out, sems = refs[13 + ny :]
        x_at, y_at, x_even, y_even = where_am_i()
        for step, window in enumerate(windows):
            every[jnp.bitwise_xor(y_at, step)] = window[...]

        row = iota((16, 128), 0)
        valid = ((row >= 4) | (x_at > 0)) & ((row < 8) | (x_at < nx - 1)) & (row < 12)
        blank = jnp.zeros((4, 128), F32)

        def twelve(value):
            return jnp.concatenate([value, blank], axis=0)

        centre = (CHEB_HIGH + CHEB_LOW) / 2.0
        half_range = (CHEB_HIGH - CHEB_LOW) / 2.0
        aspect = centre / half_range
        factor = 1.0 / aspect
        empty = jnp.zeros((16, 128), F32)
        for ref in (one, two, sol):
            ref[0] = empty
            ref[planes + 1] = empty
        for at in range(ny):
            for cy in range(4):
                plane = 4 * at + cy
                value = every[at, 24 * cy : 24 * cy + 12, :]
                if cy == 0 and at > 0:
                    value = value + every[at - 1, 108:120, :]
                if cy == 3 and at < ny - 1:
                    value = value + every[at + 1, 96:108, :]
                value = jnp.where(valid, twelve(value), 0.0)
                centre_value = 6.0 + twelve(every[at, 24 * cy + 12 : 24 * cy + 24, :]) / 16.0
                inverse = jnp.where(valid, 1.0 / (16.0 * centre_value), 0.0)
                res[plane] = value
                diag[plane] = centre_value
                inv[plane] = inverse
                direction = inverse * value / centre
                one[plane + 1] = direction
                sol[plane + 1] = direction
        now, later = one, two
        for number in range(1, SWEEPS):
            factor_next = 1.0 / (2.0 * aspect - factor)
            keep, gain = factor_next * factor, 2.0 * factor_next / half_range

            lane = iota((16, 128), 1)
            for plane in range(planes):
                here = now[plane + 1]
                total = now[plane] + now[plane + 2]
                total = total + pltpu.roll(here, 15, 0) + pltpu.roll(here, 1, 0)
                total = total + jnp.where(lane == 127, 0.0, pltpu.roll(here, 127, 1))
                total = total + jnp.where(lane == 0, 0.0, pltpu.roll(here, 1, 1))
                residual = res[plane] - 16.0 * (diag[plane] * here - total)
                res[plane] = residual
                direction = keep * here + gain * inv[plane] * residual
                later[plane + 1] = direction
                sol[plane + 1] = sol[plane + 1] + direction
            now, later = later, now
            factor = factor_next
        for plane in range(planes):
            for cx in range(4):
                slab_out[cx, plane : plane + 1, :] = sol[plane + 1, 4 + cx : 5 + cx, :]
        moves = [pltpu.make_async_copy(slab_out, coarse, sems.at[8])]
        moves[0].start()

        first_plane = 4 * y_at + 1
        for at in range(6):
            Pc[at] = spread_lanes(spread_planes(sol, first_plane, 3 + at))
        s_left, s_right = halo_x(s_core, s_chip, 0, x_at, x_even)
        s_left2, s_right2 = halo_x(s_core, s_chip, 64, x_at, x_even)
        T[0], T[1] = s_left2 + Pc[0], s_left + Pc[0]
        T[18], T[19] = s_right + Pc[5], s_right2 + Pc[5]

        for x in range(16):
            T[x + 2] = s[x] + Pc[x // 4 + 1]
        below, above = first_plane - 1, first_plane + 4
        y1_low, y1_high = halo_y(s_row, s_odd, 0, y_at, y_even)
        y2_low, y2_high = halo_y(s_row, s_odd, 64, y_at, y_even)
        g_low, g_high = halo_y(s_row, s_odd, 128, y_at, y_even)
        f_low, f_high = halo_y(a_row, a_odd, 0, y_at, y_even)
        before, after = jnp.maximum(y_at - 1, 0), jnp.minimum(y_at + 1, ny - 1)
        outer = {}
        for name, ref, plane, s1, s2, who, inside, line in (
            ("low", tl, below, y1_low, y2_low, before, y_at > 0, 1),
            ("high", th, above, y1_high, y2_high, after, y_at < ny - 1, 0),
        ):
            spread = spread_lanes(spread_rows(sol, plane, 4))
            ref[8:24, :] = s1 + spread
            outer[name] = s2 + spread
            for at, cx, base, there in ((7, 3, 0, x_at > 0), (24, 8, 2, x_at < nx - 1)):
                corner = jnp.concatenate(
                    [every[who, pl.ds(120 + 4 * (base + line) + j, 1), :] for j in range(4)], axis=1
                )
                corner = jnp.where(inside & there, corner, 0.0)
                ref[at : at + 1, :] = corner + spread_lanes(sol[plane, cx : cx + 1, :])

        f_left, f_right = halo_x(a_core, a_chip, 0, x_at, x_even)
        g_left, g_right = halo_x(s_core, s_chip, 128, x_at, x_even)

        def fourth_at(at, forcing, scale):
            here = T[at + 1]
            total = T[at] + T[at + 2] + beside(here, tl[at + 7 : at + 8, :], th[at + 7 : at + 8, :])
            return 0.2 * here + forcing + scale * total

        U[0] = fourth_at(0, f_left, g_left)
        U[17] = fourth_at(17, f_right, g_right)

        for x in range(16):
            U[x + 1] = fourth_at(x + 1, f[x], g[x])
            here = T[x + 2]
            yl[x : x + 1, :] = here[0:1, :]
            yh[x : x + 1, :] = here[15:16, :]
        for ref, out, edge, far, forcing, scale in (
            (tl, ul, yl, outer["low"], f_low, g_low),
            (th, uh, yh, outer["high"], f_high, g_high),
        ):
            here = ref[8:24, :]
            total = far + edge[...] + ref[7:23, :] + ref[9:25, :] + beside_z(here)
            out[...] = 0.2 * here + forcing + scale * total

        for x in range(16):
            here = U[x + 1]
            total = U[x] + U[x + 2] + beside(here, ul[x : x + 1, :], uh[x : x + 1, :])
            result[x] = 0.2 * here + f[x] + g[x] * total
            if x % 2 == 1:
                part = pl.ds(x - 1, 2)
                moves.append(pltpu.make_async_copy(result.at[part], pressure.at[part], sems.at[x // 2]))
                moves[-1].start()
        for move in moves:
            move.wait()

    slab, field, long = (16, 512), (16, 16, 512), (18, 16, 512)
    core_pairs, chip_pairs = pairs_core(nx, ny), pairs_chip(nx, ny)
    row_pairs = [pairs_row(nx, ny, step) for step in range(1, ny)]
    odd_pairs = pairs_odd(nx, ny)

    def swap(array, pairs):
        return lax.ppermute(array, axes, pairs)

    def local(source, reaction, boundary_kind, disk_id, disk_mask, thrust):
        inputs = (source, reaction, boundary_kind, disk_id, disk_mask, thrust.reshape(1, -1))
        some = (4, 16, 512)
        core, chip, row, odd = call(
            faces,
            [(64, 128)] * 4,
            *(pltpu.with_memory_space_constraint(array, pltpu.HBM) for array in inputs),
            in_specs=[HBM] * 6,
            scratch=[some, some]
            + [pltpu.VMEM(some, jnp.int32)] * 3
            + [(1, thrust.shape[0]), pltpu.SemaphoreType.DMA((5, 4)), pltpu.SemaphoreType.DMA(())],
            name="faces",
        )
        a_core, a_chip = swap(core, core_pairs), swap(chip, chip_pairs)
        a_odd, a_row = swap(odd, odd_pairs), swap(row, row_pairs[0])
        f, g, d, absorb = call(set_up, [field, field, field, (64, 512)], *inputs, name="set_up")
        a_odd, a_row, a_chip, a_core, f, g, d, absorb = lax.optimization_barrier(
            (a_odd, a_row, a_chip, a_core, f, g, d, absorb)
        )
        s, to_core, y_faces, x_faces, y_more = call(
            smooth,
            [field, (200, 128), (32, 512), (8, 128), (64, 512)],
            f, g, a_core, a_chip, a_row, a_odd,
            scratch=[slab] * 8,
            name="smooth",
        )
        s_core = swap(to_core, core_pairs)
        (block,) = call(restrict, [(40, 128)], f, d, absorb, s, y_faces, scratch=[(160, 512)], name="restrict")
        mine, to_chip, to_row, to_odd = call(
            to_chip_kernel,
            [(40, 128), (240, 128), (192, 128), (192, 128)],
            block, x_faces, s_core, s, g, y_faces, y_more,
            name="to_chip",
        )
        s_chip = swap(to_chip, chip_pairs)
        s_row, s_odd = swap(to_row, row_pairs[0]), swap(to_odd, odd_pairs)
        full, beyond = call(from_chip_kernel, [(40, 128), (40, 128)], mine, x_faces, s_chip, name="from_chip")
        c_core = swap(full, core_pairs)
        (window,) = call(window_kernel, [(136, 128)], full, beyond, c_core, s_chip, s_core, name="window")
        windows = [window] + [swap(window, pairs) for pairs in row_pairs]
        pressure, coarse = call(
            finish,
            [field, (4, planes, 128)],
            f, g, s, a_core, a_chip, a_row, a_odd, s_core, s_chip, s_row, s_odd, *windows,
            scratch=[(ny, 136, 128)]
            + [(planes, 16, 128)] * 3
            + [(planes + 2, 16, 128)] * 3
            + [(6, 16, 512), (20, 16, 512), long, slab, slab, (32, 512), (32, 512), slab, slab, field]
            + [(4, planes, 128), pltpu.SemaphoreType.DMA((9,))],
            out_specs=[HBM, HBM],
            name="finish",
        )
        return pressure, coarse

    spec = P("gx", "gy", None)
    return jax.shard_map(
        local,
        mesh=mesh,
        in_specs=(spec, spec, spec, spec, spec, P()),
        out_specs=(spec, P("gx", None, None)),
        check_vma=False,
    )
```

```python
import jax
import jax.numpy as jnp
from jax import lax
from jax.experimental import pallas as pl
from jax.experimental.pallas import tpu as pltpu
from jax.sharding import PartitionSpec as P

SWEEPS = 4
OMEGA = 0.8
WALL_PENALTY = 0.4
INFLOW_PENALTY = 0.2
CHEB_LOW = 0.1
CHEB_HIGH = 2.0
F32 = jnp.float32
VMEM = pl.BlockSpec(memory_space=pltpu.VMEM)


HBM = pl.BlockSpec(memory_space=pltpu.HBM)


def call(kernel, outs, *args, scratch=(), name=None, in_specs=None, out_specs=None):
    return pl.pallas_call(
        kernel,
        out_shape=[jax.ShapeDtypeStruct(s, F32) for s in outs],
        in_specs=in_specs or [VMEM] * len(args),
        out_specs=out_specs or [VMEM] * len(outs),
        scratch_shapes=[pltpu.VMEM(s, F32) if isinstance(s, tuple) else s for s in scratch],
        compiler_params=pltpu.CompilerParams(vmem_limit_bytes=16 << 20),
        name=name,
    )(*args)


def pairs_core(nx, ny):
    return [(x * ny + y, (x ^ 1) * ny + y) for x in range(nx) for y in range(ny)]


def pairs_chip(nx, ny):
    found = []
    for x in range(nx):
        for y in range(ny):
            if x in (0, nx - 1):
                found.append((x * ny + y, x * ny + (y ^ (ny // 2))))
            else:
                found.append((x * ny + y, (x + 1 if x % 2 else x - 1) * ny + y))
    return found


def pairs_row(nx, ny, step):
    return [(x * ny + y, x * ny + (y ^ step)) for x in range(nx) for y in range(ny)]


def pairs_odd(nx, ny):
    return [
        (x * ny + y, x * ny + (y + 1 if y % 2 else y - 1) % ny) for x in range(nx) for y in range(ny)
    ]


def put(ref, row, slab):
    rows = slab.shape[0]
    for j in range(slab.shape[1] // 128):
        ref[row + rows * j : row + rows * (j + 1), :] = slab[:, 128 * j : 128 * (j + 1)]


def get(ref, row, rows, width):
    return jnp.concatenate(
        [ref[row + rows * j : row + rows * (j + 1), :] for j in range(width // 128)], axis=1
    )


def iota(shape, dim):
    return lax.broadcasted_iota(jnp.int32, shape, dim)


def beside_z(slab):
    depth = slab.shape[1]
    lane = iota(slab.shape, 1)
    above = jnp.where(lane == depth - 1, 0.0, pltpu.roll(slab, depth - 1, 1))
    below = jnp.where(lane == 0, 0.0, pltpu.roll(slab, 1, 1))
    return above + below


def beside(slab, low=None, high=None):
    rows, depth = slab.shape
    tiles, columns = rows // 8, depth // 128
    lane, row = iota((8, 128), 1), iota((8, 128), 0)
    piece = [[slab[8 * t : 8 * t + 8, 128 * j : 128 * j + 128] for j in range(columns)] for t in range(tiles)]
    left = [[pltpu.roll(p, 127, 1) for p in line] for line in piece]
    right = [[pltpu.roll(p, 1, 1) for p in line] for line in piece]
    up = [[pltpu.roll(p, 7, 0) for p in line] for line in piece]
    down = [[pltpu.roll(p, 1, 0) for p in line] for line in piece]

    def outer(line, j):
        return 0.0 if line is None else jnp.broadcast_to(line[:, 128 * j : 128 * j + 128], (8, 128))

    lines = []
    for t in range(tiles):
        parts = []
        for j in range(columns):
            above = jnp.where(lane == 127, left[t][j + 1] if j + 1 < columns else 0.0, left[t][j])
            below = jnp.where(lane == 0, right[t][j - 1] if j > 0 else 0.0, right[t][j])
            after = jnp.where(row == 7, up[t + 1][j] if t + 1 < tiles else outer(high, j), up[t][j])
            before = jnp.where(row == 0, down[t - 1][j] if t > 0 else outer(low, j), down[t][j])
            parts.append((above + below) + (after + before))
        lines.append(jnp.concatenate(parts, axis=1))
    return jnp.concatenate(lines, axis=0)


def dot(left, right):
    return lax.dot_general(
        left,
        right,
        (((1,), (0,)), ((), ())),
        precision=lax.Precision.HIGHEST,
        preferred_element_type=F32,
    )


def group_lanes(depth):
    return (iota((depth, depth // 4), 0) // 4 == iota((depth, depth // 4), 1)).astype(F32)


def spread_lanes(rows):
    count, lanes = rows.shape
    pad = -count % 8
    if pad:
        rows = jnp.concatenate([rows, jnp.zeros((pad, lanes), F32)], axis=0)
    parts = []
    for j in range(4):
        index = iota(rows.shape, 1) // 4 + (lanes // 4) * j
        parts.append(jnp.take_along_axis(rows, index, axis=1, mode="promise_in_bounds"))
    return jnp.concatenate(parts, axis=1)[:count]


def spread_rows(ref, plane, start):
    row = iota((16, 128), 0) // 4
    value = jnp.zeros((16, 128), F32)
    for q in range(4):
        value = jnp.where(row == q, jnp.broadcast_to(ref[plane, start + q : start + q + 1, :], (16, 128)), value)
    return value


def spread_planes(ref, plane, column):
    row = iota((16, 128), 0) // 4
    value = jnp.zeros((16, 128), F32)
    for q in range(4):
        value = jnp.where(row == q, jnp.broadcast_to(ref[plane + q, column : column + 1, :], (16, 128)), value)
    return value


def solution(mesh):
    nx, ny = mesh.shape["gx"], mesh.shape["gy"]
    assert nx % 2 == 0 and ny % 2 == 0 and ny & (ny - 1) == 0
    axes = ("gx", "gy")

    def where_am_i():
        x, y = lax.axis_index("gx"), lax.axis_index("gy")
        return x, y, x % 2 == 0, y % 2 == 0

    def look_up(table, ids):
        spare = jnp.zeros((1, 128 - table.shape[1]), F32)
        row = jnp.broadcast_to(jnp.concatenate([table, spare], axis=1), (16, 128))
        parts = [
            jnp.take_along_axis(row, ids[:, 128 * j : 128 * (j + 1)], axis=1, mode="promise_in_bounds") for j in range(4)
        ]
        return jnp.concatenate(parts, axis=1)

    def first_of(source, reaction, kinds, ids, mask, table):
        a = reaction + jnp.where(kinds == 1, WALL_PENALTY, jnp.where(kinds == 2, INFLOW_PENALTY, 0.0))
        diagonal = 6.0 + a
        scale = OMEGA / diagonal
        return (source + mask.astype(F32) * look_up(table, ids)) * scale, scale, diagonal, a

    def faces(*refs):
        inputs, thrust, messages, buffers, table, sems, table_sem = (
            refs[:5], refs[5], refs[6:10], refs[10:15], refs[15], refs[16], refs[17]
        )
        core, chip, row, odd = messages
        _, _, x_even, y_even = where_am_i()
        near, far = jnp.where(x_even, 15, 0), jnp.where(x_even, 0, 15)
        moves = [pltpu.make_async_copy(thrust, table, table_sem)]
        for i, (hbm, buffer) in enumerate(zip(inputs, buffers)):
            for j, part in enumerate((hbm.at[:, 0, :], hbm.at[:, 15, :], hbm.at[far], hbm.at[near])):
                moves.append(pltpu.make_async_copy(part, buffer.at[j], sems.at[i, j]))
        for move in moves:
            move.start()
        for move in moves:
            move.wait()
        (low, g_low), (high, g_high), (f_far, _), (f_near, _) = (
            first_of(*(buffer[j] for buffer in buffers), table[...])[:2] for j in range(4)
        )
        put(row, 0, jnp.where(y_even, high, low))
        put(row, 64, jnp.where(y_even, g_high, g_low))
        put(odd, 0, jnp.where(y_even, low, high))
        put(odd, 64, jnp.where(y_even, g_low, g_high))
        put(chip, 0, f_far)
        put(core, 0, f_near)

    def set_up(source, reaction, kind, disk_id, disk_mask, table, f, g, d, absorb, V):
        for k in range(4):
            total = jnp.zeros((16, 512), F32)
            for x in range(4 * k, 4 * k + 4):
                f[x], g[x], d[x], a = first_of(source[x], reaction[x], kind[x], disk_id[x], disk_mask[x], table[...])
                total = total + a
            V[16 * k : 16 * k + 16, :] = total
        out, src = iota((16, 64), 0), iota((16, 64), 1)
        pick = ((src // 16 == out % 4) & ((src % 16) // 4 == out // 4)).astype(F32)
        absorb[...] = dot(dot(pick, V[...]), group_lanes(512))

    def halo_x(core, chip, row, x, x_even):
        a, b = get(core, row, 16, 512), get(chip, row, 16, 512)
        left = jnp.where(x > 0, jnp.where(x_even, b, a), 0.0)
        right = jnp.where(x < nx - 1, jnp.where(x_even, a, b), 0.0)
        return left, right

    def halo_y(row, odd, at, y, y_even):
        a, b = get(row, at, 16, 512), get(odd, at, 16, 512)
        low = jnp.where(y > 0, jnp.where(y_even, b, a), 0.0)
        high = jnp.where(y < ny - 1, jnp.where(y_even, a, b), 0.0)
        return low, high

    def smooth(f, g, absorb, core, chip, row, odd, s, to_core, sums, y_faces, y_more, lo, hi, y0, y1, y14, y15):
        x_at, y_at, x_even, y_even = where_am_i()
        left, right = halo_x(core, chip, 0, x_at, x_even)
        lo[...], hi[...] = halo_y(row, odd, 0, y_at, y_even)
        for x in range(16):
            here = f[x]
            scale = g[x]
            total = (f[x - 1] if x > 0 else left) + (f[x + 1] if x < 15 else right)
            total = total + beside(here, lo[x : x + 1, :], hi[x : x + 1, :])
            value = 1.2 * here + scale * total
            s[x] = value
            y0[x : x + 1, :] = value[0:1, :]
            y1[x : x + 1, :] = value[1:2, :]
            y14[x : x + 1, :] = value[14:15, :]
            y15[x : x + 1, :] = value[15:16, :]
        y_faces[0:16, :] = y0[...]
        y_faces[16:32, :] = y15[...]
        out, src = iota((16, 64), 0), iota((16, 64), 1)
        pick = ((out // 4 == src // 16) & (out % 4 == (src % 16) // 4)).astype(F32)
        sides = jnp.concatenate([s[0], s[15], y0[...], y15[...]], axis=0)
        sums[...] = dot(dot(pick, sides), group_lanes(512))
        put(to_core, 0, s[jnp.where(x_even, 15, 0)])
        put(to_core, 64, s[jnp.where(x_even, 14, 1)])
        put(to_core, 128, g[jnp.where(x_even, 15, 0)])
        to_core[192:196, :] = jnp.where(x_even, sums[4:8, :], sums[0:4, :])
        to_core[196:200, :] = jnp.zeros((4, 128), F32)
        to_core[200:208, :] = sums[8:16, :]
        to_core[208:224, :] = absorb[...]
        for at, ref in enumerate((y1, y14)):
            y_more[16 * at : 16 * at + 16, :] = ref[...]

    def restrict(f, d, absorb, s, sums, block, V):
        for k in range(4):
            total = jnp.zeros((16, 512), F32)
            for x in range(4 * k, 4 * k + 4):
                here = s[x]
                total = total + d[x] * (1.25 * f[x] - here)
                total = total + beside(here)
                if x > 0:
                    total = total + s[x - 1]
                if x < 15:
                    total = total + s[x + 1]
            V[16 * k : 16 * k + 16, :] = total
        out, src = iota((16, 64), 0), iota((16, 64), 1)
        pick = ((src // 16 == out % 4) & ((src % 16) // 4 == out // 4)).astype(F32)
        found = dot(dot(pick, V[...]), group_lanes(512))
        for cy in range(4):
            block[8 * cy : 8 * cy + 4, :] = found[4 * cy : 4 * cy + 4, :]
            block[8 * cy + 4 : 8 * cy + 8, :] = absorb[4 * cy : 4 * cy + 4, :]
        block[32:40, :] = sums[8:16, :]

    def to_chip_kernel(block, sums, absorb, core, s, g, y_faces, y_more, mine, to_chip, to_row, to_odd):
        _, _, x_even, y_even = where_am_i()
        mine[...] = block[...]
        face = core[192:200, :]
        for cy in range(4):
            line = face[cy : cy + 1, :]
            a, b = 8 * cy, 8 * cy + 3
            mine[a : a + 1, :] = block[a : a + 1, :] + jnp.where(x_even, 0.0, line)
            mine[b : b + 1, :] = block[b : b + 1, :] + jnp.where(x_even, line, 0.0)
        put(to_chip, 0, s[jnp.where(x_even, 0, 15)])
        put(to_chip, 64, s[jnp.where(x_even, 1, 14)])
        put(to_chip, 128, g[jnp.where(x_even, 0, 15)])
        to_chip[192:232, :] = mine[...]
        to_chip[232:236, :] = jnp.where(x_even, sums[0:4, :], sums[4:8, :])
        to_chip[236:240, :] = jnp.zeros((4, 128), F32)
        for at, ref in enumerate((y_faces, y_more)):
            a, b = ref[0:16, :], ref[16:32, :]
            put(to_row, 64 * at, jnp.where(y_even, b, a))
            put(to_odd, 64 * at, jnp.where(y_even, a, b))
        first_line, last_line = (
            jnp.concatenate([core[16 * j + line : 16 * j + line + 1, :] for j in range(4)], axis=0) for line in (0, 15)
        )
        for ref, corner in (
            (to_row, jnp.where(y_even, last_line, first_line)),
            (to_odd, jnp.where(y_even, first_line, last_line)),
        ):
            ref[128:144, :] = absorb[...]
            ref[144:160, :] = core[208:224, :]
            ref[160:168, :] = sums[8:16, :]
            ref[168:176, :] = core[200:208, :]
            ref[176:180, :] = corner
            ref[180:192, :] = jnp.zeros((12, 128), F32)

    def from_chip_kernel(mine, sums, chip, full, beyond):
        x_at, _, x_even, _ = where_am_i()
        has = jnp.where(x_even, x_at > 0, x_at < nx - 1)
        full[...] = mine[...]
        beyond[...] = chip[192:232, :]
        mine_face = jnp.where(x_even, sums[0:4, :], sums[4:8, :])
        face = chip[232:240, :]
        for cy in range(4):
            line = jnp.where(has, face[cy : cy + 1, :], 0.0)
            own = mine_face[cy : cy + 1, :]
            a, b = 8 * cy, 8 * cy + 3
            full[a : a + 1, :] = mine[a : a + 1, :] + jnp.where(x_even, line, 0.0)
            full[b : b + 1, :] = mine[b : b + 1, :] + jnp.where(x_even, 0.0, line)
            beyond[a : a + 1, :] = chip[192 + a : 193 + a, :] + jnp.where(x_even, 0.0, own)
            beyond[b : b + 1, :] = chip[192 + b : 193 + b, :] + jnp.where(x_even, own, 0.0)

    def window_kernel(full, beyond, core, chip, s_core, window, short):
        x_at, _, x_even, _ = where_am_i()
        mid = full[...]
        a, b = core[...], beyond[...]
        left, right = jnp.where(x_even, b, a), jnp.where(x_even, a, b)
        for at, block in enumerate((left, mid, right)):
            for cy in range(4):
                window[24 * cy + 4 * at : 24 * cy + 4 * at + 4, :] = block[8 * cy : 8 * cy + 4, :]
                window[24 * cy + 12 + 4 * at : 24 * cy + 16 + 4 * at, :] = block[8 * cy + 4 : 8 * cy + 8, :]
            window[96 + 4 * at : 100 + 4 * at, :] = block[32:36, :]
            window[108 + 4 * at : 112 + 4 * at, :] = block[36:40, :]
        for at, line in enumerate((0, 15)):
            near = jnp.concatenate([s_core[16 * j + line : 16 * j + line + 1, :] for j in range(4)], axis=0)
            far = jnp.concatenate([chip[16 * j + line : 16 * j + line + 1, :] for j in range(4)], axis=0)
            window[120 + 4 * at : 124 + 4 * at, :] = jnp.where(x_at > 0, jnp.where(x_even, far, near), 0.0)
            window[128 + 4 * at : 132 + 4 * at, :] = jnp.where(x_at < nx - 1, jnp.where(x_even, near, far), 0.0)
            short[72 + 4 * at : 76 + 4 * at, :] = far
        for cy in range(4):
            for at, block in enumerate((left, mid, right)):
                short[12 * cy + 4 * at : 12 * cy + 4 * at + 4, :] = block[8 * cy : 8 * cy + 4, :]
            short[48 + 4 * cy : 52 + 4 * cy, :] = beyond[8 * cy + 4 : 8 * cy + 8, :]
        short[64:72, :] = beyond[32:40, :]

    planes = 4 * ny
    short_steps = (1, 3) if ny == 4 else (1,)

    def finish(*refs):
        f, g, s, a_core, a_chip, a_row, a_odd, s_core, s_chip, s_row, s_odd = refs[:11]
        windows = refs[11 : 11 + ny]
        pressure, coarse = refs[11 + ny : 13 + ny]
        every, res, diag, inv, one, two, sol, Pc, T, U, yl, yh, tl, th, ul, uh, result, slab_out, sems = refs[13 + ny :]
        x_at, y_at, x_even, y_even = where_am_i()
        for step, window in enumerate(windows):
            there = jnp.bitwise_xor(y_at, step)
            if step not in short_steps:
                every[there] = window[...]
                continue
            faces_of = s_row if step == 1 else s_odd

            def three(at, own, core, chip):
                every[there, at : at + 4, :] = jnp.where(x_even, chip, core)
                if own is not None:
                    every[there, at + 4 : at + 8, :] = own
                every[there, at + 8 : at + 12, :] = jnp.where(x_even, core, chip)

            for cy in range(4):
                at = 4 * cy
                every[there, 24 * cy : 24 * cy + 12, :] = window[12 * cy : 12 * cy + 12, :]
                three(
                    24 * cy + 12, faces_of[128 + at : 132 + at, :], faces_of[144 + at : 148 + at, :],
                    window[48 + at : 52 + at, :],
                )
            for at in (0, 4):
                three(
                    96 + 3 * at, faces_of[160 + at : 164 + at, :], faces_of[168 + at : 172 + at, :],
                    window[64 + at : 68 + at, :],
                )
                three(120 + at, None, faces_of[176:180, :], window[72 + at : 76 + at, :])

        row = iota((16, 128), 0)
        valid = ((row >= 4) | (x_at > 0)) & ((row < 8) | (x_at < nx - 1)) & (row < 12)
        blank = jnp.zeros((4, 128), F32)

        def twelve(value):
            return jnp.concatenate([value, blank], axis=0)

        centre = (CHEB_HIGH + CHEB_LOW) / 2.0
        half_range = (CHEB_HIGH - CHEB_LOW) / 2.0
        aspect = centre / half_range
        factor = 1.0 / aspect
        empty = jnp.zeros((16, 128), F32)
        for ref in (one, two, sol):
            ref[0] = empty
            ref[planes + 1] = empty
        for at in range(ny):
            for cy in range(4):
                plane = 4 * at + cy
                value = every[at, 24 * cy : 24 * cy + 12, :]
                if cy == 0 and at > 0:
                    value = value + every[at - 1, 108:120, :]
                if cy == 3 and at < ny - 1:
                    value = value + every[at + 1, 96:108, :]
                value = jnp.where(valid, twelve(value), 0.0)
                centre_value = 6.0 + twelve(every[at, 24 * cy + 12 : 24 * cy + 24, :]) / 16.0
                inverse = jnp.where(valid, 1.0 / (16.0 * centre_value), 0.0)
                res[plane] = value
                diag[plane] = centre_value
                inv[plane] = inverse
                direction = inverse * value / centre
                one[plane + 1] = direction
                sol[plane + 1] = direction
        now, later = one, two
        for number in range(1, SWEEPS):
            factor_next = 1.0 / (2.0 * aspect - factor)
            keep, gain = factor_next * factor, 2.0 * factor_next / half_range

            lane = iota((16, 128), 1)
            for plane in range(planes):
                here = now[plane + 1]
                total = now[plane] + now[plane + 2]
                total = total + pltpu.roll(here, 15, 0) + pltpu.roll(here, 1, 0)
                total = total + jnp.where(lane == 127, 0.0, pltpu.roll(here, 127, 1))
                total = total + jnp.where(lane == 0, 0.0, pltpu.roll(here, 1, 1))
                residual = res[plane] - 16.0 * (diag[plane] * here - total)
                res[plane] = residual
                direction = keep * here + gain * inv[plane] * residual
                later[plane + 1] = direction
                sol[plane + 1] = sol[plane + 1] + direction
            now, later = later, now
            factor = factor_next
        for plane in range(planes):
            for cx in range(4):
                slab_out[cx, plane : plane + 1, :] = sol[plane + 1, 4 + cx : 5 + cx, :]
        moves = [pltpu.make_async_copy(slab_out, coarse, sems.at[8])]
        moves[0].start()

        first_plane = 4 * y_at + 1
        for at in range(6):
            Pc[at] = spread_lanes(spread_planes(sol, first_plane, 3 + at))
        s_left, s_right = halo_x(s_core, s_chip, 0, x_at, x_even)
        s_left2, s_right2 = halo_x(s_core, s_chip, 64, x_at, x_even)
        T[0], T[1] = s_left2 + Pc[0], s_left + Pc[0]
        T[18], T[19] = s_right + Pc[5], s_right2 + Pc[5]

        for x in range(16):
            T[x + 2] = s[x] + Pc[x // 4 + 1]
        below, above = first_plane - 1, first_plane + 4
        y1_low, y1_high = halo_y(s_row, s_odd, 0, y_at, y_even)
        y2_low, y2_high = halo_y(s_row, s_odd, 64, y_at, y_even)
        g_low, g_high = halo_y(a_row, a_odd, 64, y_at, y_even)
        f_low, f_high = halo_y(a_row, a_odd, 0, y_at, y_even)
        before, after = jnp.maximum(y_at - 1, 0), jnp.minimum(y_at + 1, ny - 1)
        outer = {}
        for name, ref, plane, s1, s2, who, inside, line in (
            ("low", tl, below, y1_low, y2_low, before, y_at > 0, 1),
            ("high", th, above, y1_high, y2_high, after, y_at < ny - 1, 0),
        ):
            spread = spread_lanes(spread_rows(sol, plane, 4))
            ref[8:24, :] = s1 + spread
            outer[name] = s2 + spread
            for at, cx, base, there in ((7, 3, 0, x_at > 0), (24, 8, 2, x_at < nx - 1)):
                corner = jnp.concatenate(
                    [every[who, pl.ds(120 + 4 * (base + line) + j, 1), :] for j in range(4)], axis=1
                )
                corner = jnp.where(inside & there, corner, 0.0)
                ref[at : at + 1, :] = corner + spread_lanes(sol[plane, cx : cx + 1, :])

        f_left, f_right = halo_x(a_core, a_chip, 0, x_at, x_even)
        g_left, g_right = halo_x(s_core, s_chip, 128, x_at, x_even)

        def fourth_at(at, forcing, scale):
            here = T[at + 1]
            total = T[at] + T[at + 2] + beside(here, tl[at + 7 : at + 8, :], th[at + 7 : at + 8, :])
            return 0.2 * here + forcing + scale * total

        U[0] = fourth_at(0, f_left, g_left)
        U[17] = fourth_at(17, f_right, g_right)

        for x in range(16):
            U[x + 1] = fourth_at(x + 1, f[x], g[x])
            here = T[x + 2]
            yl[x : x + 1, :] = here[0:1, :]
            yh[x : x + 1, :] = here[15:16, :]
        for ref, out, edge, far, forcing, scale in (
            (tl, ul, yl, outer["low"], f_low, g_low),
            (th, uh, yh, outer["high"], f_high, g_high),
        ):
            here = ref[8:24, :]
            total = far + edge[...] + ref[7:23, :] + ref[9:25, :] + beside_z(here)
            out[...] = 0.2 * here + forcing + scale * total

        for x in range(16):
            here = U[x + 1]
            total = U[x] + U[x + 2] + beside(here, ul[x : x + 1, :], uh[x : x + 1, :])
            result[x] = 0.2 * here + f[x] + g[x] * total
            if x % 2 == 1:
                part = pl.ds(x - 1, 2)
                moves.append(pltpu.make_async_copy(result.at[part], pressure.at[part], sems.at[x // 2]))
                moves[-1].start()
        for move in moves:
            move.wait()

    slab, field, long = (16, 512), (16, 16, 512), (18, 16, 512)
    core_pairs, chip_pairs = pairs_core(nx, ny), pairs_chip(nx, ny)
    row_pairs = [pairs_row(nx, ny, step) for step in range(1, ny)]
    odd_pairs = pairs_odd(nx, ny)

    def swap(array, pairs):
        return lax.ppermute(array, axes, pairs)

    def local(source, reaction, boundary_kind, disk_id, disk_mask, thrust):
        inputs = (source, reaction, boundary_kind, disk_id, disk_mask, thrust.reshape(1, -1))
        some = (4, 16, 512)
        core, chip, row, odd = call(
            faces,
            [(64, 128), (64, 128), (128, 128), (128, 128)],
            *(pltpu.with_memory_space_constraint(array, pltpu.HBM) for array in inputs),
            in_specs=[HBM] * 6,
            scratch=[some, some]
            + [pltpu.VMEM(some, jnp.int32)] * 3
            + [(1, thrust.shape[0]), pltpu.SemaphoreType.DMA((5, 4)), pltpu.SemaphoreType.DMA(())],
            name="faces",
        )
        a_core, a_chip = swap(core, core_pairs), swap(chip, chip_pairs)
        a_odd, a_row = swap(odd, odd_pairs), swap(row, row_pairs[0])
        f, g, d, absorb = call(
            set_up, [field, field, field, (16, 128)], *inputs, scratch=[(64, 512)], name="set_up"
        )
        a_odd, a_row, a_chip, a_core, f, g, d, absorb = lax.optimization_barrier(
            (a_odd, a_row, a_chip, a_core, f, g, d, absorb)
        )
        s, to_core, sums, y_faces, y_more = call(
            smooth,
            [field, (224, 128), (16, 128), (32, 512), (32, 512)],
            f, g, absorb, a_core, a_chip, a_row, a_odd,
            scratch=[slab] * 6,
            name="smooth",
        )
        s_core = swap(to_core, core_pairs)
        (block,) = call(restrict, [(40, 128)], f, d, absorb, s, sums, scratch=[(64, 512)], name="restrict")
        mine, to_chip, to_row, to_odd = call(
            to_chip_kernel,
            [(40, 128), (240, 128), (192, 128), (192, 128)],
            block, sums, absorb, s_core, s, g, y_faces, y_more,
            name="to_chip",
        )
        s_chip = swap(to_chip, chip_pairs)
        s_row, s_odd = swap(to_row, row_pairs[0]), swap(to_odd, odd_pairs)
        full, beyond = call(from_chip_kernel, [(40, 128), (40, 128)], mine, sums, s_chip, name="from_chip")
        c_core = swap(full, core_pairs)
        window, short = call(
            window_kernel, [(136, 128), (80, 128)], full, beyond, c_core, s_chip, s_core, name="window"
        )
        windows = [window] + [
            swap(short if step in short_steps else window, row_pairs[step - 1]) for step in range(1, ny)
        ]
        pressure, coarse = call(
            finish,
            [field, (4, planes, 128)],
            f, g, s, a_core, a_chip, a_row, a_odd, s_core, s_chip, s_row, s_odd, *windows,
            scratch=[(ny, 136, 128)]
            + [(planes, 16, 128)] * 3
            + [(planes + 2, 16, 128)] * 3
            + [(6, 16, 512), (20, 16, 512), long, slab, slab, (32, 512), (32, 512), slab, slab, field]
            + [(4, planes, 128), pltpu.SemaphoreType.DMA((9,))],
            out_specs=[HBM, HBM],
            name="finish",
        )
        return pressure, coarse

    spec = P("gx", "gy", None)
    return jax.shard_map(
        local,
        mesh=mesh,
        in_specs=(spec, spec, spec, spec, spec, P()),
        out_specs=(spec, P("gx", None, None)),
        check_vma=False,
    )
```

```python
import jax
import jax.numpy as jnp
from jax import lax
from jax.experimental import pallas as pl
from jax.experimental.pallas import tpu as pltpu
from jax.sharding import PartitionSpec as P

SWEEPS = 4
OMEGA = 0.8
WALL_PENALTY = 0.4
INFLOW_PENALTY = 0.2
CHEB_LOW = 0.1
CHEB_HIGH = 2.0
F32 = jnp.float32
VMEM = pl.BlockSpec(memory_space=pltpu.VMEM)


HBM = pl.BlockSpec(memory_space=pltpu.HBM)


def call(kernel, outs, *args, scratch=(), name=None, in_specs=None, out_specs=None):
    return pl.pallas_call(
        kernel,
        out_shape=[jax.ShapeDtypeStruct(s, F32) for s in outs],
        in_specs=in_specs or [VMEM] * len(args),
        out_specs=out_specs or [VMEM] * len(outs),
        scratch_shapes=[pltpu.VMEM(s, F32) if isinstance(s, tuple) else s for s in scratch],
        compiler_params=pltpu.CompilerParams(vmem_limit_bytes=16 << 20),
        name=name,
    )(*args)


def pairs_core(nx, ny):
    return [(x * ny + y, (x ^ 1) * ny + y) for x in range(nx) for y in range(ny)]


def pairs_chip(nx, ny):
    found = []
    for x in range(nx):
        for y in range(ny):
            if x in (0, nx - 1):
                found.append((x * ny + y, x * ny + (y ^ (ny // 2))))
            else:
                found.append((x * ny + y, (x + 1 if x % 2 else x - 1) * ny + y))
    return found


def pairs_row(nx, ny, step):
    return [(x * ny + y, x * ny + (y ^ step)) for x in range(nx) for y in range(ny)]


def pairs_odd(nx, ny):
    return [
        (x * ny + y, x * ny + (y + 1 if y % 2 else y - 1) % ny) for x in range(nx) for y in range(ny)
    ]


def put(ref, row, slab):
    rows = slab.shape[0]
    for j in range(slab.shape[1] // 128):
        ref[row + rows * j : row + rows * (j + 1), :] = slab[:, 128 * j : 128 * (j + 1)]


def get(ref, row, rows, width):
    return jnp.concatenate(
        [ref[row + rows * j : row + rows * (j + 1), :] for j in range(width // 128)], axis=1
    )


def iota(shape, dim):
    return lax.broadcasted_iota(jnp.int32, shape, dim)


def beside_z(slab):
    depth = slab.shape[1]
    lane = iota(slab.shape, 1)
    above = jnp.where(lane == depth - 1, 0.0, pltpu.roll(slab, depth - 1, 1))
    below = jnp.where(lane == 0, 0.0, pltpu.roll(slab, 1, 1))
    return above + below


def beside(slab, low=None, high=None):
    rows, depth = slab.shape
    tiles, columns = rows // 8, depth // 128
    lane, row = iota((8, 128), 1), iota((8, 128), 0)
    piece = [[slab[8 * t : 8 * t + 8, 128 * j : 128 * j + 128] for j in range(columns)] for t in range(tiles)]
    left = [[pltpu.roll(p, 127, 1) for p in line] for line in piece]
    right = [[pltpu.roll(p, 1, 1) for p in line] for line in piece]
    up = [[pltpu.roll(p, 7, 0) for p in line] for line in piece]
    down = [[pltpu.roll(p, 1, 0) for p in line] for line in piece]

    def outer(line, j):
        return 0.0 if line is None else jnp.broadcast_to(line[:, 128 * j : 128 * j + 128], (8, 128))

    lines = []
    for t in range(tiles):
        parts = []
        for j in range(columns):
            above = jnp.where(lane == 127, left[t][j + 1] if j + 1 < columns else 0.0, left[t][j])
            below = jnp.where(lane == 0, right[t][j - 1] if j > 0 else 0.0, right[t][j])
            after = jnp.where(row == 7, up[t + 1][j] if t + 1 < tiles else outer(high, j), up[t][j])
            before = jnp.where(row == 0, down[t - 1][j] if t > 0 else outer(low, j), down[t][j])
            parts.append((above + below) + (after + before))
        lines.append(jnp.concatenate(parts, axis=1))
    return jnp.concatenate(lines, axis=0)


def dot(left, right):
    return lax.dot_general(
        left,
        right,
        (((1,), (0,)), ((), ())),
        precision=lax.Precision.HIGHEST,
        preferred_element_type=F32,
    )


def group_lanes(depth):
    return (iota((depth, depth // 4), 0) // 4 == iota((depth, depth // 4), 1)).astype(F32)


def spread_lanes(rows):
    count, lanes = rows.shape
    pad = -count % 8
    if pad:
        rows = jnp.concatenate([rows, jnp.zeros((pad, lanes), F32)], axis=0)
    parts = []
    for j in range(4):
        index = iota(rows.shape, 1) // 4 + (lanes // 4) * j
        parts.append(jnp.take_along_axis(rows, index, axis=1, mode="promise_in_bounds"))
    return jnp.concatenate(parts, axis=1)[:count]


def spread_rows(ref, plane, start):
    row = iota((16, 128), 0) // 4
    value = jnp.zeros((16, 128), F32)
    for q in range(4):
        value = jnp.where(row == q, jnp.broadcast_to(ref[plane, start + q : start + q + 1, :], (16, 128)), value)
    return value


def spread_planes(ref, plane, column):
    row = iota((16, 128), 0) // 4
    value = jnp.zeros((16, 128), F32)
    for q in range(4):
        value = jnp.where(row == q, jnp.broadcast_to(ref[plane + q, column : column + 1, :], (16, 128)), value)
    return value


def solution(mesh):
    nx, ny = mesh.shape["gx"], mesh.shape["gy"]
    assert nx % 2 == 0 and ny % 2 == 0 and ny & (ny - 1) == 0
    axes = ("gx", "gy")

    def where_am_i():
        x, y = lax.axis_index("gx"), lax.axis_index("gy")
        return x, y, x % 2 == 0, y % 2 == 0

    def look_up(table, ids):
        spare = jnp.zeros((1, 128 - table.shape[1]), F32)
        row = jnp.broadcast_to(jnp.concatenate([table, spare], axis=1), (16, 128))
        parts = [
            jnp.take_along_axis(row, ids[:, 128 * j : 128 * (j + 1)], axis=1, mode="promise_in_bounds") for j in range(4)
        ]
        return jnp.concatenate(parts, axis=1)

    def first_of(source, reaction, kinds, ids, mask, table):
        a = reaction + jnp.where(kinds == 1, WALL_PENALTY, jnp.where(kinds == 2, INFLOW_PENALTY, 0.0))
        diagonal = 6.0 + a
        scale = OMEGA / diagonal
        return (source + mask.astype(F32) * look_up(table, ids)) * scale, scale, diagonal, a

    def faces(*refs):
        inputs, thrust, messages, buffers, table, sems, table_sem = (
            refs[:5], refs[5], refs[6:10], refs[10:15], refs[15], refs[16], refs[17]
        )
        core, chip, row, odd = messages
        _, _, x_even, y_even = where_am_i()
        near, far = jnp.where(x_even, 15, 0), jnp.where(x_even, 0, 15)
        moves = [pltpu.make_async_copy(thrust, table, table_sem)]
        for i, (hbm, buffer) in enumerate(zip(inputs, buffers)):
            for j, part in enumerate((hbm.at[:, 0, :], hbm.at[:, 15, :], hbm.at[far], hbm.at[near])):
                moves.append(pltpu.make_async_copy(part, buffer.at[j], sems.at[i, j]))
        for move in moves:
            move.start()
        for move in moves:
            move.wait()
        (low, g_low), (high, g_high), (f_far, _), (f_near, _) = (
            first_of(*(buffer[j] for buffer in buffers), table[...])[:2] for j in range(4)
        )
        put(row, 0, jnp.where(y_even, high, low))
        put(row, 64, jnp.where(y_even, g_high, g_low))
        put(odd, 0, jnp.where(y_even, low, high))
        put(odd, 64, jnp.where(y_even, g_low, g_high))
        put(chip, 0, f_far)
        put(core, 0, f_near)

    def set_up(source, reaction, kind, disk_id, disk_mask, table, f, g, d, absorb, V):
        for k in range(4):
            total = jnp.zeros((16, 512), F32)
            for x in range(4 * k, 4 * k + 4):
                f[x], g[x], d[x], a = first_of(source[x], reaction[x], kind[x], disk_id[x], disk_mask[x], table[...])
                total = total + a
            V[16 * k : 16 * k + 16, :] = total
        out, src = iota((16, 64), 0), iota((16, 64), 1)
        pick = ((src // 16 == out % 4) & ((src % 16) // 4 == out // 4)).astype(F32)
        absorb[...] = dot(dot(pick, V[...]), group_lanes(512))

    def halo_x(core, chip, row, x, x_even):
        a, b = get(core, row, 16, 512), get(chip, row, 16, 512)
        left = jnp.where(x > 0, jnp.where(x_even, b, a), 0.0)
        right = jnp.where(x < nx - 1, jnp.where(x_even, a, b), 0.0)
        return left, right

    def halo_y(row, odd, at, y, y_even):
        a, b = get(row, at, 16, 512), get(odd, at, 16, 512)
        low = jnp.where(y > 0, jnp.where(y_even, b, a), 0.0)
        high = jnp.where(y < ny - 1, jnp.where(y_even, a, b), 0.0)
        return low, high

    def smooth(f, g, absorb, core, chip, row, odd, s, to_core, sums, y_faces, y_more, lo, hi, y0, y1, y14, y15):
        x_at, y_at, x_even, y_even = where_am_i()
        left, right = halo_x(core, chip, 0, x_at, x_even)
        lo[...], hi[...] = halo_y(row, odd, 0, y_at, y_even)
        for x in range(16):
            here = f[x]
            scale = g[x]
            total = (f[x - 1] if x > 0 else left) + (f[x + 1] if x < 15 else right)
            total = total + beside(here, lo[x : x + 1, :], hi[x : x + 1, :])
            value = 1.2 * here + scale * total
            s[x] = value
            y0[x : x + 1, :] = value[0:1, :]
            y1[x : x + 1, :] = value[1:2, :]
            y14[x : x + 1, :] = value[14:15, :]
            y15[x : x + 1, :] = value[15:16, :]
        y_faces[0:16, :] = y0[...]
        y_faces[16:32, :] = y15[...]
        out, src = iota((16, 64), 0), iota((16, 64), 1)
        pick = ((out // 4 == src // 16) & (out % 4 == (src % 16) // 4)).astype(F32)
        sides = jnp.concatenate([s[0], s[15], y0[...], y15[...]], axis=0)
        sums[...] = dot(dot(pick, sides), group_lanes(512))
        put(to_core, 0, s[jnp.where(x_even, 15, 0)])
        put(to_core, 64, s[jnp.where(x_even, 14, 1)])
        put(to_core, 128, g[jnp.where(x_even, 15, 0)])
        to_core[192:196, :] = jnp.where(x_even, sums[4:8, :], sums[0:4, :])
        to_core[196:200, :] = jnp.zeros((4, 128), F32)
        to_core[200:208, :] = sums[8:16, :]
        to_core[208:224, :] = absorb[...]
        for at, ref in enumerate((y1, y14)):
            y_more[16 * at : 16 * at + 16, :] = ref[...]

    def restrict(f, d, absorb, s, sums, block, V):
        for k in range(4):
            total = jnp.zeros((16, 512), F32)
            for x in range(4 * k, 4 * k + 4):
                here = s[x]
                total = total + d[x] * (1.25 * f[x] - here)
                total = total + beside(here)
                if x > 0:
                    total = total + s[x - 1]
                if x < 15:
                    total = total + s[x + 1]
            V[16 * k : 16 * k + 16, :] = total
        out, src = iota((16, 64), 0), iota((16, 64), 1)
        pick = ((src // 16 == out % 4) & ((src % 16) // 4 == out // 4)).astype(F32)
        found = dot(dot(pick, V[...]), group_lanes(512))
        for cy in range(4):
            block[8 * cy : 8 * cy + 4, :] = found[4 * cy : 4 * cy + 4, :]
            block[8 * cy + 4 : 8 * cy + 8, :] = absorb[4 * cy : 4 * cy + 4, :]
        block[32:40, :] = sums[8:16, :]

    def to_chip_kernel(block, sums, absorb, core, s, g, y_faces, y_more, mine, to_chip, to_row, to_odd):
        _, _, x_even, y_even = where_am_i()
        mine[...] = block[...]
        face = core[192:200, :]
        for cy in range(4):
            line = face[cy : cy + 1, :]
            a, b = 8 * cy, 8 * cy + 3
            mine[a : a + 1, :] = block[a : a + 1, :] + jnp.where(x_even, 0.0, line)
            mine[b : b + 1, :] = block[b : b + 1, :] + jnp.where(x_even, line, 0.0)
        put(to_chip, 0, s[jnp.where(x_even, 0, 15)])
        put(to_chip, 64, s[jnp.where(x_even, 1, 14)])
        put(to_chip, 128, g[jnp.where(x_even, 0, 15)])
        to_chip[192:232, :] = mine[...]
        to_chip[232:236, :] = jnp.where(x_even, sums[0:4, :], sums[4:8, :])
        to_chip[236:240, :] = jnp.zeros((4, 128), F32)
        for at, ref in enumerate((y_faces, y_more)):
            a, b = ref[0:16, :], ref[16:32, :]
            put(to_row, 64 * at, jnp.where(y_even, b, a))
            put(to_odd, 64 * at, jnp.where(y_even, a, b))
        first_line, last_line = (
            jnp.concatenate([core[16 * j + line : 16 * j + line + 1, :] for j in range(4)], axis=0) for line in (0, 15)
        )
        for ref, corner in (
            (to_row, jnp.where(y_even, last_line, first_line)),
            (to_odd, jnp.where(y_even, first_line, last_line)),
        ):
            ref[128:144, :] = absorb[...]
            ref[144:160, :] = core[208:224, :]
            ref[160:168, :] = sums[8:16, :]
            ref[168:176, :] = core[200:208, :]
            ref[176:180, :] = corner
            ref[180:192, :] = jnp.zeros((12, 128), F32)

    def from_chip_kernel(mine, sums, chip, full, beyond):
        x_at, _, x_even, _ = where_am_i()
        has = jnp.where(x_even, x_at > 0, x_at < nx - 1)
        full[...] = mine[...]
        beyond[...] = chip[192:232, :]
        mine_face = jnp.where(x_even, sums[0:4, :], sums[4:8, :])
        face = chip[232:240, :]
        for cy in range(4):
            line = jnp.where(has, face[cy : cy + 1, :], 0.0)
            own = mine_face[cy : cy + 1, :]
            a, b = 8 * cy, 8 * cy + 3
            full[a : a + 1, :] = mine[a : a + 1, :] + jnp.where(x_even, line, 0.0)
            full[b : b + 1, :] = mine[b : b + 1, :] + jnp.where(x_even, 0.0, line)
            beyond[a : a + 1, :] = chip[192 + a : 193 + a, :] + jnp.where(x_even, 0.0, own)
            beyond[b : b + 1, :] = chip[192 + b : 193 + b, :] + jnp.where(x_even, own, 0.0)

    def window_kernel(full, beyond, core, chip, s_core, window, short):
        x_at, _, x_even, _ = where_am_i()
        mid = full[...]
        a, b = core[...], beyond[...]
        left, right = jnp.where(x_even, b, a), jnp.where(x_even, a, b)
        for at, block in enumerate((left, mid, right)):
            for cy in range(4):
                window[24 * cy + 4 * at : 24 * cy + 4 * at + 4, :] = block[8 * cy : 8 * cy + 4, :]
                window[24 * cy + 12 + 4 * at : 24 * cy + 16 + 4 * at, :] = block[8 * cy + 4 : 8 * cy + 8, :]
            window[96 + 4 * at : 100 + 4 * at, :] = block[32:36, :]
            window[108 + 4 * at : 112 + 4 * at, :] = block[36:40, :]
        for at, line in enumerate((0, 15)):
            near = jnp.concatenate([s_core[16 * j + line : 16 * j + line + 1, :] for j in range(4)], axis=0)
            far = jnp.concatenate([chip[16 * j + line : 16 * j + line + 1, :] for j in range(4)], axis=0)
            window[120 + 4 * at : 124 + 4 * at, :] = jnp.where(x_at > 0, jnp.where(x_even, far, near), 0.0)
            window[128 + 4 * at : 132 + 4 * at, :] = jnp.where(x_at < nx - 1, jnp.where(x_even, near, far), 0.0)
            short[72 + 4 * at : 76 + 4 * at, :] = far
        for cy in range(4):
            for at, block in enumerate((left, mid, right)):
                short[12 * cy + 4 * at : 12 * cy + 4 * at + 4, :] = block[8 * cy : 8 * cy + 4, :]
            short[48 + 4 * cy : 52 + 4 * cy, :] = beyond[8 * cy + 4 : 8 * cy + 8, :]
        short[64:72, :] = beyond[32:40, :]

    planes = 4 * ny
    short_steps = (1, 3) if ny == 4 else (1,)

    def prepare(f, g, s, a_core, a_chip, a_row, a_odd, s_core, s_chip, s_row, s_odd, u, u_low, u_high, g_x, g_y, edge):
        x_at, y_at, x_even, y_even = where_am_i()
        s_left, s_right = halo_x(s_core, s_chip, 0, x_at, x_even)
        s_left2, s_right2 = halo_x(s_core, s_chip, 64, x_at, x_even)
        f_left, f_right = halo_x(a_core, a_chip, 0, x_at, x_even)
        g_x[0], g_x[1] = halo_x(s_core, s_chip, 128, x_at, x_even)
        y1 = halo_y(s_row, s_odd, 0, y_at, y_even)
        y2 = halo_y(s_row, s_odd, 64, y_at, y_even)
        f_y = halo_y(a_row, a_odd, 0, y_at, y_even)
        g_y[0], g_y[1] = halo_y(a_row, a_odd, 64, y_at, y_even)
        u[0] = 0.2 * s_left + f_left + g_x[0] * (s_left2 + s[0] + beside(s_left))
        u[17] = 0.2 * s_right + f_right + g_x[1] * (s_right2 + s[15] + beside(s_right))
        for x in range(16):
            here = s[x]
            total = (s[x - 1] if x > 0 else s_left) + (s[x + 1] if x < 15 else s_right)
            total = total + beside(here, y1[0][x : x + 1, :], y1[1][x : x + 1, :])
            u[x + 1] = 0.2 * here + f[x] + g[x] * total
            edge[0, x : x + 1, :] = here[0:1, :]
            edge[1, x : x + 1, :] = here[15:16, :]
        for at, out in enumerate((u_low, u_high)):
            out[...] = 0.2 * y1[at] + f_y[at] + g_y[at] * (y2[at] + edge[at] + beside(y1[at]))

    def finish(*refs):
        f, g, u, u_low, u_high, g_x, g_y, s_row, s_odd = refs[:9]
        windows = refs[9 : 9 + ny]
        pressure, coarse = refs[9 + ny : 11 + ny]
        every, res, diag, inv, one, two, sol, C, U, ul, uh, result, slab_out, sems = refs[11 + ny :]
        x_at, y_at, x_even, y_even = where_am_i()
        for step, window in enumerate(windows):
            there = jnp.bitwise_xor(y_at, step)
            if step not in short_steps:
                every[there] = window[...]
                continue
            faces_of = s_row if step == 1 else s_odd

            def three(at, own, core, chip):
                every[there, at : at + 4, :] = jnp.where(x_even, chip, core)
                if own is not None:
                    every[there, at + 4 : at + 8, :] = own
                every[there, at + 8 : at + 12, :] = jnp.where(x_even, core, chip)

            for cy in range(4):
                at = 4 * cy
                every[there, 24 * cy : 24 * cy + 12, :] = window[12 * cy : 12 * cy + 12, :]
                three(
                    24 * cy + 12, faces_of[128 + at : 132 + at, :], faces_of[144 + at : 148 + at, :],
                    window[48 + at : 52 + at, :],
                )
            for at in (0, 4):
                three(
                    96 + 3 * at, faces_of[160 + at : 164 + at, :], faces_of[168 + at : 172 + at, :],
                    window[64 + at : 68 + at, :],
                )
                three(120 + at, None, faces_of[176:180, :], window[72 + at : 76 + at, :])

        row = iota((16, 128), 0)
        valid = ((row >= 4) | (x_at > 0)) & ((row < 8) | (x_at < nx - 1)) & (row < 12)
        blank = jnp.zeros((4, 128), F32)

        def twelve(value):
            return jnp.concatenate([value, blank], axis=0)

        centre = (CHEB_HIGH + CHEB_LOW) / 2.0
        half_range = (CHEB_HIGH - CHEB_LOW) / 2.0
        aspect = centre / half_range
        factor = 1.0 / aspect
        empty = jnp.zeros((16, 128), F32)
        for ref in (one, two, sol):
            ref[0] = empty
            ref[planes + 1] = empty
        for at in range(ny):
            for cy in range(4):
                plane = 4 * at + cy
                value = every[at, 24 * cy : 24 * cy + 12, :]
                if cy == 0 and at > 0:
                    value = value + every[at - 1, 108:120, :]
                if cy == 3 and at < ny - 1:
                    value = value + every[at + 1, 96:108, :]
                value = jnp.where(valid, twelve(value), 0.0)
                centre_value = 6.0 + twelve(every[at, 24 * cy + 12 : 24 * cy + 24, :]) / 16.0
                inverse = jnp.where(valid, 1.0 / (16.0 * centre_value), 0.0)
                res[plane] = value
                diag[plane] = centre_value
                inv[plane] = inverse
                direction = inverse * value / centre
                one[plane + 1] = direction
                sol[plane + 1] = direction
        now, later = one, two
        for number in range(1, SWEEPS):
            factor_next = 1.0 / (2.0 * aspect - factor)
            keep, gain = factor_next * factor, 2.0 * factor_next / half_range

            lane = iota((16, 128), 1)
            for plane in range(planes):
                here = now[plane + 1]
                total = now[plane] + now[plane + 2]
                total = total + pltpu.roll(here, 15, 0) + pltpu.roll(here, 1, 0)
                total = total + jnp.where(lane == 127, 0.0, pltpu.roll(here, 127, 1))
                total = total + jnp.where(lane == 0, 0.0, pltpu.roll(here, 1, 1))
                residual = res[plane] - 16.0 * (diag[plane] * here - total)
                res[plane] = residual
                direction = keep * here + gain * inv[plane] * residual
                later[plane + 1] = direction
                sol[plane + 1] = sol[plane + 1] + direction
            now, later = later, now
            factor = factor_next
        for plane in range(planes):
            for cx in range(4):
                slab_out[cx, plane : plane + 1, :] = sol[plane + 1, 4 + cx : 5 + cx, :]
        moves = [pltpu.make_async_copy(slab_out, coarse, sems.at[8])]
        moves[0].start()

        first_plane = 4 * y_at + 1
        below, above = first_plane - 1, first_plane + 4
        for at in range(6):
            C[at] = spread_lanes(spread_planes(sol, first_plane, 3 + at))
        outside = [[spread_lanes(sol[plane, 3 + at : 4 + at, :]) for at in range(6)] for plane in (below, above)]
        before, after = jnp.maximum(y_at - 1, 0), jnp.minimum(y_at + 1, ny - 1)
        corners = []
        for who, inside, line in ((before, y_at > 0, 1), (after, y_at < ny - 1, 0)):
            for base, there in ((0, x_at > 0), (2, x_at < nx - 1)):
                corner = jnp.concatenate(
                    [every[who, pl.ds(120 + 4 * (base + line) + j, 1), :] for j in range(4)], axis=1
                )
                corners.append(jnp.where(inside & there, corner, 0.0))
        edge_row = iota((16, 512), 0)

        def ends(first, last):
            first, last = (jnp.broadcast_to(line, (16, 512)) for line in (first, last))
            return jnp.where(edge_row == 0, first, jnp.where(edge_row == 15, last, 0.0))

        for at in range(6):
            here = C[at]
            around = beside(here, outside[0][at], outside[1][at])
            fifth_of = 0.2 * here
            if at == 0:
                U[0] = u[0] + fifth_of + g_x[0] * (around + here + C[1] + ends(corners[0], corners[2]))
            elif at == 5:
                U[17] = u[17] + fifth_of + g_x[1] * (around + here + C[4] + ends(corners[1], corners[3]))
            else:
                inner = around + 2.0 * here
                sides = [around + here + C[at - 1], inner, inner, around + here + C[at + 1]]
                for q in range(4):
                    x = 4 * (at - 1) + q
                    U[x + 1] = u[x + 1] + fifth_of + g[x] * sides[q]
        for at, (part, out, plane, inside) in enumerate(
            ((u_low, ul, below, first_plane), (u_high, uh, above, first_plane + 3))
        ):
            beyond = spread_lanes(spread_rows(sol, plane, 4))
            edge = spread_lanes(spread_rows(sol, inside, 4))
            around = beside(beyond, outside[at][0], outside[at][5])
            total = beyond + edge + around + ends(corners[2 * at], corners[2 * at + 1])
            out[...] = part[...] + 0.2 * beyond + g_y[at] * total

        for x in range(16):
            here = U[x + 1]
            total = U[x] + U[x + 2] + beside(here, ul[x : x + 1, :], uh[x : x + 1, :])
            result[x] = 0.2 * here + f[x] + g[x] * total
            if x % 2 == 1:
                part = pl.ds(x - 1, 2)
                moves.append(pltpu.make_async_copy(result.at[part], pressure.at[part], sems.at[x // 2]))
                moves[-1].start()
        for move in moves:
            move.wait()

    slab, field, long = (16, 512), (16, 16, 512), (18, 16, 512)
    core_pairs, chip_pairs = pairs_core(nx, ny), pairs_chip(nx, ny)
    row_pairs = [pairs_row(nx, ny, step) for step in range(1, ny)]
    odd_pairs = pairs_odd(nx, ny)

    def swap(array, pairs):
        return lax.ppermute(array, axes, pairs)

    def local(source, reaction, boundary_kind, disk_id, disk_mask, thrust):
        inputs = (source, reaction, boundary_kind, disk_id, disk_mask, thrust.reshape(1, -1))
        some = (4, 16, 512)
        core, chip, row, odd = call(
            faces,
            [(64, 128), (64, 128), (128, 128), (128, 128)],
            *(pltpu.with_memory_space_constraint(array, pltpu.HBM) for array in inputs),
            in_specs=[HBM] * 6,
            scratch=[some, some]
            + [pltpu.VMEM(some, jnp.int32)] * 3
            + [(1, thrust.shape[0]), pltpu.SemaphoreType.DMA((5, 4)), pltpu.SemaphoreType.DMA(())],
            name="faces",
        )
        a_core, a_chip = swap(core, core_pairs), swap(chip, chip_pairs)
        a_odd, a_row = swap(odd, odd_pairs), swap(row, row_pairs[0])
        f, g, d, absorb = call(
            set_up, [field, field, field, (16, 128)], *inputs, scratch=[(64, 512)], name="set_up"
        )
        a_odd, a_row, a_chip, a_core, f, g, d, absorb = lax.optimization_barrier(
            (a_odd, a_row, a_chip, a_core, f, g, d, absorb)
        )
        s, to_core, sums, y_faces, y_more = call(
            smooth,
            [field, (224, 128), (16, 128), (32, 512), (32, 512)],
            f, g, absorb, a_core, a_chip, a_row, a_odd,
            scratch=[slab] * 6,
            name="smooth",
        )
        s_core = swap(to_core, core_pairs)
        (block,) = call(restrict, [(40, 128)], f, d, absorb, s, sums, scratch=[(64, 512)], name="restrict")
        mine, to_chip, to_row, to_odd = call(
            to_chip_kernel,
            [(40, 128), (240, 128), (192, 128), (192, 128)],
            block, sums, absorb, s_core, s, g, y_faces, y_more,
            name="to_chip",
        )
        s_chip = swap(to_chip, chip_pairs)
        s_row, s_odd = swap(to_row, row_pairs[0]), swap(to_odd, odd_pairs)
        full, beyond = call(from_chip_kernel, [(40, 128), (40, 128)], mine, sums, s_chip, name="from_chip")
        c_core = swap(full, core_pairs)
        window, short = call(
            window_kernel, [(136, 128), (80, 128)], full, beyond, c_core, s_chip, s_core, name="window"
        )
        windows = [window] + [
            swap(short if step in short_steps else window, row_pairs[step - 1]) for step in range(1, ny)
        ]
        prepared = call(
            prepare,
            [long, slab, slab, (2, 16, 512), (2, 16, 512)],
            f, g, s, a_core, a_chip, a_row, a_odd, s_core, s_chip, s_row, s_odd,
            scratch=[(2, 16, 512)],
            name="prepare",
        )
        pressure, coarse = call(
            finish,
            [field, (4, planes, 128)],
            f, g, *prepared, s_row, s_odd, *windows,
            scratch=[(ny, 136, 128)]
            + [(planes, 16, 128)] * 3
            + [(planes + 2, 16, 128)] * 3
            + [(6, 16, 512), long, slab, slab, field, (4, planes, 128), pltpu.SemaphoreType.DMA((9,))],
            out_specs=[HBM, HBM],
            name="finish",
        )
        return pressure, coarse

    spec = P("gx", "gy", None)
    return jax.shard_map(
        local,
        mesh=mesh,
        in_specs=(spec, spec, spec, spec, spec, P()),
        out_specs=(spec, P("gx", None, None)),
        check_vma=False,
    )
```

```python
import jax
import jax.numpy as jnp
from jax import lax
from jax.experimental import pallas as pl
from jax.experimental.pallas import tpu as pltpu
from jax.sharding import PartitionSpec as P

SWEEPS = 4
OMEGA = 0.8
WALL_PENALTY = 0.4
INFLOW_PENALTY = 0.2
CHEB_LOW = 0.1
CHEB_HIGH = 2.0
F32 = jnp.float32
VMEM = pl.BlockSpec(memory_space=pltpu.VMEM)


HBM = pl.BlockSpec(memory_space=pltpu.HBM)
MORE = 152
FACES = 192


def call(kernel, outs, *args, scratch=(), name=None, in_specs=None, out_specs=None):
    return pl.pallas_call(
        kernel,
        out_shape=[jax.ShapeDtypeStruct(s, F32) for s in outs],
        in_specs=in_specs or [VMEM] * len(args),
        out_specs=out_specs or [VMEM] * len(outs),
        scratch_shapes=[pltpu.VMEM(s, F32) if isinstance(s, tuple) else s for s in scratch],
        compiler_params=pltpu.CompilerParams(vmem_limit_bytes=16 << 20),
        name=name,
    )(*args)


def pairs_core(nx, ny):
    return [(x * ny + y, (x ^ 1) * ny + y) for x in range(nx) for y in range(ny)]


def pairs_chip(nx, ny):
    found = []
    for x in range(nx):
        for y in range(ny):
            if x in (0, nx - 1):
                found.append((x * ny + y, x * ny + (y ^ (ny // 2))))
            else:
                found.append((x * ny + y, (x + 1 if x % 2 else x - 1) * ny + y))
    return found


def pairs_row(nx, ny, step):
    return [(x * ny + y, x * ny + (y ^ step)) for x in range(nx) for y in range(ny)]


def pairs_odd(nx, ny):
    return [
        (x * ny + y, x * ny + (y + 1 if y % 2 else y - 1) % ny) for x in range(nx) for y in range(ny)
    ]


def put(ref, row, slab):
    rows = slab.shape[0]
    for j in range(slab.shape[1] // 128):
        ref[row + rows * j : row + rows * (j + 1), :] = slab[:, 128 * j : 128 * (j + 1)]


def get(ref, row, rows, width):
    return jnp.concatenate(
        [ref[row + rows * j : row + rows * (j + 1), :] for j in range(width // 128)], axis=1
    )


def iota(shape, dim):
    return lax.broadcasted_iota(jnp.int32, shape, dim)


def beside_z(slab):
    depth = slab.shape[1]
    lane = iota(slab.shape, 1)
    above = jnp.where(lane == depth - 1, 0.0, pltpu.roll(slab, depth - 1, 1))
    below = jnp.where(lane == 0, 0.0, pltpu.roll(slab, 1, 1))
    return above + below


def beside(slab, low=None, high=None):
    rows, depth = slab.shape
    tiles, columns = rows // 8, depth // 128
    lane, row = iota((8, 128), 1), iota((8, 128), 0)
    piece = [[slab[8 * t : 8 * t + 8, 128 * j : 128 * j + 128] for j in range(columns)] for t in range(tiles)]
    left = [[pltpu.roll(p, 127, 1) for p in line] for line in piece]
    right = [[pltpu.roll(p, 1, 1) for p in line] for line in piece]
    up = [[pltpu.roll(p, 7, 0) for p in line] for line in piece]
    down = [[pltpu.roll(p, 1, 0) for p in line] for line in piece]

    def outer(line, j):
        return 0.0 if line is None else jnp.broadcast_to(line[:, 128 * j : 128 * j + 128], (8, 128))

    lines = []
    for t in range(tiles):
        parts = []
        for j in range(columns):
            above = jnp.where(lane == 127, left[t][j + 1] if j + 1 < columns else 0.0, left[t][j])
            below = jnp.where(lane == 0, right[t][j - 1] if j > 0 else 0.0, right[t][j])
            after = jnp.where(row == 7, up[t + 1][j] if t + 1 < tiles else outer(high, j), up[t][j])
            before = jnp.where(row == 0, down[t - 1][j] if t > 0 else outer(low, j), down[t][j])
            parts.append((above + below) + (after + before))
        lines.append(jnp.concatenate(parts, axis=1))
    return jnp.concatenate(lines, axis=0)


def dot(left, right):
    return lax.dot_general(
        left,
        right,
        (((1,), (0,)), ((), ())),
        precision=lax.Precision.HIGHEST,
        preferred_element_type=F32,
    )


def group_lanes(depth):
    return (iota((depth, depth // 4), 0) // 4 == iota((depth, depth // 4), 1)).astype(F32)


def spread_lanes(rows):
    count, lanes = rows.shape
    pad = -count % 8
    if pad:
        rows = jnp.concatenate([rows, jnp.zeros((pad, lanes), F32)], axis=0)
    parts = []
    for j in range(4):
        index = iota(rows.shape, 1) // 4 + (lanes // 4) * j
        parts.append(jnp.take_along_axis(rows, index, axis=1, mode="promise_in_bounds"))
    return jnp.concatenate(parts, axis=1)[:count]


def spread_rows(ref, plane, start):
    row = iota((16, 128), 0) // 4
    value = jnp.zeros((16, 128), F32)
    for q in range(4):
        value = jnp.where(row == q, jnp.broadcast_to(ref[plane, start + q : start + q + 1, :], (16, 128)), value)
    return value


def spread_planes(ref, plane, column):
    row = iota((16, 128), 0) // 4
    value = jnp.zeros((16, 128), F32)
    for q in range(4):
        value = jnp.where(row == q, jnp.broadcast_to(ref[plane + q, column : column + 1, :], (16, 128)), value)
    return value


def solution(mesh):
    nx, ny = mesh.shape["gx"], mesh.shape["gy"]
    assert nx % 2 == 0 and ny % 2 == 0 and ny & (ny - 1) == 0
    axes = ("gx", "gy")

    def where_am_i():
        x, y = lax.axis_index("gx"), lax.axis_index("gy")
        return x, y, x % 2 == 0, y % 2 == 0

    def look_up(table, ids):
        spare = jnp.zeros((1, 128 - table.shape[1]), F32)
        row = jnp.broadcast_to(jnp.concatenate([table, spare], axis=1), (16, 128))
        parts = [
            jnp.take_along_axis(row, ids[:, 128 * j : 128 * (j + 1)], axis=1, mode="promise_in_bounds") for j in range(4)
        ]
        return jnp.concatenate(parts, axis=1)

    def first_of(source, reaction, kinds, ids, mask, table):
        a = reaction + jnp.where(kinds == 1, WALL_PENALTY, jnp.where(kinds == 2, INFLOW_PENALTY, 0.0))
        diagonal = 6.0 + a
        scale = OMEGA / diagonal
        return (source + mask.astype(F32) * look_up(table, ids)) * scale, scale, diagonal, a

    def faces(*refs):
        inputs, thrust, messages, buffers, table, sems, table_sem = (
            refs[:5], refs[5], refs[6:10], refs[10:15], refs[15], refs[16], refs[17]
        )
        core, chip, row, odd = messages
        _, _, x_even, y_even = where_am_i()
        near, far = jnp.where(x_even, 15, 0), jnp.where(x_even, 0, 15)
        moves = [pltpu.make_async_copy(thrust, table, table_sem)]
        for i, (hbm, buffer) in enumerate(zip(inputs, buffers)):
            for j, part in enumerate((hbm.at[:, 0, :], hbm.at[:, 15, :], hbm.at[far], hbm.at[near])):
                moves.append(pltpu.make_async_copy(part, buffer.at[j], sems.at[i, j]))
        for move in moves:
            move.start()
        for move in moves:
            move.wait()
        (low, g_low), (high, g_high), (f_far, _), (f_near, _) = (
            first_of(*(buffer[j] for buffer in buffers), table[...])[:2] for j in range(4)
        )
        put(row, 0, jnp.where(y_even, high, low))
        put(row, 64, jnp.where(y_even, g_high, g_low))
        put(odd, 0, jnp.where(y_even, low, high))
        put(odd, 64, jnp.where(y_even, g_low, g_high))
        put(chip, 0, f_far)
        put(core, 0, f_near)

    def set_up(source, reaction, kind, disk_id, disk_mask, table, f, g, d, absorb, V):
        for k in range(4):
            total = jnp.zeros((16, 512), F32)
            for x in range(4 * k, 4 * k + 4):
                f[x], g[x], d[x], a = first_of(source[x], reaction[x], kind[x], disk_id[x], disk_mask[x], table[...])
                total = total + a
            V[16 * k : 16 * k + 16, :] = total
        out, src = iota((16, 64), 0), iota((16, 64), 1)
        pick = ((src // 16 == out % 4) & ((src % 16) // 4 == out // 4)).astype(F32)
        absorb[...] = dot(dot(pick, V[...]), group_lanes(512))

    def halo_x(core, chip, row, x, x_even, chip_row=None):
        a, b = get(core, row, 16, 512), get(chip, row if chip_row is None else chip_row, 16, 512)
        left = jnp.where(x > 0, jnp.where(x_even, b, a), 0.0)
        right = jnp.where(x < nx - 1, jnp.where(x_even, a, b), 0.0)
        return left, right

    def halo_y(row, odd, at, y, y_even):
        a, b = get(row, at, 16, 512), get(odd, at, 16, 512)
        low = jnp.where(y > 0, jnp.where(y_even, b, a), 0.0)
        high = jnp.where(y < ny - 1, jnp.where(y_even, a, b), 0.0)
        return low, high

    def smooth(f, g, absorb, core, chip, row, odd, s, to_core, sums, y_faces, y_more, lo, hi, y0, y1, y14, y15):
        x_at, y_at, x_even, y_even = where_am_i()
        left, right = halo_x(core, chip, 0, x_at, x_even)
        lo[...], hi[...] = halo_y(row, odd, 0, y_at, y_even)
        for x in range(16):
            here = f[x]
            scale = g[x]
            total = (f[x - 1] if x > 0 else left) + (f[x + 1] if x < 15 else right)
            total = total + beside(here, lo[x : x + 1, :], hi[x : x + 1, :])
            value = 1.2 * here + scale * total
            s[x] = value
            y0[x : x + 1, :] = value[0:1, :]
            y1[x : x + 1, :] = value[1:2, :]
            y14[x : x + 1, :] = value[14:15, :]
            y15[x : x + 1, :] = value[15:16, :]
        y_faces[0:16, :] = y0[...]
        y_faces[16:32, :] = y15[...]
        out, src = iota((16, 64), 0), iota((16, 64), 1)
        pick = ((out // 4 == src // 16) & (out % 4 == (src % 16) // 4)).astype(F32)
        sides = jnp.concatenate([s[0], s[15], y0[...], y15[...]], axis=0)
        sums[...] = dot(dot(pick, sides), group_lanes(512))
        put(to_core, 0, s[jnp.where(x_even, 15, 0)])
        put(to_core, 64, s[jnp.where(x_even, 14, 1)])
        put(to_core, 128, g[jnp.where(x_even, 15, 0)])
        to_core[192:196, :] = jnp.where(x_even, sums[4:8, :], sums[0:4, :])
        to_core[196:200, :] = jnp.zeros((4, 128), F32)
        to_core[200:208, :] = sums[8:16, :]
        to_core[208:224, :] = absorb[...]
        for at, ref in enumerate((y1, y14)):
            y_more[16 * at : 16 * at + 16, :] = ref[...]

    def restrict(f, d, absorb, s, sums, block, V):
        for k in range(4):
            total = jnp.zeros((16, 512), F32)
            for x in range(4 * k, 4 * k + 4):
                here = s[x]
                total = total + d[x] * (1.25 * f[x] - here)
                total = total + beside(here)
                if x > 0:
                    total = total + s[x - 1]
                if x < 15:
                    total = total + s[x + 1]
            V[16 * k : 16 * k + 16, :] = total
        out, src = iota((16, 64), 0), iota((16, 64), 1)
        pick = ((src // 16 == out % 4) & ((src % 16) // 4 == out // 4)).astype(F32)
        found = dot(dot(pick, V[...]), group_lanes(512))
        for cy in range(4):
            block[8 * cy : 8 * cy + 4, :] = found[4 * cy : 4 * cy + 4, :]
            block[8 * cy + 4 : 8 * cy + 8, :] = absorb[4 * cy : 4 * cy + 4, :]
        block[32:40, :] = sums[8:16, :]

    def to_chip_kernel(block, sums, absorb, core, s, g, y_faces, y_more, mine, to_chip, to_row, to_odd):
        _, _, x_even, y_even = where_am_i()
        mine[...] = block[...]
        face = core[192:200, :]
        for cy in range(4):
            line = face[cy : cy + 1, :]
            a, b = 8 * cy, 8 * cy + 3
            mine[a : a + 1, :] = block[a : a + 1, :] + jnp.where(x_even, 0.0, line)
            mine[b : b + 1, :] = block[b : b + 1, :] + jnp.where(x_even, line, 0.0)
        put(to_chip, 0, s[jnp.where(x_even, 0, 15)])
        to_chip[64:104, :] = mine[...]
        to_chip[104:108, :] = jnp.where(x_even, sums[0:4, :], sums[4:8, :])
        to_chip[108:112, :] = jnp.zeros((4, 128), F32)
        for at, ref in enumerate((y_faces, y_more)):
            a, b = ref[0:16, :], ref[16:32, :]
            put(to_row, 64 * at, jnp.where(y_even, b, a))
            put(to_odd, 64 * at, jnp.where(y_even, a, b))
        first_line, last_line = (
            jnp.concatenate([core[16 * j + line : 16 * j + line + 1, :] for j in range(4)], axis=0) for line in (0, 15)
        )
        for ref, corner in (
            (to_row, jnp.where(y_even, last_line, first_line)),
            (to_odd, jnp.where(y_even, first_line, last_line)),
        ):
            ref[128:144, :] = absorb[...]
            ref[144:160, :] = core[208:224, :]
            ref[160:168, :] = sums[8:16, :]
            ref[168:176, :] = core[200:208, :]
            ref[176:180, :] = corner
            ref[180:FACES, :] = jnp.zeros((FACES - 180, 128), F32)

    def from_chip_kernel(mine, sums, chip, s, g, full, beyond, more):
        x_at, _, x_even, _ = where_am_i()
        has = jnp.where(x_even, x_at > 0, x_at < nx - 1)
        full[...] = mine[...]
        beyond[...] = chip[64:104, :]
        mine_face = jnp.where(x_even, sums[0:4, :], sums[4:8, :])
        face = chip[104:112, :]
        for cy in range(4):
            line = jnp.where(has, face[cy : cy + 1, :], 0.0)
            own = mine_face[cy : cy + 1, :]
            a, b = 8 * cy, 8 * cy + 3
            full[a : a + 1, :] = mine[a : a + 1, :] + jnp.where(x_even, line, 0.0)
            full[b : b + 1, :] = mine[b : b + 1, :] + jnp.where(x_even, 0.0, line)
            beyond[a : a + 1, :] = chip[64 + a : 65 + a, :] + jnp.where(x_even, 0.0, own)
            beyond[b : b + 1, :] = chip[64 + b : 65 + b, :] + jnp.where(x_even, own, 0.0)
        put(more, 0, s[jnp.where(x_even, 1, 14)])
        put(more, 64, g[jnp.where(x_even, 0, 15)])
        more[128:MORE, :] = jnp.zeros((MORE - 128, 128), F32)

    def window_kernel(full, beyond, core, chip, s_core, window, short):
        x_at, _, x_even, _ = where_am_i()
        mid = full[...]
        a, b = core[...], beyond[...]
        left, right = jnp.where(x_even, b, a), jnp.where(x_even, a, b)
        for at, block in enumerate((left, mid, right)):
            for cy in range(4):
                window[24 * cy + 4 * at : 24 * cy + 4 * at + 4, :] = block[8 * cy : 8 * cy + 4, :]
                window[24 * cy + 12 + 4 * at : 24 * cy + 16 + 4 * at, :] = block[8 * cy + 4 : 8 * cy + 8, :]
            window[96 + 4 * at : 100 + 4 * at, :] = block[32:36, :]
            window[108 + 4 * at : 112 + 4 * at, :] = block[36:40, :]
        for at, line in enumerate((0, 15)):
            near = jnp.concatenate([s_core[16 * j + line : 16 * j + line + 1, :] for j in range(4)], axis=0)
            far = jnp.concatenate([chip[16 * j + line : 16 * j + line + 1, :] for j in range(4)], axis=0)
            window[120 + 4 * at : 124 + 4 * at, :] = jnp.where(x_at > 0, jnp.where(x_even, far, near), 0.0)
            window[128 + 4 * at : 132 + 4 * at, :] = jnp.where(x_at < nx - 1, jnp.where(x_even, near, far), 0.0)
            short[72 + 4 * at : 76 + 4 * at, :] = far
        for cy in range(4):
            for at, block in enumerate((left, mid, right)):
                short[12 * cy + 4 * at : 12 * cy + 4 * at + 4, :] = block[8 * cy : 8 * cy + 4, :]
            short[48 + 4 * cy : 52 + 4 * cy, :] = beyond[8 * cy + 4 : 8 * cy + 8, :]
        short[64:72, :] = beyond[32:40, :]

    planes = 4 * ny
    short_steps = (1, 3) if ny == 4 else (1,)

    def prepare(f, g, s, a_core, a_chip, a_row, a_odd, s_core, s_chip, s_more, s_row, s_odd, u, u_low, u_high, g_x, g_y, edge):
        x_at, y_at, x_even, y_even = where_am_i()
        s_left, s_right = halo_x(s_core, s_chip, 0, x_at, x_even)
        s_left2, s_right2 = halo_x(s_core, s_more, 64, x_at, x_even, 0)
        f_left, f_right = halo_x(a_core, a_chip, 0, x_at, x_even)
        g_x[0], g_x[1] = halo_x(s_core, s_more, 128, x_at, x_even, 64)
        y1 = halo_y(s_row, s_odd, 0, y_at, y_even)
        y2 = halo_y(s_row, s_odd, 64, y_at, y_even)
        f_y = halo_y(a_row, a_odd, 0, y_at, y_even)
        g_y[0], g_y[1] = halo_y(a_row, a_odd, 64, y_at, y_even)
        u[0] = 0.2 * s_left + f_left + g_x[0] * (s_left2 + s[0] + beside(s_left))
        u[17] = 0.2 * s_right + f_right + g_x[1] * (s_right2 + s[15] + beside(s_right))
        for x in range(16):
            here = s[x]
            total = (s[x - 1] if x > 0 else s_left) + (s[x + 1] if x < 15 else s_right)
            total = total + beside(here, y1[0][x : x + 1, :], y1[1][x : x + 1, :])
            u[x + 1] = 0.2 * here + f[x] + g[x] * total
            edge[0, x : x + 1, :] = here[0:1, :]
            edge[1, x : x + 1, :] = here[15:16, :]
        for at, out in enumerate((u_low, u_high)):
            out[...] = 0.2 * y1[at] + f_y[at] + g_y[at] * (y2[at] + edge[at] + beside(y1[at]))

    def finish(*refs):
        f, g, u, u_low, u_high, g_x, g_y, s_row, s_odd = refs[:9]
        windows = refs[9 : 9 + ny]
        pressure, coarse = refs[9 + ny : 11 + ny]
        every, res, diag, inv, one, two, sol, C, U, ul, uh, result, slab_out, sems = refs[11 + ny :]
        x_at, y_at, x_even, y_even = where_am_i()
        for step, window in enumerate(windows):
            there = jnp.bitwise_xor(y_at, step)
            if step not in short_steps:
                every[there] = window[...]
                continue
            faces_of = s_row if step == 1 else s_odd

            def three(at, own, core, chip):
                every[there, at : at + 4, :] = jnp.where(x_even, chip, core)
                if own is not None:
                    every[there, at + 4 : at + 8, :] = own
                every[there, at + 8 : at + 12, :] = jnp.where(x_even, core, chip)

            for cy in range(4):
                at = 4 * cy
                every[there, 24 * cy : 24 * cy + 12, :] = window[12 * cy : 12 * cy + 12, :]
                three(
                    24 * cy + 12, faces_of[128 + at : 132 + at, :], faces_of[144 + at : 148 + at, :],
                    window[48 + at : 52 + at, :],
                )
            for at in (0, 4):
                three(
                    96 + 3 * at, faces_of[160 + at : 164 + at, :], faces_of[168 + at : 172 + at, :],
                    window[64 + at : 68 + at, :],
                )
                three(120 + at, None, faces_of[176:180, :], window[72 + at : 76 + at, :])

        row = iota((16, 128), 0)
        valid = ((row >= 4) | (x_at > 0)) & ((row < 8) | (x_at < nx - 1)) & (row < 12)
        blank = jnp.zeros((4, 128), F32)

        def twelve(value):
            return jnp.concatenate([value, blank], axis=0)

        centre = (CHEB_HIGH + CHEB_LOW) / 2.0
        half_range = (CHEB_HIGH - CHEB_LOW) / 2.0
        aspect = centre / half_range
        factor = 1.0 / aspect
        empty = jnp.zeros((16, 128), F32)
        for ref in (one, two, sol):
            ref[0] = empty
            ref[planes + 1] = empty
        for at in range(ny):
            for cy in range(4):
                plane = 4 * at + cy
                value = every[at, 24 * cy : 24 * cy + 12, :]
                if cy == 0 and at > 0:
                    value = value + every[at - 1, 108:120, :]
                if cy == 3 and at < ny - 1:
                    value = value + every[at + 1, 96:108, :]
                value = jnp.where(valid, twelve(value), 0.0)
                centre_value = 6.0 + twelve(every[at, 24 * cy + 12 : 24 * cy + 24, :]) / 16.0
                inverse = jnp.where(valid, 1.0 / (16.0 * centre_value), 0.0)
                res[plane] = value
                diag[plane] = centre_value
                inv[plane] = inverse
                direction = inverse * value / centre
                one[plane + 1] = direction
                sol[plane + 1] = direction
        now, later = one, two
        for number in range(1, SWEEPS):
            factor_next = 1.0 / (2.0 * aspect - factor)
            keep, gain = factor_next * factor, 2.0 * factor_next / half_range

            lane = iota((16, 128), 1)
            for plane in range(planes):
                here = now[plane + 1]
                total = now[plane] + now[plane + 2]
                total = total + pltpu.roll(here, 15, 0) + pltpu.roll(here, 1, 0)
                total = total + jnp.where(lane == 127, 0.0, pltpu.roll(here, 127, 1))
                total = total + jnp.where(lane == 0, 0.0, pltpu.roll(here, 1, 1))
                residual = res[plane] - 16.0 * (diag[plane] * here - total)
                res[plane] = residual
                direction = keep * here + gain * inv[plane] * residual
                later[plane + 1] = direction
                sol[plane + 1] = sol[plane + 1] + direction
            now, later = later, now
            factor = factor_next
        for plane in range(planes):
            for cx in range(4):
                slab_out[cx, plane : plane + 1, :] = sol[plane + 1, 4 + cx : 5 + cx, :]
        moves = [pltpu.make_async_copy(slab_out, coarse, sems.at[8])]
        moves[0].start()

        first_plane = 4 * y_at + 1
        below, above = first_plane - 1, first_plane + 4
        for at in range(6):
            C[at] = spread_lanes(spread_planes(sol, first_plane, 3 + at))
        outside = [[spread_lanes(sol[plane, 3 + at : 4 + at, :]) for at in range(6)] for plane in (below, above)]
        before, after = jnp.maximum(y_at - 1, 0), jnp.minimum(y_at + 1, ny - 1)
        corners = []
        for who, inside, line in ((before, y_at > 0, 1), (after, y_at < ny - 1, 0)):
            for base, there in ((0, x_at > 0), (2, x_at < nx - 1)):
                corner = jnp.concatenate(
                    [every[who, pl.ds(120 + 4 * (base + line) + j, 1), :] for j in range(4)], axis=1
                )
                corners.append(jnp.where(inside & there, corner, 0.0))
        edge_row = iota((16, 512), 0)

        def ends(first, last):
            first, last = (jnp.broadcast_to(line, (16, 512)) for line in (first, last))
            return jnp.where(edge_row == 0, first, jnp.where(edge_row == 15, last, 0.0))

        for at in range(6):
            here = C[at]
            around = beside(here, outside[0][at], outside[1][at])
            fifth_of = 0.2 * here
            if at == 0:
                U[0] = u[0] + fifth_of + g_x[0] * (around + here + C[1] + ends(corners[0], corners[2]))
            elif at == 5:
                U[17] = u[17] + fifth_of + g_x[1] * (around + here + C[4] + ends(corners[1], corners[3]))
            else:
                inner = around + 2.0 * here
                sides = [around + here + C[at - 1], inner, inner, around + here + C[at + 1]]
                for q in range(4):
                    x = 4 * (at - 1) + q
                    U[x + 1] = u[x + 1] + fifth_of + g[x] * sides[q]
        for at, (part, out, plane, inside) in enumerate(
            ((u_low, ul, below, first_plane), (u_high, uh, above, first_plane + 3))
        ):
            beyond = spread_lanes(spread_rows(sol, plane, 4))
            edge = spread_lanes(spread_rows(sol, inside, 4))
            around = beside(beyond, outside[at][0], outside[at][5])
            total = beyond + edge + around + ends(corners[2 * at], corners[2 * at + 1])
            out[...] = part[...] + 0.2 * beyond + g_y[at] * total

        for x in range(16):
            here = U[x + 1]
            total = U[x] + U[x + 2] + beside(here, ul[x : x + 1, :], uh[x : x + 1, :])
            result[x] = 0.2 * here + f[x] + g[x] * total
            if x % 2 == 1:
                part = pl.ds(x - 1, 2)
                moves.append(pltpu.make_async_copy(result.at[part], pressure.at[part], sems.at[x // 2]))
                moves[-1].start()
        for move in moves:
            move.wait()

    slab, field, long = (16, 512), (16, 16, 512), (18, 16, 512)
    core_pairs, chip_pairs = pairs_core(nx, ny), pairs_chip(nx, ny)
    row_pairs = [pairs_row(nx, ny, step) for step in range(1, ny)]
    odd_pairs = pairs_odd(nx, ny)

    def swap(array, pairs):
        return lax.ppermute(array, axes, pairs)

    def local(source, reaction, boundary_kind, disk_id, disk_mask, thrust):
        inputs = (source, reaction, boundary_kind, disk_id, disk_mask, thrust.reshape(1, -1))
        some = (4, 16, 512)
        core, chip, row, odd = call(
            faces,
            [(64, 128), (64, 128), (128, 128), (128, 128)],
            *(pltpu.with_memory_space_constraint(array, pltpu.HBM) for array in inputs),
            in_specs=[HBM] * 6,
            scratch=[some, some]
            + [pltpu.VMEM(some, jnp.int32)] * 3
            + [(1, thrust.shape[0]), pltpu.SemaphoreType.DMA((5, 4)), pltpu.SemaphoreType.DMA(())],
            name="faces",
        )
        a_core, a_chip = swap(core, core_pairs), swap(chip, chip_pairs)
        a_odd, a_row = swap(odd, odd_pairs), swap(row, row_pairs[0])
        f, g, d, absorb = call(
            set_up, [field, field, field, (16, 128)], *inputs, scratch=[(64, 512)], name="set_up"
        )
        a_odd, a_row, a_chip, a_core, f, g, d, absorb = lax.optimization_barrier(
            (a_odd, a_row, a_chip, a_core, f, g, d, absorb)
        )
        s, to_core, sums, y_faces, y_more = call(
            smooth,
            [field, (224, 128), (16, 128), (32, 512), (32, 512)],
            f, g, absorb, a_core, a_chip, a_row, a_odd,
            scratch=[slab] * 6,
            name="smooth",
        )
        s_core = swap(to_core, core_pairs)
        (block,) = call(restrict, [(40, 128)], f, d, absorb, s, sums, scratch=[(64, 512)], name="restrict")
        mine, to_chip, to_row, to_odd = call(
            to_chip_kernel,
            [(40, 128), (112, 128), (FACES, 128), (FACES, 128)],
            block, sums, absorb, s_core, s, g, y_faces, y_more,
            name="to_chip",
        )
        s_chip = swap(to_chip, chip_pairs)
        s_row, s_odd = swap(to_row, row_pairs[0]), swap(to_odd, odd_pairs)
        full, beyond, more = call(
            from_chip_kernel, [(40, 128), (40, 128), (MORE, 128)], mine, sums, s_chip, s, g, name="from_chip"
        )
        c_core, s_more = swap(full, core_pairs), swap(more, chip_pairs)
        window, short = call(
            window_kernel, [(136, 128), (80, 128)], full, beyond, c_core, s_chip, s_core, name="window"
        )
        windows = [window] + [
            swap(short if step in short_steps else window, row_pairs[step - 1]) for step in range(1, ny)
        ]
        prepared = call(
            prepare,
            [long, slab, slab, (2, 16, 512), (2, 16, 512)],
            f, g, s, a_core, a_chip, a_row, a_odd, s_core, s_chip, s_more, s_row, s_odd,
            scratch=[(2, 16, 512)],
            name="prepare",
        )
        pressure, coarse = call(
            finish,
            [field, (4, planes, 128)],
            f, g, *prepared, s_row, s_odd, *windows,
            scratch=[(ny, 136, 128)]
            + [(planes, 16, 128)] * 3
            + [(planes + 2, 16, 128)] * 3
            + [(6, 16, 512), long, slab, slab, field, (4, planes, 128), pltpu.SemaphoreType.DMA((9,))],
            out_specs=[HBM, HBM],
            name="finish",
        )
        return pressure, coarse

    spec = P("gx", "gy", None)
    return jax.shard_map(
        local,
        mesh=mesh,
        in_specs=(spec, spec, spec, spec, spec, P()),
        out_specs=(spec, P("gx", None, None)),
        check_vma=False,
    )
```

```python
import jax
import jax.numpy as jnp
from jax import lax
from jax.experimental import pallas as pl
from jax.experimental.pallas import tpu as pltpu
from jax.sharding import PartitionSpec as P

SWEEPS = 4
OMEGA = 0.8
WALL_PENALTY = 0.4
INFLOW_PENALTY = 0.2
CHEB_LOW = 0.1
CHEB_HIGH = 2.0
F32 = jnp.float32
VMEM = pl.BlockSpec(memory_space=pltpu.VMEM)


HBM = pl.BlockSpec(memory_space=pltpu.HBM)
MORE = 152
FACES = 192


def call(kernel, outs, *args, scratch=(), name=None, in_specs=None, out_specs=None):
    return pl.pallas_call(
        kernel,
        out_shape=[jax.ShapeDtypeStruct(s, F32) for s in outs],
        in_specs=in_specs or [VMEM] * len(args),
        out_specs=out_specs or [VMEM] * len(outs),
        scratch_shapes=[pltpu.VMEM(s, F32) if isinstance(s, tuple) else s for s in scratch],
        compiler_params=pltpu.CompilerParams(vmem_limit_bytes=16 << 20),
        name=name,
    )(*args)


def pairs_core(nx, ny):
    return [(x * ny + y, (x ^ 1) * ny + y) for x in range(nx) for y in range(ny)]


def pairs_chip(nx, ny):
    found = []
    for x in range(nx):
        for y in range(ny):
            if x in (0, nx - 1):
                found.append((x * ny + y, x * ny + (y ^ (ny // 2))))
            else:
                found.append((x * ny + y, (x + 1 if x % 2 else x - 1) * ny + y))
    return found


def pairs_row(nx, ny, step):
    return [(x * ny + y, x * ny + (y ^ step)) for x in range(nx) for y in range(ny)]


def pairs_odd(nx, ny):
    return [
        (x * ny + y, x * ny + (y + 1 if y % 2 else y - 1) % ny) for x in range(nx) for y in range(ny)
    ]


def put(ref, row, slab):
    rows = slab.shape[0]
    for j in range(slab.shape[1] // 128):
        ref[row + rows * j : row + rows * (j + 1), :] = slab[:, 128 * j : 128 * (j + 1)]


def get(ref, row, rows, width):
    return jnp.concatenate(
        [ref[row + rows * j : row + rows * (j + 1), :] for j in range(width // 128)], axis=1
    )


def iota(shape, dim):
    return lax.broadcasted_iota(jnp.int32, shape, dim)


def beside_z(slab):
    depth = slab.shape[1]
    lane = iota(slab.shape, 1)
    above = jnp.where(lane == depth - 1, 0.0, pltpu.roll(slab, depth - 1, 1))
    below = jnp.where(lane == 0, 0.0, pltpu.roll(slab, 1, 1))
    return above + below


def beside(slab, low=None, high=None):
    rows, depth = slab.shape
    tiles, columns = rows // 8, depth // 128
    lane, row = iota((8, 128), 1), iota((8, 128), 0)
    piece = [[slab[8 * t : 8 * t + 8, 128 * j : 128 * j + 128] for j in range(columns)] for t in range(tiles)]
    left = [[pltpu.roll(p, 127, 1) for p in line] for line in piece]
    right = [[pltpu.roll(p, 1, 1) for p in line] for line in piece]
    up = [[pltpu.roll(p, 7, 0) for p in line] for line in piece]
    down = [[pltpu.roll(p, 1, 0) for p in line] for line in piece]

    def outer(line, j):
        return 0.0 if line is None else jnp.broadcast_to(line[:, 128 * j : 128 * j + 128], (8, 128))

    lines = []
    for t in range(tiles):
        parts = []
        for j in range(columns):
            above = jnp.where(lane == 127, left[t][j + 1] if j + 1 < columns else 0.0, left[t][j])
            below = jnp.where(lane == 0, right[t][j - 1] if j > 0 else 0.0, right[t][j])
            after = jnp.where(row == 7, up[t + 1][j] if t + 1 < tiles else outer(high, j), up[t][j])
            before = jnp.where(row == 0, down[t - 1][j] if t > 0 else outer(low, j), down[t][j])
            parts.append((above + below) + (after + before))
        lines.append(jnp.concatenate(parts, axis=1))
    return jnp.concatenate(lines, axis=0)


def outer_rows(low, high):
    row = iota((8, 512), 0)
    first = jnp.where(row == 0, jnp.broadcast_to(low, row.shape), 0.0)
    last = jnp.where(row == 7, jnp.broadcast_to(high, row.shape), 0.0)
    return jnp.concatenate([first, last], axis=0)


def dot(left, right):
    return lax.dot_general(
        left,
        right,
        (((1,), (0,)), ((), ())),
        precision=lax.Precision.HIGHEST,
        preferred_element_type=F32,
    )


def group_lanes(depth):
    return (iota((depth, depth // 4), 0) // 4 == iota((depth, depth // 4), 1)).astype(F32)


def spread_lanes(rows):
    count, lanes = rows.shape
    pad = -count % 8
    if pad:
        rows = jnp.concatenate([rows, jnp.zeros((pad, lanes), F32)], axis=0)
    parts = []
    for j in range(4):
        index = iota(rows.shape, 1) // 4 + (lanes // 4) * j
        parts.append(jnp.take_along_axis(rows, index, axis=1, mode="promise_in_bounds"))
    return jnp.concatenate(parts, axis=1)[:count]


def spread_rows(ref, plane, start):
    row = iota((16, 128), 0) // 4
    value = jnp.zeros((16, 128), F32)
    for q in range(4):
        value = jnp.where(row == q, jnp.broadcast_to(ref[plane, start + q : start + q + 1, :], (16, 128)), value)
    return value


def spread_planes(ref, plane, column):
    row = iota((16, 128), 0) // 4
    value = jnp.zeros((16, 128), F32)
    for q in range(4):
        value = jnp.where(row == q, jnp.broadcast_to(ref[plane + q, column : column + 1, :], (16, 128)), value)
    return value


def solution(mesh):
    nx, ny = mesh.shape["gx"], mesh.shape["gy"]
    assert nx % 2 == 0 and ny % 2 == 0 and ny & (ny - 1) == 0
    axes = ("gx", "gy")

    def where_am_i():
        x, y = lax.axis_index("gx"), lax.axis_index("gy")
        return x, y, x % 2 == 0, y % 2 == 0

    def look_up(table, ids):
        spare = jnp.zeros((1, 128 - table.shape[1]), F32)
        row = jnp.broadcast_to(jnp.concatenate([table, spare], axis=1), (16, 128))
        parts = [
            jnp.take_along_axis(row, ids[:, 128 * j : 128 * (j + 1)], axis=1, mode="promise_in_bounds") for j in range(4)
        ]
        return jnp.concatenate(parts, axis=1)

    def first_of(source, reaction, kinds, ids, mask, table):
        a = reaction + jnp.where(kinds == 1, WALL_PENALTY, jnp.where(kinds == 2, INFLOW_PENALTY, 0.0))
        diagonal = 6.0 + a
        scale = OMEGA / diagonal
        return (source + mask.astype(F32) * look_up(table, ids)) * scale, scale, diagonal, a

    def faces(*refs):
        inputs, thrust, messages, buffers, table, sems, table_sem = (
            refs[:5], refs[5], refs[6:10], refs[10:15], refs[15], refs[16], refs[17]
        )
        core, chip, row, odd = messages
        _, _, x_even, y_even = where_am_i()
        near, far = jnp.where(x_even, 15, 0), jnp.where(x_even, 0, 15)
        moves = [pltpu.make_async_copy(thrust, table, table_sem)]
        for i, (hbm, buffer) in enumerate(zip(inputs, buffers)):
            for j, part in enumerate((hbm.at[:, 0, :], hbm.at[:, 15, :], hbm.at[far], hbm.at[near])):
                moves.append(pltpu.make_async_copy(part, buffer.at[j], sems.at[i, j]))
        for move in moves:
            move.start()
        for move in moves:
            move.wait()
        (low, g_low), (high, g_high), (f_far, _), (f_near, _) = (
            first_of(*(buffer[j] for buffer in buffers), table[...])[:2] for j in range(4)
        )
        put(row, 0, jnp.where(y_even, high, low))
        put(row, 64, jnp.where(y_even, g_high, g_low))
        put(odd, 0, jnp.where(y_even, low, high))
        put(odd, 64, jnp.where(y_even, g_low, g_high))
        put(chip, 0, f_far)
        put(core, 0, f_near)

    def set_up(source, reaction, kind, disk_id, disk_mask, table, f, g, d, absorb, inner, V):
        for k in range(4):
            total = jnp.zeros((16, 512), F32)
            for x in range(4 * k, 4 * k + 4):
                f[x], g[x], d[x], a = first_of(source[x], reaction[x], kind[x], disk_id[x], disk_mask[x], table[...])
                total = total + a
            V[16 * k : 16 * k + 16, :] = total
        out, src = iota((16, 64), 0), iota((16, 64), 1)
        pick = ((src // 16 == out % 4) & ((src % 16) // 4 == out // 4)).astype(F32)
        absorb[...] = dot(dot(pick, V[...]), group_lanes(512))
        for x in range(16):
            total = beside(f[x])
            if x > 0:
                total = total + f[x - 1]
            if x < 15:
                total = total + f[x + 1]
            inner[x] = 1.2 * f[x] + g[x] * total

    def halo_x(core, chip, row, x, x_even, chip_row=None):
        a, b = get(core, row, 16, 512), get(chip, row if chip_row is None else chip_row, 16, 512)
        left = jnp.where(x > 0, jnp.where(x_even, b, a), 0.0)
        right = jnp.where(x < nx - 1, jnp.where(x_even, a, b), 0.0)
        return left, right

    def halo_y(row, odd, at, y, y_even):
        a, b = get(row, at, 16, 512), get(odd, at, 16, 512)
        low = jnp.where(y > 0, jnp.where(y_even, b, a), 0.0)
        high = jnp.where(y < ny - 1, jnp.where(y_even, a, b), 0.0)
        return low, high

    def smooth(inner, g, absorb, core, chip, row, odd, s, to_core, sums, y_faces, y_more, lo, hi, y0, y1, y14, y15):
        x_at, y_at, x_even, y_even = where_am_i()
        left, right = halo_x(core, chip, 0, x_at, x_even)
        lo[...], hi[...] = halo_y(row, odd, 0, y_at, y_even)
        for x in range(16):
            total = outer_rows(lo[x : x + 1, :], hi[x : x + 1, :])
            if x == 0:
                total = total + left
            if x == 15:
                total = total + right
            value = inner[x] + g[x] * total
            s[x] = value
            y0[x : x + 1, :] = value[0:1, :]
            y1[x : x + 1, :] = value[1:2, :]
            y14[x : x + 1, :] = value[14:15, :]
            y15[x : x + 1, :] = value[15:16, :]
        y_faces[0:16, :] = y0[...]
        y_faces[16:32, :] = y15[...]
        out, src = iota((16, 64), 0), iota((16, 64), 1)
        pick = ((out // 4 == src // 16) & (out % 4 == (src % 16) // 4)).astype(F32)
        sides = jnp.concatenate([s[0], s[15], y0[...], y15[...]], axis=0)
        sums[...] = dot(dot(pick, sides), group_lanes(512))
        put(to_core, 0, s[jnp.where(x_even, 15, 0)])
        put(to_core, 64, s[jnp.where(x_even, 14, 1)])
        put(to_core, 128, g[jnp.where(x_even, 15, 0)])
        to_core[192:196, :] = jnp.where(x_even, sums[4:8, :], sums[0:4, :])
        to_core[196:200, :] = jnp.zeros((4, 128), F32)
        to_core[200:208, :] = sums[8:16, :]
        to_core[208:224, :] = absorb[...]
        for at, ref in enumerate((y1, y14)):
            y_more[16 * at : 16 * at + 16, :] = ref[...]

    def restrict(f, d, absorb, s, sums, block, V):
        for k in range(4):
            total = jnp.zeros((16, 512), F32)
            for x in range(4 * k, 4 * k + 4):
                here = s[x]
                total = total + d[x] * (1.25 * f[x] - here)
                total = total + beside(here)
                if x > 0:
                    total = total + s[x - 1]
                if x < 15:
                    total = total + s[x + 1]
            V[16 * k : 16 * k + 16, :] = total
        out, src = iota((16, 64), 0), iota((16, 64), 1)
        pick = ((src // 16 == out % 4) & ((src % 16) // 4 == out // 4)).astype(F32)
        found = dot(dot(pick, V[...]), group_lanes(512))
        for cy in range(4):
            block[8 * cy : 8 * cy + 4, :] = found[4 * cy : 4 * cy + 4, :]
            block[8 * cy + 4 : 8 * cy + 8, :] = absorb[4 * cy : 4 * cy + 4, :]
        block[32:40, :] = sums[8:16, :]

    def to_chip_kernel(block, sums, absorb, core, s, g, y_faces, y_more, mine, to_chip, to_row, to_odd):
        _, _, x_even, y_even = where_am_i()
        mine[...] = block[...]
        face = core[192:200, :]
        for cy in range(4):
            line = face[cy : cy + 1, :]
            a, b = 8 * cy, 8 * cy + 3
            mine[a : a + 1, :] = block[a : a + 1, :] + jnp.where(x_even, 0.0, line)
            mine[b : b + 1, :] = block[b : b + 1, :] + jnp.where(x_even, line, 0.0)
        put(to_chip, 0, s[jnp.where(x_even, 0, 15)])
        to_chip[64:104, :] = mine[...]
        to_chip[104:108, :] = jnp.where(x_even, sums[0:4, :], sums[4:8, :])
        to_chip[108:112, :] = jnp.zeros((4, 128), F32)
        for at, ref in enumerate((y_faces, y_more)):
            a, b = ref[0:16, :], ref[16:32, :]
            put(to_row, 64 * at, jnp.where(y_even, b, a))
            put(to_odd, 64 * at, jnp.where(y_even, a, b))
        first_line, last_line = (
            jnp.concatenate([core[16 * j + line : 16 * j + line + 1, :] for j in range(4)], axis=0) for line in (0, 15)
        )
        for ref, corner in (
            (to_row, jnp.where(y_even, last_line, first_line)),
            (to_odd, jnp.where(y_even, first_line, last_line)),
        ):
            ref[128:144, :] = absorb[...]
            ref[144:160, :] = core[208:224, :]
            ref[160:168, :] = sums[8:16, :]
            ref[168:176, :] = core[200:208, :]
            ref[176:180, :] = corner
            ref[180:FACES, :] = jnp.zeros((FACES - 180, 128), F32)

    def from_chip_kernel(mine, sums, chip, s, g, full, beyond, more):
        x_at, _, x_even, _ = where_am_i()
        has = jnp.where(x_even, x_at > 0, x_at < nx - 1)
        full[...] = mine[...]
        beyond[...] = chip[64:104, :]
        mine_face = jnp.where(x_even, sums[0:4, :], sums[4:8, :])
        face = chip[104:112, :]
        for cy in range(4):
            line = jnp.where(has, face[cy : cy + 1, :], 0.0)
            own = mine_face[cy : cy + 1, :]
            a, b = 8 * cy, 8 * cy + 3
            full[a : a + 1, :] = mine[a : a + 1, :] + jnp.where(x_even, line, 0.0)
            full[b : b + 1, :] = mine[b : b + 1, :] + jnp.where(x_even, 0.0, line)
            beyond[a : a + 1, :] = chip[64 + a : 65 + a, :] + jnp.where(x_even, 0.0, own)
            beyond[b : b + 1, :] = chip[64 + b : 65 + b, :] + jnp.where(x_even, own, 0.0)
        put(more, 0, s[jnp.where(x_even, 1, 14)])
        put(more, 64, g[jnp.where(x_even, 0, 15)])
        more[128:MORE, :] = jnp.zeros((MORE - 128, 128), F32)

    def window_kernel(full, beyond, core, chip, s_core, window, short):
        x_at, _, x_even, _ = where_am_i()
        mid = full[...]
        a, b = core[...], beyond[...]
        left, right = jnp.where(x_even, b, a), jnp.where(x_even, a, b)
        for at, block in enumerate((left, mid, right)):
            for cy in range(4):
                window[24 * cy + 4 * at : 24 * cy + 4 * at + 4, :] = block[8 * cy : 8 * cy + 4, :]
                window[24 * cy + 12 + 4 * at : 24 * cy + 16 + 4 * at, :] = block[8 * cy + 4 : 8 * cy + 8, :]
            window[96 + 4 * at : 100 + 4 * at, :] = block[32:36, :]
            window[108 + 4 * at : 112 + 4 * at, :] = block[36:40, :]
        for at, line in enumerate((0, 15)):
            near = jnp.concatenate([s_core[16 * j + line : 16 * j + line + 1, :] for j in range(4)], axis=0)
            far = jnp.concatenate([chip[16 * j + line : 16 * j + line + 1, :] for j in range(4)], axis=0)
            window[120 + 4 * at : 124 + 4 * at, :] = jnp.where(x_at > 0, jnp.where(x_even, far, near), 0.0)
            window[128 + 4 * at : 132 + 4 * at, :] = jnp.where(x_at < nx - 1, jnp.where(x_even, near, far), 0.0)
            short[72 + 4 * at : 76 + 4 * at, :] = far
        for cy in range(4):
            for at, block in enumerate((left, mid, right)):
                short[12 * cy + 4 * at : 12 * cy + 4 * at + 4, :] = block[8 * cy : 8 * cy + 4, :]
            short[48 + 4 * cy : 52 + 4 * cy, :] = beyond[8 * cy + 4 : 8 * cy + 8, :]
        short[64:72, :] = beyond[32:40, :]

    planes = 4 * ny
    short_steps = (1, 3) if ny == 4 else (1,)

    def prepare(f, g, s, a_core, a_chip, a_row, a_odd, s_core, s_chip, s_more, s_row, s_odd, u, u_low, u_high, g_x, g_y, edge):
        x_at, y_at, x_even, y_even = where_am_i()
        s_left, s_right = halo_x(s_core, s_chip, 0, x_at, x_even)
        s_left2, s_right2 = halo_x(s_core, s_more, 64, x_at, x_even, 0)
        f_left, f_right = halo_x(a_core, a_chip, 0, x_at, x_even)
        g_x[0], g_x[1] = halo_x(s_core, s_more, 128, x_at, x_even, 64)
        y1 = halo_y(s_row, s_odd, 0, y_at, y_even)
        y2 = halo_y(s_row, s_odd, 64, y_at, y_even)
        f_y = halo_y(a_row, a_odd, 0, y_at, y_even)
        g_y[0], g_y[1] = halo_y(a_row, a_odd, 64, y_at, y_even)
        u[0] = 0.2 * s_left + f_left + g_x[0] * (s_left2 + s[0] + beside(s_left))
        u[17] = 0.2 * s_right + f_right + g_x[1] * (s_right2 + s[15] + beside(s_right))
        for x in range(16):
            here = s[x]
            total = (s[x - 1] if x > 0 else s_left) + (s[x + 1] if x < 15 else s_right)
            total = total + beside(here, y1[0][x : x + 1, :], y1[1][x : x + 1, :])
            u[x + 1] = 0.2 * here + f[x] + g[x] * total
            edge[0, x : x + 1, :] = here[0:1, :]
            edge[1, x : x + 1, :] = here[15:16, :]
        for at, out in enumerate((u_low, u_high)):
            out[...] = 0.2 * y1[at] + f_y[at] + g_y[at] * (y2[at] + edge[at] + beside(y1[at]))

    def finish(*refs):
        f, g, u, u_low, u_high, g_x, g_y, s_row, s_odd = refs[:9]
        windows = refs[9 : 9 + ny]
        pressure, coarse = refs[9 + ny : 11 + ny]
        every, res, diag, inv, one, two, sol, C, U, ul, uh, result, slab_out, sems = refs[11 + ny :]
        x_at, y_at, x_even, y_even = where_am_i()
        for step, window in enumerate(windows):
            there = jnp.bitwise_xor(y_at, step)
            if step not in short_steps:
                every[there] = window[...]
                continue
            faces_of = s_row if step == 1 else s_odd

            def three(at, own, core, chip):
                every[there, at : at + 4, :] = jnp.where(x_even, chip, core)
                if own is not None:
                    every[there, at + 4 : at + 8, :] = own
                every[there, at + 8 : at + 12, :] = jnp.where(x_even, core, chip)

            for cy in range(4):
                at = 4 * cy
                every[there, 24 * cy : 24 * cy + 12, :] = window[12 * cy : 12 * cy + 12, :]
                three(
                    24 * cy + 12, faces_of[128 + at : 132 + at, :], faces_of[144 + at : 148 + at, :],
                    window[48 + at : 52 + at, :],
                )
            for at in (0, 4):
                three(
                    96 + 3 * at, faces_of[160 + at : 164 + at, :], faces_of[168 + at : 172 + at, :],
                    window[64 + at : 68 + at, :],
                )
                three(120 + at, None, faces_of[176:180, :], window[72 + at : 76 + at, :])

        row = iota((16, 128), 0)
        valid = ((row >= 4) | (x_at > 0)) & ((row < 8) | (x_at < nx - 1)) & (row < 12)
        blank = jnp.zeros((4, 128), F32)

        def twelve(value):
            return jnp.concatenate([value, blank], axis=0)

        centre = (CHEB_HIGH + CHEB_LOW) / 2.0
        half_range = (CHEB_HIGH - CHEB_LOW) / 2.0
        aspect = centre / half_range
        factor = 1.0 / aspect
        empty = jnp.zeros((16, 128), F32)
        for ref in (one, two, sol):
            ref[0] = empty
            ref[planes + 1] = empty
        for at in range(ny):
            for cy in range(4):
                plane = 4 * at + cy
                value = every[at, 24 * cy : 24 * cy + 12, :]
                if cy == 0 and at > 0:
                    value = value + every[at - 1, 108:120, :]
                if cy == 3 and at < ny - 1:
                    value = value + every[at + 1, 96:108, :]
                value = jnp.where(valid, twelve(value), 0.0)
                centre_value = 6.0 + twelve(every[at, 24 * cy + 12 : 24 * cy + 24, :]) / 16.0
                inverse = jnp.where(valid, 1.0 / (16.0 * centre_value), 0.0)
                res[plane] = value
                diag[plane] = centre_value
                inv[plane] = inverse
                direction = inverse * value / centre
                one[plane + 1] = direction
                sol[plane + 1] = direction
        now, later = one, two
        for number in range(1, SWEEPS):
            factor_next = 1.0 / (2.0 * aspect - factor)
            keep, gain = factor_next * factor, 2.0 * factor_next / half_range

            lane = iota((16, 128), 1)
            for plane in range(planes):
                here = now[plane + 1]
                total = now[plane] + now[plane + 2]
                total = total + pltpu.roll(here, 15, 0) + pltpu.roll(here, 1, 0)
                total = total + jnp.where(lane == 127, 0.0, pltpu.roll(here, 127, 1))
                total = total + jnp.where(lane == 0, 0.0, pltpu.roll(here, 1, 1))
                residual = res[plane] - 16.0 * (diag[plane] * here - total)
                res[plane] = residual
                direction = keep * here + gain * inv[plane] * residual
                later[plane + 1] = direction
                sol[plane + 1] = sol[plane + 1] + direction
            now, later = later, now
            factor = factor_next
        for plane in range(planes):
            for cx in range(4):
                slab_out[cx, plane : plane + 1, :] = sol[plane + 1, 4 + cx : 5 + cx, :]
        moves = [pltpu.make_async_copy(slab_out, coarse, sems.at[8])]
        moves[0].start()

        first_plane = 4 * y_at + 1
        below, above = first_plane - 1, first_plane + 4
        for at in range(6):
            C[at] = spread_lanes(spread_planes(sol, first_plane, 3 + at))
        outside = [[spread_lanes(sol[plane, 3 + at : 4 + at, :]) for at in range(6)] for plane in (below, above)]
        before, after = jnp.maximum(y_at - 1, 0), jnp.minimum(y_at + 1, ny - 1)
        corners = []
        for who, inside, line in ((before, y_at > 0, 1), (after, y_at < ny - 1, 0)):
            for base, there in ((0, x_at > 0), (2, x_at < nx - 1)):
                corner = jnp.concatenate(
                    [every[who, pl.ds(120 + 4 * (base + line) + j, 1), :] for j in range(4)], axis=1
                )
                corners.append(jnp.where(inside & there, corner, 0.0))
        edge_row = iota((16, 512), 0)

        def ends(first, last):
            first, last = (jnp.broadcast_to(line, (16, 512)) for line in (first, last))
            return jnp.where(edge_row == 0, first, jnp.where(edge_row == 15, last, 0.0))

        for at in range(6):
            here = C[at]
            around = beside(here, outside[0][at], outside[1][at])
            fifth_of = 0.2 * here
            if at == 0:
                U[0] = u[0] + fifth_of + g_x[0] * (around + here + C[1] + ends(corners[0], corners[2]))
            elif at == 5:
                U[17] = u[17] + fifth_of + g_x[1] * (around + here + C[4] + ends(corners[1], corners[3]))
            else:
                inner = around + 2.0 * here
                sides = [around + here + C[at - 1], inner, inner, around + here + C[at + 1]]
                for q in range(4):
                    x = 4 * (at - 1) + q
                    U[x + 1] = u[x + 1] + fifth_of + g[x] * sides[q]
        for at, (part, out, plane, inside) in enumerate(
            ((u_low, ul, below, first_plane), (u_high, uh, above, first_plane + 3))
        ):
            beyond = spread_lanes(spread_rows(sol, plane, 4))
            edge = spread_lanes(spread_rows(sol, inside, 4))
            around = beside(beyond, outside[at][0], outside[at][5])
            total = beyond + edge + around + ends(corners[2 * at], corners[2 * at + 1])
            out[...] = part[...] + 0.2 * beyond + g_y[at] * total

        for x in range(16):
            here = U[x + 1]
            total = U[x] + U[x + 2] + beside(here, ul[x : x + 1, :], uh[x : x + 1, :])
            result[x] = 0.2 * here + f[x] + g[x] * total
            if x % 2 == 1:
                part = pl.ds(x - 1, 2)
                moves.append(pltpu.make_async_copy(result.at[part], pressure.at[part], sems.at[x // 2]))
                moves[-1].start()
        for move in moves:
            move.wait()

    slab, field, long = (16, 512), (16, 16, 512), (18, 16, 512)
    core_pairs, chip_pairs = pairs_core(nx, ny), pairs_chip(nx, ny)
    row_pairs = [pairs_row(nx, ny, step) for step in range(1, ny)]
    odd_pairs = pairs_odd(nx, ny)

    def swap(array, pairs):
        return lax.ppermute(array, axes, pairs)

    def local(source, reaction, boundary_kind, disk_id, disk_mask, thrust):
        inputs = (source, reaction, boundary_kind, disk_id, disk_mask, thrust.reshape(1, -1))
        some = (4, 16, 512)
        core, chip, row, odd = call(
            faces,
            [(64, 128), (64, 128), (128, 128), (128, 128)],
            *(pltpu.with_memory_space_constraint(array, pltpu.HBM) for array in inputs),
            in_specs=[HBM] * 6,
            scratch=[some, some]
            + [pltpu.VMEM(some, jnp.int32)] * 3
            + [(1, thrust.shape[0]), pltpu.SemaphoreType.DMA((5, 4)), pltpu.SemaphoreType.DMA(())],
            name="faces",
        )
        a_core, a_chip = swap(core, core_pairs), swap(chip, chip_pairs)
        a_odd, a_row = swap(odd, odd_pairs), swap(row, row_pairs[0])
        f, g, d, absorb, inner = call(
            set_up, [field, field, field, (16, 128), field], *inputs, scratch=[(64, 512)], name="set_up"
        )
        a_odd, a_row, a_chip, a_core, f, g, d, absorb, inner = lax.optimization_barrier(
            (a_odd, a_row, a_chip, a_core, f, g, d, absorb, inner)
        )
        s, to_core, sums, y_faces, y_more = call(
            smooth,
            [field, (224, 128), (16, 128), (32, 512), (32, 512)],
            inner, g, absorb, a_core, a_chip, a_row, a_odd,
            scratch=[slab] * 6,
            name="smooth",
        )
        s_core = swap(to_core, core_pairs)
        (block,) = call(restrict, [(40, 128)], f, d, absorb, s, sums, scratch=[(64, 512)], name="restrict")
        mine, to_chip, to_row, to_odd = call(
            to_chip_kernel,
            [(40, 128), (112, 128), (FACES, 128), (FACES, 128)],
            block, sums, absorb, s_core, s, g, y_faces, y_more,
            name="to_chip",
        )
        s_chip = swap(to_chip, chip_pairs)
        s_row, s_odd = swap(to_row, row_pairs[0]), swap(to_odd, odd_pairs)
        full, beyond, more = call(
            from_chip_kernel, [(40, 128), (40, 128), (MORE, 128)], mine, sums, s_chip, s, g, name="from_chip"
        )
        c_core, s_more = swap(full, core_pairs), swap(more, chip_pairs)
        window, short = call(
            window_kernel, [(136, 128), (80, 128)], full, beyond, c_core, s_chip, s_core, name="window"
        )
        windows = [window] + [
            swap(short if step in short_steps else window, row_pairs[step - 1]) for step in range(1, ny)
        ]
        prepared = call(
            prepare,
            [long, slab, slab, (2, 16, 512), (2, 16, 512)],
            f, g, s, a_core, a_chip, a_row, a_odd, s_core, s_chip, s_more, s_row, s_odd,
            scratch=[(2, 16, 512)],
            name="prepare",
        )
        pressure, coarse = call(
            finish,
            [field, (4, planes, 128)],
            f, g, *prepared, s_row, s_odd, *windows,
            scratch=[(ny, 136, 128)]
            + [(planes, 16, 128)] * 3
            + [(planes + 2, 16, 128)] * 3
            + [(6, 16, 512), long, slab, slab, field, (4, planes, 128), pltpu.SemaphoreType.DMA((9,))],
            out_specs=[HBM, HBM],
            name="finish",
        )
        return pressure, coarse

    spec = P("gx", "gy", None)
    return jax.shard_map(
        local,
        mesh=mesh,
        in_specs=(spec, spec, spec, spec, spec, P()),
        out_specs=(spec, P("gx", None, None)),
        check_vma=False,
    )
```

```python
import jax
import jax.numpy as jnp
from jax import lax
from jax.experimental import pallas as pl
from jax.experimental.pallas import tpu as pltpu
from jax.sharding import PartitionSpec as P

SWEEPS = 4
OMEGA = 0.8
WALL_PENALTY = 0.4
INFLOW_PENALTY = 0.2
CHEB_LOW = 0.1
CHEB_HIGH = 2.0
F32 = jnp.float32
VMEM = pl.BlockSpec(memory_space=pltpu.VMEM)


HBM = pl.BlockSpec(memory_space=pltpu.HBM)
MORE = 152
FACES = 192


def call(kernel, outs, *args, scratch=(), name=None, in_specs=None, out_specs=None):
    return pl.pallas_call(
        kernel,
        out_shape=[jax.ShapeDtypeStruct(s, F32) for s in outs],
        in_specs=in_specs or [VMEM] * len(args),
        out_specs=out_specs or [VMEM] * len(outs),
        scratch_shapes=[pltpu.VMEM(s, F32) if isinstance(s, tuple) else s for s in scratch],
        compiler_params=pltpu.CompilerParams(vmem_limit_bytes=16 << 20),
        name=name,
    )(*args)


def pairs_core(nx, ny):
    return [(x * ny + y, (x ^ 1) * ny + y) for x in range(nx) for y in range(ny)]


def pairs_chip(nx, ny):
    found = []
    for x in range(nx):
        for y in range(ny):
            if x in (0, nx - 1):
                found.append((x * ny + y, x * ny + (y ^ (ny // 2))))
            else:
                found.append((x * ny + y, (x + 1 if x % 2 else x - 1) * ny + y))
    return found


def pairs_row(nx, ny, step):
    return [(x * ny + y, x * ny + (y ^ step)) for x in range(nx) for y in range(ny)]


def pairs_odd(nx, ny):
    return [
        (x * ny + y, x * ny + (y + 1 if y % 2 else y - 1) % ny) for x in range(nx) for y in range(ny)
    ]


def put(ref, row, slab):
    rows = slab.shape[0]
    for j in range(slab.shape[1] // 128):
        ref[row + rows * j : row + rows * (j + 1), :] = slab[:, 128 * j : 128 * (j + 1)]


def get(ref, row, rows, width):
    return jnp.concatenate(
        [ref[row + rows * j : row + rows * (j + 1), :] for j in range(width // 128)], axis=1
    )


def iota(shape, dim):
    return lax.broadcasted_iota(jnp.int32, shape, dim)


def beside_z(slab):
    depth = slab.shape[1]
    lane = iota(slab.shape, 1)
    above = jnp.where(lane == depth - 1, 0.0, pltpu.roll(slab, depth - 1, 1))
    below = jnp.where(lane == 0, 0.0, pltpu.roll(slab, 1, 1))
    return above + below


def beside(slab, low=None, high=None):
    rows, depth = slab.shape
    tiles, columns = rows // 8, depth // 128
    lane, row = iota((8, 128), 1), iota((8, 128), 0)
    piece = [[slab[8 * t : 8 * t + 8, 128 * j : 128 * j + 128] for j in range(columns)] for t in range(tiles)]
    left = [[pltpu.roll(p, 127, 1) for p in line] for line in piece]
    right = [[pltpu.roll(p, 1, 1) for p in line] for line in piece]
    up = [[pltpu.roll(p, 7, 0) for p in line] for line in piece]
    down = [[pltpu.roll(p, 1, 0) for p in line] for line in piece]

    def outer(line, j):
        return 0.0 if line is None else jnp.broadcast_to(line[:, 128 * j : 128 * j + 128], (8, 128))

    lines = []
    for t in range(tiles):
        parts = []
        for j in range(columns):
            above = jnp.where(lane == 127, left[t][j + 1] if j + 1 < columns else 0.0, left[t][j])
            below = jnp.where(lane == 0, right[t][j - 1] if j > 0 else 0.0, right[t][j])
            after = jnp.where(row == 7, up[t + 1][j] if t + 1 < tiles else outer(high, j), up[t][j])
            before = jnp.where(row == 0, down[t - 1][j] if t > 0 else outer(low, j), down[t][j])
            parts.append((above + below) + (after + before))
        lines.append(jnp.concatenate(parts, axis=1))
    return jnp.concatenate(lines, axis=0)


def outer_rows(low, high):
    row = iota((8, 512), 0)
    first = jnp.where(row == 0, jnp.broadcast_to(low, row.shape), 0.0)
    last = jnp.where(row == 7, jnp.broadcast_to(high, row.shape), 0.0)
    return jnp.concatenate([first, last], axis=0)


def dot(left, right):
    return lax.dot_general(
        left,
        right,
        (((1,), (0,)), ((), ())),
        precision=lax.Precision.HIGHEST,
        preferred_element_type=F32,
    )


def group_lanes(depth):
    return (iota((depth, depth // 4), 0) // 4 == iota((depth, depth // 4), 1)).astype(F32)


def spread_lanes(rows):
    count, lanes = rows.shape
    pad = -count % 8
    if pad:
        rows = jnp.concatenate([rows, jnp.zeros((pad, lanes), F32)], axis=0)
    parts = []
    for j in range(4):
        index = iota(rows.shape, 1) // 4 + (lanes // 4) * j
        parts.append(jnp.take_along_axis(rows, index, axis=1, mode="promise_in_bounds"))
    return jnp.concatenate(parts, axis=1)[:count]


def spread_rows(ref, plane, start):
    row = iota((16, 128), 0) // 4
    value = jnp.zeros((16, 128), F32)
    for q in range(4):
        value = jnp.where(row == q, jnp.broadcast_to(ref[plane, start + q : start + q + 1, :], (16, 128)), value)
    return value


def spread_planes(ref, plane, column):
    row = iota((16, 128), 0) // 4
    value = jnp.zeros((16, 128), F32)
    for q in range(4):
        value = jnp.where(row == q, jnp.broadcast_to(ref[plane + q, column : column + 1, :], (16, 128)), value)
    return value


def solution(mesh):
    nx, ny = mesh.shape["gx"], mesh.shape["gy"]
    assert nx % 2 == 0 and ny % 2 == 0 and ny & (ny - 1) == 0
    axes = ("gx", "gy")

    def where_am_i():
        x, y = lax.axis_index("gx"), lax.axis_index("gy")
        return x, y, x % 2 == 0, y % 2 == 0

    def look_up(table, ids):
        spare = jnp.zeros((1, 128 - table.shape[1]), F32)
        row = jnp.broadcast_to(jnp.concatenate([table, spare], axis=1), (16, 128))
        parts = [
            jnp.take_along_axis(row, ids[:, 128 * j : 128 * (j + 1)], axis=1, mode="promise_in_bounds") for j in range(4)
        ]
        return jnp.concatenate(parts, axis=1)

    def first_of(source, reaction, kinds, ids, mask, table):
        a = reaction + jnp.where(kinds == 1, WALL_PENALTY, jnp.where(kinds == 2, INFLOW_PENALTY, 0.0))
        diagonal = 6.0 + a
        scale = OMEGA / diagonal
        return (source + mask.astype(F32) * look_up(table, ids)) * scale, scale, diagonal, a

    def faces(*refs):
        inputs, thrust, messages, buffers, table, sems, table_sem = (
            refs[:5], refs[5], refs[6:10], refs[10:15], refs[15], refs[16], refs[17]
        )
        core, chip, row, odd = messages
        _, _, x_even, y_even = where_am_i()
        near, far = jnp.where(x_even, 15, 0), jnp.where(x_even, 0, 15)
        moves = [pltpu.make_async_copy(thrust, table, table_sem)]
        for i, (hbm, buffer) in enumerate(zip(inputs, buffers)):
            for j, part in enumerate((hbm.at[:, 0, :], hbm.at[:, 15, :], hbm.at[far], hbm.at[near])):
                moves.append(pltpu.make_async_copy(part, buffer.at[j], sems.at[i, j]))
        for move in moves:
            move.start()
        for move in moves:
            move.wait()
        (low, g_low), (high, g_high), (f_far, _), (f_near, _) = (
            first_of(*(buffer[j] for buffer in buffers), table[...])[:2] for j in range(4)
        )
        put(row, 0, jnp.where(y_even, high, low))
        put(row, 64, jnp.where(y_even, g_high, g_low))
        put(odd, 0, jnp.where(y_even, low, high))
        put(odd, 64, jnp.where(y_even, g_low, g_high))
        put(chip, 0, f_far)
        put(core, 0, f_near)

    def set_up(source, reaction, kind, disk_id, disk_mask, table, f, g, d, absorb, inner, rows, V):
        for k in range(4):
            total = jnp.zeros((16, 512), F32)
            for x in range(4 * k, 4 * k + 4):
                f[x], g[x], d[x], a = first_of(source[x], reaction[x], kind[x], disk_id[x], disk_mask[x], table[...])
                total = total + a
            V[16 * k : 16 * k + 16, :] = total
        out, src = iota((16, 64), 0), iota((16, 64), 1)
        pick = ((src // 16 == out % 4) & ((src % 16) // 4 == out // 4)).astype(F32)
        absorb[...] = dot(dot(pick, V[...]), group_lanes(512))
        for x in range(16):
            total = beside(f[x])
            if x > 0:
                total = total + f[x - 1]
            if x < 15:
                total = total + f[x + 1]
            value = 1.2 * f[x] + g[x] * total
            inner[x] = value
            for at, part in enumerate((value[0:1, :], value[15:16, :], g[x, 0:1, :], g[x, 15:16, :])):
                rows[at, x : x + 1, :] = part

    def halo_x(core, chip, row, x, x_even, chip_row=None):
        a, b = get(core, row, 16, 512), get(chip, row if chip_row is None else chip_row, 16, 512)
        left = jnp.where(x > 0, jnp.where(x_even, b, a), 0.0)
        right = jnp.where(x < nx - 1, jnp.where(x_even, a, b), 0.0)
        return left, right

    def halo_y(row, odd, at, y, y_even):
        a, b = get(row, at, 16, 512), get(odd, at, 16, 512)
        low = jnp.where(y > 0, jnp.where(y_even, b, a), 0.0)
        high = jnp.where(y < ny - 1, jnp.where(y_even, a, b), 0.0)
        return low, high

    def early(inner, g, rows, absorb, core, chip, row, odd, to_core, sums, y_faces, lo, hi):
        x_at, y_at, x_even, y_even = where_am_i()
        left, right = halo_x(core, chip, 0, x_at, x_even)
        lo[...], hi[...] = halo_y(row, odd, 0, y_at, y_even)

        def second_at(x, outer=0.0):
            return inner[x] + g[x] * (outer_rows(lo[pl.ds(x, 1), :], hi[pl.ds(x, 1), :]) + outer)

        s_first, s_last = second_at(0, left), second_at(15, right)
        row_of = iota((16, 512), 0)
        for at, (outer, line) in enumerate(((lo, slice(0, 1)), (hi, slice(15, 16)))):
            first, last = (jnp.broadcast_to(side[line, :], (16, 512)) for side in (left, right))
            more = jnp.where(row_of == 0, first, jnp.where(row_of == 15, last, 0.0))
            y_faces[16 * at : 16 * at + 16, :] = rows[at] + rows[2 + at] * (outer[...] + more)
        out, src = iota((16, 64), 0), iota((16, 64), 1)
        pick = ((out // 4 == src // 16) & (out % 4 == (src % 16) // 4)).astype(F32)
        sides = jnp.concatenate([s_first, s_last, y_faces[...]], axis=0)
        sums[...] = dot(dot(pick, sides), group_lanes(512))
        put(to_core, 0, jnp.where(x_even, s_last, s_first))
        put(to_core, 64, second_at(jnp.where(x_even, 14, 1)))
        put(to_core, 128, g[jnp.where(x_even, 15, 0)])
        to_core[192:196, :] = jnp.where(x_even, sums[4:8, :], sums[0:4, :])
        to_core[196:200, :] = jnp.zeros((4, 128), F32)
        to_core[200:208, :] = sums[8:16, :]
        to_core[208:224, :] = absorb[...]

    def restrict(f, g, d, absorb, inner, sums, core, chip, row, odd, s, block, y_more, lo, hi, V):
        x_at, y_at, x_even, y_even = where_am_i()
        left, right = halo_x(core, chip, 0, x_at, x_even)
        lo[...], hi[...] = halo_y(row, odd, 0, y_at, y_even)
        for x in range(16):
            total = outer_rows(lo[x : x + 1, :], hi[x : x + 1, :])
            if x == 0:
                total = total + left
            if x == 15:
                total = total + right
            value = inner[x] + g[x] * total
            s[x] = value
            y_more[x : x + 1, :] = value[1:2, :]
            y_more[16 + x : 17 + x, :] = value[14:15, :]
        for k in range(4):
            total = jnp.zeros((16, 512), F32)
            for x in range(4 * k, 4 * k + 4):
                here = s[x]
                total = total + d[x] * (1.25 * f[x] - here)
                total = total + beside(here)
                if x > 0:
                    total = total + s[x - 1]
                if x < 15:
                    total = total + s[x + 1]
            V[16 * k : 16 * k + 16, :] = total
        out, src = iota((16, 64), 0), iota((16, 64), 1)
        pick = ((src // 16 == out % 4) & ((src % 16) // 4 == out // 4)).astype(F32)
        found = dot(dot(pick, V[...]), group_lanes(512))
        for cy in range(4):
            block[8 * cy : 8 * cy + 4, :] = found[4 * cy : 4 * cy + 4, :]
            block[8 * cy + 4 : 8 * cy + 8, :] = absorb[4 * cy : 4 * cy + 4, :]
        block[32:40, :] = sums[8:16, :]

    def to_chip_kernel(block, sums, absorb, core, s, g, y_faces, y_more, mine, to_chip, to_row, to_odd):
        _, _, x_even, y_even = where_am_i()
        mine[...] = block[...]
        face = core[192:200, :]
        for cy in range(4):
            line = face[cy : cy + 1, :]
            a, b = 8 * cy, 8 * cy + 3
            mine[a : a + 1, :] = block[a : a + 1, :] + jnp.where(x_even, 0.0, line)
            mine[b : b + 1, :] = block[b : b + 1, :] + jnp.where(x_even, line, 0.0)
        put(to_chip, 0, s[jnp.where(x_even, 0, 15)])
        to_chip[64:104, :] = mine[...]
        to_chip[104:108, :] = jnp.where(x_even, sums[0:4, :], sums[4:8, :])
        to_chip[108:112, :] = jnp.zeros((4, 128), F32)
        for at, ref in enumerate((y_faces, y_more)):
            a, b = ref[0:16, :], ref[16:32, :]
            put(to_row, 64 * at, jnp.where(y_even, b, a))
            put(to_odd, 64 * at, jnp.where(y_even, a, b))
        first_line, last_line = (
            jnp.concatenate([core[16 * j + line : 16 * j + line + 1, :] for j in range(4)], axis=0) for line in (0, 15)
        )
        for ref, corner in (
            (to_row, jnp.where(y_even, last_line, first_line)),
            (to_odd, jnp.where(y_even, first_line, last_line)),
        ):
            ref[128:144, :] = absorb[...]
            ref[144:160, :] = core[208:224, :]
            ref[160:168, :] = sums[8:16, :]
            ref[168:176, :] = core[200:208, :]
            ref[176:180, :] = corner
            ref[180:FACES, :] = jnp.zeros((FACES - 180, 128), F32)

    def from_chip_kernel(mine, sums, chip, s, g, full, beyond, more):
        x_at, _, x_even, _ = where_am_i()
        has = jnp.where(x_even, x_at > 0, x_at < nx - 1)
        full[...] = mine[...]
        beyond[...] = chip[64:104, :]
        mine_face = jnp.where(x_even, sums[0:4, :], sums[4:8, :])
        face = chip[104:112, :]
        for cy in range(4):
            line = jnp.where(has, face[cy : cy + 1, :], 0.0)
            own = mine_face[cy : cy + 1, :]
            a, b = 8 * cy, 8 * cy + 3
            full[a : a + 1, :] = mine[a : a + 1, :] + jnp.where(x_even, line, 0.0)
            full[b : b + 1, :] = mine[b : b + 1, :] + jnp.where(x_even, 0.0, line)
            beyond[a : a + 1, :] = chip[64 + a : 65 + a, :] + jnp.where(x_even, 0.0, own)
            beyond[b : b + 1, :] = chip[64 + b : 65 + b, :] + jnp.where(x_even, own, 0.0)
        put(more, 0, s[jnp.where(x_even, 1, 14)])
        put(more, 64, g[jnp.where(x_even, 0, 15)])
        more[128:MORE, :] = jnp.zeros((MORE - 128, 128), F32)

    def window_kernel(full, beyond, core, chip, s_core, window, short):
        x_at, _, x_even, _ = where_am_i()
        mid = full[...]
        a, b = core[...], beyond[...]
        left, right = jnp.where(x_even, b, a), jnp.where(x_even, a, b)
        for at, block in enumerate((left, mid, right)):
            for cy in range(4):
                window[24 * cy + 4 * at : 24 * cy + 4 * at + 4, :] = block[8 * cy : 8 * cy + 4, :]
                window[24 * cy + 12 + 4 * at : 24 * cy + 16 + 4 * at, :] = block[8 * cy + 4 : 8 * cy + 8, :]
            window[96 + 4 * at : 100 + 4 * at, :] = block[32:36, :]
            window[108 + 4 * at : 112 + 4 * at, :] = block[36:40, :]
        for at, line in enumerate((0, 15)):
            near = jnp.concatenate([s_core[16 * j + line : 16 * j + line + 1, :] for j in range(4)], axis=0)
            far = jnp.concatenate([chip[16 * j + line : 16 * j + line + 1, :] for j in range(4)], axis=0)
            window[120 + 4 * at : 124 + 4 * at, :] = jnp.where(x_at > 0, jnp.where(x_even, far, near), 0.0)
            window[128 + 4 * at : 132 + 4 * at, :] = jnp.where(x_at < nx - 1, jnp.where(x_even, near, far), 0.0)
            short[72 + 4 * at : 76 + 4 * at, :] = far
        for cy in range(4):
            for at, block in enumerate((left, mid, right)):
                short[12 * cy + 4 * at : 12 * cy + 4 * at + 4, :] = block[8 * cy : 8 * cy + 4, :]
            short[48 + 4 * cy : 52 + 4 * cy, :] = beyond[8 * cy + 4 : 8 * cy + 8, :]
        short[64:72, :] = beyond[32:40, :]

    planes = 4 * ny
    short_steps = (1, 3) if ny == 4 else (1,)

    def prepare(f, g, s, a_core, a_chip, a_row, a_odd, s_core, s_chip, s_more, s_row, s_odd, u, u_low, u_high, g_x, g_y, edge):
        x_at, y_at, x_even, y_even = where_am_i()
        s_left, s_right = halo_x(s_core, s_chip, 0, x_at, x_even)
        s_left2, s_right2 = halo_x(s_core, s_more, 64, x_at, x_even, 0)
        f_left, f_right = halo_x(a_core, a_chip, 0, x_at, x_even)
        g_x[0], g_x[1] = halo_x(s_core, s_more, 128, x_at, x_even, 64)
        y1 = halo_y(s_row, s_odd, 0, y_at, y_even)
        y2 = halo_y(s_row, s_odd, 64, y_at, y_even)
        f_y = halo_y(a_row, a_odd, 0, y_at, y_even)
        g_y[0], g_y[1] = halo_y(a_row, a_odd, 64, y_at, y_even)
        u[0] = 0.2 * s_left + f_left + g_x[0] * (s_left2 + s[0] + beside(s_left))
        u[17] = 0.2 * s_right + f_right + g_x[1] * (s_right2 + s[15] + beside(s_right))
        for x in range(16):
            here = s[x]
            total = (s[x - 1] if x > 0 else s_left) + (s[x + 1] if x < 15 else s_right)
            total = total + beside(here, y1[0][x : x + 1, :], y1[1][x : x + 1, :])
            u[x + 1] = 0.2 * here + f[x] + g[x] * total
            edge[0, x : x + 1, :] = here[0:1, :]
            edge[1, x : x + 1, :] = here[15:16, :]
        for at, out in enumerate((u_low, u_high)):
            out[...] = 0.2 * y1[at] + f_y[at] + g_y[at] * (y2[at] + edge[at] + beside(y1[at]))

    def finish(*refs):
        f, g, u, u_low, u_high, g_x, g_y, s_row, s_odd = refs[:9]
        windows = refs[9 : 9 + ny]
        pressure, coarse = refs[9 + ny : 11 + ny]
        every, res, diag, inv, one, two, sol, C, U, ul, uh, result, slab_out, sems = refs[11 + ny :]
        x_at, y_at, x_even, y_even = where_am_i()
        for step, window in enumerate(windows):
            there = jnp.bitwise_xor(y_at, step)
            if step not in short_steps:
                every[there] = window[...]
                continue
            faces_of = s_row if step == 1 else s_odd

            def three(at, own, core, chip):
                every[there, at : at + 4, :] = jnp.where(x_even, chip, core)
                if own is not None:
                    every[there, at + 4 : at + 8, :] = own
                every[there, at + 8 : at + 12, :] = jnp.where(x_even, core, chip)

            for cy in range(4):
                at = 4 * cy
                every[there, 24 * cy : 24 * cy + 12, :] = window[12 * cy : 12 * cy + 12, :]
                three(
                    24 * cy + 12, faces_of[128 + at : 132 + at, :], faces_of[144 + at : 148 + at, :],
                    window[48 + at : 52 + at, :],
                )
            for at in (0, 4):
                three(
                    96 + 3 * at, faces_of[160 + at : 164 + at, :], faces_of[168 + at : 172 + at, :],
                    window[64 + at : 68 + at, :],
                )
                three(120 + at, None, faces_of[176:180, :], window[72 + at : 76 + at, :])

        row = iota((16, 128), 0)
        valid = ((row >= 4) | (x_at > 0)) & ((row < 8) | (x_at < nx - 1)) & (row < 12)
        blank = jnp.zeros((4, 128), F32)

        def twelve(value):
            return jnp.concatenate([value, blank], axis=0)

        centre = (CHEB_HIGH + CHEB_LOW) / 2.0
        half_range = (CHEB_HIGH - CHEB_LOW) / 2.0
        aspect = centre / half_range
        factor = 1.0 / aspect
        empty = jnp.zeros((16, 128), F32)
        for ref in (one, two, sol):
            ref[0] = empty
            ref[planes + 1] = empty
        for at in range(ny):
            for cy in range(4):
                plane = 4 * at + cy
                value = every[at, 24 * cy : 24 * cy + 12, :]
                if cy == 0 and at > 0:
                    value = value + every[at - 1, 108:120, :]
                if cy == 3 and at < ny - 1:
                    value = value + every[at + 1, 96:108, :]
                value = jnp.where(valid, twelve(value), 0.0)
                centre_value = 6.0 + twelve(every[at, 24 * cy + 12 : 24 * cy + 24, :]) / 16.0
                inverse = jnp.where(valid, 1.0 / (16.0 * centre_value), 0.0)
                res[plane] = value
                diag[plane] = centre_value
                inv[plane] = inverse
                direction = inverse * value / centre
                one[plane + 1] = direction
                sol[plane + 1] = direction
        now, later = one, two
        for number in range(1, SWEEPS):
            factor_next = 1.0 / (2.0 * aspect - factor)
            keep, gain = factor_next * factor, 2.0 * factor_next / half_range

            lane = iota((16, 128), 1)
            for plane in range(planes):
                here = now[plane + 1]
                total = now[plane] + now[plane + 2]
                total = total + pltpu.roll(here, 15, 0) + pltpu.roll(here, 1, 0)
                total = total + jnp.where(lane == 127, 0.0, pltpu.roll(here, 127, 1))
                total = total + jnp.where(lane == 0, 0.0, pltpu.roll(here, 1, 1))
                residual = res[plane] - 16.0 * (diag[plane] * here - total)
                res[plane] = residual
                direction = keep * here + gain * inv[plane] * residual
                later[plane + 1] = direction
                sol[plane + 1] = sol[plane + 1] + direction
            now, later = later, now
            factor = factor_next
        for plane in range(planes):
            for cx in range(4):
                slab_out[cx, plane : plane + 1, :] = sol[plane + 1, 4 + cx : 5 + cx, :]
        moves = [pltpu.make_async_copy(slab_out, coarse, sems.at[8])]
        moves[0].start()

        first_plane = 4 * y_at + 1
        below, above = first_plane - 1, first_plane + 4
        for at in range(6):
            C[at] = spread_lanes(spread_planes(sol, first_plane, 3 + at))
        outside = [[spread_lanes(sol[plane, 3 + at : 4 + at, :]) for at in range(6)] for plane in (below, above)]
        before, after = jnp.maximum(y_at - 1, 0), jnp.minimum(y_at + 1, ny - 1)
        corners = []
        for who, inside, line in ((before, y_at > 0, 1), (after, y_at < ny - 1, 0)):
            for base, there in ((0, x_at > 0), (2, x_at < nx - 1)):
                corner = jnp.concatenate(
                    [every[who, pl.ds(120 + 4 * (base + line) + j, 1), :] for j in range(4)], axis=1
                )
                corners.append(jnp.where(inside & there, corner, 0.0))
        edge_row = iota((16, 512), 0)

        def ends(first, last):
            first, last = (jnp.broadcast_to(line, (16, 512)) for line in (first, last))
            return jnp.where(edge_row == 0, first, jnp.where(edge_row == 15, last, 0.0))

        for at in range(6):
            here = C[at]
            around = beside(here, outside[0][at], outside[1][at])
            fifth_of = 0.2 * here
            if at == 0:
                U[0] = u[0] + fifth_of + g_x[0] * (around + here + C[1] + ends(corners[0], corners[2]))
            elif at == 5:
                U[17] = u[17] + fifth_of + g_x[1] * (around + here + C[4] + ends(corners[1], corners[3]))
            else:
                inner = around + 2.0 * here
                sides = [around + here + C[at - 1], inner, inner, around + here + C[at + 1]]
                for q in range(4):
                    x = 4 * (at - 1) + q
                    U[x + 1] = u[x + 1] + fifth_of + g[x] * sides[q]
        for at, (part, out, plane, inside) in enumerate(
            ((u_low, ul, below, first_plane), (u_high, uh, above, first_plane + 3))
        ):
            beyond = spread_lanes(spread_rows(sol, plane, 4))
            edge = spread_lanes(spread_rows(sol, inside, 4))
            around = beside(beyond, outside[at][0], outside[at][5])
            total = beyond + edge + around + ends(corners[2 * at], corners[2 * at + 1])
            out[...] = part[...] + 0.2 * beyond + g_y[at] * total

        for x in range(16):
            here = U[x + 1]
            total = U[x] + U[x + 2] + beside(here, ul[x : x + 1, :], uh[x : x + 1, :])
            result[x] = 0.2 * here + f[x] + g[x] * total
            if x % 2 == 1:
                part = pl.ds(x - 1, 2)
                moves.append(pltpu.make_async_copy(result.at[part], pressure.at[part], sems.at[x // 2]))
                moves[-1].start()
        for move in moves:
            move.wait()

    slab, field, long = (16, 512), (16, 16, 512), (18, 16, 512)
    core_pairs, chip_pairs = pairs_core(nx, ny), pairs_chip(nx, ny)
    row_pairs = [pairs_row(nx, ny, step) for step in range(1, ny)]
    odd_pairs = pairs_odd(nx, ny)

    def swap(array, pairs):
        return lax.ppermute(array, axes, pairs)

    def local(source, reaction, boundary_kind, disk_id, disk_mask, thrust):
        inputs = (source, reaction, boundary_kind, disk_id, disk_mask, thrust.reshape(1, -1))
        some = (4, 16, 512)
        core, chip, row, odd = call(
            faces,
            [(64, 128), (64, 128), (128, 128), (128, 128)],
            *(pltpu.with_memory_space_constraint(array, pltpu.HBM) for array in inputs),
            in_specs=[HBM] * 6,
            scratch=[some, some]
            + [pltpu.VMEM(some, jnp.int32)] * 3
            + [(1, thrust.shape[0]), pltpu.SemaphoreType.DMA((5, 4)), pltpu.SemaphoreType.DMA(())],
            name="faces",
        )
        a_core, a_chip = swap(core, core_pairs), swap(chip, chip_pairs)
        a_odd, a_row = swap(odd, odd_pairs), swap(row, row_pairs[0])
        f, g, d, absorb, inner, rows = call(
            set_up, [field, field, field, (16, 128), field, (4, 16, 512)], *inputs, scratch=[(64, 512)], name="set_up"
        )
        a_odd, a_row, a_chip, a_core, f, g, d, absorb, inner, rows = lax.optimization_barrier(
            (a_odd, a_row, a_chip, a_core, f, g, d, absorb, inner, rows)
        )
        to_core, sums, y_faces = call(
            early,
            [(224, 128), (16, 128), (32, 512)],
            inner, g, rows, absorb, a_core, a_chip, a_row, a_odd,
            scratch=[slab] * 2,
            name="early",
        )
        s_core = swap(to_core, core_pairs)
        s, block, y_more = call(
            restrict,
            [field, (40, 128), (32, 512)],
            f, g, d, absorb, inner, sums, a_core, a_chip, a_row, a_odd,
            scratch=[slab, slab, (64, 512)],
            name="restrict",
        )
        mine, to_chip, to_row, to_odd = call(
            to_chip_kernel,
            [(40, 128), (112, 128), (FACES, 128), (FACES, 128)],
            block, sums, absorb, s_core, s, g, y_faces, y_more,
            name="to_chip",
        )
        s_chip = swap(to_chip, chip_pairs)
        s_row, s_odd = swap(to_row, row_pairs[0]), swap(to_odd, odd_pairs)
        full, beyond, more = call(
            from_chip_kernel, [(40, 128), (40, 128), (MORE, 128)], mine, sums, s_chip, s, g, name="from_chip"
        )
        c_core, s_more = swap(full, core_pairs), swap(more, chip_pairs)
        window, short = call(
            window_kernel, [(136, 128), (80, 128)], full, beyond, c_core, s_chip, s_core, name="window"
        )
        windows = [window] + [
            swap(short if step in short_steps else window, row_pairs[step - 1]) for step in range(1, ny)
        ]
        prepared = call(
            prepare,
            [long, slab, slab, (2, 16, 512), (2, 16, 512)],
            f, g, s, a_core, a_chip, a_row, a_odd, s_core, s_chip, s_more, s_row, s_odd,
            scratch=[(2, 16, 512)],
            name="prepare",
        )
        pressure, coarse = call(
            finish,
            [field, (4, planes, 128)],
            f, g, *prepared, s_row, s_odd, *windows,
            scratch=[(ny, 136, 128)]
            + [(planes, 16, 128)] * 3
            + [(planes + 2, 16, 128)] * 3
            + [(6, 16, 512), long, slab, slab, field, (4, planes, 128), pltpu.SemaphoreType.DMA((9,))],
            out_specs=[HBM, HBM],
            name="finish",
        )
        return pressure, coarse

    spec = P("gx", "gy", None)
    return jax.shard_map(
        local,
        mesh=mesh,
        in_specs=(spec, spec, spec, spec, spec, P()),
        out_specs=(spec, P("gx", None, None)),
        check_vma=False,
    )
```

```python
import jax
import jax.numpy as jnp
from jax import lax
from jax.experimental import pallas as pl
from jax.experimental.pallas import tpu as pltpu
from jax.sharding import PartitionSpec as P

SWEEPS = 4
OMEGA = 0.8
WALL_PENALTY = 0.4
INFLOW_PENALTY = 0.2
CHEB_LOW = 0.1
CHEB_HIGH = 2.0
F32 = jnp.float32
VMEM = pl.BlockSpec(memory_space=pltpu.VMEM)


HBM = pl.BlockSpec(memory_space=pltpu.HBM)
MORE = 152
FACES = 184


def call(kernel, outs, *args, scratch=(), name=None, in_specs=None, out_specs=None):
    return pl.pallas_call(
        kernel,
        out_shape=[jax.ShapeDtypeStruct(s, F32) for s in outs],
        in_specs=in_specs or [VMEM] * len(args),
        out_specs=out_specs or [VMEM] * len(outs),
        scratch_shapes=[pltpu.VMEM(s, F32) if isinstance(s, tuple) else s for s in scratch],
        compiler_params=pltpu.CompilerParams(vmem_limit_bytes=16 << 20),
        name=name,
    )(*args)


def pairs_core(nx, ny):
    return [(x * ny + y, (x ^ 1) * ny + y) for x in range(nx) for y in range(ny)]


def pairs_chip(nx, ny):
    found = []
    for x in range(nx):
        for y in range(ny):
            if x in (0, nx - 1):
                found.append((x * ny + y, x * ny + (y ^ (ny // 2))))
            else:
                found.append((x * ny + y, (x + 1 if x % 2 else x - 1) * ny + y))
    return found


def pairs_row(nx, ny, step):
    return [(x * ny + y, x * ny + (y ^ step)) for x in range(nx) for y in range(ny)]


def pairs_odd(nx, ny):
    return [
        (x * ny + y, x * ny + (y + 1 if y % 2 else y - 1) % ny) for x in range(nx) for y in range(ny)
    ]


def put(ref, row, slab):
    rows = slab.shape[0]
    for j in range(slab.shape[1] // 128):
        ref[row + rows * j : row + rows * (j + 1), :] = slab[:, 128 * j : 128 * (j + 1)]


def get(ref, row, rows, width):
    return jnp.concatenate(
        [ref[row + rows * j : row + rows * (j + 1), :] for j in range(width // 128)], axis=1
    )


def iota(shape, dim):
    return lax.broadcasted_iota(jnp.int32, shape, dim)


def beside_z(slab):
    depth = slab.shape[1]
    lane = iota(slab.shape, 1)
    above = jnp.where(lane == depth - 1, 0.0, pltpu.roll(slab, depth - 1, 1))
    below = jnp.where(lane == 0, 0.0, pltpu.roll(slab, 1, 1))
    return above + below


def beside(slab, low=None, high=None):
    rows, depth = slab.shape
    tiles, columns = rows // 8, depth // 128
    lane, row = iota((8, 128), 1), iota((8, 128), 0)
    piece = [[slab[8 * t : 8 * t + 8, 128 * j : 128 * j + 128] for j in range(columns)] for t in range(tiles)]
    left = [[pltpu.roll(p, 127, 1) for p in line] for line in piece]
    right = [[pltpu.roll(p, 1, 1) for p in line] for line in piece]
    up = [[pltpu.roll(p, 7, 0) for p in line] for line in piece]
    down = [[pltpu.roll(p, 1, 0) for p in line] for line in piece]

    def outer(line, j):
        return 0.0 if line is None else jnp.broadcast_to(line[:, 128 * j : 128 * j + 128], (8, 128))

    lines = []
    for t in range(tiles):
        parts = []
        for j in range(columns):
            above = jnp.where(lane == 127, left[t][j + 1] if j + 1 < columns else 0.0, left[t][j])
            below = jnp.where(lane == 0, right[t][j - 1] if j > 0 else 0.0, right[t][j])
            after = jnp.where(row == 7, up[t + 1][j] if t + 1 < tiles else outer(high, j), up[t][j])
            before = jnp.where(row == 0, down[t - 1][j] if t > 0 else outer(low, j), down[t][j])
            parts.append((above + below) + (after + before))
        lines.append(jnp.concatenate(parts, axis=1))
    return jnp.concatenate(lines, axis=0)


def outer_rows(low, high):
    row = iota((8, 512), 0)
    first = jnp.where(row == 0, jnp.broadcast_to(low, row.shape), 0.0)
    last = jnp.where(row == 7, jnp.broadcast_to(high, row.shape), 0.0)
    return jnp.concatenate([first, last], axis=0)


def dot(left, right):
    return lax.dot_general(
        left,
        right,
        (((1,), (0,)), ((), ())),
        precision=lax.Precision.HIGHEST,
        preferred_element_type=F32,
    )


def group_lanes(depth):
    return (iota((depth, depth // 4), 0) // 4 == iota((depth, depth // 4), 1)).astype(F32)


def spread_lanes(rows):
    count, lanes = rows.shape
    pad = -count % 8
    if pad:
        rows = jnp.concatenate([rows, jnp.zeros((pad, lanes), F32)], axis=0)
    parts = []
    for j in range(4):
        index = iota(rows.shape, 1) // 4 + (lanes // 4) * j
        parts.append(jnp.take_along_axis(rows, index, axis=1, mode="promise_in_bounds"))
    return jnp.concatenate(parts, axis=1)[:count]


def spread_rows(ref, plane, start):
    row = iota((16, 128), 0) // 4
    value = jnp.zeros((16, 128), F32)
    for q in range(4):
        value = jnp.where(row == q, jnp.broadcast_to(ref[plane, start + q : start + q + 1, :], (16, 128)), value)
    return value


def spread_planes(ref, plane, column):
    row = iota((16, 128), 0) // 4
    value = jnp.zeros((16, 128), F32)
    for q in range(4):
        value = jnp.where(row == q, jnp.broadcast_to(ref[plane + q, column : column + 1, :], (16, 128)), value)
    return value


def solution(mesh):
    nx, ny = mesh.shape["gx"], mesh.shape["gy"]
    assert nx % 2 == 0 and ny % 2 == 0 and ny & (ny - 1) == 0
    axes = ("gx", "gy")

    def where_am_i():
        x, y = lax.axis_index("gx"), lax.axis_index("gy")
        return x, y, x % 2 == 0, y % 2 == 0

    def look_up(table, ids):
        spare = jnp.zeros((1, 128 - table.shape[1]), F32)
        row = jnp.broadcast_to(jnp.concatenate([table, spare], axis=1), (16, 128))
        parts = [
            jnp.take_along_axis(row, ids[:, 128 * j : 128 * (j + 1)], axis=1, mode="promise_in_bounds") for j in range(4)
        ]
        return jnp.concatenate(parts, axis=1)

    def first_of(source, reaction, kinds, ids, mask, table):
        a = reaction + jnp.where(kinds == 1, WALL_PENALTY, jnp.where(kinds == 2, INFLOW_PENALTY, 0.0))
        diagonal = 6.0 + a
        scale = OMEGA / diagonal
        return (source + mask.astype(F32) * look_up(table, ids)) * scale, scale, diagonal, a

    def faces(*refs):
        inputs, thrust, messages, buffers, table, sems, table_sem = (
            refs[:5], refs[5], refs[6:10], refs[10:15], refs[15], refs[16], refs[17]
        )
        core, chip, row, odd = messages
        _, _, x_even, y_even = where_am_i()
        near, far = jnp.where(x_even, 15, 0), jnp.where(x_even, 0, 15)
        moves = [pltpu.make_async_copy(thrust, table, table_sem)]
        for i, (hbm, buffer) in enumerate(zip(inputs, buffers)):
            for j, part in enumerate((hbm.at[:, 0, :], hbm.at[:, 15, :], hbm.at[far], hbm.at[near])):
                moves.append(pltpu.make_async_copy(part, buffer.at[j], sems.at[i, j]))
        for move in moves:
            move.start()
        for move in moves:
            move.wait()
        (low, g_low), (high, g_high), (f_far, _), (f_near, _) = (
            first_of(*(buffer[j] for buffer in buffers), table[...])[:2] for j in range(4)
        )
        put(row, 0, jnp.where(y_even, high, low))
        put(row, 64, jnp.where(y_even, g_high, g_low))
        put(odd, 0, jnp.where(y_even, low, high))
        put(odd, 64, jnp.where(y_even, g_low, g_high))
        put(chip, 0, f_far)
        put(core, 0, f_near)

    def set_up(source, reaction, kind, disk_id, disk_mask, table, f, g, d, absorb, inner, rows, V):
        for k in range(4):
            total = jnp.zeros((16, 512), F32)
            for x in range(4 * k, 4 * k + 4):
                f[x], g[x], d[x], a = first_of(source[x], reaction[x], kind[x], disk_id[x], disk_mask[x], table[...])
                total = total + a
            V[16 * k : 16 * k + 16, :] = total
        out, src = iota((16, 64), 0), iota((16, 64), 1)
        pick = ((src // 16 == out % 4) & ((src % 16) // 4 == out // 4)).astype(F32)
        absorb[...] = dot(dot(pick, V[...]), group_lanes(512))
        for x in range(16):
            total = beside(f[x])
            if x > 0:
                total = total + f[x - 1]
            if x < 15:
                total = total + f[x + 1]
            value = 1.2 * f[x] + g[x] * total
            inner[x] = value
            for at, part in enumerate((value[0:1, :], value[15:16, :], g[x, 0:1, :], g[x, 15:16, :])):
                rows[at, x : x + 1, :] = part

    def halo_x(core, chip, row, x, x_even, chip_row=None):
        a, b = get(core, row, 16, 512), get(chip, row if chip_row is None else chip_row, 16, 512)
        left = jnp.where(x > 0, jnp.where(x_even, b, a), 0.0)
        right = jnp.where(x < nx - 1, jnp.where(x_even, a, b), 0.0)
        return left, right

    def halo_y(row, odd, at, y, y_even):
        a, b = get(row, at, 16, 512), get(odd, at, 16, 512)
        low = jnp.where(y > 0, jnp.where(y_even, b, a), 0.0)
        high = jnp.where(y < ny - 1, jnp.where(y_even, a, b), 0.0)
        return low, high

    def early(inner, g, rows, absorb, core, chip, row, odd, to_core, sums, y_faces, lo, hi):
        x_at, y_at, x_even, y_even = where_am_i()
        left, right = halo_x(core, chip, 0, x_at, x_even)
        lo[...], hi[...] = halo_y(row, odd, 0, y_at, y_even)

        def second_at(x, outer=0.0):
            return inner[x] + g[x] * (outer_rows(lo[pl.ds(x, 1), :], hi[pl.ds(x, 1), :]) + outer)

        s_first, s_last = second_at(0, left), second_at(15, right)
        row_of = iota((16, 512), 0)
        for at, (outer, line) in enumerate(((lo, slice(0, 1)), (hi, slice(15, 16)))):
            first, last = (jnp.broadcast_to(side[line, :], (16, 512)) for side in (left, right))
            more = jnp.where(row_of == 0, first, jnp.where(row_of == 15, last, 0.0))
            y_faces[16 * at : 16 * at + 16, :] = rows[at] + rows[2 + at] * (outer[...] + more)
        out, src = iota((16, 64), 0), iota((16, 64), 1)
        pick = ((out // 4 == src // 16) & (out % 4 == (src % 16) // 4)).astype(F32)
        sides = jnp.concatenate([s_first, s_last, y_faces[...]], axis=0)
        sums[...] = dot(dot(pick, sides), group_lanes(512))
        put(to_core, 0, jnp.where(x_even, s_last, s_first))
        put(to_core, 64, second_at(jnp.where(x_even, 14, 1)))
        put(to_core, 128, g[jnp.where(x_even, 15, 0)])
        to_core[192:196, :] = jnp.where(x_even, sums[4:8, :], sums[0:4, :])
        to_core[196:200, :] = jnp.zeros((4, 128), F32)
        to_core[200:208, :] = sums[8:16, :]
        to_core[208:224, :] = absorb[...]

    def restrict(f, g, d, absorb, inner, sums, core, chip, row, odd, s, block, y_more, lo, hi, V):
        x_at, y_at, x_even, y_even = where_am_i()
        left, right = halo_x(core, chip, 0, x_at, x_even)
        lo[...], hi[...] = halo_y(row, odd, 0, y_at, y_even)
        for x in range(16):
            total = outer_rows(lo[x : x + 1, :], hi[x : x + 1, :])
            if x == 0:
                total = total + left
            if x == 15:
                total = total + right
            value = inner[x] + g[x] * total
            s[x] = value
            y_more[x : x + 1, :] = value[1:2, :]
            y_more[16 + x : 17 + x, :] = value[14:15, :]
        for k in range(4):
            total = jnp.zeros((16, 512), F32)
            for x in range(4 * k, 4 * k + 4):
                here = s[x]
                total = total + d[x] * (1.25 * f[x] - here)
                total = total + beside(here)
                if x > 0:
                    total = total + s[x - 1]
                if x < 15:
                    total = total + s[x + 1]
            V[16 * k : 16 * k + 16, :] = total
        out, src = iota((16, 64), 0), iota((16, 64), 1)
        pick = ((src // 16 == out % 4) & ((src % 16) // 4 == out // 4)).astype(F32)
        found = dot(dot(pick, V[...]), group_lanes(512))
        for cy in range(4):
            block[8 * cy : 8 * cy + 4, :] = found[4 * cy : 4 * cy + 4, :]
            block[8 * cy + 4 : 8 * cy + 8, :] = absorb[4 * cy : 4 * cy + 4, :]
        block[32:40, :] = sums[8:16, :]

    def to_chip_kernel(block, sums, absorb, core, s, g, y_faces, y_more, mine, to_chip, to_row, to_odd):
        _, _, x_even, y_even = where_am_i()
        mine[...] = block[...]
        face = core[192:200, :]
        for cy in range(4):
            line = face[cy : cy + 1, :]
            a, b = 8 * cy, 8 * cy + 3
            mine[a : a + 1, :] = block[a : a + 1, :] + jnp.where(x_even, 0.0, line)
            mine[b : b + 1, :] = block[b : b + 1, :] + jnp.where(x_even, line, 0.0)
        put(to_chip, 0, s[jnp.where(x_even, 0, 15)])
        to_chip[64:104, :] = mine[...]
        to_chip[104:108, :] = jnp.where(x_even, sums[0:4, :], sums[4:8, :])
        to_chip[108:112, :] = jnp.zeros((4, 128), F32)
        for at, ref in enumerate((y_faces, y_more)):
            a, b = ref[0:16, :], ref[16:32, :]
            put(to_row, 64 * at, jnp.where(y_even, b, a))
            put(to_odd, 64 * at, jnp.where(y_even, a, b))
        first_line, last_line = (
            jnp.concatenate([core[16 * j + line : 16 * j + line + 1, :] for j in range(4)], axis=0) for line in (0, 15)
        )
        for ref, corner in (
            (to_row, jnp.where(y_even, last_line, first_line)),
            (to_odd, jnp.where(y_even, first_line, last_line)),
        ):
            ref[128:144, :] = absorb[...]
            ref[144:160, :] = core[208:224, :]
            ref[160:168, :] = sums[8:16, :]
            ref[168:176, :] = core[200:208, :]
            ref[176:180, :] = corner
            ref[180:FACES, :] = jnp.zeros((FACES - 180, 128), F32)

    def from_chip_kernel(mine, sums, chip, s, g, full, beyond, more):
        x_at, _, x_even, _ = where_am_i()
        has = jnp.where(x_even, x_at > 0, x_at < nx - 1)
        full[...] = mine[...]
        beyond[...] = chip[64:104, :]
        mine_face = jnp.where(x_even, sums[0:4, :], sums[4:8, :])
        face = chip[104:112, :]
        for cy in range(4):
            line = jnp.where(has, face[cy : cy + 1, :], 0.0)
            own = mine_face[cy : cy + 1, :]
            a, b = 8 * cy, 8 * cy + 3
            full[a : a + 1, :] = mine[a : a + 1, :] + jnp.where(x_even, line, 0.0)
            full[b : b + 1, :] = mine[b : b + 1, :] + jnp.where(x_even, 0.0, line)
            beyond[a : a + 1, :] = chip[64 + a : 65 + a, :] + jnp.where(x_even, 0.0, own)
            beyond[b : b + 1, :] = chip[64 + b : 65 + b, :] + jnp.where(x_even, own, 0.0)
        put(more, 0, s[jnp.where(x_even, 1, 14)])
        put(more, 64, g[jnp.where(x_even, 0, 15)])
        more[128:MORE, :] = jnp.zeros((MORE - 128, 128), F32)

    def window_kernel(full, beyond, core, chip, s_core, window, short):
        x_at, _, x_even, _ = where_am_i()
        mid = full[...]
        a, b = core[...], beyond[...]
        left, right = jnp.where(x_even, b, a), jnp.where(x_even, a, b)
        for at, block in enumerate((left, mid, right)):
            for cy in range(4):
                window[24 * cy + 4 * at : 24 * cy + 4 * at + 4, :] = block[8 * cy : 8 * cy + 4, :]
                window[24 * cy + 12 + 4 * at : 24 * cy + 16 + 4 * at, :] = block[8 * cy + 4 : 8 * cy + 8, :]
            window[96 + 4 * at : 100 + 4 * at, :] = block[32:36, :]
            window[108 + 4 * at : 112 + 4 * at, :] = block[36:40, :]
        for at, line in enumerate((0, 15)):
            near = jnp.concatenate([s_core[16 * j + line : 16 * j + line + 1, :] for j in range(4)], axis=0)
            far = jnp.concatenate([chip[16 * j + line : 16 * j + line + 1, :] for j in range(4)], axis=0)
            window[120 + 4 * at : 124 + 4 * at, :] = jnp.where(x_at > 0, jnp.where(x_even, far, near), 0.0)
            window[128 + 4 * at : 132 + 4 * at, :] = jnp.where(x_at < nx - 1, jnp.where(x_even, near, far), 0.0)
            short[72 + 4 * at : 76 + 4 * at, :] = far
        for cy in range(4):
            for at, block in enumerate((left, mid, right)):
                short[12 * cy + 4 * at : 12 * cy + 4 * at + 4, :] = block[8 * cy : 8 * cy + 4, :]
            short[48 + 4 * cy : 52 + 4 * cy, :] = beyond[8 * cy + 4 : 8 * cy + 8, :]
        short[64:72, :] = beyond[32:40, :]

    planes = 4 * ny
    short_steps = (1, 3) if ny == 4 else (1,)

    def prepare(f, g, s, a_core, a_chip, a_row, a_odd, s_core, s_chip, s_more, s_row, s_odd, u, u_low, u_high, g_x, g_y, edge):
        x_at, y_at, x_even, y_even = where_am_i()
        s_left, s_right = halo_x(s_core, s_chip, 0, x_at, x_even)
        s_left2, s_right2 = halo_x(s_core, s_more, 64, x_at, x_even, 0)
        f_left, f_right = halo_x(a_core, a_chip, 0, x_at, x_even)
        g_x[0], g_x[1] = halo_x(s_core, s_more, 128, x_at, x_even, 64)
        y1 = halo_y(s_row, s_odd, 0, y_at, y_even)
        y2 = halo_y(s_row, s_odd, 64, y_at, y_even)
        f_y = halo_y(a_row, a_odd, 0, y_at, y_even)
        g_y[0], g_y[1] = halo_y(a_row, a_odd, 64, y_at, y_even)
        u[0] = 0.2 * s_left + f_left + g_x[0] * (s_left2 + s[0] + beside(s_left))
        u[17] = 0.2 * s_right + f_right + g_x[1] * (s_right2 + s[15] + beside(s_right))
        for x in range(16):
            here = s[x]
            total = (s[x - 1] if x > 0 else s_left) + (s[x + 1] if x < 15 else s_right)
            total = total + beside(here, y1[0][x : x + 1, :], y1[1][x : x + 1, :])
            u[x + 1] = 0.2 * here + f[x] + g[x] * total
            edge[0, x : x + 1, :] = here[0:1, :]
            edge[1, x : x + 1, :] = here[15:16, :]
        for at, out in enumerate((u_low, u_high)):
            out[...] = 0.2 * y1[at] + f_y[at] + g_y[at] * (y2[at] + edge[at] + beside(y1[at]))

    def finish(*refs):
        f, g, u, u_low, u_high, g_x, g_y, s_row, s_odd = refs[:9]
        windows = refs[9 : 9 + ny][::-1]
        pressure, coarse = refs[9 + ny : 11 + ny]
        every, res, diag, inv, one, two, sol, C, U, ul, uh, result, slab_out, sems = refs[11 + ny :]
        x_at, y_at, x_even, y_even = where_am_i()
        for step, window in enumerate(windows):
            there = jnp.bitwise_xor(y_at, step)
            if step not in short_steps:
                every[there] = window[...]
                continue
            faces_of = s_row if step == 1 else s_odd

            def three(at, own, core, chip):
                every[there, at : at + 4, :] = jnp.where(x_even, chip, core)
                if own is not None:
                    every[there, at + 4 : at + 8, :] = own
                every[there, at + 8 : at + 12, :] = jnp.where(x_even, core, chip)

            for cy in range(4):
                at = 4 * cy
                every[there, 24 * cy : 24 * cy + 12, :] = window[12 * cy : 12 * cy + 12, :]
                three(
                    24 * cy + 12, faces_of[128 + at : 132 + at, :], faces_of[144 + at : 148 + at, :],
                    window[48 + at : 52 + at, :],
                )
            for at in (0, 4):
                three(
                    96 + 3 * at, faces_of[160 + at : 164 + at, :], faces_of[168 + at : 172 + at, :],
                    window[64 + at : 68 + at, :],
                )
                three(120 + at, None, faces_of[176:180, :], window[72 + at : 76 + at, :])

        row = iota((16, 128), 0)
        valid = ((row >= 4) | (x_at > 0)) & ((row < 8) | (x_at < nx - 1)) & (row < 12)
        blank = jnp.zeros((4, 128), F32)

        def twelve(value):
            return jnp.concatenate([value, blank], axis=0)

        centre = (CHEB_HIGH + CHEB_LOW) / 2.0
        half_range = (CHEB_HIGH - CHEB_LOW) / 2.0
        aspect = centre / half_range
        factor = 1.0 / aspect
        empty = jnp.zeros((16, 128), F32)
        for ref in (one, two, sol):
            ref[0] = empty
            ref[planes + 1] = empty
        for at in range(ny):
            for cy in range(4):
                plane = 4 * at + cy
                value = every[at, 24 * cy : 24 * cy + 12, :]
                if cy == 0 and at > 0:
                    value = value + every[at - 1, 108:120, :]
                if cy == 3 and at < ny - 1:
                    value = value + every[at + 1, 96:108, :]
                value = jnp.where(valid, twelve(value), 0.0)
                centre_value = 6.0 + twelve(every[at, 24 * cy + 12 : 24 * cy + 24, :]) / 16.0
                inverse = jnp.where(valid, 1.0 / (16.0 * centre_value), 0.0)
                res[plane] = value
                diag[plane] = centre_value
                inv[plane] = inverse
                direction = inverse * value / centre
                one[plane + 1] = direction
                sol[plane + 1] = direction
        now, later = one, two
        for number in range(1, SWEEPS):
            factor_next = 1.0 / (2.0 * aspect - factor)
            keep, gain = factor_next * factor, 2.0 * factor_next / half_range

            lane = iota((16, 128), 1)
            for plane in range(planes):
                here = now[plane + 1]
                total = now[plane] + now[plane + 2]
                total = total + pltpu.roll(here, 15, 0) + pltpu.roll(here, 1, 0)
                total = total + jnp.where(lane == 127, 0.0, pltpu.roll(here, 127, 1))
                total = total + jnp.where(lane == 0, 0.0, pltpu.roll(here, 1, 1))
                residual = res[plane] - 16.0 * (diag[plane] * here - total)
                res[plane] = residual
                direction = keep * here + gain * inv[plane] * residual
                later[plane + 1] = direction
                sol[plane + 1] = sol[plane + 1] + direction
            now, later = later, now
            factor = factor_next
        for plane in range(planes):
            for cx in range(4):
                slab_out[cx, plane : plane + 1, :] = sol[plane + 1, 4 + cx : 5 + cx, :]
        moves = [pltpu.make_async_copy(slab_out, coarse, sems.at[8])]
        moves[0].start()

        first_plane = 4 * y_at + 1
        below, above = first_plane - 1, first_plane + 4
        for at in range(6):
            C[at] = spread_lanes(spread_planes(sol, first_plane, 3 + at))
        outside = [[spread_lanes(sol[plane, 3 + at : 4 + at, :]) for at in range(6)] for plane in (below, above)]
        before, after = jnp.maximum(y_at - 1, 0), jnp.minimum(y_at + 1, ny - 1)
        corners = []
        for who, inside, line in ((before, y_at > 0, 1), (after, y_at < ny - 1, 0)):
            for base, there in ((0, x_at > 0), (2, x_at < nx - 1)):
                corner = jnp.concatenate(
                    [every[who, pl.ds(120 + 4 * (base + line) + j, 1), :] for j in range(4)], axis=1
                )
                corners.append(jnp.where(inside & there, corner, 0.0))
        edge_row = iota((16, 512), 0)

        def ends(first, last):
            first, last = (jnp.broadcast_to(line, (16, 512)) for line in (first, last))
            return jnp.where(edge_row == 0, first, jnp.where(edge_row == 15, last, 0.0))

        for at in range(6):
            here = C[at]
            around = beside(here, outside[0][at], outside[1][at])
            fifth_of = 0.2 * here
            if at == 0:
                U[0] = u[0] + fifth_of + g_x[0] * (around + here + C[1] + ends(corners[0], corners[2]))
            elif at == 5:
                U[17] = u[17] + fifth_of + g_x[1] * (around + here + C[4] + ends(corners[1], corners[3]))
            else:
                inner = around + 2.0 * here
                sides = [around + here + C[at - 1], inner, inner, around + here + C[at + 1]]
                for q in range(4):
                    x = 4 * (at - 1) + q
                    U[x + 1] = u[x + 1] + fifth_of + g[x] * sides[q]
        for at, (part, out, plane, inside) in enumerate(
            ((u_low, ul, below, first_plane), (u_high, uh, above, first_plane + 3))
        ):
            beyond = spread_lanes(spread_rows(sol, plane, 4))
            edge = spread_lanes(spread_rows(sol, inside, 4))
            around = beside(beyond, outside[at][0], outside[at][5])
            total = beyond + edge + around + ends(corners[2 * at], corners[2 * at + 1])
            out[...] = part[...] + 0.2 * beyond + g_y[at] * total

        for x in range(16):
            here = U[x + 1]
            total = U[x] + U[x + 2] + beside(here, ul[x : x + 1, :], uh[x : x + 1, :])
            result[x] = 0.2 * here + f[x] + g[x] * total
            if x % 2 == 1:
                part = pl.ds(x - 1, 2)
                moves.append(pltpu.make_async_copy(result.at[part], pressure.at[part], sems.at[x // 2]))
                moves[-1].start()
        for move in moves:
            move.wait()

    slab, field, long = (16, 512), (16, 16, 512), (18, 16, 512)
    core_pairs, chip_pairs = pairs_core(nx, ny), pairs_chip(nx, ny)
    row_pairs = [pairs_row(nx, ny, step) for step in range(1, ny)]
    odd_pairs = pairs_odd(nx, ny)

    def swap(array, pairs):
        return lax.ppermute(array, axes, pairs)

    def local(source, reaction, boundary_kind, disk_id, disk_mask, thrust):
        inputs = (source, reaction, boundary_kind, disk_id, disk_mask, thrust.reshape(1, -1))
        some = (4, 16, 512)
        core, chip, row, odd = call(
            faces,
            [(64, 128), (64, 128), (128, 128), (128, 128)],
            *(pltpu.with_memory_space_constraint(array, pltpu.HBM) for array in inputs),
            in_specs=[HBM] * 6,
            scratch=[some, some]
            + [pltpu.VMEM(some, jnp.int32)] * 3
            + [(1, thrust.shape[0]), pltpu.SemaphoreType.DMA((5, 4)), pltpu.SemaphoreType.DMA(())],
            name="faces",
        )
        a_core, a_chip = swap(core, core_pairs), swap(chip, chip_pairs)
        a_odd, a_row = swap(odd, odd_pairs), swap(row, row_pairs[0])
        f, g, d, absorb, inner, rows = call(
            set_up, [field, field, field, (16, 128), field, (4, 16, 512)], *inputs, scratch=[(64, 512)], name="set_up"
        )
        a_odd, a_row, a_chip, a_core, f, g, d, absorb, inner, rows = lax.optimization_barrier(
            (a_odd, a_row, a_chip, a_core, f, g, d, absorb, inner, rows)
        )
        to_core, sums, y_faces = call(
            early,
            [(224, 128), (16, 128), (32, 512)],
            inner, g, rows, absorb, a_core, a_chip, a_row, a_odd,
            scratch=[slab] * 2,
            name="early",
        )
        s_core = swap(to_core, core_pairs)
        s, block, y_more = call(
            restrict,
            [field, (40, 128), (32, 512)],
            f, g, d, absorb, inner, sums, a_core, a_chip, a_row, a_odd,
            scratch=[slab, slab, (64, 512)],
            name="restrict",
        )
        mine, to_chip, to_row, to_odd = call(
            to_chip_kernel,
            [(40, 128), (112, 128), (FACES, 128), (FACES, 128)],
            block, sums, absorb, s_core, s, g, y_faces, y_more,
            name="to_chip",
        )
        s_chip = swap(to_chip, chip_pairs)
        s_row, s_odd = swap(to_row, row_pairs[0]), swap(to_odd, odd_pairs)
        full, beyond, more = call(
            from_chip_kernel, [(40, 128), (40, 128), (MORE, 128)], mine, sums, s_chip, s, g, name="from_chip"
        )
        c_core, s_more = swap(full, core_pairs), swap(more, chip_pairs)
        window, short = call(
            window_kernel, [(136, 128), (80, 128)], full, beyond, c_core, s_chip, s_core, name="window"
        )
        windows = [window] + [
            swap(short if step in short_steps else window, row_pairs[step - 1]) for step in range(1, ny)
        ]
        prepared = call(
            prepare,
            [long, slab, slab, (2, 16, 512), (2, 16, 512)],
            f, g, s, a_core, a_chip, a_row, a_odd, s_core, s_chip, s_more, s_row, s_odd,
            scratch=[(2, 16, 512)],
            name="prepare",
        )
        pressure, coarse = call(
            finish,
            [field, (4, planes, 128)],
            f, g, *prepared, s_row, s_odd, *windows[::-1],
            scratch=[(ny, 136, 128)]
            + [(planes, 16, 128)] * 3
            + [(planes + 2, 16, 128)] * 3
            + [(6, 16, 512), long, slab, slab, field, (4, planes, 128), pltpu.SemaphoreType.DMA((9,))],
            out_specs=[HBM, HBM],
            name="finish",
        )
        return pressure, coarse

    spec = P("gx", "gy", None)
    return jax.shard_map(
        local,
        mesh=mesh,
        in_specs=(spec, spec, spec, spec, spec, P()),
        out_specs=(spec, P("gx", None, None)),
        check_vma=False,
    )
```

```python
import jax
import jax.numpy as jnp
from jax import lax
from jax.experimental import pallas as pl
from jax.experimental.pallas import tpu as pltpu
from jax.sharding import PartitionSpec as P

SWEEPS = 4
OMEGA = 0.8
WALL_PENALTY = 0.4
INFLOW_PENALTY = 0.2
CHEB_LOW = 0.1
CHEB_HIGH = 2.0
F32 = jnp.float32
VMEM = pl.BlockSpec(memory_space=pltpu.VMEM)


HBM = pl.BlockSpec(memory_space=pltpu.HBM)
MORE = 152
FACES = 184


def call(kernel, outs, *args, scratch=(), name=None, in_specs=None, out_specs=None):
    return pl.pallas_call(
        kernel,
        out_shape=[jax.ShapeDtypeStruct(s, F32) for s in outs],
        in_specs=in_specs or [VMEM] * len(args),
        out_specs=out_specs or [VMEM] * len(outs),
        scratch_shapes=[pltpu.VMEM(s, F32) if isinstance(s, tuple) else s for s in scratch],
        compiler_params=pltpu.CompilerParams(vmem_limit_bytes=16 << 20),
        name=name,
    )(*args)


def pairs_core(nx, ny):
    return [(x * ny + y, (x ^ 1) * ny + y) for x in range(nx) for y in range(ny)]


def pairs_chip(nx, ny):
    found = []
    for x in range(nx):
        for y in range(ny):
            if x in (0, nx - 1):
                found.append((x * ny + y, x * ny + (y ^ (ny // 2))))
            else:
                found.append((x * ny + y, (x + 1 if x % 2 else x - 1) * ny + y))
    return found


def pairs_row(nx, ny, step):
    return [(x * ny + y, x * ny + (y ^ step)) for x in range(nx) for y in range(ny)]


def pairs_odd(nx, ny):
    return [
        (x * ny + y, x * ny + (y + 1 if y % 2 else y - 1) % ny) for x in range(nx) for y in range(ny)
    ]


def put(ref, row, slab):
    rows = slab.shape[0]
    for j in range(slab.shape[1] // 128):
        ref[row + rows * j : row + rows * (j + 1), :] = slab[:, 128 * j : 128 * (j + 1)]


def get(ref, row, rows, width):
    return jnp.concatenate(
        [ref[row + rows * j : row + rows * (j + 1), :] for j in range(width // 128)], axis=1
    )


def iota(shape, dim):
    return lax.broadcasted_iota(jnp.int32, shape, dim)


def beside_z(slab):
    depth = slab.shape[1]
    lane = iota(slab.shape, 1)
    above = jnp.where(lane == depth - 1, 0.0, pltpu.roll(slab, depth - 1, 1))
    below = jnp.where(lane == 0, 0.0, pltpu.roll(slab, 1, 1))
    return above + below


def beside(slab, low=None, high=None):
    rows, depth = slab.shape
    tiles, columns = rows // 8, depth // 128
    lane, row = iota((8, 128), 1), iota((8, 128), 0)
    piece = [[slab[8 * t : 8 * t + 8, 128 * j : 128 * j + 128] for j in range(columns)] for t in range(tiles)]
    left = [[pltpu.roll(p, 127, 1) for p in line] for line in piece]
    right = [[pltpu.roll(p, 1, 1) for p in line] for line in piece]
    up = [[pltpu.roll(p, 7, 0) for p in line] for line in piece]
    down = [[pltpu.roll(p, 1, 0) for p in line] for line in piece]

    def outer(line, j):
        return 0.0 if line is None else jnp.broadcast_to(line[:, 128 * j : 128 * j + 128], (8, 128))

    lines = []
    for t in range(tiles):
        parts = []
        for j in range(columns):
            above = jnp.where(lane == 127, left[t][j + 1] if j + 1 < columns else 0.0, left[t][j])
            below = jnp.where(lane == 0, right[t][j - 1] if j > 0 else 0.0, right[t][j])
            after = jnp.where(row == 7, up[t + 1][j] if t + 1 < tiles else outer(high, j), up[t][j])
            before = jnp.where(row == 0, down[t - 1][j] if t > 0 else outer(low, j), down[t][j])
            parts.append((above + below) + (after + before))
        lines.append(jnp.concatenate(parts, axis=1))
    return jnp.concatenate(lines, axis=0)


def outer_rows(low, high):
    row = iota((8, 512), 0)
    first = jnp.where(row == 0, jnp.broadcast_to(low, row.shape), 0.0)
    last = jnp.where(row == 7, jnp.broadcast_to(high, row.shape), 0.0)
    return jnp.concatenate([first, last], axis=0)


def dot(left, right):
    return lax.dot_general(
        left,
        right,
        (((1,), (0,)), ((), ())),
        precision=lax.Precision.HIGHEST,
        preferred_element_type=F32,
    )


def group_lanes(depth):
    return (iota((depth, depth // 4), 0) // 4 == iota((depth, depth // 4), 1)).astype(F32)


def spread_lanes(rows):
    count, lanes = rows.shape
    pad = -count % 8
    if pad:
        rows = jnp.concatenate([rows, jnp.zeros((pad, lanes), F32)], axis=0)
    parts = []
    for j in range(4):
        index = iota(rows.shape, 1) // 4 + (lanes // 4) * j
        parts.append(jnp.take_along_axis(rows, index, axis=1, mode="promise_in_bounds"))
    return jnp.concatenate(parts, axis=1)[:count]


def spread_rows(ref, plane, start):
    row = iota((16, 128), 0) // 4
    value = jnp.zeros((16, 128), F32)
    for q in range(4):
        value = jnp.where(row == q, jnp.broadcast_to(ref[plane, start + q : start + q + 1, :], (16, 128)), value)
    return value


def spread_planes(ref, plane, column):
    row = iota((16, 128), 0) // 4
    value = jnp.zeros((16, 128), F32)
    for q in range(4):
        value = jnp.where(row == q, jnp.broadcast_to(ref[plane + q, column : column + 1, :], (16, 128)), value)
    return value


def solution(mesh):
    nx, ny = mesh.shape["gx"], mesh.shape["gy"]
    assert nx % 2 == 0 and ny % 2 == 0 and ny & (ny - 1) == 0
    axes = ("gx", "gy")

    def where_am_i():
        x, y = lax.axis_index("gx"), lax.axis_index("gy")
        return x, y, x % 2 == 0, y % 2 == 0

    def look_up(table, ids):
        spare = jnp.zeros((1, 128 - table.shape[1]), F32)
        row = jnp.broadcast_to(jnp.concatenate([table, spare], axis=1), (16, 128))
        parts = [
            jnp.take_along_axis(row, ids[:, 128 * j : 128 * (j + 1)], axis=1, mode="promise_in_bounds") for j in range(4)
        ]
        return jnp.concatenate(parts, axis=1)

    def first_of(source, reaction, kinds, ids, mask, table):
        a = reaction + jnp.where(kinds == 1, WALL_PENALTY, jnp.where(kinds == 2, INFLOW_PENALTY, 0.0))
        diagonal = 6.0 + a
        scale = OMEGA / diagonal
        return (source + mask.astype(F32) * look_up(table, ids)) * scale, scale, diagonal, a

    def faces(*refs):
        inputs, thrust, messages, buffers, table, sems, table_sem = (
            refs[:5], refs[5], refs[6:10], refs[10:15], refs[15], refs[16], refs[17]
        )
        core, chip, row, odd = messages
        _, _, x_even, y_even = where_am_i()
        near, far = jnp.where(x_even, 15, 0), jnp.where(x_even, 0, 15)
        moves = [pltpu.make_async_copy(thrust, table, table_sem)]
        for i, (hbm, buffer) in enumerate(zip(inputs, buffers)):
            for j, part in enumerate((hbm.at[:, 0, :], hbm.at[:, 15, :], hbm.at[far], hbm.at[near])):
                moves.append(pltpu.make_async_copy(part, buffer.at[j], sems.at[i, j]))
        for move in moves:
            move.start()
        for move in moves:
            move.wait()
        (low, g_low), (high, g_high), (f_far, _), (f_near, _) = (
            first_of(*(buffer[j] for buffer in buffers), table[...])[:2] for j in range(4)
        )
        put(row, 0, jnp.where(y_even, high, low))
        put(row, 64, jnp.where(y_even, g_high, g_low))
        put(odd, 0, jnp.where(y_even, low, high))
        put(odd, 64, jnp.where(y_even, g_low, g_high))
        put(chip, 0, f_far)
        put(core, 0, f_near)

    def set_up(source, reaction, kind, disk_id, disk_mask, table, f, g, d, absorb, inner, rows, V):
        for k in range(4):
            total = jnp.zeros((16, 512), F32)
            for x in range(4 * k, 4 * k + 4):
                f[x], g[x], d[x], a = first_of(source[x], reaction[x], kind[x], disk_id[x], disk_mask[x], table[...])
                total = total + a
            V[16 * k : 16 * k + 16, :] = total
        out, src = iota((16, 64), 0), iota((16, 64), 1)
        pick = ((src // 16 == out % 4) & ((src % 16) // 4 == out // 4)).astype(F32)
        absorb[...] = dot(dot(pick, V[...]), group_lanes(512))
        for x in range(16):
            total = beside(f[x])
            if x > 0:
                total = total + f[x - 1]
            if x < 15:
                total = total + f[x + 1]
            value = 1.2 * f[x] + g[x] * total
            inner[x] = value
            for at, part in enumerate((value[0:1, :], value[15:16, :], g[x, 0:1, :], g[x, 15:16, :])):
                rows[at, x : x + 1, :] = part

    def halo_x(core, chip, row, x, x_even, chip_row=None):
        a, b = get(core, row, 16, 512), get(chip, row if chip_row is None else chip_row, 16, 512)
        left = jnp.where(x > 0, jnp.where(x_even, b, a), 0.0)
        right = jnp.where(x < nx - 1, jnp.where(x_even, a, b), 0.0)
        return left, right

    def halo_y(row, odd, at, y, y_even):
        a, b = get(row, at, 16, 512), get(odd, at, 16, 512)
        low = jnp.where(y > 0, jnp.where(y_even, b, a), 0.0)
        high = jnp.where(y < ny - 1, jnp.where(y_even, a, b), 0.0)
        return low, high

    def early(inner, g, rows, absorb, core, chip, row, odd, to_core, sums, y_faces, lo, hi):
        x_at, y_at, x_even, y_even = where_am_i()
        left, right = halo_x(core, chip, 0, x_at, x_even)
        lo[...], hi[...] = halo_y(row, odd, 0, y_at, y_even)

        def second_at(x, outer=0.0):
            return inner[x] + g[x] * (outer_rows(lo[pl.ds(x, 1), :], hi[pl.ds(x, 1), :]) + outer)

        s_first, s_last = second_at(0, left), second_at(15, right)
        row_of = iota((16, 512), 0)
        for at, (outer, line) in enumerate(((lo, slice(0, 1)), (hi, slice(15, 16)))):
            first, last = (jnp.broadcast_to(side[line, :], (16, 512)) for side in (left, right))
            more = jnp.where(row_of == 0, first, jnp.where(row_of == 15, last, 0.0))
            y_faces[16 * at : 16 * at + 16, :] = rows[at] + rows[2 + at] * (outer[...] + more)
        out, src = iota((16, 64), 0), iota((16, 64), 1)
        pick = ((out // 4 == src // 16) & (out % 4 == (src % 16) // 4)).astype(F32)
        sides = jnp.concatenate([s_first, s_last, y_faces[...]], axis=0)
        sums[...] = dot(dot(pick, sides), group_lanes(512))
        put(to_core, 0, jnp.where(x_even, s_last, s_first))
        put(to_core, 64, second_at(jnp.where(x_even, 14, 1)))
        put(to_core, 128, g[jnp.where(x_even, 15, 0)])
        to_core[192:196, :] = jnp.where(x_even, sums[4:8, :], sums[0:4, :])
        to_core[196:200, :] = jnp.zeros((4, 128), F32)
        to_core[200:208, :] = sums[8:16, :]
        to_core[208:224, :] = absorb[...]

    def restrict(f, g, d, absorb, inner, sums, core, chip, row, odd, s, block, y_more, lo, hi, V):
        x_at, y_at, x_even, y_even = where_am_i()
        left, right = halo_x(core, chip, 0, x_at, x_even)
        lo[...], hi[...] = halo_y(row, odd, 0, y_at, y_even)
        for x in range(16):
            total = outer_rows(lo[x : x + 1, :], hi[x : x + 1, :])
            if x == 0:
                total = total + left
            if x == 15:
                total = total + right
            value = inner[x] + g[x] * total
            s[x] = value
            y_more[x : x + 1, :] = value[1:2, :]
            y_more[16 + x : 17 + x, :] = value[14:15, :]
        for k in range(4):
            total = jnp.zeros((16, 512), F32)
            for x in range(4 * k, 4 * k + 4):
                here = s[x]
                total = total + d[x] * (1.25 * f[x] - here)
                total = total + beside(here)
                if x > 0:
                    total = total + s[x - 1]
                if x < 15:
                    total = total + s[x + 1]
            V[16 * k : 16 * k + 16, :] = total
        out, src = iota((16, 64), 0), iota((16, 64), 1)
        pick = ((src // 16 == out % 4) & ((src % 16) // 4 == out // 4)).astype(F32)
        found = dot(dot(pick, V[...]), group_lanes(512))
        for cy in range(4):
            block[8 * cy : 8 * cy + 4, :] = found[4 * cy : 4 * cy + 4, :]
            block[8 * cy + 4 : 8 * cy + 8, :] = absorb[4 * cy : 4 * cy + 4, :]
        block[32:40, :] = sums[8:16, :]

    def to_chip_kernel(block, sums, absorb, core, s, g, y_faces, y_more, mine, to_chip, to_row, to_odd):
        _, _, x_even, y_even = where_am_i()
        mine[...] = block[...]
        face = core[192:200, :]
        for cy in range(4):
            line = face[cy : cy + 1, :]
            a, b = 8 * cy, 8 * cy + 3
            mine[a : a + 1, :] = block[a : a + 1, :] + jnp.where(x_even, 0.0, line)
            mine[b : b + 1, :] = block[b : b + 1, :] + jnp.where(x_even, line, 0.0)
        put(to_chip, 0, s[jnp.where(x_even, 0, 15)])
        to_chip[64:104, :] = mine[...]
        to_chip[104:108, :] = jnp.where(x_even, sums[0:4, :], sums[4:8, :])
        to_chip[108:112, :] = jnp.zeros((4, 128), F32)
        for at, ref in enumerate((y_faces, y_more)):
            a, b = ref[0:16, :], ref[16:32, :]
            put(to_row, 64 * at, jnp.where(y_even, b, a))
            put(to_odd, 64 * at, jnp.where(y_even, a, b))
        first_line, last_line = (
            jnp.concatenate([core[16 * j + line : 16 * j + line + 1, :] for j in range(4)], axis=0) for line in (0, 15)
        )
        for ref, corner in (
            (to_row, jnp.where(y_even, last_line, first_line)),
            (to_odd, jnp.where(y_even, first_line, last_line)),
        ):
            ref[128:144, :] = absorb[...]
            ref[144:160, :] = core[208:224, :]
            ref[160:168, :] = sums[8:16, :]
            ref[168:176, :] = core[200:208, :]
            ref[176:180, :] = corner
            ref[180:FACES, :] = jnp.zeros((FACES - 180, 128), F32)

    def from_chip_kernel(mine, sums, chip, s, g, full, beyond, more):
        x_at, _, x_even, _ = where_am_i()
        has = jnp.where(x_even, x_at > 0, x_at < nx - 1)
        full[...] = mine[...]
        beyond[...] = chip[64:104, :]
        mine_face = jnp.where(x_even, sums[0:4, :], sums[4:8, :])
        face = chip[104:112, :]
        for cy in range(4):
            line = jnp.where(has, face[cy : cy + 1, :], 0.0)
            own = mine_face[cy : cy + 1, :]
            a, b = 8 * cy, 8 * cy + 3
            full[a : a + 1, :] = mine[a : a + 1, :] + jnp.where(x_even, line, 0.0)
            full[b : b + 1, :] = mine[b : b + 1, :] + jnp.where(x_even, 0.0, line)
            beyond[a : a + 1, :] = chip[64 + a : 65 + a, :] + jnp.where(x_even, 0.0, own)
            beyond[b : b + 1, :] = chip[64 + b : 65 + b, :] + jnp.where(x_even, own, 0.0)
        put(more, 0, s[jnp.where(x_even, 1, 14)])
        put(more, 64, g[jnp.where(x_even, 0, 15)])
        more[128:MORE, :] = jnp.zeros((MORE - 128, 128), F32)

    def window_kernel(full, beyond, core, chip, s_core, window, short):
        x_at, _, x_even, _ = where_am_i()
        mid = full[...]
        a, b = core[...], beyond[...]
        left, right = jnp.where(x_even, b, a), jnp.where(x_even, a, b)
        for at, block in enumerate((left, mid, right)):
            for cy in range(4):
                window[24 * cy + 4 * at : 24 * cy + 4 * at + 4, :] = block[8 * cy : 8 * cy + 4, :]
                window[24 * cy + 12 + 4 * at : 24 * cy + 16 + 4 * at, :] = block[8 * cy + 4 : 8 * cy + 8, :]
            window[96 + 4 * at : 100 + 4 * at, :] = block[32:36, :]
            window[108 + 4 * at : 112 + 4 * at, :] = block[36:40, :]
        for at, line in enumerate((0, 15)):
            near = jnp.concatenate([s_core[16 * j + line : 16 * j + line + 1, :] for j in range(4)], axis=0)
            far = jnp.concatenate([chip[16 * j + line : 16 * j + line + 1, :] for j in range(4)], axis=0)
            window[120 + 4 * at : 124 + 4 * at, :] = jnp.where(x_at > 0, jnp.where(x_even, far, near), 0.0)
            window[128 + 4 * at : 132 + 4 * at, :] = jnp.where(x_at < nx - 1, jnp.where(x_even, near, far), 0.0)
            short[72 + 4 * at : 76 + 4 * at, :] = far
        for cy in range(4):
            for at, block in enumerate((left, mid, right)):
                short[12 * cy + 4 * at : 12 * cy + 4 * at + 4, :] = block[8 * cy : 8 * cy + 4, :]
            short[48 + 4 * cy : 52 + 4 * cy, :] = beyond[8 * cy + 4 : 8 * cy + 8, :]
        short[64:72, :] = beyond[32:40, :]

    planes = 4 * ny
    short_steps = (1, 3) if ny == 4 else (1,)

    def prepare(f, g, s, a_core, a_chip, a_row, a_odd, s_core, s_chip, s_more, s_row, s_odd, u, u_low, u_high, g_x, g_y, edge):
        x_at, y_at, x_even, y_even = where_am_i()
        s_left, s_right = halo_x(s_core, s_chip, 0, x_at, x_even)
        s_left2, s_right2 = halo_x(s_core, s_more, 64, x_at, x_even, 0)
        f_left, f_right = halo_x(a_core, a_chip, 0, x_at, x_even)
        g_x[0], g_x[1] = halo_x(s_core, s_more, 128, x_at, x_even, 64)
        y1 = halo_y(s_row, s_odd, 0, y_at, y_even)
        y2 = halo_y(s_row, s_odd, 64, y_at, y_even)
        f_y = halo_y(a_row, a_odd, 0, y_at, y_even)
        g_y[0], g_y[1] = halo_y(a_row, a_odd, 64, y_at, y_even)
        u[0] = 0.2 * s_left + f_left + g_x[0] * (s_left2 + s[0] + beside(s_left))
        u[17] = 0.2 * s_right + f_right + g_x[1] * (s_right2 + s[15] + beside(s_right))
        for x in range(16):
            here = s[x]
            total = (s[x - 1] if x > 0 else s_left) + (s[x + 1] if x < 15 else s_right)
            total = total + beside(here, y1[0][x : x + 1, :], y1[1][x : x + 1, :])
            u[x + 1] = 0.2 * here + f[x] + g[x] * total
            edge[0, x : x + 1, :] = here[0:1, :]
            edge[1, x : x + 1, :] = here[15:16, :]
        for at, out in enumerate((u_low, u_high)):
            out[...] = 0.2 * y1[at] + f_y[at] + g_y[at] * (y2[at] + edge[at] + beside(y1[at]))

    def finish(*refs):
        f, g, u, u_low, u_high, g_x, g_y, s_row, s_odd = refs[:9]
        windows = refs[9 : 9 + ny][::-1]
        pressure, coarse = refs[9 + ny : 11 + ny]
        every, res, diag, inv, one, two, sol, C, U, ul, uh, result, slab_out, sems = refs[11 + ny :]
        x_at, y_at, x_even, y_even = where_am_i()
        for step, window in enumerate(windows):
            there = jnp.bitwise_xor(y_at, step)
            if step not in short_steps:
                every[there] = window[...]
                continue
            faces_of = s_row if step == 1 else s_odd

            def three(at, own, core, chip):
                every[there, at : at + 4, :] = jnp.where(x_even, chip, core)
                if own is not None:
                    every[there, at + 4 : at + 8, :] = own
                every[there, at + 8 : at + 12, :] = jnp.where(x_even, core, chip)

            for cy in range(4):
                at = 4 * cy
                every[there, 24 * cy : 24 * cy + 12, :] = window[12 * cy : 12 * cy + 12, :]
                three(
                    24 * cy + 12, faces_of[128 + at : 132 + at, :], faces_of[144 + at : 148 + at, :],
                    window[48 + at : 52 + at, :],
                )
            for at in (0, 4):
                three(
                    96 + 3 * at, faces_of[160 + at : 164 + at, :], faces_of[168 + at : 172 + at, :],
                    window[64 + at : 68 + at, :],
                )
                three(120 + at, None, faces_of[176:180, :], window[72 + at : 76 + at, :])

        row = iota((16, 128), 0)
        valid = ((row >= 4) | (x_at > 0)) & ((row < 8) | (x_at < nx - 1)) & (row < 12)
        blank = jnp.zeros((4, 128), F32)

        def twelve(value):
            return jnp.concatenate([value, blank], axis=0)

        centre = (CHEB_HIGH + CHEB_LOW) / 2.0
        half_range = (CHEB_HIGH - CHEB_LOW) / 2.0
        aspect = centre / half_range
        factor = 1.0 / aspect
        empty = jnp.zeros((16, 128), F32)
        for ref in (one, two, sol):
            ref[0] = empty
            ref[planes + 1] = empty
        for at in range(ny):
            for cy in range(4):
                plane = 4 * at + cy
                value = every[at, 24 * cy : 24 * cy + 12, :]
                if cy == 0 and at > 0:
                    value = value + every[at - 1, 108:120, :]
                if cy == 3 and at < ny - 1:
                    value = value + every[at + 1, 96:108, :]
                value = jnp.where(valid, twelve(value), 0.0)
                centre_value = 6.0 + twelve(every[at, 24 * cy + 12 : 24 * cy + 24, :]) / 16.0
                inverse = jnp.where(valid, 1.0 / (16.0 * centre_value), 0.0)
                res[plane] = value
                diag[plane] = centre_value
                inv[plane] = inverse
                direction = inverse * value / centre
                one[plane + 1] = direction
                sol[plane + 1] = direction
        now, later = one, two
        for number in range(1, SWEEPS):
            factor_next = 1.0 / (2.0 * aspect - factor)
            keep, gain = factor_next * factor, 2.0 * factor_next / half_range

            lane = iota((16, 128), 1)
            for plane in range(planes):
                here = now[plane + 1]
                total = now[plane] + now[plane + 2]
                total = total + pltpu.roll(here, 15, 0) + pltpu.roll(here, 1, 0)
                total = total + jnp.where(lane == 127, 0.0, pltpu.roll(here, 127, 1))
                total = total + jnp.where(lane == 0, 0.0, pltpu.roll(here, 1, 1))
                residual = res[plane] - 16.0 * (diag[plane] * here - total)
                res[plane] = residual
                direction = keep * here + gain * inv[plane] * residual
                later[plane + 1] = direction
                sol[plane + 1] = sol[plane + 1] + direction
            now, later = later, now
            factor = factor_next
        for plane in range(planes):
            for cx in range(4):
                slab_out[cx, plane : plane + 1, :] = sol[plane + 1, 4 + cx : 5 + cx, :]
        moves = [pltpu.make_async_copy(slab_out, coarse, sems.at[8])]
        moves[0].start()

        first_plane = 4 * y_at + 1
        below, above = first_plane - 1, first_plane + 4
        for at in range(6):
            C[at] = spread_lanes(spread_planes(sol, first_plane, 3 + at))
        outside = [[spread_lanes(sol[plane, 3 + at : 4 + at, :]) for at in range(6)] for plane in (below, above)]
        before, after = jnp.maximum(y_at - 1, 0), jnp.minimum(y_at + 1, ny - 1)
        corners = []
        for who, inside, line in ((before, y_at > 0, 1), (after, y_at < ny - 1, 0)):
            for base, there in ((0, x_at > 0), (2, x_at < nx - 1)):
                corner = jnp.concatenate(
                    [every[who, pl.ds(120 + 4 * (base + line) + j, 1), :] for j in range(4)], axis=1
                )
                corners.append(jnp.where(inside & there, corner, 0.0))
        edge_row = iota((16, 512), 0)

        def ends(first, last):
            first, last = (jnp.broadcast_to(line, (16, 512)) for line in (first, last))
            return jnp.where(edge_row == 0, first, jnp.where(edge_row == 15, last, 0.0))

        for at in range(6):
            here = C[at]
            around = beside(here, outside[0][at], outside[1][at])
            fifth_of = 0.2 * here
            if at == 0:
                U[0] = u[0] + fifth_of + g_x[0] * (around + here + C[1] + ends(corners[0], corners[2]))
            elif at == 5:
                U[17] = u[17] + fifth_of + g_x[1] * (around + here + C[4] + ends(corners[1], corners[3]))
            else:
                inner = around + 2.0 * here
                sides = [around + here + C[at - 1], inner, inner, around + here + C[at + 1]]
                for q in range(4):
                    x = 4 * (at - 1) + q
                    U[x + 1] = u[x + 1] + fifth_of + g[x] * sides[q]
        for at, (part, out, plane, inside) in enumerate(
            ((u_low, ul, below, first_plane), (u_high, uh, above, first_plane + 3))
        ):
            beyond = spread_lanes(spread_rows(sol, plane, 4))
            edge = spread_lanes(spread_rows(sol, inside, 4))
            around = beside(beyond, outside[at][0], outside[at][5])
            total = beyond + edge + around + ends(corners[2 * at], corners[2 * at + 1])
            out[...] = part[...] + 0.2 * beyond + g_y[at] * total

        for x in range(16):
            here = U[x + 1]
            total = U[x] + U[x + 2] + beside(here, ul[x : x + 1, :], uh[x : x + 1, :])
            result[x] = 0.2 * here + f[x] + g[x] * total
            if x % 2 == 1:
                part = pl.ds(x - 1, 2)
                moves.append(pltpu.make_async_copy(result.at[part], pressure.at[part], sems.at[x // 2]))
                moves[-1].start()
        for move in moves:
            move.wait()

    slab, field, long = (16, 512), (16, 16, 512), (18, 16, 512)
    core_pairs, chip_pairs = pairs_core(nx, ny), pairs_chip(nx, ny)
    row_pairs = [pairs_row(nx, ny, step) for step in range(1, ny)]
    odd_pairs = pairs_odd(nx, ny)
    inner_pairs = [
        (a, b) if 0 < a % ny < ny - 1 else (a, ((a // ny) ^ 1) * ny + a % ny) for a, b in odd_pairs
    ]

    def swap(array, pairs):
        return lax.ppermute(array, axes, pairs)

    def local(source, reaction, boundary_kind, disk_id, disk_mask, thrust):
        inputs = (source, reaction, boundary_kind, disk_id, disk_mask, thrust.reshape(1, -1))
        some = (4, 16, 512)
        core, chip, row, odd = call(
            faces,
            [(64, 128), (64, 128), (128, 128), (128, 128)],
            *(pltpu.with_memory_space_constraint(array, pltpu.HBM) for array in inputs),
            in_specs=[HBM] * 6,
            scratch=[some, some]
            + [pltpu.VMEM(some, jnp.int32)] * 3
            + [(1, thrust.shape[0]), pltpu.SemaphoreType.DMA((5, 4)), pltpu.SemaphoreType.DMA(())],
            name="faces",
        )
        a_core, a_chip = swap(core, core_pairs), swap(chip, chip_pairs)
        a_odd, a_row = swap(odd, inner_pairs), swap(row, row_pairs[0])
        f, g, d, absorb, inner, rows = call(
            set_up, [field, field, field, (16, 128), field, (4, 16, 512)], *inputs, scratch=[(64, 512)], name="set_up"
        )
        a_odd, a_row, a_chip, a_core, f, g, d, absorb, inner, rows = lax.optimization_barrier(
            (a_odd, a_row, a_chip, a_core, f, g, d, absorb, inner, rows)
        )
        to_core, sums, y_faces = call(
            early,
            [(224, 128), (16, 128), (32, 512)],
            inner, g, rows, absorb, a_core, a_chip, a_row, a_odd,
            scratch=[slab] * 2,
            name="early",
        )
        s_core = swap(to_core, core_pairs)
        s, block, y_more = call(
            restrict,
            [field, (40, 128), (32, 512)],
            f, g, d, absorb, inner, sums, a_core, a_chip, a_row, a_odd,
            scratch=[slab, slab, (64, 512)],
            name="restrict",
        )
        mine, to_chip, to_row, to_odd = call(
            to_chip_kernel,
            [(40, 128), (112, 128), (FACES, 128), (FACES, 128)],
            block, sums, absorb, s_core, s, g, y_faces, y_more,
            name="to_chip",
        )
        s_chip = swap(to_chip, chip_pairs)
        s_row, s_odd = swap(to_row, row_pairs[0]), swap(to_odd, odd_pairs)
        full, beyond, more = call(
            from_chip_kernel, [(40, 128), (40, 128), (MORE, 128)], mine, sums, s_chip, s, g, name="from_chip"
        )
        c_core, s_more = swap(full, core_pairs), swap(more, chip_pairs)
        window, short = call(
            window_kernel, [(136, 128), (80, 128)], full, beyond, c_core, s_chip, s_core, name="window"
        )
        windows = [window] + [
            swap(short if step in short_steps else window, row_pairs[step - 1]) for step in range(1, ny)
        ]
        prepared = call(
            prepare,
            [long, slab, slab, (2, 16, 512), (2, 16, 512)],
            f, g, s, a_core, a_chip, a_row, a_odd, s_core, s_chip, s_more, s_row, s_odd,
            scratch=[(2, 16, 512)],
            name="prepare",
        )
        pressure, coarse = call(
            finish,
            [field, (4, planes, 128)],
            f, g, *prepared, s_row, s_odd, *windows[::-1],
            scratch=[(ny, 136, 128)]
            + [(planes, 16, 128)] * 3
            + [(planes + 2, 16, 128)] * 3
            + [(6, 16, 512), long, slab, slab, field, (4, planes, 128), pltpu.SemaphoreType.DMA((9,))],
            out_specs=[HBM, HBM],
            name="finish",
        )
        return pressure, coarse

    spec = P("gx", "gy", None)
    return jax.shard_map(
        local,
        mesh=mesh,
        in_specs=(spec, spec, spec, spec, spec, P()),
        out_specs=(spec, P("gx", None, None)),
        check_vma=False,
    )
```

```python
import jax
import jax.numpy as jnp
from jax import lax
from jax.experimental import pallas as pl
from jax.experimental.pallas import tpu as pltpu
from jax.sharding import PartitionSpec as P

SWEEPS = 4
OMEGA = 0.8
WALL_PENALTY = 0.4
INFLOW_PENALTY = 0.2
CHEB_LOW = 0.1
CHEB_HIGH = 2.0
F32 = jnp.float32
VMEM = pl.BlockSpec(memory_space=pltpu.VMEM)


HBM = pl.BlockSpec(memory_space=pltpu.HBM)
MORE = 152
FACES = 184


def call(kernel, outs, *args, scratch=(), name=None, in_specs=None, out_specs=None):
    return pl.pallas_call(
        kernel,
        out_shape=[jax.ShapeDtypeStruct(s, F32) for s in outs],
        in_specs=in_specs or [VMEM] * len(args),
        out_specs=out_specs or [VMEM] * len(outs),
        scratch_shapes=[pltpu.VMEM(s, F32) if isinstance(s, tuple) else s for s in scratch],
        compiler_params=pltpu.CompilerParams(vmem_limit_bytes=16 << 20),
        name=name,
    )(*args)


def pairs_core(nx, ny):
    return [(x * ny + y, (x ^ 1) * ny + y) for x in range(nx) for y in range(ny)]


def pairs_chip(nx, ny):
    found = []
    for x in range(nx):
        for y in range(ny):
            if x in (0, nx - 1):
                found.append((x * ny + y, x * ny + (y ^ (ny // 2))))
            else:
                found.append((x * ny + y, (x + 1 if x % 2 else x - 1) * ny + y))
    return found


def pairs_row(nx, ny, step):
    return [(x * ny + y, x * ny + (y ^ step)) for x in range(nx) for y in range(ny)]


def pairs_odd(nx, ny):
    return [
        (x * ny + y, x * ny + (y + 1 if y % 2 else y - 1) % ny) for x in range(nx) for y in range(ny)
    ]


def put(ref, row, slab):
    rows = slab.shape[0]
    for j in range(slab.shape[1] // 128):
        ref[row + rows * j : row + rows * (j + 1), :] = slab[:, 128 * j : 128 * (j + 1)]


def get(ref, row, rows, width):
    return jnp.concatenate(
        [ref[row + rows * j : row + rows * (j + 1), :] for j in range(width // 128)], axis=1
    )


def iota(shape, dim):
    return lax.broadcasted_iota(jnp.int32, shape, dim)


def beside_z(slab):
    depth = slab.shape[1]
    lane = iota(slab.shape, 1)
    above = jnp.where(lane == depth - 1, 0.0, pltpu.roll(slab, depth - 1, 1))
    below = jnp.where(lane == 0, 0.0, pltpu.roll(slab, 1, 1))
    return above + below


def beside(slab, low=None, high=None):
    rows, depth = slab.shape
    tiles, columns = rows // 8, depth // 128
    lane, row = iota((8, 128), 1), iota((8, 128), 0)
    piece = [[slab[8 * t : 8 * t + 8, 128 * j : 128 * j + 128] for j in range(columns)] for t in range(tiles)]
    left = [[pltpu.roll(p, 127, 1) for p in line] for line in piece]
    right = [[pltpu.roll(p, 1, 1) for p in line] for line in piece]
    up = [[pltpu.roll(p, 7, 0) for p in line] for line in piece]
    down = [[pltpu.roll(p, 1, 0) for p in line] for line in piece]

    def outer(line, j):
        return 0.0 if line is None else jnp.broadcast_to(line[:, 128 * j : 128 * j + 128], (8, 128))

    lines = []
    for t in range(tiles):
        parts = []
        for j in range(columns):
            above = jnp.where(lane == 127, left[t][j + 1] if j + 1 < columns else 0.0, left[t][j])
            below = jnp.where(lane == 0, right[t][j - 1] if j > 0 else 0.0, right[t][j])
            after = jnp.where(row == 7, up[t + 1][j] if t + 1 < tiles else outer(high, j), up[t][j])
            before = jnp.where(row == 0, down[t - 1][j] if t > 0 else outer(low, j), down[t][j])
            parts.append((above + below) + (after + before))
        lines.append(jnp.concatenate(parts, axis=1))
    return jnp.concatenate(lines, axis=0)


def outer_rows(low, high):
    row = iota((8, 512), 0)
    first = jnp.where(row == 0, jnp.broadcast_to(low, row.shape), 0.0)
    last = jnp.where(row == 7, jnp.broadcast_to(high, row.shape), 0.0)
    return jnp.concatenate([first, last], axis=0)


def dot(left, right):
    return lax.dot_general(
        left,
        right,
        (((1,), (0,)), ((), ())),
        precision=lax.Precision.HIGHEST,
        preferred_element_type=F32,
    )


def group_lanes(depth):
    return (iota((depth, depth // 4), 0) // 4 == iota((depth, depth // 4), 1)).astype(F32)


def spread_lanes(rows):
    count, lanes = rows.shape
    pad = -count % 8
    if pad:
        rows = jnp.concatenate([rows, jnp.zeros((pad, lanes), F32)], axis=0)
    parts = []
    for j in range(4):
        index = iota(rows.shape, 1) // 4 + (lanes // 4) * j
        parts.append(jnp.take_along_axis(rows, index, axis=1, mode="promise_in_bounds"))
    return jnp.concatenate(parts, axis=1)[:count]


def spread_rows(ref, plane, start):
    row = iota((16, 128), 0) // 4
    value = jnp.zeros((16, 128), F32)
    for q in range(4):
        value = jnp.where(row == q, jnp.broadcast_to(ref[plane, start + q : start + q + 1, :], (16, 128)), value)
    return value


def spread_planes(ref, plane, column):
    row = iota((16, 128), 0) // 4
    value = jnp.zeros((16, 128), F32)
    for q in range(4):
        value = jnp.where(row == q, jnp.broadcast_to(ref[plane + q, column : column + 1, :], (16, 128)), value)
    return value


def solution(mesh):
    nx, ny = mesh.shape["gx"], mesh.shape["gy"]
    assert nx % 2 == 0 and ny % 2 == 0 and ny & (ny - 1) == 0
    axes = ("gx", "gy")

    def where_am_i():
        x, y = lax.axis_index("gx"), lax.axis_index("gy")
        return x, y, x % 2 == 0, y % 2 == 0

    def look_up(table, ids):
        spare = jnp.zeros((1, 128 - table.shape[1]), F32)
        row = jnp.broadcast_to(jnp.concatenate([table, spare], axis=1), (16, 128))
        parts = [
            jnp.take_along_axis(row, ids[:, 128 * j : 128 * (j + 1)], axis=1, mode="promise_in_bounds") for j in range(4)
        ]
        return jnp.concatenate(parts, axis=1)

    def first_of(source, reaction, kinds, ids, mask, table):
        a = reaction + jnp.where(kinds == 1, WALL_PENALTY, jnp.where(kinds == 2, INFLOW_PENALTY, 0.0))
        diagonal = 6.0 + a
        scale = OMEGA / diagonal
        return (source + mask.astype(F32) * look_up(table, ids)) * scale, scale, diagonal, a

    def faces(*refs):
        inputs, thrust, messages, buffers, table, sems, table_sem = (
            refs[:5], refs[5], refs[6:10], refs[10:15], refs[15], refs[16], refs[17]
        )
        core, chip, row, odd = messages
        _, _, x_even, y_even = where_am_i()
        near, far = jnp.where(x_even, 15, 0), jnp.where(x_even, 0, 15)
        moves = [pltpu.make_async_copy(thrust, table, table_sem)]
        for i, (hbm, buffer) in enumerate(zip(inputs, buffers)):
            for j, part in enumerate((hbm.at[:, 0, :], hbm.at[:, 15, :], hbm.at[far], hbm.at[near])):
                moves.append(pltpu.make_async_copy(part, buffer.at[j], sems.at[i, j]))
        for move in moves:
            move.start()
        for move in moves:
            move.wait()
        (low, g_low), (high, g_high), (f_far, _), (f_near, _) = (
            first_of(*(buffer[j] for buffer in buffers), table[...])[:2] for j in range(4)
        )
        put(row, 0, jnp.where(y_even, high, low))
        put(row, 64, jnp.where(y_even, g_high, g_low))
        put(odd, 0, jnp.where(y_even, low, high))
        put(odd, 64, jnp.where(y_even, g_low, g_high))
        put(chip, 0, f_far)
        put(core, 0, f_near)

    def set_up(source, reaction, kind, disk_id, disk_mask, table, f, g, d, absorb, inner, rows, V):
        for k in range(4):
            total = jnp.zeros((16, 512), F32)
            for x in range(4 * k, 4 * k + 4):
                f[x], g[x], d[x], a = first_of(source[x], reaction[x], kind[x], disk_id[x], disk_mask[x], table[...])
                total = total + a
            V[16 * k : 16 * k + 16, :] = total
        out, src = iota((16, 64), 0), iota((16, 64), 1)
        pick = ((src // 16 == out % 4) & ((src % 16) // 4 == out // 4)).astype(F32)
        absorb[...] = dot(dot(pick, V[...]), group_lanes(512))
        for x in range(16):
            total = beside(f[x])
            if x > 0:
                total = total + f[x - 1]
            if x < 15:
                total = total + f[x + 1]
            value = 1.2 * f[x] + g[x] * total
            inner[x] = value
            for at, part in enumerate((value[0:1, :], value[15:16, :], g[x, 0:1, :], g[x, 15:16, :])):
                rows[at, x : x + 1, :] = part

    def halo_x(core, chip, row, x, x_even, chip_row=None):
        a, b = get(core, row, 16, 512), get(chip, row if chip_row is None else chip_row, 16, 512)
        left = jnp.where(x > 0, jnp.where(x_even, b, a), 0.0)
        right = jnp.where(x < nx - 1, jnp.where(x_even, a, b), 0.0)
        return left, right

    def halo_y(row, odd, at, y, y_even):
        a, b = get(row, at, 16, 512), get(odd, at, 16, 512)
        low = jnp.where(y > 0, jnp.where(y_even, b, a), 0.0)
        high = jnp.where(y < ny - 1, jnp.where(y_even, a, b), 0.0)
        return low, high

    def early(inner, g, rows, absorb, core, chip, row, odd, to_core, sums, y_faces, lo, hi):
        x_at, y_at, x_even, y_even = where_am_i()
        left, right = halo_x(core, chip, 0, x_at, x_even)
        lo[...], hi[...] = halo_y(row, odd, 0, y_at, y_even)

        def second_at(x, outer=0.0):
            return inner[x] + g[x] * (outer_rows(lo[pl.ds(x, 1), :], hi[pl.ds(x, 1), :]) + outer)

        s_first, s_last = second_at(0, left), second_at(15, right)
        row_of = iota((16, 512), 0)
        for at, (outer, line) in enumerate(((lo, slice(0, 1)), (hi, slice(15, 16)))):
            first, last = (jnp.broadcast_to(side[line, :], (16, 512)) for side in (left, right))
            more = jnp.where(row_of == 0, first, jnp.where(row_of == 15, last, 0.0))
            y_faces[16 * at : 16 * at + 16, :] = rows[at] + rows[2 + at] * (outer[...] + more)
        out, src = iota((16, 64), 0), iota((16, 64), 1)
        pick = ((out // 4 == src // 16) & (out % 4 == (src % 16) // 4)).astype(F32)
        sides = jnp.concatenate([s_first, s_last, y_faces[...]], axis=0)
        sums[...] = dot(dot(pick, sides), group_lanes(512))
        put(to_core, 0, jnp.where(x_even, s_last, s_first))
        put(to_core, 64, second_at(jnp.where(x_even, 14, 1)))
        put(to_core, 128, g[jnp.where(x_even, 15, 0)])
        to_core[192:196, :] = jnp.where(x_even, sums[4:8, :], sums[0:4, :])
        to_core[196:200, :] = jnp.zeros((4, 128), F32)
        to_core[200:208, :] = sums[8:16, :]
        to_core[208:224, :] = absorb[...]

    def restrict(f, g, d, absorb, inner, sums, core, chip, row, odd, s, block, y_more, lo, hi, V):
        x_at, y_at, x_even, y_even = where_am_i()
        left, right = halo_x(core, chip, 0, x_at, x_even)
        lo[...], hi[...] = halo_y(row, odd, 0, y_at, y_even)
        for x in range(16):
            total = outer_rows(lo[x : x + 1, :], hi[x : x + 1, :])
            if x == 0:
                total = total + left
            if x == 15:
                total = total + right
            value = inner[x] + g[x] * total
            s[x] = value
            y_more[x : x + 1, :] = value[1:2, :]
            y_more[16 + x : 17 + x, :] = value[14:15, :]
        for k in range(4):
            total = jnp.zeros((16, 512), F32)
            for x in range(4 * k, 4 * k + 4):
                here = s[x]
                total = total + d[x] * (1.25 * f[x] - here)
                total = total + beside(here)
                if x > 0:
                    total = total + s[x - 1]
                if x < 15:
                    total = total + s[x + 1]
            V[16 * k : 16 * k + 16, :] = total
        out, src = iota((16, 64), 0), iota((16, 64), 1)
        pick = ((src // 16 == out % 4) & ((src % 16) // 4 == out // 4)).astype(F32)
        found = dot(dot(pick, V[...]), group_lanes(512))
        for cy in range(4):
            block[8 * cy : 8 * cy + 4, :] = found[4 * cy : 4 * cy + 4, :]
            block[8 * cy + 4 : 8 * cy + 8, :] = absorb[4 * cy : 4 * cy + 4, :]
        block[32:40, :] = sums[8:16, :]

    def to_chip_kernel(block, sums, absorb, core, s, g, y_faces, y_more, mine, to_chip, to_row, to_odd):
        _, _, x_even, y_even = where_am_i()
        mine[...] = block[...]
        face = core[192:200, :]
        for cy in range(4):
            line = face[cy : cy + 1, :]
            a, b = 8 * cy, 8 * cy + 3
            mine[a : a + 1, :] = block[a : a + 1, :] + jnp.where(x_even, 0.0, line)
            mine[b : b + 1, :] = block[b : b + 1, :] + jnp.where(x_even, line, 0.0)
        put(to_chip, 0, s[jnp.where(x_even, 0, 15)])
        to_chip[64:104, :] = mine[...]
        to_chip[104:108, :] = jnp.where(x_even, sums[0:4, :], sums[4:8, :])
        to_chip[108:112, :] = jnp.zeros((4, 128), F32)
        for at, ref in enumerate((y_faces, y_more)):
            a, b = ref[0:16, :], ref[16:32, :]
            put(to_row, 64 * at, jnp.where(y_even, b, a))
            put(to_odd, 64 * at, jnp.where(y_even, a, b))
        first_line, last_line = (
            jnp.concatenate([core[16 * j + line : 16 * j + line + 1, :] for j in range(4)], axis=0) for line in (0, 15)
        )
        for ref, corner in (
            (to_row, jnp.where(y_even, last_line, first_line)),
            (to_odd, jnp.where(y_even, first_line, last_line)),
        ):
            ref[128:144, :] = absorb[...]
            ref[144:160, :] = core[208:224, :]
            ref[160:168, :] = sums[8:16, :]
            ref[168:176, :] = core[200:208, :]
            ref[176:180, :] = corner
            ref[180:FACES, :] = jnp.zeros((FACES - 180, 128), F32)

    def from_chip_kernel(mine, sums, chip, s, g, full, beyond, more):
        x_at, _, x_even, _ = where_am_i()
        has = jnp.where(x_even, x_at > 0, x_at < nx - 1)
        full[...] = mine[...]
        beyond[...] = chip[64:104, :]
        mine_face = jnp.where(x_even, sums[0:4, :], sums[4:8, :])
        face = chip[104:112, :]
        for cy in range(4):
            line = jnp.where(has, face[cy : cy + 1, :], 0.0)
            own = mine_face[cy : cy + 1, :]
            a, b = 8 * cy, 8 * cy + 3
            full[a : a + 1, :] = mine[a : a + 1, :] + jnp.where(x_even, line, 0.0)
            full[b : b + 1, :] = mine[b : b + 1, :] + jnp.where(x_even, 0.0, line)
            beyond[a : a + 1, :] = chip[64 + a : 65 + a, :] + jnp.where(x_even, 0.0, own)
            beyond[b : b + 1, :] = chip[64 + b : 65 + b, :] + jnp.where(x_even, own, 0.0)
        put(more, 0, s[jnp.where(x_even, 1, 14)])
        put(more, 64, g[jnp.where(x_even, 0, 15)])
        more[128:MORE, :] = jnp.zeros((MORE - 128, 128), F32)

    def window_kernel(full, beyond, core, chip, s_core, window, short):
        x_at, _, x_even, _ = where_am_i()
        mid = full[...]
        a, b = core[...], beyond[...]
        left, right = jnp.where(x_even, b, a), jnp.where(x_even, a, b)
        for at, block in enumerate((left, mid, right)):
            for cy in range(4):
                window[24 * cy + 4 * at : 24 * cy + 4 * at + 4, :] = block[8 * cy : 8 * cy + 4, :]
                window[24 * cy + 12 + 4 * at : 24 * cy + 16 + 4 * at, :] = block[8 * cy + 4 : 8 * cy + 8, :]
            window[96 + 4 * at : 100 + 4 * at, :] = block[32:36, :]
            window[108 + 4 * at : 112 + 4 * at, :] = block[36:40, :]
        for at, line in enumerate((0, 15)):
            near = jnp.concatenate([s_core[16 * j + line : 16 * j + line + 1, :] for j in range(4)], axis=0)
            far = jnp.concatenate([chip[16 * j + line : 16 * j + line + 1, :] for j in range(4)], axis=0)
            window[120 + 4 * at : 124 + 4 * at, :] = jnp.where(x_at > 0, jnp.where(x_even, far, near), 0.0)
            window[128 + 4 * at : 132 + 4 * at, :] = jnp.where(x_at < nx - 1, jnp.where(x_even, near, far), 0.0)
            short[72 + 4 * at : 76 + 4 * at, :] = far
        for cy in range(4):
            for at, block in enumerate((left, mid, right)):
                short[12 * cy + 4 * at : 12 * cy + 4 * at + 4, :] = block[8 * cy : 8 * cy + 4, :]
            short[48 + 4 * cy : 52 + 4 * cy, :] = beyond[8 * cy + 4 : 8 * cy + 8, :]
        short[64:72, :] = beyond[32:40, :]

    planes = 4 * ny
    short_steps = (1, 3) if ny == 4 else (1,)

    def prepare(f, g, s, a_core, a_chip, a_row, a_odd, s_core, s_chip, s_more, s_row, s_odd, u, u_low, u_high, g_x, g_y, edge):
        x_at, y_at, x_even, y_even = where_am_i()
        s_left, s_right = halo_x(s_core, s_chip, 0, x_at, x_even)
        s_left2, s_right2 = halo_x(s_core, s_more, 64, x_at, x_even, 0)
        f_left, f_right = halo_x(a_core, a_chip, 0, x_at, x_even)
        g_x[0], g_x[1] = halo_x(s_core, s_more, 128, x_at, x_even, 64)
        y1 = halo_y(s_row, s_odd, 0, y_at, y_even)
        y2 = halo_y(s_row, s_odd, 64, y_at, y_even)
        f_y = halo_y(a_row, a_odd, 0, y_at, y_even)
        g_y[0], g_y[1] = halo_y(a_row, a_odd, 64, y_at, y_even)
        u[0] = 0.2 * s_left + f_left + g_x[0] * (s_left2 + s[0] + beside(s_left))
        u[17] = 0.2 * s_right + f_right + g_x[1] * (s_right2 + s[15] + beside(s_right))
        for x in range(16):
            here = s[x]
            total = (s[x - 1] if x > 0 else s_left) + (s[x + 1] if x < 15 else s_right)
            total = total + beside(here, y1[0][x : x + 1, :], y1[1][x : x + 1, :])
            u[x + 1] = 0.2 * here + f[x] + g[x] * total
            edge[0, x : x + 1, :] = here[0:1, :]
            edge[1, x : x + 1, :] = here[15:16, :]
        for at, out in enumerate((u_low, u_high)):
            out[...] = 0.2 * y1[at] + f_y[at] + g_y[at] * (y2[at] + edge[at] + beside(y1[at]))

    def finish(*refs):
        f, g, u, u_low, u_high, g_x, g_y, s_row, s_odd = refs[:9]
        windows = refs[9 : 9 + ny][::-1]
        pressure, coarse = refs[9 + ny : 11 + ny]
        every, res, diag, inv, one, two, sol, C, U, ul, uh, result, slab_out, sems = refs[11 + ny :]
        x_at, y_at, x_even, y_even = where_am_i()
        for step, window in enumerate(windows):
            there = jnp.bitwise_xor(y_at, step)
            if step not in short_steps:
                every[there] = window[...]
                continue
            faces_of = s_row if step == 1 else s_odd

            def three(at, own, core, chip):
                every[there, at : at + 4, :] = jnp.where(x_even, chip, core)
                if own is not None:
                    every[there, at + 4 : at + 8, :] = own
                every[there, at + 8 : at + 12, :] = jnp.where(x_even, core, chip)

            for cy in range(4):
                at = 4 * cy
                every[there, 24 * cy : 24 * cy + 12, :] = window[12 * cy : 12 * cy + 12, :]
                three(
                    24 * cy + 12, faces_of[128 + at : 132 + at, :], faces_of[144 + at : 148 + at, :],
                    window[48 + at : 52 + at, :],
                )
            for at in (0, 4):
                three(
                    96 + 3 * at, faces_of[160 + at : 164 + at, :], faces_of[168 + at : 172 + at, :],
                    window[64 + at : 68 + at, :],
                )
                three(120 + at, None, faces_of[176:180, :], window[72 + at : 76 + at, :])

        row = iota((16, 128), 0)
        valid = ((row >= 4) | (x_at > 0)) & ((row < 8) | (x_at < nx - 1)) & (row < 12)
        blank = jnp.zeros((4, 128), F32)

        def twelve(value):
            return jnp.concatenate([value, blank], axis=0)

        centre = (CHEB_HIGH + CHEB_LOW) / 2.0
        half_range = (CHEB_HIGH - CHEB_LOW) / 2.0
        aspect = centre / half_range
        factor = 1.0 / aspect
        empty = jnp.zeros((16, 128), F32)
        for ref in (one, two, sol):
            ref[0] = empty
            ref[planes + 1] = empty
        for at in range(ny):
            for cy in range(4):
                plane = 4 * at + cy
                value = every[at, 24 * cy : 24 * cy + 12, :]
                if cy == 0 and at > 0:
                    value = value + every[at - 1, 108:120, :]
                if cy == 3 and at < ny - 1:
                    value = value + every[at + 1, 96:108, :]
                value = jnp.where(valid, twelve(value), 0.0)
                centre_value = 6.0 + twelve(every[at, 24 * cy + 12 : 24 * cy + 24, :]) / 16.0
                inverse = jnp.where(valid, 1.0 / (16.0 * centre_value), 0.0)
                res[plane] = value
                diag[plane] = centre_value
                inv[plane] = inverse
                direction = inverse * value / centre
                one[plane + 1] = direction
                sol[plane + 1] = direction
        now, later = one, two
        for number in range(1, SWEEPS):
            factor_next = 1.0 / (2.0 * aspect - factor)
            keep, gain = factor_next * factor, 2.0 * factor_next / half_range

            lane = iota((16, 128), 1)
            for plane in range(planes):
                here = now[plane + 1]
                total = now[plane] + now[plane + 2]
                total = total + pltpu.roll(here, 15, 0) + pltpu.roll(here, 1, 0)
                total = total + jnp.where(lane == 127, 0.0, pltpu.roll(here, 127, 1))
                total = total + jnp.where(lane == 0, 0.0, pltpu.roll(here, 1, 1))
                residual = res[plane] - 16.0 * (diag[plane] * here - total)
                res[plane] = residual
                direction = keep * here + gain * inv[plane] * residual
                later[plane + 1] = direction
                sol[plane + 1] = sol[plane + 1] + direction
            now, later = later, now
            factor = factor_next
        for plane in range(planes):
            for cx in range(4):
                slab_out[cx, plane : plane + 1, :] = sol[plane + 1, 4 + cx : 5 + cx, :]
        moves = [pltpu.make_async_copy(slab_out, coarse, sems.at[8])]
        moves[0].start()

        first_plane = 4 * y_at + 1
        below, above = first_plane - 1, first_plane + 4
        for at in range(6):
            C[at] = spread_lanes(spread_planes(sol, first_plane, 3 + at))
        outside = [[spread_lanes(sol[plane, 3 + at : 4 + at, :]) for at in range(6)] for plane in (below, above)]
        before, after = jnp.maximum(y_at - 1, 0), jnp.minimum(y_at + 1, ny - 1)
        corners = []
        for who, inside, line in ((before, y_at > 0, 1), (after, y_at < ny - 1, 0)):
            for base, there in ((0, x_at > 0), (2, x_at < nx - 1)):
                corner = jnp.concatenate(
                    [every[who, pl.ds(120 + 4 * (base + line) + j, 1), :] for j in range(4)], axis=1
                )
                corners.append(jnp.where(inside & there, corner, 0.0))
        edge_row = iota((16, 512), 0)

        def ends(first, last):
            first, last = (jnp.broadcast_to(line, (16, 512)) for line in (first, last))
            return jnp.where(edge_row == 0, first, jnp.where(edge_row == 15, last, 0.0))

        for at in range(6):
            here = C[at]
            around = beside(here, outside[0][at], outside[1][at])
            fifth_of = 0.2 * here
            if at == 0:
                U[0] = u[0] + fifth_of + g_x[0] * (around + here + C[1] + ends(corners[0], corners[2]))
            elif at == 5:
                U[17] = u[17] + fifth_of + g_x[1] * (around + here + C[4] + ends(corners[1], corners[3]))
            else:
                inner = around + 2.0 * here
                sides = [around + here + C[at - 1], inner, inner, around + here + C[at + 1]]
                for q in range(4):
                    x = 4 * (at - 1) + q
                    U[x + 1] = u[x + 1] + fifth_of + g[x] * sides[q]
        for at, (part, out, plane, inside) in enumerate(
            ((u_low, ul, below, first_plane), (u_high, uh, above, first_plane + 3))
        ):
            beyond = spread_lanes(spread_rows(sol, plane, 4))
            edge = spread_lanes(spread_rows(sol, inside, 4))
            around = beside(beyond, outside[at][0], outside[at][5])
            total = beyond + edge + around + ends(corners[2 * at], corners[2 * at + 1])
            out[...] = part[...] + 0.2 * beyond + g_y[at] * total

        for x in range(16):
            here = U[x + 1]
            total = U[x] + U[x + 2] + beside(here, ul[x : x + 1, :], uh[x : x + 1, :])
            result[x] = 0.2 * here + f[x] + g[x] * total
            if x % 2 == 1:
                part = pl.ds(x - 1, 2)
                moves.append(pltpu.make_async_copy(result.at[part], pressure.at[part], sems.at[x // 2]))
                moves[-1].start()
        for move in moves:
            move.wait()

    slab, field, long = (16, 512), (16, 16, 512), (18, 16, 512)
    core_pairs, chip_pairs = pairs_core(nx, ny), pairs_chip(nx, ny)
    row_pairs = [pairs_row(nx, ny, step) for step in range(1, ny)]
    odd_pairs = pairs_odd(nx, ny)
    inner_pairs = [
        (a, b) if 0 < a % ny < ny - 1 else (a, ((a // ny) ^ 1) * ny + a % ny) for a, b in odd_pairs
    ]

    def swap(array, pairs):
        return lax.ppermute(array, axes, pairs)

    def local(source, reaction, boundary_kind, disk_id, disk_mask, thrust):
        inputs = (source, reaction, boundary_kind, disk_id, disk_mask, thrust.reshape(1, -1))
        some = (4, 16, 512)
        core, chip, row, odd = call(
            faces,
            [(64, 128), (64, 128), (128, 128), (128, 128)],
            *(pltpu.with_memory_space_constraint(array, pltpu.HBM) for array in inputs),
            in_specs=[HBM] * 6,
            scratch=[some, some]
            + [pltpu.VMEM(some, jnp.int32)] * 3
            + [(1, thrust.shape[0]), pltpu.SemaphoreType.DMA((5, 4)), pltpu.SemaphoreType.DMA(())],
            name="faces",
        )
        a_core, a_chip = swap(core, core_pairs), swap(chip, chip_pairs)
        a_odd, a_row = swap(odd, inner_pairs), swap(row, row_pairs[0])
        f, g, d, absorb, inner, rows = call(
            set_up, [field, field, field, (16, 128), field, (4, 16, 512)], *inputs, scratch=[(64, 512)], name="set_up"
        )
        a_row, a_odd, a_chip, a_core, f, g, d, absorb, inner, rows = lax.optimization_barrier(
            (a_row, a_odd, a_chip, a_core, f, g, d, absorb, inner, rows)
        )
        to_core, sums, y_faces = call(
            early,
            [(224, 128), (16, 128), (32, 512)],
            inner, g, rows, absorb, a_core, a_chip, a_row, a_odd,
            scratch=[slab] * 2,
            name="early",
        )
        s_core = swap(to_core, core_pairs)
        s, block, y_more = call(
            restrict,
            [field, (40, 128), (32, 512)],
            f, g, d, absorb, inner, sums, a_core, a_chip, a_row, a_odd,
            scratch=[slab, slab, (64, 512)],
            name="restrict",
        )
        mine, to_chip, to_row, to_odd = call(
            to_chip_kernel,
            [(40, 128), (112, 128), (FACES, 128), (FACES, 128)],
            block, sums, absorb, s_core, s, g, y_faces, y_more,
            name="to_chip",
        )
        s_chip = swap(to_chip, chip_pairs)
        s_row, s_odd = swap(to_row, row_pairs[0]), swap(to_odd, odd_pairs)
        full, beyond, more = call(
            from_chip_kernel, [(40, 128), (40, 128), (MORE, 128)], mine, sums, s_chip, s, g, name="from_chip"
        )
        c_core, s_more = swap(full, core_pairs), swap(more, chip_pairs)
        window, short = call(
            window_kernel, [(136, 128), (80, 128)], full, beyond, c_core, s_chip, s_core, name="window"
        )
        windows = [window] + [
            swap(short if step in short_steps else window, row_pairs[step - 1]) for step in range(1, ny)
        ]
        prepared = call(
            prepare,
            [long, slab, slab, (2, 16, 512), (2, 16, 512)],
            f, g, s, a_core, a_chip, a_row, a_odd, s_core, s_chip, s_more, s_row, s_odd,
            scratch=[(2, 16, 512)],
            name="prepare",
        )
        pressure, coarse = call(
            finish,
            [field, (4, planes, 128)],
            f, g, *prepared, s_row, s_odd, *windows[::-1],
            scratch=[(ny, 136, 128)]
            + [(planes, 16, 128)] * 3
            + [(planes + 2, 16, 128)] * 3
            + [(6, 16, 512), long, slab, slab, field, (4, planes, 128), pltpu.SemaphoreType.DMA((9,))],
            out_specs=[HBM, HBM],
            name="finish",
        )
        return pressure, coarse

    spec = P("gx", "gy", None)
    return jax.shard_map(
        local,
        mesh=mesh,
        in_specs=(spec, spec, spec, spec, spec, P()),
        out_specs=(spec, P("gx", None, None)),
        check_vma=False,
    )
```
